32 devices in a mesh: dp: 4 (over y, core), seq: 8 (over z, x).
Axes of the slice: x: 2, y: 2, z: 4, core: 2. Of those that a mesh axis runs over, the one named last changes fastest.
Arguments:
- tokens: bfloat16 [8, 1024, 2048], P('dp', 'seq'), may hold values from -6 to 6
- lengths: int32 [8], P('dp'), may hold values from 256 to 1024, as said below
- norm_gain: float32 [2048], replicated, may hold values from 0.5 to 1.5
- in_weight: bfloat16 [2048, 6144], P('seq'), may hold values from -0.125 to 0.125
- conv_taps: float32 [3, 6144], replicated, may hold values from -3 to 3
- filter_residue: float32 [2048, 16], replicated, may hold values from -0.0625 to 0.0625
- filter_decay: float32 [2048, 16], replicated, may hold values from 0.00048828125 to 0.03125
- out_weight: bfloat16 [2048, 2048], P('seq'), may hold values from -0.125 to 0.125
- feed_gain: float32 [2048], replicated, may hold values from 0.5 to 1.5
- gate_weight: bfloat16 [2048, 5632], P('seq'), may hold values from -0.125 to 0.125
- up_weight: bfloat16 [2048, 5632], P('seq'), may hold values from -0.125 to 0.125
- down_weight: bfloat16 [5632, 2048], P('seq'), may hold values from -0.078125 to 0.078125
- cotangent: bfloat16 [8, 1024, 2048], P('dp', 'seq'), may hold values from -6 to 6
Outputs:
- output: bfloat16 [8, 1024, 2048], P('dp', 'seq')
- grad_tokens: bfloat16 [8, 1024, 2048], P('dp', 'seq')
- grad_norm_gain: float32 [2048], replicated
- grad_in_weight: float32 [2048, 6144], P('seq')
- grad_conv_taps: float32 [3, 6144], replicated
- grad_filter_residue: float32 [2048, 16], replicated
- grad_filter_decay: float32 [2048, 16], replicated
- grad_out_weight: float32 [2048, 2048], P('seq')
- grad_feed_gain: float32 [2048], replicated
- grad_gate_weight: float32 [2048, 5632], P('seq')
- grad_up_weight: float32 [2048, 5632], P('seq')
- grad_down_weight: float32 [5632, 2048], P('seq')
The draws below stay inside these ranges and needn't reach their ends.
Inputs may be any that keep to these rules, and one draw needn't show every extreme that they name: `lengths`: in each aligned block of 2 sequences (those of one index of dp) one sequence is valid to the full 1024 positions.
All inputs are finite; a program needn't handle non-finite values.
Results may differ from the reference program's by a relative error of at most 0.019.
Values may be sent and summed in bfloat16 or wider, within the bound.
No kernel may reach another device: no remote copies, remote signals or barrier semaphores. Data moves between devices by JAX's collectives and lax.ppermute only.
A program may use at most 640 MiB of HBM per device.

```python
import jax
import jax.numpy as jnp
from jax import lax

D = 2048
FF = 5632
POLES = 16
SEQS_DEV = 2
SEQ_LEN = 1024
SEQS = 8


def draw_lengths(key, part):
    key_span, key_pick = jax.random.split(key)
    groups = SEQS // SEQS_DEV
    spans = jax.random.randint(key_span, (groups, SEQS_DEV), SEQ_LEN // 4, SEQ_LEN + 1)
    chosen = jax.random.randint(key_pick, (groups, 1), 0, SEQS_DEV)
    spans = jnp.where(jnp.arange(SEQS_DEV)[None, :] == chosen, SEQ_LEN, spans)
    return spans.reshape(SEQS).astype(jnp.int32)


def draw_filter_decay(key, part):
    lowest = 0.5 / SEQ_LEN
    top_rate = 0.03125
    share = jax.random.uniform(key, (D, POLES), jnp.float32)
    spread = jnp.log(jnp.float32(top_rate)) - jnp.log(jnp.float32(lowest))
    return jnp.exp(jnp.log(jnp.float32(lowest)) + share * spread).astype(jnp.float32)


def steps_of(rng, extent, shards, least, top_value):
    def one(axis_at, parts):
        heights = jax.random.uniform(jax.random.fold_in(jax.random.fold_in(rng, 6), axis_at), (parts,), jnp.float32, least / len(shards), top_value / len(shards))
        return jnp.repeat(jnp.exp(heights), extent[axis_at] // parts).reshape((-1,) + (1,) * (len(extent) - axis_at - 1))

    level = one(*shards[0])
    for cut in shards[1:]:
        level = level * one(*cut)
    return level


def normal_values(own_key, shape, deviation, most, cuts=(), held_as=jnp.bfloat16):
    array = jax.random.normal(own_key, shape, jnp.float32) * deviation
    if len(cuts) > 0:
        array = steps_of(own_key, shape, cuts, -0.22, 0.18) * array
    return jnp.clip(array, min=-most, max=most).astype(held_as)


def setup_inputs(seed: int = 0) -> dict:
    key_list = jax.random.split(jax.random.key(seed), 14)
    tokens = normal_values(key_list[0], (SEQS, SEQ_LEN, D), 1.0, 6.0, ((0, 4), (1, 8)))
    lengths = draw_lengths(jax.random.fold_in(key_list[13], 71), 0)
    norm_gain = jnp.clip(1.0 + 0.1 * jax.random.normal(key_list[2], (D,), jnp.float32), 0.5, 1.5)
    in_weight = normal_values(key_list[3], (D, 3 * D), D ** -0.5, 0.125, ((0, 8),))
    conv_taps = normal_values(key_list[4], (3, 3 * D), 0.6, 3.0, (), jnp.float32)
    filter_residue = normal_values(key_list[5], (D, POLES), ((4 * SEQ_LEN) ** -0.5), 0.0625, (), jnp.float32)
    filter_decay = draw_filter_decay(jax.random.fold_in(key_list[13], 71), 0)
    out_weight = normal_values(key_list[7], (D, D), D ** -0.5, 0.125, ((0, 8),))
    feed_gain = jnp.clip(1.0 + 0.1 * jax.random.normal(key_list[8], (D,), jnp.float32), 0.5, 1.5)
    gate_weight = normal_values(key_list[9], (D, FF), D ** -0.5, 0.125, ((0, 8),))
    up_weight = normal_values(key_list[10], (D, FF), D ** -0.5, 0.125, ((0, 8),))
    down_weight = normal_values(key_list[11], (FF, D), FF ** -0.5, 0.078125, ((0, 8),))
    cotangent = normal_values(key_list[12], (SEQS, SEQ_LEN, D), 1.0, 6.0, ((0, 4), (1, 8)))
    return dict(tokens=tokens, lengths=lengths, norm_gain=norm_gain, in_weight=in_weight, conv_taps=conv_taps, filter_residue=filter_residue, filter_decay=filter_decay, out_weight=out_weight, feed_gain=feed_gain, gate_weight=gate_weight, up_weight=up_weight, down_weight=down_weight, cotangent=cotangent)


epsilon = 1e-06
highest = lax.Precision.HIGHEST

@jax.custom_vjp
def low(v):
    return lax.optimization_barrier(v.astype(jnp.bfloat16)).astype(jnp.float32)

@jax.custom_vjp
def low_back(v):
    return v

def low_keep(v):
    return (low(v), None)

def low_pass(kept, grad):
    return (grad,)

def back_keep(v):
    return (v, None)

def back_low(kept, grad):
    return (low(grad),)
low.defvjp(low_keep, low_pass)
low_back.defvjp(back_keep, back_low)

def rms_scale(values):
    return lax.rsqrt(lax.optimization_barrier(jnp.mean(values * values, axis=-1, keepdims=True)) + epsilon)

def mode_filter(residue, decay):
    steps = jnp.arange(SEQ_LEN).astype(jnp.float32)[:, None]
    total = jnp.zeros((SEQ_LEN, D), jnp.float32)
    for pole in range(POLES):
        total = total + residue[:, pole][None, :] * jnp.exp(-decay[:, pole][None, :] * steps)
    return total

def long_conv(signal, response):
    size = 2 * SEQ_LEN
    spectrum = jnp.fft.rfft(signal, n=size, axis=1) * jnp.fft.rfft(response, n=size, axis=0)[None]
    return jnp.fft.irfft(spectrum, n=size, axis=1)[:, :SEQ_LEN]

def block_forward(params, hidden, mask):
    norm_gain, in_weight, conv_taps, filter_residue, filter_decay, out_weight, feed_gain, gate_weight, up_weight, down_weight = params
    normed = low(hidden * rms_scale(hidden) * norm_gain)
    mixed = low(low_back(jnp.einsum('gtd,de->gte', normed, in_weight, precision=highest)))
    padded = jnp.pad(mixed, ((0, 0), (2, 0), (0, 0)))
    short = conv_taps[0] * mixed + conv_taps[1] * padded[:, 1:SEQ_LEN + 1] + conv_taps[2] * padded[:, :SEQ_LEN]
    query = short[..., :D]
    keys = short[..., D:2 * D]
    values = short[..., 2 * D:]
    product = low(low_back(keys * values))
    response = mode_filter(filter_residue, filter_decay)
    convolved = low(low_back(long_conv(product, response)))
    gated = low(query * convolved)
    mixer_out = low_back(jnp.einsum('gtd,de->gte', gated, out_weight, precision=highest))
    middle = hidden + mixer_out
    normed_two = low(middle * rms_scale(middle) * feed_gain)
    gate = low_back(jnp.einsum('gtd,df->gtf', normed_two, gate_weight, precision=highest))
    upper = low_back(jnp.einsum('gtd,df->gtf', normed_two, up_weight, precision=highest))
    active = low(jax.nn.silu(gate) * upper)
    feed = low_back(jnp.einsum('gtf,fd->gtd', active, down_weight, precision=highest))
    return mask * (middle + feed)

def reference(tokens, lengths, norm_gain, in_weight, conv_taps, filter_residue, filter_decay, out_weight, feed_gain, gate_weight, up_weight, down_weight, cotangent):
    params = tuple((item.astype(jnp.float32) for item in (norm_gain, in_weight, conv_taps, filter_residue, filter_decay, out_weight, feed_gain, gate_weight, up_weight, down_weight)))
    group = 1
    for option in range(1, SEQS + 1):
        if SEQS % option == 0 and option * SEQ_LEN <= 4096:
            group = option
    rounds = SEQS // group
    inputs = tokens.reshape(rounds, group, SEQ_LEN, D)
    spans = lengths.reshape(rounds, group)
    upstream = cotangent.reshape(rounds, group, SEQ_LEN, D)
    positions = jnp.arange(SEQ_LEN).astype(jnp.int32)

    def one_round(totals, pieces):
        block, span, upstream_part = pieces
        mask = (positions[None, :] < span[:, None]).astype(jnp.float32)[..., None]

        def run_block(weights, values):
            return block_forward(weights, values, mask)
        result, pull = jax.vjp(run_block, params, block.astype(jnp.float32))
        weight_grads, input_grad = pull(upstream_part.astype(jnp.float32))
        totals = jax.tree.map(jnp.add, totals, weight_grads)
        return (totals, (result.astype(jnp.bfloat16), input_grad.astype(jnp.bfloat16)))
    zeros = jax.tree.map(jnp.zeros_like, params)
    totals, (outputs, input_grads) = lax.scan(one_round, zeros, (inputs, spans, upstream))
    return (outputs.reshape(SEQS, SEQ_LEN, D), input_grads.reshape(SEQS, SEQ_LEN, D), totals[0], totals[1], totals[2], totals[3], totals[4], totals[5], totals[6], totals[7], totals[8], totals[9])
```

```python
import jax
import jax.numpy as jnp
from jax import lax
from jax.experimental import pallas as pl
from jax.experimental.pallas import tpu as pltpu
from jax.sharding import Mesh, PartitionSpec as P

epsilon = 1e-06
low = jnp.bfloat16
wide = jnp.float32
tile = 8
depth = 4
cores = 2


def turned(value, axis, by):
    length = lax.axis_size(axis)
    return lax.ppermute(value, axis, [(i, (i + by) % length) for i in range(length)])


def passed(value, axis, by):
    length = lax.axis_size(axis)
    pairs = [(i, i + by) for i in range(length) if 0 <= i + by < length]
    return lax.ppermute(value, axis, pairs)


def gather_slots(value, axis):
    length = lax.axis_size(axis)
    return jnp.stack([value] + [turned(value, axis, -d) for d in range(1, length)])


def sum_slots(partial, axis):
    length = lax.axis_size(axis)
    total = partial[0]
    for d in range(1, length):
        total = total + turned(partial[d].astype(low), axis, d).astype(wide)
    return total


def sum_axis(value, axis):
    length = lax.axis_size(axis)
    total = value
    for d in range(1, length):
        total = total + turned(value, axis, d)
    return total


def in_order(slots, axis):
    length = lax.axis_size(axis)
    place = lax.axis_index(axis)
    return jnp.stack(
        [lax.dynamic_index_in_dim(slots, (j - place) % length, 0, False) for j in range(length)]
    )


def gather_tokens(value):
    half = value.shape[0] // 2
    width = value.shape[-1]
    first = gather_slots(gather_slots(value[:half], "x"), "y")
    second = gather_slots(gather_slots(value[half:], "y"), "x")
    own = jnp.stack([first, jnp.swapaxes(second, 0, 1)])
    own = own.reshape(-1, width)
    length = lax.axis_size("c")
    return [own] + [turned(own, "c", -d) for d in range(1, length)]


def scatter_tokens(near, far, batch):
    width = near.shape[-1]
    total = near
    for d, part in enumerate(far):
        total = total + turned(part, "c", d + 1).astype(wide)
    grid = total.reshape(2, lax.axis_size("y"), lax.axis_size("x"), batch // 2, -1, width)
    first = sum_slots(sum_slots(jnp.swapaxes(grid[0], 0, 1), "x"), "y")
    second = sum_slots(sum_slots(grid[1], "y"), "x")
    return jnp.concatenate([first, second], axis=0)


def segments(weight, groups, offset):
    rows = weight.shape[0]
    spread = lax.axis_size("x")
    pairs = lax.axis_size("y") * lax.axis_size("c")
    pair = lax.axis_index("y") * lax.axis_size("c") + lax.axis_index("c")
    part = weight.shape[1] // (groups * depth * spread * pairs)
    place = (lax.axis_index("x") + offset) % spread
    picked = []
    for g in range(groups):
        for k in range(depth):
            start = (((g * depth + k) * spread + place) * pairs + pair) * part
            picked.append(lax.dynamic_slice_in_dim(weight, start, part, 1))
    return jnp.concatenate(picked, axis=1)


def column_tile(weight, groups):
    spread = lax.axis_size("x")
    place = lax.axis_index("x")
    got = jnp.stack(
        [segments(weight, groups, 0)]
        + [turned(segments(weight, groups, d), "x", d) for d in range(1, spread)]
    )
    ordered = jnp.stack(
        [lax.dynamic_index_in_dim(got, (place - j) % spread, 0, False) for j in range(spread)]
    )
    return lax.all_gather(ordered.reshape(-1, got.shape[-1]), "z", axis=0, tiled=True)


def row_tile(weight):
    pairs = lax.axis_size("y") * lax.axis_size("c")
    pair = lax.axis_index("y") * lax.axis_size("c") + lax.axis_index("c")
    part = weight.shape[0] // pairs
    return lax.all_gather(
        lax.dynamic_slice_in_dim(weight, pair * part, part, 0), "z", axis=0, tiled=True
    )


def column_owner(term, groups):
    spread, ycount, ccount = lax.axis_size("x"), lax.axis_size("y"), lax.axis_size("c")
    place = lax.axis_index("x")
    mine = lax.psum_scatter(term, "z", scatter_dimension=0, tiled=True)
    rows = mine.shape[0] // spread
    parts = mine.reshape(spread, rows, -1)
    slots = jnp.stack(
        [lax.dynamic_index_in_dim(parts, place, 0, False)]
        + [
            turned(lax.dynamic_index_in_dim(parts, (place - d) % spread, 0, False), "x", -d)
            for d in range(1, spread)
        ]
    )
    whole = gather_slots(gather_slots(slots, "y"), "c")
    part = mine.shape[1] // (groups * depth)
    pieces = []
    cplace, yplace = lax.axis_index("c"), lax.axis_index("y")
    ranks = {}
    flat = whole.reshape(-1, rows, mine.shape[1])
    for j in range(spread):
        for yy in range(ycount):
            for cc in range(ccount):
                slot = ((cc - cplace) % ccount * ycount + (yy - yplace) % ycount) * spread + (
                    j - place
                ) % spread
                ranks[j, yy, cc] = lax.dynamic_index_in_dim(flat, slot, 0, False)
    for g in range(groups):
        for k in range(depth):
            for j in range(spread):
                for yy in range(ycount):
                    for cc in range(ccount):
                        at = (g * depth + k) * part
                        pieces.append(ranks[j, yy, cc][:, at : at + part])
    return jnp.concatenate(pieces, axis=1).astype(wide)


def row_owner(term):
    mine = lax.psum_scatter(term, "z", scatter_dimension=0, tiled=True)
    whole = in_order(gather_slots(mine, "y"), "y")
    whole = in_order(gather_slots(whole, "c"), "c")
    return jnp.swapaxes(whole, 0, 1).reshape(-1, term.shape[1]).astype(wide)


def rank_rows(values, axis):
    spread, pairs = lax.axis_size("x"), lax.axis_size("y") * lax.axis_size("c")
    pair = lax.axis_index("y") * lax.axis_size("c") + lax.axis_index("c")
    part = values.shape[axis] // (depth * spread * pairs)
    return jnp.concatenate(
        [
            lax.dynamic_slice_in_dim(
                values, ((k * spread + lax.axis_index("x")) * pairs + pair) * part, part, axis
            )
            for k in range(depth)
        ],
        axis=axis,
    )


def all_channels(values):
    rows = values.shape[0]
    whole = in_order(gather_slots(values, "x"), "x")
    whole = in_order(gather_slots(whole, "y"), "y")
    whole = in_order(gather_slots(whole, "c"), "c")
    spread, ycount, ccount = lax.axis_size("x"), lax.axis_size("y"), lax.axis_size("c")
    whole = whole.reshape(ccount, ycount, spread, rows, depth, -1)
    return jnp.transpose(whole, (3, 4, 2, 1, 0, 5)).reshape(rows, -1)


def fill(source, target, place):
    groups, parts, inner, length = source.shape[:4]
    for j in range(parts):
        slot = lax.rem(j + parts - place, parts)
        for g in range(groups):
            for b in range(inner):
                target[g * inner + b, j * length : (j + 1) * length, :] = source[g, slot, b].astype(
                    wide
                )


def empty(source, target, place):
    groups, parts, inner, length = target.shape[:4]
    for j in range(parts):
        slot = lax.rem(j + parts - place, parts)
        for g in range(groups):
            for b in range(inner):
                target[g, slot, b] = source[g * inner + b, j * length : (j + 1) * length, :].astype(
                    low
                )


def halves(ref):
    return [ref[k * tile : (k + 1) * tile, :] for k in range(ref.shape[0] // tile)]


def row_of(ref, seq, at):
    return ref[seq, pl.ds(at, tile, stride=0), :]


def states_kernel(place_ref, signal_ref, decay_ref, state_ref, slope_ref, held):
    fill(signal_ref, held, place_ref[0])
    seqs, length, lanes = held.shape
    keep = [jnp.exp(-d) for d in halves(decay_ref)]
    count = len(keep)
    zero = jnp.zeros((tile, lanes), wide)

    def step(i, carry):
        state, slope = [list(v) for v in carry]
        for k in range(tile):
            for n in range(seqs):
                new = row_of(held, n, i * tile + k)
                for h in range(count):
                    at = n * count + h
                    slope[at] = keep[h] * (slope[at] + state[at])
                    state[at] = keep[h] * state[at] + new
        return tuple(state), tuple(slope)

    start = tuple(zero for _ in range(seqs * count))
    state, slope = lax.fori_loop(0, length // tile, step, (start, start))
    for n in range(seqs):
        for h in range(count):
            state_ref[n, h * tile : (h + 1) * tile, :] = state[n * count + h]
            slope_ref[n, h * tile : (h + 1) * tile, :] = slope[n * count + h]


def forward_kernel(place_ref, signal_ref, decay_ref, residue_ref, start_ref, out_ref, held, terms, made):
    fill(signal_ref, held, place_ref[0])
    seqs, length, lanes = held.shape
    keep = [jnp.exp(-d) for d in halves(decay_ref)]
    weigh = halves(residue_ref)
    count = len(keep)

    def step(i, carry):
        state = list(carry)
        for k in range(tile):
            for n in range(seqs):
                new = row_of(held, n, i * tile + k)
                total = None
                for h in range(count):
                    at = n * count + h
                    state[at] = keep[h] * state[at] + new
                    term = weigh[h] * state[at]
                    total = term if total is None else total + term
                terms[n, k * tile : (k + 1) * tile, :] = total
        for n in range(seqs):
            result = terms[n, pl.ds(0, tile, stride=tile), :]
            for p in range(1, tile):
                result = result + terms[n, pl.ds(p, tile, stride=tile), :]
            made[n, pl.ds(i * tile, tile), :] = result
        return tuple(state)

    start = tuple(
        start_ref[n, h * tile : (h + 1) * tile, :] for n in range(seqs) for h in range(count)
    )
    lax.fori_loop(0, length // tile, step, start)
    empty(made, out_ref, place_ref[0])


def later_kernel(place_ref, signal_ref, decay_ref, state_ref, held):
    fill(signal_ref, held, place_ref[0])
    seqs, length, lanes = held.shape
    keep = [jnp.exp(-d) for d in halves(decay_ref)]
    count = len(keep)

    def step(i, carry):
        state = list(carry)
        base = length - tile - i * tile
        for k in range(tile - 1, -1, -1):
            for n in range(seqs):
                new = row_of(held, n, base + k)
                for h in range(count):
                    at = n * count + h
                    state[at] = keep[h] * state[at] + new
        return tuple(state)

    zero = jnp.zeros((tile, lanes), wide)
    state = lax.fori_loop(0, length // tile, step, tuple(zero for _ in range(seqs * count)))
    for n in range(seqs):
        for h in range(count):
            state_ref[n, h * tile : (h + 1) * tile, :] = state[n * count + h]


def backward_kernel(
    place_ref,
    signal_ref,
    grad_ref,
    decay_ref,
    residue_ref,
    start_ref,
    slope_ref,
    end_ref,
    out_ref,
    residue_grad_ref,
    decay_grad_ref,
    held,
    grads,
    terms,
    made,
):
    fill(signal_ref, held, place_ref[0])
    fill(grad_ref, grads, place_ref[0])
    seqs, length, lanes = held.shape
    keep = [jnp.exp(-d) for d in halves(decay_ref)]
    weigh = halves(residue_ref)
    count = len(keep)
    zero = jnp.zeros((tile, lanes), wide)

    def ahead(i, carry):
        state, slope, first, second = [list(v) for v in carry]
        for k in range(tile):
            for n in range(seqs):
                new = row_of(held, n, i * tile + k)
                back = row_of(grads, n, i * tile + k)
                for h in range(count):
                    at = n * count + h
                    slope[at] = keep[h] * (slope[at] + state[at])
                    state[at] = keep[h] * state[at] + new
                    first[at] = first[at] + back * state[at]
                    second[at] = second[at] + back * slope[at]
        return tuple(state), tuple(slope), tuple(first), tuple(second)

    def load(ref):
        return tuple(
            ref[n, h * tile : (h + 1) * tile, :] for n in range(seqs) for h in range(count)
        )

    none = tuple(zero for _ in range(seqs * count))
    _, _, first, second = lax.fori_loop(
        0, length // tile, ahead, (load(start_ref), load(slope_ref), none, none)
    )
    for h in range(count):
        sum_first, sum_second = first[h], second[h]
        for n in range(1, seqs):
            sum_first = sum_first + first[n * count + h]
            sum_second = sum_second + second[n * count + h]
        residue_grad_ref[h * tile : (h + 1) * tile, :] = sum_first
        decay_grad_ref[h * tile : (h + 1) * tile, :] = -weigh[h] * sum_second

    def back_step(i, carry):
        state = list(carry)
        base = length - tile - i * tile
        for k in range(tile - 1, -1, -1):
            for n in range(seqs):
                new = row_of(grads, n, base + k)
                total = None
                for h in range(count):
                    at = n * count + h
                    state[at] = keep[h] * state[at] + new
                    term = weigh[h] * state[at]
                    total = term if total is None else total + term
                terms[n, k * tile : (k + 1) * tile, :] = total
        for n in range(seqs):
            result = terms[n, pl.ds(0, tile, stride=tile), :]
            for p in range(1, tile):
                result = result + terms[n, pl.ds(p, tile, stride=tile), :]
            made[n, pl.ds(base, tile), :] = result
        return tuple(state)

    lax.fori_loop(0, length // tile, back_step, load(end_ref))
    empty(made, out_ref, place_ref[0])


def conv_call(kernel, place, arrays, results, scratch, flops):
    channels = arrays[0].shape[-1]
    lanes = min(channels, 128)

    def spec(shape):
        lead = len(shape) - 1
        return pl.BlockSpec(shape[:-1] + (lanes,), lambda i, *_: (0,) * lead + (i,))

    return pl.pallas_call(
        kernel,
        out_shape=results,
        grid_spec=pltpu.PrefetchScalarGridSpec(
            num_scalar_prefetch=1,
            grid=(channels // lanes,),
            in_specs=[spec(a.shape) for a in arrays],
            out_specs=[spec(r.shape) for r in results],
            scratch_shapes=[pltpu.VMEM(s + (lanes,), wide) for s in scratch],
        ),
        compiler_params=pltpu.CompilerParams(
            dimension_semantics=("arbitrary",), vmem_limit_bytes=48 << 20
        ),
        cost_estimate=pl.CostEstimate(
            flops=flops, transcendentals=0, bytes_accessed=sum(a.size * 4 for a in arrays)
        ),
    )(place, *arrays)


def sizes(signal, poles):
    groups, parts, inner, length, channels = signal.shape
    return groups * inner, parts * length, channels, signal.size * poles


def states_of(place, signal, decay):
    seqs, length, channels, work = sizes(signal, decay.shape[0])
    shape = jax.ShapeDtypeStruct((seqs, decay.shape[0], channels), wide)
    return conv_call(
        states_kernel, place, [signal, decay], [shape, shape], [(seqs, length)], 4 * work
    )


def forward_of(place, signal, decay, residue, start):
    seqs, length, channels, work = sizes(signal, decay.shape[0])
    return conv_call(
        forward_kernel,
        place,
        [signal, decay, residue, start],
        [jax.ShapeDtypeStruct(signal.shape, low)],
        [(seqs, length), (seqs, tile * tile), (seqs, length)],
        4 * work,
    )[0]


def later_of(place, signal, decay):
    seqs, length, channels, work = sizes(signal, decay.shape[0])
    shape = jax.ShapeDtypeStruct((seqs, decay.shape[0], channels), wide)
    return conv_call(later_kernel, place, [signal, decay], [shape], [(seqs, length)], 2 * work)[0]


def backward_of(place, signal, grad, decay, residue, start, slope, end):
    seqs, length, channels, work = sizes(signal, decay.shape[0])
    shape = jax.ShapeDtypeStruct(decay.shape, wide)
    return conv_call(
        backward_kernel,
        place,
        [signal, grad, decay, residue, start, slope, end],
        [jax.ShapeDtypeStruct(signal.shape, low), shape, shape],
        [(seqs, length), (seqs, length), (seqs, tile * tile), (seqs, length)],
        12 * work,
    )


def rms_scale(values):
    return lax.rsqrt(jnp.mean(values * values, axis=-1, keepdims=True) + epsilon)


def norm_back(values, scale, gain, grad_normed):
    grad_gain = jnp.sum(grad_normed * values * scale, axis=(0, 1))
    scaled = grad_normed * gain
    grad_values = scale * scaled - values * scale * scale * scale * jnp.mean(
        scaled * values, axis=-1, keepdims=True
    )
    return (grad_values, grad_gain)


def dot(a, b, kind=wide):
    return jnp.dot(a, b, preferred_element_type=wide).astype(kind)


def dot_t(a, b, kind=wide):
    return lax.dot_general(a, b, (((1,), (1,)), ((), ())), preferred_element_type=wide).astype(kind)


def dot_w(a, b):
    return lax.dot_general(a, b, (((0,), (0,)), ((), ())), preferred_element_type=wide).astype(low)


def body(
    tokens,
    lengths,
    norm_gain,
    in_weight,
    conv_taps,
    filter_residue,
    filter_decay,
    out_weight,
    feed_gain,
    gate_weight,
    up_weight,
    down_weight,
    cotangent,
):
    spread = lax.axis_size("x")
    batch, local, width = tokens.shape
    place = lax.axis_index("z") * spread + lax.axis_index("x")
    position = place * local + jnp.arange(local)
    mask = (position[None, :] < lengths[:, None]).astype(wide)[..., None]
    block = spread * local

    w_in = column_tile(in_weight, 3)
    w_out = row_tile(out_weight)
    w_gate = column_tile(gate_weight, 1)
    w_up = column_tile(up_weight, 1)
    w_down = row_tile(down_weight)

    hidden = tokens.astype(wide)
    scale_one = rms_scale(hidden)
    normed = (hidden * scale_one * norm_gain).astype(low)
    normed_all = gather_tokens(normed)
    grad_out = cotangent.astype(wide) * mask
    grad_feed_all = gather_tokens(grad_out.astype(low))

    channels = w_out.shape[0]
    ycount = lax.axis_size("y")
    grid = (2 * ycount, spread, batch // 2, local)
    taps = jnp.concatenate(
        [rank_rows(conv_taps[:, g * width : (g + 1) * width], 1) for g in range(3)], axis=1
    )
    decay = rank_rows(filter_decay, 0).T
    residue = rank_rows(filter_residue, 0).T
    mixed = [dot(v, w_in, low).reshape(grid + (3 * channels,)) for v in normed_all]
    opening = (lax.axis_index("x") + jnp.arange(spread)) % spread == 0
    opening = opening[None, :, None, None, None]
    closing = (lax.axis_index("x") + jnp.arange(spread)) % spread == spread - 1
    closing = closing[None, :, None, None, None]

    tails = jnp.stack([jnp.roll(m[:, :, :, local - 2 :], 1, axis=1) for m in mixed])
    from_z = passed(tails, "z", 1)
    extended = []
    for m, tail, behind in zip(mixed, tails, from_z):
        extended.append(jnp.concatenate([jnp.where(opening, behind, tail), m], axis=3).astype(wide))
    short = [
        taps[0] * e[:, :, :, 2:] + taps[1] * e[:, :, :, 1:-1] + taps[2] * e[:, :, :, :-2]
        for e in extended
    ]
    query = [s[..., :channels] for s in short]
    keys = [s[..., channels : 2 * channels] for s in short]
    values = [s[..., 2 * channels :] for s in short]
    product = [(k * v).astype(low) for k, v in zip(keys, values)]

    spot = lax.axis_index("x").astype(jnp.int32).reshape(1)
    ends = [states_of(spot, p, decay) for p in product]
    state_end = jnp.stack([e[0] for e in ends])
    slope_end = jnp.stack([e[1] for e in ends])
    states = [passed(state_end, "z", k) for k in range(1, depth)]
    start = states[0]
    for k in range(1, depth - 1):
        start = start + jnp.exp(-decay * (k * block)) * states[k]
    convolved = [forward_of(spot, p, decay, residue, s) for p, s in zip(product, start)]
    gated = [(q * c.astype(wide)).astype(low).reshape(-1, channels) for q, c in zip(query, convolved)]
    mixer = scatter_tokens(dot(gated[0], w_out), [dot(g, w_out, low) for g in gated[1:]], batch)
    middle = hidden + mixer

    scale_two = rms_scale(middle)
    normed_two = (middle * scale_two * feed_gain).astype(low)
    normed_two_all = gather_tokens(normed_two)
    active, grad_gate, grad_upper = [], [], []
    for v, g in zip(normed_two_all, grad_feed_all):
        gate = dot(v, w_gate)
        upper = dot(v, w_up)
        sigma = jax.nn.sigmoid(gate)
        active.append((gate * sigma * upper).astype(low))
        grad_active = dot_t(g, w_down)
        grad_gate.append((grad_active * upper * sigma * (1.0 + gate * (1.0 - sigma))).astype(low))
        grad_upper.append((grad_active * gate * sigma).astype(low))

    def back_of(k, kind):
        return (dot_t(grad_gate[k], w_gate) + dot_t(grad_upper[k], w_up)).astype(kind)

    far = [back_of(k, low) for k in range(1, len(active))]
    grad_normed_two = scatter_tokens(back_of(0, wide), far, batch)
    feed = scatter_tokens(dot(active[0], w_down), [dot(a, w_down, low) for a in active[1:]], batch)
    output = (mask * (middle + feed)).astype(low)

    def joined(parts):
        return jnp.concatenate(parts, axis=0)

    normed_two_full = joined(normed_two_all)
    grad_down = row_owner(dot_w(joined(active), joined(grad_feed_all)))
    grad_gate_weight = column_owner(dot_w(normed_two_full, joined(grad_gate)), 1)
    grad_up_weight = column_owner(dot_w(normed_two_full, joined(grad_upper)), 1)

    grad_middle, grad_feed_gain = norm_back(middle, scale_two, feed_gain, grad_normed_two)
    grad_middle = grad_middle + grad_out
    grad_mix_all = gather_tokens(grad_middle.astype(low))
    grad_out_weight = row_owner(dot_w(joined(gated), joined(grad_mix_all)))

    grad_gated = [dot_t(g, w_out).reshape(grid + (channels,)) for g in grad_mix_all]
    grad_query = [g * c.astype(wide) for g, c in zip(grad_gated, convolved)]
    grad_conv = [(g * q).astype(low) for g, q in zip(grad_gated, query)]
    slopes = [passed(slope_end, "z", k) for k in range(1, depth)]
    slope = slopes[0]
    for k in range(1, depth - 1):
        slope = slope + jnp.exp(-decay * (k * block)) * (slopes[k] + (k * block) * states[k])
    later_end = jnp.stack([later_of(spot, g, decay) for g in grad_conv])
    laters = [passed(later_end, "z", -k) for k in range(1, depth)]
    later = laters[0]
    for k in range(1, depth - 1):
        later = later + jnp.exp(-decay * (k * block)) * laters[k]
    backs = [
        backward_of(spot, product[k], grad_conv[k], decay, residue, start[k], slope[k], later[k])
        for k in range(len(product))
    ]
    grad_product = [b[0].astype(wide) for b in backs]
    grad_poles = jnp.concatenate(
        [sum(b[1] for b in backs[1:]) + backs[0][1], sum(b[2] for b in backs[1:]) + backs[0][2]],
        axis=0,
    )
    grad_short = [
        jnp.concatenate([q, p * v, p * k], axis=-1)
        for q, p, v, k in zip(grad_query, grad_product, values, keys)
    ]
    heads = jnp.stack([jnp.roll(g[:, :, :, :2].astype(low), -1, axis=1) for g in grad_short])
    from_next = passed(heads, "z", -1)
    grad_mixed, grad_taps = [], []
    for g, e, head, ahead in zip(grad_short, extended, heads, from_next):
        whole = jnp.concatenate([g, jnp.where(closing, ahead, head).astype(wide)], axis=3)
        grad_mixed.append(
            (
                taps[0] * whole[:, :, :, :-2] + taps[1] * whole[:, :, :, 1:-1] + taps[2] * whole[:, :, :, 2:]
            )
            .astype(low)
            .reshape(-1, 3 * channels)
        )
        grad_taps.append(
            jnp.stack(
                [
                    jnp.sum(g * e[:, :, :, 2:], axis=(0, 1, 2, 3)),
                    jnp.sum(g * e[:, :, :, 1:-1], axis=(0, 1, 2, 3)),
                    jnp.sum(g * e[:, :, :, :-2], axis=(0, 1, 2, 3)),
                ]
            )
        )
    grad_taps = sum(grad_taps[1:]) + grad_taps[0]
    grad_in_weight = column_owner(dot_w(joined(normed_all), joined(grad_mixed)), 3)
    grad_normed = scatter_tokens(
        dot_t(grad_mixed[0], w_in), [dot_t(g, w_in, low) for g in grad_mixed[1:]], batch
    )
    grad_hidden, grad_norm_gain = norm_back(hidden, scale_one, norm_gain, grad_normed)
    grad_tokens = (grad_hidden + grad_middle).astype(low)

    gains = jnp.stack([grad_norm_gain, grad_feed_gain])
    for axis in ("x", "y", "c", "z"):
        gains = sum_axis(gains, axis)
    small = jnp.concatenate(
        [grad_poles]
        + [grad_taps[:, g * channels : (g + 1) * channels] for g in range(3)],
        axis=0,
    )
    small = all_channels(sum_axis(small, "z"))
    poles = decay.shape[0]
    grad_residue = small[:poles].T
    grad_decay = small[poles : 2 * poles].T
    grad_conv_taps = jnp.concatenate(
        [small[2 * poles + 3 * g : 2 * poles + 3 * g + 3] for g in range(3)], axis=1
    )
    return (
        output,
        grad_tokens,
        gains[0],
        grad_in_weight,
        grad_conv_taps,
        grad_residue,
        grad_decay,
        grad_out_weight,
        gains[1],
        grad_gate_weight,
        grad_up_weight,
        grad_down,
    )


def solution(mesh):
    pairs, blocks = mesh.shape["dp"], mesh.shape["seq"]
    devices = mesh.devices.reshape(pairs // cores, cores, depth, blocks // depth)
    inner = Mesh(devices, ("y", "c", "z", "x"))
    dp, seq = ("y", "c"), ("z", "x")
    tokens, rows = P(dp, seq, None), P(seq, None)
    return jax.shard_map(
        body,
        mesh=inner,
        in_specs=(
            tokens,
            P(dp),
            P(),
            rows,
            P(),
            P(),
            P(),
            rows,
            P(),
            rows,
            rows,
            rows,
            tokens,
        ),
        out_specs=(tokens, tokens, P(), rows, P(), P(), P(), rows, P(), rows, rows, rows),
        check_vma=False,
    )
```

```python
import jax
import jax.numpy as jnp
from jax import lax
from jax.experimental import pallas as pl
from jax.experimental.pallas import tpu as pltpu
from jax.sharding import Mesh, PartitionSpec as P

epsilon = 1e-06
low = jnp.bfloat16
wide = jnp.float32
tile = 8
depth = 4
cores = 2


def after(value, *earlier):
    return lax.optimization_barrier((value, earlier))[0]


def turned(value, axis, by):
    length = lax.axis_size(axis)
    return lax.ppermute(value, axis, [(i, (i + by) % length) for i in range(length)])


def passed(value, axis, by):
    length = lax.axis_size(axis)
    pairs = [(i, i + by) for i in range(length) if 0 <= i + by < length]
    return lax.ppermute(value, axis, pairs)


def gather_slots(value, axis):
    length = lax.axis_size(axis)
    return jnp.stack([value] + [turned(value, axis, -d) for d in range(1, length)])


def sum_slots(partial, axis):
    length = lax.axis_size(axis)
    total = partial[0].astype(wide)
    for d in range(1, length):
        total = total + turned(partial[d].astype(low), axis, d).astype(wide)
    return total


def sum_axis(value, axis):
    length = lax.axis_size(axis)
    total = value
    for d in range(1, length):
        total = total + turned(value, axis, d)
    return total


def swap_slots(slots):
    ycount, spread = lax.axis_size("y"), lax.axis_size("x")
    result = []
    for dy in range(ycount):
        line = []
        for dx in range(spread):
            sy, sx = (ycount - dy) % ycount, (spread - dx) % spread
            if sy == 0 and sx == 0:
                line.append(slots[0][0])
                continue
            pairs = [
                (i * spread + j, (i + sy) % ycount * spread + (j + sx) % spread)
                for i in range(ycount)
                for j in range(spread)
            ]
            line.append(lax.ppermute(slots[sy][sx], ("y", "x"), pairs))
        result.append(line)
    return result


def gather_tokens(value):
    half = value.shape[0] // 2
    width = value.shape[-1]
    first = gather_slots(value[:half], "x")
    second = gather_slots(value[half:], "y")
    first = gather_slots(first, "y")
    second = gather_slots(second, "x")
    return jnp.stack([first, jnp.swapaxes(second, 0, 1)]).reshape(-1, width)


def scatter_tokens(partial, batch):
    width = partial.shape[-1]
    grid = partial.reshape(2, lax.axis_size("y"), lax.axis_size("x"), batch // 2, -1, width)
    first = sum_slots(jnp.swapaxes(grid[0], 0, 1), "x")
    second = sum_slots(grid[1], "y")
    first = sum_slots(first, "y")
    second = sum_slots(second, "x")
    return jnp.concatenate([first, second], axis=0)


def pick_kernel(start_ref, *refs):
    count = len(refs) // 2
    for source, target in zip(refs[:count], refs[count:]):
        target[...] = source[...]


def column_pieces(weight, groups):
    spread, ycount = lax.axis_size("x"), lax.axis_size("y")
    rows = weight.shape[0]
    count = groups * depth
    part = weight.shape[1] // (count * spread * ycount)
    starts = [
        (lax.axis_index("x") + d) % spread * ycount + lax.axis_index("y") for d in range(spread)
    ]
    if part % 128 == 0:

        def source(d):
            return pl.BlockSpec(
                (rows, part), lambda i, start, d=d: (0, i * spread * ycount + start[d])
            )

        return pl.pallas_call(
            pick_kernel,
            out_shape=[jax.ShapeDtypeStruct((rows, count * part), weight.dtype)] * spread,
            grid_spec=pltpu.PrefetchScalarGridSpec(
                num_scalar_prefetch=1,
                grid=(count,),
                in_specs=[source(d) for d in range(spread)],
                out_specs=[pl.BlockSpec((rows, part), lambda i, start: (0, i))] * spread,
            ),
            cost_estimate=pl.CostEstimate(
                flops=0, transcendentals=0, bytes_accessed=4 * rows * count * part * spread
            ),
        )(jnp.stack(starts).astype(jnp.int32), *[weight] * spread)
    return [
        jnp.concatenate(
            [
                lax.dynamic_slice_in_dim(weight, (k * spread * ycount + start) * part, part, 1)
                for k in range(count)
            ],
            axis=1,
        )
        for start in starts
    ]


def column_block(pieces):
    spread, ccount = lax.axis_size("x"), lax.axis_size("c")
    share = spread // ccount
    place, core = lax.axis_index("x"), lax.axis_index("c")
    got = [pieces[0]]
    for d in range(1, spread):
        pairs = [
            (i // share * spread + i, i // share * spread + (i + d) % spread) for i in range(spread)
        ]
        got.append(lax.ppermute(pieces[d], ("c", "x"), pairs))
    got = jnp.stack(got)
    return jnp.concatenate(
        [
            lax.dynamic_index_in_dim(got, (place - core * share - j) % spread, 0, False)
            for j in range(share)
        ]
    )


def row_block(weight):
    ycount, ccount = lax.axis_size("y"), lax.axis_size("c")
    part = weight.shape[0] // (ycount * ccount)
    pair = lax.axis_index("y") * ccount + lax.axis_index("c")
    return lax.dynamic_slice_in_dim(weight, pair * part, part, 0)


def core_halves(value):
    ccount = lax.axis_size("c")
    width = value.shape[1] // ccount
    core = lax.axis_index("c")
    return [
        lax.dynamic_slice_in_dim(value, (core + d) % ccount * width, width, 1)
        for d in range(ccount)
    ]


def gather_halves(value):
    return gather_tokens(value.reshape(2, value.shape[0] // 2, -1))


def gather_out(weight):
    ycount = lax.axis_size("y")
    part = weight.shape[0] // ycount
    rows = lax.dynamic_slice_in_dim(weight, lax.axis_index("y") * part, part, 0)
    block = core_halves(rows)[0]
    held = in_order(gather_slots(block, "z"), "z").reshape(depth * part, -1)
    mine = gather_halves(held)
    return [mine] + [turned(mine, "c", -d) for d in range(1, lax.axis_size("c"))]


def out_owner(terms):
    total = terms[0].astype(wide)
    for d in range(1, len(terms)):
        total = total + turned(terms[d], "c", d).astype(wide)
    mine = scatter_tokens(total.astype(low), 2)
    mine = mine.reshape(depth, -1, mine.shape[-1]).astype(low)
    place = lax.axis_index("z")
    slots = jnp.stack(
        [lax.dynamic_index_in_dim(mine, (place + d) % depth, 0, False) for d in range(depth)]
    )
    mine = sum_slots(slots, "z").astype(low)
    whole = in_order(gather_slots(mine, "y"), "y")
    whole = in_order(gather_slots(whole, "c"), "c")
    ccount, ycount, rows, width = whole.shape
    return jnp.transpose(whole, (1, 2, 0, 3)).reshape(ycount * rows, ccount * width).astype(wide)


def gather_tile(block):
    return lax.all_gather(block, ("z", "c"), axis=0, tiled=True)


def scatter_tile(term):
    return lax.psum_scatter(term, ("z", "c"), scatter_dimension=0, tiled=True)


def column_owner(mine, groups):
    spread, ycount, ccount = lax.axis_size("x"), lax.axis_size("y"), lax.axis_size("c")
    share = spread // ccount
    place, core, yplace = lax.axis_index("x"), lax.axis_index("c"), lax.axis_index("y")
    rows = mine.shape[0] // share
    width = mine.shape[1]
    parts = mine.reshape(share, rows, width)
    got = []
    for d in range(spread):
        send = lax.dynamic_index_in_dim(
            parts, jnp.clip((place + d) % spread - core * share, 0, share - 1), 0, False
        )
        if d > 0:
            pairs = [
                ((i + d) % spread // share * spread + i, i // share * spread + (i + d) % spread)
                for i in range(spread)
            ]
            send = lax.ppermute(send, ("c", "x"), pairs)
        got.append(send)
    got = jnp.stack(got)
    held = jnp.stack(
        [
            lax.dynamic_index_in_dim(got, (place - core * share - j) % spread, 0, False)
            for j in range(share)
        ]
    )
    flat = gather_slots(gather_slots(held, "y"), "c").reshape(-1, rows, width)
    part = width // (groups * depth)
    ranks = []
    for i in range(spread):
        for k in range(ycount):
            slot = (i // share - core) % ccount * ycount + (k - yplace) % ycount
            ranks.append(lax.dynamic_index_in_dim(flat, slot * share + i % share, 0, False))
    pieces = []
    for at in range(groups * depth):
        pieces += [r[:, at * part : (at + 1) * part] for r in ranks]
    return jnp.concatenate(pieces, axis=1).astype(wide)


def in_order(slots, axis):
    length = lax.axis_size(axis)
    place = lax.axis_index(axis)
    return jnp.stack(
        [lax.dynamic_index_in_dim(slots, (j - place) % length, 0, False) for j in range(length)]
    )


def row_owner(mine):
    whole = in_order(gather_slots(mine, "y"), "y")
    whole = in_order(gather_slots(whole, "c"), "c")
    return jnp.swapaxes(whole, 0, 1).reshape(-1, mine.shape[1]).astype(wide)


def rank_rows(values, axis):
    spread, ycount = lax.axis_size("x"), lax.axis_size("y")
    part = values.shape[axis] // (depth * spread * ycount)
    place = lax.axis_index("x") * ycount + lax.axis_index("y")
    return jnp.concatenate(
        [
            lax.dynamic_slice_in_dim(values, (k * spread * ycount + place) * part, part, axis)
            for k in range(depth)
        ],
        axis=axis,
    )


def all_channels(slots):
    whole = in_order(slots, "y")
    whole = in_order(jnp.swapaxes(whole, 0, 1), "x")
    spread, ycount, rows = whole.shape[:3]
    whole = whole.reshape(spread, ycount, rows, depth, -1)
    return jnp.transpose(whole, (2, 3, 0, 1, 4)).reshape(rows, -1)


def fill(source, target, place):
    groups, parts, inner, length = source.shape[:4]
    for j in range(parts):
        slot = lax.rem(j + parts - place, parts)
        for g in range(groups):
            for b in range(inner):
                target[g * inner + b, j * length : (j + 1) * length, :] = source[g, slot, b].astype(
                    wide
                )


def empty(source, target, place):
    groups, parts, inner, length = target.shape[:4]
    for j in range(parts):
        slot = lax.rem(j + parts - place, parts)
        for g in range(groups):
            for b in range(inner):
                target[g, slot, b] = source[g * inner + b, j * length : (j + 1) * length, :].astype(
                    low
                )


def halves(ref):
    return [ref[k * tile : (k + 1) * tile, :] for k in range(ref.shape[0] // tile)]


def row_of(ref, seq, at):
    return ref[seq, pl.ds(at, tile, stride=0), :]


def states_kernel(place_ref, signal_ref, decay_ref, state_ref, slope_ref, held):
    fill(signal_ref, held, place_ref[0])
    seqs, length, lanes = held.shape
    keep = [jnp.exp(-d) for d in halves(decay_ref)]
    count = len(keep)
    zero = jnp.zeros((tile, lanes), wide)

    def step(i, carry):
        state, slope = [list(v) for v in carry]
        for k in range(tile):
            for n in range(seqs):
                new = row_of(held, n, i * tile + k)
                for h in range(count):
                    at = n * count + h
                    slope[at] = keep[h] * (slope[at] + state[at])
                    state[at] = keep[h] * state[at] + new
        return tuple(state), tuple(slope)

    start = tuple(zero for _ in range(seqs * count))
    state, slope = lax.fori_loop(0, length // tile, step, (start, start))
    for n in range(seqs):
        for h in range(count):
            state_ref[n, h * tile : (h + 1) * tile, :] = state[n * count + h]
            slope_ref[n, h * tile : (h + 1) * tile, :] = slope[n * count + h]


def forward_kernel(place_ref, signal_ref, decay_ref, residue_ref, start_ref, out_ref, held, terms, made):
    fill(signal_ref, held, place_ref[0])
    seqs, length, lanes = held.shape
    keep = [jnp.exp(-d) for d in halves(decay_ref)]
    weigh = halves(residue_ref)
    count = len(keep)

    def step(i, carry):
        state = list(carry)
        for k in range(tile):
            for n in range(seqs):
                new = row_of(held, n, i * tile + k)
                total = None
                for h in range(count):
                    at = n * count + h
                    state[at] = keep[h] * state[at] + new
                    term = weigh[h] * state[at]
                    total = term if total is None else total + term
                terms[n, k * tile : (k + 1) * tile, :] = total
        for n in range(seqs):
            result = terms[n, pl.ds(0, tile, stride=tile), :]
            for p in range(1, tile):
                result = result + terms[n, pl.ds(p, tile, stride=tile), :]
            made[n, pl.ds(i * tile, tile), :] = result
        return tuple(state)

    start = tuple(
        start_ref[n, h * tile : (h + 1) * tile, :] for n in range(seqs) for h in range(count)
    )
    lax.fori_loop(0, length // tile, step, start)
    empty(made, out_ref, place_ref[0])


def later_kernel(place_ref, signal_ref, decay_ref, state_ref, held):
    fill(signal_ref, held, place_ref[0])
    seqs, length, lanes = held.shape
    keep = [jnp.exp(-d) for d in halves(decay_ref)]
    count = len(keep)

    def step(i, carry):
        state = list(carry)
        base = length - tile - i * tile
        for k in range(tile - 1, -1, -1):
            for n in range(seqs):
                new = row_of(held, n, base + k)
                for h in range(count):
                    at = n * count + h
                    state[at] = keep[h] * state[at] + new
        return tuple(state)

    zero = jnp.zeros((tile, lanes), wide)
    state = lax.fori_loop(0, length // tile, step, tuple(zero for _ in range(seqs * count)))
    for n in range(seqs):
        for h in range(count):
            state_ref[n, h * tile : (h + 1) * tile, :] = state[n * count + h]


def backward_kernel(
    place_ref,
    signal_ref,
    grad_ref,
    decay_ref,
    residue_ref,
    start_ref,
    slope_ref,
    end_ref,
    out_ref,
    residue_grad_ref,
    decay_grad_ref,
    held,
    grads,
    terms,
    made,
):
    fill(signal_ref, held, place_ref[0])
    fill(grad_ref, grads, place_ref[0])
    seqs, length, lanes = held.shape
    keep = [jnp.exp(-d) for d in halves(decay_ref)]
    weigh = halves(residue_ref)
    count = len(keep)
    zero = jnp.zeros((tile, lanes), wide)

    def ahead(i, carry):
        state, slope, first, second = [list(v) for v in carry]
        for k in range(tile):
            for n in range(seqs):
                new = row_of(held, n, i * tile + k)
                back = row_of(grads, n, i * tile + k)
                for h in range(count):
                    at = n * count + h
                    slope[at] = keep[h] * (slope[at] + state[at])
                    state[at] = keep[h] * state[at] + new
                    first[at] = first[at] + back * state[at]
                    second[at] = second[at] + back * slope[at]
        return tuple(state), tuple(slope), tuple(first), tuple(second)

    def load(ref):
        return tuple(
            ref[n, h * tile : (h + 1) * tile, :] for n in range(seqs) for h in range(count)
        )

    none = tuple(zero for _ in range(seqs * count))
    _, _, first, second = lax.fori_loop(
        0, length // tile, ahead, (load(start_ref), load(slope_ref), none, none)
    )
    for h in range(count):
        sum_first, sum_second = first[h], second[h]
        for n in range(1, seqs):
            sum_first = sum_first + first[n * count + h]
            sum_second = sum_second + second[n * count + h]
        residue_grad_ref[h * tile : (h + 1) * tile, :] = sum_first
        decay_grad_ref[h * tile : (h + 1) * tile, :] = -weigh[h] * sum_second

    def back_step(i, carry):
        state = list(carry)
        base = length - tile - i * tile
        for k in range(tile - 1, -1, -1):
            for n in range(seqs):
                new = row_of(grads, n, base + k)
                total = None
                for h in range(count):
                    at = n * count + h
                    state[at] = keep[h] * state[at] + new
                    term = weigh[h] * state[at]
                    total = term if total is None else total + term
                terms[n, k * tile : (k + 1) * tile, :] = total
        for n in range(seqs):
            result = terms[n, pl.ds(0, tile, stride=tile), :]
            for p in range(1, tile):
                result = result + terms[n, pl.ds(p, tile, stride=tile), :]
            made[n, pl.ds(base, tile), :] = result
        return tuple(state)

    lax.fori_loop(0, length // tile, back_step, load(end_ref))
    empty(made, out_ref, place_ref[0])


def conv_call(kernel, place, arrays, results, scratch, flops):
    channels = arrays[0].shape[-1]
    lanes = min(channels, 128)

    def spec(shape):
        lead = len(shape) - 1
        return pl.BlockSpec(shape[:-1] + (lanes,), lambda i, *_: (0,) * lead + (i,))

    return pl.pallas_call(
        kernel,
        out_shape=results,
        grid_spec=pltpu.PrefetchScalarGridSpec(
            num_scalar_prefetch=1,
            grid=(channels // lanes,),
            in_specs=[spec(a.shape) for a in arrays],
            out_specs=[spec(r.shape) for r in results],
            scratch_shapes=[pltpu.VMEM(s + (lanes,), wide) for s in scratch],
        ),
        compiler_params=pltpu.CompilerParams(
            dimension_semantics=("arbitrary",), vmem_limit_bytes=48 << 20
        ),
        cost_estimate=pl.CostEstimate(
            flops=flops, transcendentals=0, bytes_accessed=sum(a.size * 4 for a in arrays)
        ),
    )(place, *arrays)


def sizes(signal, poles):
    groups, parts, inner, length, channels = signal.shape
    return groups * inner, parts * length, channels, signal.size * poles


def states_of(place, signal, decay):
    seqs, length, channels, work = sizes(signal, decay.shape[0])
    shape = jax.ShapeDtypeStruct((seqs, decay.shape[0], channels), wide)
    return conv_call(
        states_kernel, place, [signal, decay], [shape, shape], [(seqs, length)], 4 * work
    )


def forward_of(place, signal, decay, residue, start):
    seqs, length, channels, work = sizes(signal, decay.shape[0])
    return conv_call(
        forward_kernel,
        place,
        [signal, decay, residue, start],
        [jax.ShapeDtypeStruct(signal.shape, low)],
        [(seqs, length), (seqs, tile * tile), (seqs, length)],
        4 * work,
    )[0]


def later_of(place, signal, decay):
    seqs, length, channels, work = sizes(signal, decay.shape[0])
    shape = jax.ShapeDtypeStruct((seqs, decay.shape[0], channels), wide)
    return conv_call(later_kernel, place, [signal, decay], [shape], [(seqs, length)], 2 * work)[0]


def backward_of(place, signal, grad, decay, residue, start, slope, end):
    seqs, length, channels, work = sizes(signal, decay.shape[0])
    shape = jax.ShapeDtypeStruct(decay.shape, wide)
    return conv_call(
        backward_kernel,
        place,
        [signal, grad, decay, residue, start, slope, end],
        [jax.ShapeDtypeStruct(signal.shape, low), shape, shape],
        [(seqs, length), (seqs, length), (seqs, tile * tile), (seqs, length)],
        12 * work,
    )


def rms_scale(values):
    return lax.rsqrt(jnp.mean(values * values, axis=-1, keepdims=True) + epsilon)


def norm_back(values, scale, gain, grad_normed):
    grad_gain = jnp.sum(grad_normed * values * scale, axis=(0, 1))
    scaled = grad_normed * gain
    grad_values = scale * scaled - values * scale * scale * scale * jnp.mean(
        scaled * values, axis=-1, keepdims=True
    )
    return (grad_values, grad_gain)


def dot(a, b, kind=wide):
    return jnp.dot(a, b, preferred_element_type=wide).astype(kind)


def dot_t(a, b, kind=wide):
    return lax.dot_general(a, b, (((1,), (1,)), ((), ())), preferred_element_type=wide).astype(kind)


def dot_w(a, b):
    return lax.dot_general(a, b, (((0,), (0,)), ((), ())), preferred_element_type=wide).astype(low)


def body(
    tokens,
    lengths,
    norm_gain,
    in_weight,
    conv_taps,
    filter_residue,
    filter_decay,
    out_weight,
    feed_gain,
    gate_weight,
    up_weight,
    down_weight,
    cotangent,
):
    spread, ycount = lax.axis_size("x"), lax.axis_size("y")
    batch, local, width = tokens.shape
    place = lax.axis_index("z") * spread + lax.axis_index("x")
    position = place * local + jnp.arange(local)
    mask = (position[None, :] < lengths[:, None]).astype(wide)[..., None]
    block = spread * local

    in_pieces = column_pieces(in_weight, 3)
    out_weight, tokens = after((out_weight, tokens), in_pieces)
    in_block = column_block(in_pieces)
    hidden = tokens.astype(wide)
    scale_one = rms_scale(hidden)
    normed = (hidden * scale_one * norm_gain).astype(low)
    normed_all = gather_tokens(normed)
    gate_weight, down_weight, up_weight = after(
        (gate_weight, down_weight, up_weight), normed, in_block
    )
    gate_block = column_block(column_pieces(gate_weight, 1))
    up_block = column_block(column_pieces(up_weight, 1))
    down_piece = after(row_block(down_weight), gate_block)
    up_block = after(up_block, down_piece)
    w_in = gather_tile(in_block)
    w_gate = gather_tile(gate_block)
    w_down = gather_tile(down_piece)
    w_up = gather_tile(up_block)
    w_out = gather_out(out_weight)
    cotangent = after(cotangent, normed_all, gate_block, up_block)
    grad_out = cotangent.astype(wide) * mask
    grad_feed_all = gather_tokens(grad_out.astype(low))

    channels = w_in.shape[1] // 3
    grid = (2 * ycount, spread, batch // 2, local)
    taps = jnp.concatenate(
        [rank_rows(conv_taps[:, g * width : (g + 1) * width], 1) for g in range(3)], axis=1
    )
    decay = rank_rows(filter_decay, 0).T
    residue = rank_rows(filter_residue, 0).T
    mixed = dot(normed_all, w_in, low).reshape(grid + (3 * channels,))
    opening = (lax.axis_index("x") + jnp.arange(spread)) % spread == 0
    opening = opening[None, :, None, None, None]
    closing = (lax.axis_index("x") + jnp.arange(spread)) % spread == spread - 1
    closing = closing[None, :, None, None, None]

    tail = jnp.roll(mixed[:, :, :, local - 2 :], 1, axis=1)
    behind = passed(tail, "z", 1)
    extended = jnp.concatenate([jnp.where(opening, behind, tail), mixed], axis=3).astype(wide)
    short = (
        taps[0] * extended[:, :, :, 2:]
        + taps[1] * extended[:, :, :, 1:-1]
        + taps[2] * extended[:, :, :, :-2]
    )
    query = short[..., :channels]
    keys = short[..., channels : 2 * channels]
    values = short[..., 2 * channels :]
    product = (keys * values).astype(low)

    spot = lax.axis_index("x").astype(jnp.int32).reshape(1)
    state_end, slope_end = states_of(spot, product, decay)
    states = [passed(state_end, "z", k) for k in range(1, depth)]
    start = states[0]
    for k in range(1, depth - 1):
        start = start + jnp.exp(-decay * (k * block)) * states[k]
    convolved = forward_of(spot, product, decay, residue, start)
    gated = (query * convolved.astype(wide)).astype(low)
    gated_slots = gated.reshape(2, ycount, spread, -1, channels)
    got = swap_slots(
        [
            [gated_slots[:, k, i].reshape(-1, channels) for i in range(spread)]
            for k in range(ycount)
        ]
    )
    half = channels // 2
    gated_own = jnp.concatenate(
        [g[:, h * half : (h + 1) * half] for h in range(2) for line in got for g in line], axis=1
    )
    mixer = in_order(jnp.stack([dot(gated_own, w) for w in w_out]), "c")
    mixer = jnp.concatenate([m for m in mixer], axis=1).reshape(batch, local, width)
    middle = hidden + mixer

    scale_two = rms_scale(middle)
    normed_two = (middle * scale_two * feed_gain).astype(low)
    normed_two_all = gather_tokens(normed_two)
    gate = dot(normed_two_all, w_gate)
    sigma = jax.nn.sigmoid(gate)
    grad_active = dot_t(grad_feed_all, w_down)
    grad_upper = (grad_active * gate * sigma).astype(low)
    up_term = dot_w(normed_two_all, grad_upper)
    up_mine = scatter_tile(up_term)
    upper = dot(normed_two_all, after(w_up, up_term))
    active = (gate * sigma * upper).astype(low)
    grad_gate = (grad_active * upper * sigma * (1.0 + gate * (1.0 - sigma))).astype(low)
    partial_two = (dot_t(grad_gate, w_gate) + dot_t(grad_upper, w_up)).astype(low)
    grad_normed_two = scatter_tokens(partial_two, batch)
    weigh_two, weigh_gate = after((normed_two_all, grad_gate), partial_two)
    gate_mine = scatter_tile(dot_w(weigh_two, weigh_gate))

    grad_middle, grad_feed_gain = norm_back(middle, scale_two, feed_gain, grad_normed_two)
    grad_middle = grad_middle + grad_out
    grad_mix = grad_middle.astype(low).reshape(-1, width)

    mix_parts = core_halves(grad_mix)
    grad_gated_own = sum(dot_t(m, w) for m, w in zip(mix_parts, w_out)).astype(low)
    grad_slots = grad_gated_own.reshape(-1, 2, ycount, spread, half)
    got = swap_slots(
        [
            [grad_slots[:, :, k, i].reshape(-1, channels) for i in range(spread)]
            for k in range(ycount)
        ]
    )
    grad_gated = jnp.stack([jnp.stack(line) for line in got])
    grad_gated = grad_gated.reshape(ycount, spread, 2, batch // 2, local, channels)
    grad_gated = jnp.moveaxis(grad_gated, 2, 0).reshape(grid + (channels,)).astype(wide)
    grad_query = grad_gated * convolved.astype(wide)
    grad_conv = (grad_gated * query).astype(low)

    later_end = later_of(spot, grad_conv, decay)
    laters = [passed(later_end, "z", -k) for k in range(1, depth)]
    later = laters[0]
    for k in range(1, depth - 1):
        later = later + jnp.exp(-decay * (k * block)) * laters[k]
    slope_end = after(slope_end, normed_two_all)
    slopes = [passed(slope_end, "z", k) for k in range(1, depth)]
    slope = slopes[0]
    for k in range(1, depth - 1):
        slope = slope + jnp.exp(-decay * (k * block)) * (slopes[k] + (k * block) * states[k])

    low_taps = [taps[:, g * channels : (g + 1) * channels] for g in range(3)]

    def short_back(grad_short, weights):
        head = jnp.roll(grad_short[:, :, :, :2].astype(low), -1, axis=1)
        ahead = passed(head, "z", -1)
        whole = jnp.concatenate([grad_short, jnp.where(closing, ahead, head).astype(wide)], axis=3)
        result = (
            weights[0] * whole[:, :, :, :-2]
            + weights[1] * whole[:, :, :, 1:-1]
            + weights[2] * whole[:, :, :, 2:]
        )
        return result.astype(low).reshape(-1, grad_short.shape[-1])

    weigh_active, weigh_feed = after((active, grad_feed_all), grad_gated)
    down_mine = scatter_tile(dot_w(weigh_active, weigh_feed))
    grad_mixed_query = short_back(grad_query, low_taps[0])
    query_mine = scatter_tile(dot_w(normed_all, grad_mixed_query))

    grad_product, grad_residue, grad_decay = backward_of(
        spot, product, grad_conv, decay, residue, start, slope, later
    )
    grad_product = grad_product.astype(wide)
    grad_pair = jnp.concatenate([grad_product * values, grad_product * keys], axis=-1)
    grad_mixed_pair = short_back(grad_pair, jnp.concatenate(low_taps[1:], axis=1))
    pair_mine = scatter_tile(dot_w(normed_all, grad_mixed_pair))
    grad_mixed = jnp.concatenate([grad_mixed_query, grad_mixed_pair], axis=1)
    grad_normed = scatter_tokens(dot_t(grad_mixed, w_in, low), batch)
    grad_hidden, grad_norm_gain = norm_back(hidden, scale_one, norm_gain, grad_normed)
    grad_tokens = (grad_hidden + grad_middle).astype(low)

    feed_active = after(active, grad_mixed_pair)
    feed = scatter_tokens(dot(feed_active, w_down, low), batch)
    output = (mask * (middle + feed)).astype(low)
    up_mine = after(up_mine, grad_conv)
    gate_mine = after(gate_mine, grad_product)
    down_mine = after(down_mine, grad_mixed_pair)
    gated_late, mix_late = after((gated_own, mix_parts), grad_gated)
    grad_out_weight = out_owner([dot_w(gated_late, m) for m in mix_late])
    grad_up_weight = column_owner(up_mine, 1)
    grad_gate_weight = column_owner(gate_mine, 1)
    grad_down = row_owner(down_mine)
    grad_in_weight = jnp.concatenate(
        [column_owner(query_mine, 1), column_owner(pair_mine, 2)], axis=1
    )

    query_late, pair_late, extended_late = after((grad_query, grad_pair, extended), grad_mixed_pair)
    grad_taps = []
    for g, part in enumerate((query_late, pair_late[..., :channels], pair_late[..., channels:])):
        own = extended_late[..., g * channels : (g + 1) * channels]
        grad_taps += [
            jnp.sum(part * own[:, :, :, 2 - j : local + 2 - j], axis=(0, 1, 2, 3)) for j in range(3)
        ]
    gains = jnp.stack([grad_norm_gain, grad_feed_gain]).reshape(-1, channels)
    small = jnp.concatenate([grad_residue, grad_decay, jnp.stack(grad_taps)], axis=0)
    count = small.shape[0]
    small = sum_axis(sum_axis(jnp.concatenate([small, gains], axis=0), "c"), "z")
    small = gather_slots(gather_slots(small, "x"), "y")
    gains = jnp.sum(small[:, :, count:], axis=(0, 1)).reshape(2, width)
    small = all_channels(small[:, :, :count])
    poles = decay.shape[0]
    grad_conv_taps = jnp.concatenate(
        [small[2 * poles + 3 * g : 2 * poles + 3 * g + 3] for g in range(3)], axis=1
    )
    return (
        output,
        grad_tokens,
        gains[0],
        grad_in_weight,
        grad_conv_taps,
        small[:poles].T,
        small[poles : 2 * poles].T,
        grad_out_weight,
        gains[1],
        grad_gate_weight,
        grad_up_weight,
        grad_down,
    )


def solution(mesh):
    pairs, blocks = mesh.shape["dp"], mesh.shape["seq"]
    devices = mesh.devices.reshape(pairs // cores, cores, depth, blocks // depth)
    inner = Mesh(devices, ("y", "c", "z", "x"))
    dp, seq = ("y", "c"), ("z", "x")
    tokens, rows = P(dp, seq, None), P(seq, None)
    return jax.shard_map(
        body,
        mesh=inner,
        in_specs=(
            tokens,
            P(dp),
            P(),
            rows,
            P(),
            P(),
            P(),
            rows,
            P(),
            rows,
            rows,
            rows,
            tokens,
        ),
        out_specs=(tokens, tokens, P(), rows, P(), P(), P(), rows, P(), rows, rows, rows),
        check_vma=False,
    )
```

```python
import functools

import jax
import jax.numpy as jnp
from jax import lax
from jax.experimental import pallas as pl
from jax.experimental.pallas import tpu as pltpu
from jax.sharding import Mesh, PartitionSpec as P

epsilon = 1e-06
low = jnp.bfloat16
wide = jnp.float32
tile = 8
depth = 4
cores = 2


def after(value, *earlier):
    return lax.optimization_barrier((value, earlier))[0]


def turned(value, axis, by):
    length = lax.axis_size(axis)
    return lax.ppermute(value, axis, [(i, (i + by) % length) for i in range(length)])


def passed(value, axis, by):
    length = lax.axis_size(axis)
    pairs = [(i, i + by) for i in range(length) if 0 <= i + by < length]
    return lax.ppermute(value, axis, pairs)


def gather_slots(value, axis):
    length = lax.axis_size(axis)
    return jnp.stack([value] + [turned(value, axis, -d) for d in range(1, length)])


def sum_slots(partial, axis):
    length = lax.axis_size(axis)
    total = partial[0].astype(wide)
    for d in range(1, length):
        total = total + turned(partial[d].astype(low), axis, d).astype(wide)
    return total


def sum_axis(value, axis):
    length = lax.axis_size(axis)
    total = value
    for d in range(1, length):
        total = total + turned(value, axis, d)
    return total


def swap_slots(slots):
    ycount, spread = lax.axis_size("y"), lax.axis_size("x")
    result = []
    for dy in range(ycount):
        line = []
        for dx in range(spread):
            sy, sx = (ycount - dy) % ycount, (spread - dx) % spread
            if sy == 0 and sx == 0:
                line.append(slots[0][0])
                continue
            pairs = [
                (i * spread + j, (i + sy) % ycount * spread + (j + sx) % spread)
                for i in range(ycount)
                for j in range(spread)
            ]
            line.append(lax.ppermute(slots[sy][sx], ("y", "x"), pairs))
        result.append(line)
    return result


def gather_tokens(value):
    half = value.shape[0] // 2
    width = value.shape[-1]
    first = gather_slots(value[:half], "x")
    second = gather_slots(value[half:], "y")
    first = gather_slots(first, "y")
    second = gather_slots(second, "x")
    return jnp.stack([first, jnp.swapaxes(second, 0, 1)]).reshape(-1, width)


def scatter_tokens(partial, batch):
    width = partial.shape[-1]
    grid = partial.reshape(2, lax.axis_size("y"), lax.axis_size("x"), batch // 2, -1, width)
    first = sum_slots(jnp.swapaxes(grid[0], 0, 1), "x")
    second = sum_slots(grid[1], "y")
    first = sum_slots(first, "y")
    second = sum_slots(second, "x")
    return jnp.concatenate([first, second], axis=0)


def pick_kernel(count, part, stride, start_ref, source, *refs):
    targets, sems = refs[:-1], refs[-1]
    copies = []
    for d, target in enumerate(targets):
        for k in range(count):
            at = pl.multiple_of((k * stride + start_ref[d]) * part, part)
            copies.append(
                pltpu.make_async_copy(
                    source.at[:, pl.ds(at, part)],
                    target.at[:, k * part : (k + 1) * part],
                    sems.at[d * count + k],
                )
            )
    for copy in copies:
        copy.start()
    for copy in copies:
        copy.wait()


def column_pieces(weight, groups):
    spread, ycount = lax.axis_size("x"), lax.axis_size("y")
    rows = weight.shape[0]
    count = groups * depth
    part = weight.shape[1] // (count * spread * ycount)
    starts = [
        (lax.axis_index("x") + d) % spread * ycount + lax.axis_index("y") for d in range(spread)
    ]
    if part % 128 == 0:
        return pl.pallas_call(
            functools.partial(pick_kernel, count, part, spread * ycount),
            out_shape=[jax.ShapeDtypeStruct((rows, count * part), weight.dtype)] * spread,
            grid_spec=pltpu.PrefetchScalarGridSpec(
                num_scalar_prefetch=1,
                in_specs=[pl.BlockSpec(memory_space=pl.ANY)],
                out_specs=[pl.BlockSpec(memory_space=pl.ANY)] * spread,
                scratch_shapes=[pltpu.SemaphoreType.DMA((count * spread,))],
            ),
            cost_estimate=pl.CostEstimate(
                flops=0, transcendentals=0, bytes_accessed=4 * rows * count * part * spread
            ),
        )(jnp.stack(starts).astype(jnp.int32), weight)
    return [
        jnp.concatenate(
            [
                lax.dynamic_slice_in_dim(weight, (k * spread * ycount + start) * part, part, 1)
                for k in range(count)
            ],
            axis=1,
        )
        for start in starts
    ]


def column_block(pieces):
    spread, ccount = lax.axis_size("x"), lax.axis_size("c")
    share = spread // ccount
    place, core = lax.axis_index("x"), lax.axis_index("c")
    got = [pieces[0]]
    for d in range(1, spread):
        pairs = [
            (i // share * spread + i, i // share * spread + (i + d) % spread) for i in range(spread)
        ]
        got.append(lax.ppermute(pieces[d], ("c", "x"), pairs))
    got = jnp.stack(got)
    return jnp.concatenate(
        [
            lax.dynamic_index_in_dim(got, (place - core * share - j) % spread, 0, False)
            for j in range(share)
        ]
    )


def row_block(weight):
    ycount, ccount = lax.axis_size("y"), lax.axis_size("c")
    part = weight.shape[0] // (ycount * ccount)
    pair = lax.axis_index("y") * ccount + lax.axis_index("c")
    return lax.dynamic_slice_in_dim(weight, pair * part, part, 0)


def core_halves(value):
    ccount = lax.axis_size("c")
    width = value.shape[1] // ccount
    core = lax.axis_index("c")
    return [
        lax.dynamic_slice_in_dim(value, (core + d) % ccount * width, width, 1)
        for d in range(ccount)
    ]


def gather_halves(value):
    return gather_tokens(value.reshape(2, value.shape[0] // 2, -1))


def gather_out(weight):
    ycount = lax.axis_size("y")
    part = weight.shape[0] // ycount
    rows = lax.dynamic_slice_in_dim(weight, lax.axis_index("y") * part, part, 0)
    block = core_halves(rows)[0]
    held = in_order(gather_slots(block, "z"), "z").reshape(depth * part, -1)
    mine = gather_halves(held)
    return [mine] + [turned(mine, "c", -d) for d in range(1, lax.axis_size("c"))]


def out_owner(terms):
    total = terms[0].astype(wide)
    for d in range(1, len(terms)):
        total = total + turned(terms[d], "c", d).astype(wide)
    mine = scatter_tokens(total.astype(low), 2)
    mine = mine.reshape(depth, -1, mine.shape[-1]).astype(low)
    place = lax.axis_index("z")
    slots = jnp.stack(
        [lax.dynamic_index_in_dim(mine, (place + d) % depth, 0, False) for d in range(depth)]
    )
    mine = sum_slots(slots, "z").astype(low)
    whole = in_order(gather_slots(mine, "y"), "y")
    whole = in_order(gather_slots(whole, "c"), "c")
    ccount, ycount, rows, width = whole.shape
    return jnp.transpose(whole, (1, 2, 0, 3)).reshape(ycount * rows, ccount * width).astype(wide)


def gather_tile(block):
    return lax.all_gather(block, ("z", "c"), axis=0, tiled=True)


def scatter_tile(term):
    return lax.psum_scatter(term, ("z", "c"), scatter_dimension=0, tiled=True)


def column_owner(mine, groups):
    spread, ycount, ccount = lax.axis_size("x"), lax.axis_size("y"), lax.axis_size("c")
    share = spread // ccount
    place, core, yplace = lax.axis_index("x"), lax.axis_index("c"), lax.axis_index("y")
    rows = mine.shape[0] // share
    width = mine.shape[1]
    parts = mine.reshape(share, rows, width)
    got = []
    for d in range(spread):
        send = lax.dynamic_index_in_dim(
            parts, jnp.clip((place + d) % spread - core * share, 0, share - 1), 0, False
        )
        if d > 0:
            pairs = [
                ((i + d) % spread // share * spread + i, i // share * spread + (i + d) % spread)
                for i in range(spread)
            ]
            send = lax.ppermute(send, ("c", "x"), pairs)
        got.append(send)
    got = jnp.stack(got)
    held = jnp.stack(
        [
            lax.dynamic_index_in_dim(got, (place - core * share - j) % spread, 0, False)
            for j in range(share)
        ]
    )
    flat = gather_slots(gather_slots(held, "y"), "c").reshape(-1, rows, width)
    part = width // (groups * depth)
    ranks = []
    for i in range(spread):
        for k in range(ycount):
            slot = (i // share - core) % ccount * ycount + (k - yplace) % ycount
            ranks.append(lax.dynamic_index_in_dim(flat, slot * share + i % share, 0, False))
    pieces = []
    for at in range(groups * depth):
        pieces += [r[:, at * part : (at + 1) * part].astype(wide) for r in ranks]
    return jnp.concatenate(pieces, axis=1)


def in_order(slots, axis):
    length = lax.axis_size(axis)
    place = lax.axis_index(axis)
    return jnp.stack(
        [lax.dynamic_index_in_dim(slots, (j - place) % length, 0, False) for j in range(length)]
    )


def row_owner(mine):
    whole = in_order(gather_slots(mine, "y"), "y")
    whole = in_order(gather_slots(whole, "c"), "c")
    return jnp.swapaxes(whole, 0, 1).reshape(-1, mine.shape[1]).astype(wide)


def rank_rows(values, axis):
    spread, ycount = lax.axis_size("x"), lax.axis_size("y")
    part = values.shape[axis] // (depth * spread * ycount)
    place = lax.axis_index("x") * ycount + lax.axis_index("y")
    return jnp.concatenate(
        [
            lax.dynamic_slice_in_dim(values, (k * spread * ycount + place) * part, part, axis)
            for k in range(depth)
        ],
        axis=axis,
    )


def all_channels(slots):
    whole = in_order(slots, "y")
    whole = in_order(jnp.swapaxes(whole, 0, 1), "x")
    spread, ycount, rows = whole.shape[:3]
    whole = whole.reshape(spread, ycount, rows, depth, -1)
    return jnp.transpose(whole, (2, 3, 0, 1, 4)).reshape(rows, -1)


def fill(source, target, place):
    groups, parts, inner, length = source.shape[:4]
    for j in range(parts):
        slot = lax.rem(j + parts - place, parts)
        for g in range(groups):
            for b in range(inner):
                target[g * inner + b, j * length : (j + 1) * length, :] = source[g, slot, b].astype(
                    wide
                )


def empty(source, target, place):
    groups, parts, inner, length = target.shape[:4]
    for j in range(parts):
        slot = lax.rem(j + parts - place, parts)
        for g in range(groups):
            for b in range(inner):
                target[g, slot, b] = source[g * inner + b, j * length : (j + 1) * length, :].astype(
                    low
                )


def halves(ref):
    return [ref[k * tile : (k + 1) * tile, :] for k in range(ref.shape[0] // tile)]


def row_of(ref, seq, at):
    return ref[seq, pl.ds(at, tile, stride=0), :]


def states_kernel(place_ref, signal_ref, decay_ref, state_ref, slope_ref, held):
    fill(signal_ref, held, place_ref[0])
    seqs, length, lanes = held.shape
    keep = [jnp.exp(-d) for d in halves(decay_ref)]
    count = len(keep)
    zero = jnp.zeros((tile, lanes), wide)

    def step(i, carry):
        state, slope = [list(v) for v in carry]
        for k in range(tile):
            for n in range(seqs):
                new = row_of(held, n, i * tile + k)
                for h in range(count):
                    at = n * count + h
                    slope[at] = keep[h] * (slope[at] + state[at])
                    state[at] = keep[h] * state[at] + new
        return tuple(state), tuple(slope)

    start = tuple(zero for _ in range(seqs * count))
    state, slope = lax.fori_loop(0, length // tile, step, (start, start))
    for n in range(seqs):
        for h in range(count):
            state_ref[n, h * tile : (h + 1) * tile, :] = state[n * count + h]
            slope_ref[n, h * tile : (h + 1) * tile, :] = slope[n * count + h]


def forward_kernel(place_ref, signal_ref, decay_ref, residue_ref, start_ref, out_ref, held, terms, made):
    fill(signal_ref, held, place_ref[0])
    seqs, length, lanes = held.shape
    keep = [jnp.exp(-d) for d in halves(decay_ref)]
    weigh = halves(residue_ref)
    count = len(keep)

    def step(i, carry):
        state = list(carry)
        for k in range(tile):
            for n in range(seqs):
                new = row_of(held, n, i * tile + k)
                total = None
                for h in range(count):
                    at = n * count + h
                    state[at] = keep[h] * state[at] + new
                    term = weigh[h] * state[at]
                    total = term if total is None else total + term
                terms[n, k * tile : (k + 1) * tile, :] = total
        for n in range(seqs):
            result = terms[n, pl.ds(0, tile, stride=tile), :]
            for p in range(1, tile):
                result = result + terms[n, pl.ds(p, tile, stride=tile), :]
            made[n, pl.ds(i * tile, tile), :] = result
        return tuple(state)

    start = tuple(
        start_ref[n, h * tile : (h + 1) * tile, :] for n in range(seqs) for h in range(count)
    )
    lax.fori_loop(0, length // tile, step, start)
    empty(made, out_ref, place_ref[0])


def later_kernel(place_ref, signal_ref, decay_ref, state_ref, held):
    fill(signal_ref, held, place_ref[0])
    seqs, length, lanes = held.shape
    keep = [jnp.exp(-d) for d in halves(decay_ref)]
    count = len(keep)

    def step(i, carry):
        state = list(carry)
        base = length - tile - i * tile
        for k in range(tile - 1, -1, -1):
            for n in range(seqs):
                new = row_of(held, n, base + k)
                for h in range(count):
                    at = n * count + h
                    state[at] = keep[h] * state[at] + new
        return tuple(state)

    zero = jnp.zeros((tile, lanes), wide)
    state = lax.fori_loop(0, length // tile, step, tuple(zero for _ in range(seqs * count)))
    for n in range(seqs):
        for h in range(count):
            state_ref[n, h * tile : (h + 1) * tile, :] = state[n * count + h]


def backward_kernel(
    place_ref,
    signal_ref,
    grad_ref,
    decay_ref,
    residue_ref,
    start_ref,
    slope_ref,
    end_ref,
    out_ref,
    residue_grad_ref,
    decay_grad_ref,
    held,
    grads,
    terms,
    made,
):
    fill(signal_ref, held, place_ref[0])
    fill(grad_ref, grads, place_ref[0])
    seqs, length, lanes = held.shape
    keep = [jnp.exp(-d) for d in halves(decay_ref)]
    weigh = halves(residue_ref)
    count = len(keep)
    zero = jnp.zeros((tile, lanes), wide)

    def ahead(i, carry):
        state, slope, first, second = [list(v) for v in carry]
        for k in range(tile):
            for n in range(seqs):
                new = row_of(held, n, i * tile + k)
                back = row_of(grads, n, i * tile + k)
                for h in range(count):
                    at = n * count + h
                    slope[at] = keep[h] * (slope[at] + state[at])
                    state[at] = keep[h] * state[at] + new
                    first[at] = first[at] + back * state[at]
                    second[at] = second[at] + back * slope[at]
        return tuple(state), tuple(slope), tuple(first), tuple(second)

    def load(ref):
        return tuple(
            ref[n, h * tile : (h + 1) * tile, :] for n in range(seqs) for h in range(count)
        )

    none = tuple(zero for _ in range(seqs * count))
    _, _, first, second = lax.fori_loop(
        0, length // tile, ahead, (load(start_ref), load(slope_ref), none, none)
    )
    for h in range(count):
        sum_first, sum_second = first[h], second[h]
        for n in range(1, seqs):
            sum_first = sum_first + first[n * count + h]
            sum_second = sum_second + second[n * count + h]
        residue_grad_ref[h * tile : (h + 1) * tile, :] = sum_first
        decay_grad_ref[h * tile : (h + 1) * tile, :] = -weigh[h] * sum_second

    def back_step(i, carry):
        state = list(carry)
        base = length - tile - i * tile
        for k in range(tile - 1, -1, -1):
            for n in range(seqs):
                new = row_of(grads, n, base + k)
                total = None
                for h in range(count):
                    at = n * count + h
                    state[at] = keep[h] * state[at] + new
                    term = weigh[h] * state[at]
                    total = term if total is None else total + term
                terms[n, k * tile : (k + 1) * tile, :] = total
        for n in range(seqs):
            result = terms[n, pl.ds(0, tile, stride=tile), :]
            for p in range(1, tile):
                result = result + terms[n, pl.ds(p, tile, stride=tile), :]
            made[n, pl.ds(base, tile), :] = result
        return tuple(state)

    lax.fori_loop(0, length // tile, back_step, load(end_ref))
    empty(made, out_ref, place_ref[0])


def conv_call(kernel, place, arrays, results, scratch, flops):
    channels = arrays[0].shape[-1]
    lanes = min(channels, 128)

    def spec(shape):
        lead = len(shape) - 1
        return pl.BlockSpec(shape[:-1] + (lanes,), lambda i, *_: (0,) * lead + (i,))

    return pl.pallas_call(
        kernel,
        out_shape=results,
        grid_spec=pltpu.PrefetchScalarGridSpec(
            num_scalar_prefetch=1,
            grid=(channels // lanes,),
            in_specs=[spec(a.shape) for a in arrays],
            out_specs=[spec(r.shape) for r in results],
            scratch_shapes=[pltpu.VMEM(s + (lanes,), wide) for s in scratch],
        ),
        compiler_params=pltpu.CompilerParams(
            dimension_semantics=("arbitrary",), vmem_limit_bytes=48 << 20
        ),
        cost_estimate=pl.CostEstimate(
            flops=flops, transcendentals=0, bytes_accessed=sum(a.size * 4 for a in arrays)
        ),
    )(place, *arrays)


def sizes(signal, poles):
    groups, parts, inner, length, channels = signal.shape
    return groups * inner, parts * length, channels, signal.size * poles


def states_of(place, signal, decay):
    seqs, length, channels, work = sizes(signal, decay.shape[0])
    shape = jax.ShapeDtypeStruct((seqs, decay.shape[0], channels), wide)
    return conv_call(
        states_kernel, place, [signal, decay], [shape, shape], [(seqs, length)], 4 * work
    )


def forward_of(place, signal, decay, residue, start):
    seqs, length, channels, work = sizes(signal, decay.shape[0])
    return conv_call(
        forward_kernel,
        place,
        [signal, decay, residue, start],
        [jax.ShapeDtypeStruct(signal.shape, low)],
        [(seqs, length), (seqs, tile * tile), (seqs, length)],
        4 * work,
    )[0]


def later_of(place, signal, decay):
    seqs, length, channels, work = sizes(signal, decay.shape[0])
    shape = jax.ShapeDtypeStruct((seqs, decay.shape[0], channels), wide)
    return conv_call(later_kernel, place, [signal, decay], [shape], [(seqs, length)], 2 * work)[0]


def backward_of(place, signal, grad, decay, residue, start, slope, end):
    seqs, length, channels, work = sizes(signal, decay.shape[0])
    shape = jax.ShapeDtypeStruct(decay.shape, wide)
    return conv_call(
        backward_kernel,
        place,
        [signal, grad, decay, residue, start, slope, end],
        [jax.ShapeDtypeStruct(signal.shape, low), shape, shape],
        [(seqs, length), (seqs, length), (seqs, tile * tile), (seqs, length)],
        12 * work,
    )


def rms_scale(values):
    return lax.rsqrt(jnp.mean(values * values, axis=-1, keepdims=True) + epsilon)


def norm_back(values, scale, gain, grad_normed):
    grad_gain = jnp.sum(grad_normed * values * scale, axis=(0, 1))
    scaled = grad_normed * gain
    grad_values = scale * scaled - values * scale * scale * scale * jnp.mean(
        scaled * values, axis=-1, keepdims=True
    )
    return (grad_values, grad_gain)


def dot(a, b, kind=wide):
    return jnp.dot(a, b, preferred_element_type=wide).astype(kind)


def dot_t(a, b, kind=wide):
    return lax.dot_general(a, b, (((1,), (1,)), ((), ())), preferred_element_type=wide).astype(kind)


def dot_w(a, b):
    return lax.dot_general(a, b, (((0,), (0,)), ((), ())), preferred_element_type=wide).astype(low)


def body(
    tokens,
    lengths,
    norm_gain,
    in_weight,
    conv_taps,
    filter_residue,
    filter_decay,
    out_weight,
    feed_gain,
    gate_weight,
    up_weight,
    down_weight,
    cotangent,
):
    spread, ycount = lax.axis_size("x"), lax.axis_size("y")
    batch, local, width = tokens.shape
    place = lax.axis_index("z") * spread + lax.axis_index("x")
    position = place * local + jnp.arange(local)
    mask = (position[None, :] < lengths[:, None]).astype(wide)[..., None]
    block = spread * local

    in_pieces = column_pieces(in_weight, 3)
    hidden = after(tokens, in_pieces).astype(wide)
    scale_one = rms_scale(hidden)
    normed = (hidden * scale_one * norm_gain).astype(low)
    in_block = column_block(in_pieces)
    w_in = gather_tile(in_block)
    normed_all = gather_tokens(normed)
    gate_weight, out_weight, up_weight, down_weight = after(
        (gate_weight, out_weight, up_weight, down_weight), normed_all, in_block
    )
    gate_block = column_block(column_pieces(gate_weight, 1))
    w_gate = gather_tile(gate_block)
    w_out = gather_out(after(out_weight, gate_block))
    up_pieces = column_pieces(up_weight, 1)
    down_piece = after(row_block(down_weight), gate_block)
    w_down = gather_tile(down_piece)
    up_block = after(column_block(after(up_pieces, w_out)), down_piece)
    w_up = gather_tile(up_block)
    cotangent = after(cotangent, w_out)
    grad_out = cotangent.astype(wide) * mask
    grad_feed_all = gather_tokens(grad_out.astype(low))

    channels = w_in.shape[1] // 3
    grid = (2 * ycount, spread, batch // 2, local)
    taps = jnp.concatenate(
        [rank_rows(conv_taps[:, g * width : (g + 1) * width], 1) for g in range(3)], axis=1
    )
    decay = rank_rows(filter_decay, 0).T
    residue = rank_rows(filter_residue, 0).T
    mixed = dot(normed_all, w_in, low).reshape(grid + (3 * channels,))
    opening = (lax.axis_index("x") + jnp.arange(spread)) % spread == 0
    opening = opening[None, :, None, None, None]
    closing = (lax.axis_index("x") + jnp.arange(spread)) % spread == spread - 1
    closing = closing[None, :, None, None, None]

    tail = jnp.roll(mixed[:, :, :, local - 2 :], 1, axis=1)
    behind = passed(tail, "z", 1)
    extended = jnp.concatenate([jnp.where(opening, behind, tail), mixed], axis=3).astype(wide)
    short = (
        taps[0] * extended[:, :, :, 2:]
        + taps[1] * extended[:, :, :, 1:-1]
        + taps[2] * extended[:, :, :, :-2]
    )
    query = short[..., :channels]
    keys = short[..., channels : 2 * channels]
    values = short[..., 2 * channels :]
    product = (keys * values).astype(low)

    spot = lax.axis_index("x").astype(jnp.int32).reshape(1)
    state_end, slope_end = states_of(spot, product, decay)
    states = [passed(state_end, "z", k) for k in range(1, depth)]
    start = states[0]
    for k in range(1, depth - 1):
        start = start + jnp.exp(-decay * (k * block)) * states[k]
    convolved = forward_of(spot, product, decay, residue, start)
    gated = (query * convolved.astype(wide)).astype(low)
    gated_slots = gated.reshape(2, ycount, spread, -1, channels)
    got = swap_slots(
        [
            [gated_slots[:, k, i].reshape(-1, channels) for i in range(spread)]
            for k in range(ycount)
        ]
    )
    half = channels // 2
    gated_own = jnp.concatenate(
        [g[:, h * half : (h + 1) * half] for h in range(2) for line in got for g in line], axis=1
    )
    mixer = in_order(jnp.stack([dot(gated_own, w) for w in w_out]), "c")
    mixer = jnp.concatenate([m for m in mixer], axis=1).reshape(batch, local, width)
    middle = hidden + mixer

    scale_two = rms_scale(middle)
    normed_two = (middle * scale_two * feed_gain).astype(low)
    normed_two_all = gather_tokens(normed_two)
    gate = dot(normed_two_all, w_gate)
    sigma = jax.nn.sigmoid(gate)
    grad_active = dot_t(grad_feed_all, w_down)
    grad_upper = (grad_active * gate * sigma).astype(low)
    up_term = dot_w(normed_two_all, grad_upper)
    up_mine = scatter_tile(up_term)
    upper = dot(normed_two_all, after(w_up, up_term))
    active = (gate * sigma * upper).astype(low)
    grad_gate = (grad_active * upper * sigma * (1.0 + gate * (1.0 - sigma))).astype(low)
    partial_two = (dot_t(grad_gate, w_gate) + dot_t(grad_upper, w_up)).astype(low)
    grad_normed_two = scatter_tokens(partial_two, batch)
    weigh_two, weigh_gate = after((normed_two_all, grad_gate), partial_two)
    gate_term = dot_w(weigh_two, weigh_gate)
    gate_mine = scatter_tile(gate_term)
    weigh_active, weigh_feed = after((active, grad_feed_all), gate_term)
    down_term = dot_w(weigh_active, weigh_feed)
    down_mine = scatter_tile(down_term)

    grad_middle, grad_feed_gain = norm_back(middle, scale_two, feed_gain, grad_normed_two)
    grad_middle = grad_middle + grad_out
    grad_mix = grad_middle.astype(low).reshape(-1, width)

    mix_parts = core_halves(grad_mix)
    grad_gated_own = sum(dot_t(m, w) for m, w in zip(mix_parts, w_out)).astype(low)
    grad_slots = after(grad_gated_own, up_mine, gate_term).reshape(-1, 2, ycount, spread, half)
    got = swap_slots(
        [
            [grad_slots[:, :, k, i].reshape(-1, channels) for i in range(spread)]
            for k in range(ycount)
        ]
    )
    grad_gated = jnp.stack([jnp.stack(line) for line in got])
    grad_gated = grad_gated.reshape(ycount, spread, 2, batch // 2, local, channels)
    grad_gated = jnp.moveaxis(grad_gated, 2, 0).reshape(grid + (channels,)).astype(wide)
    grad_gated = after(grad_gated, down_term)
    grad_query = grad_gated * convolved.astype(wide)
    grad_conv = (grad_gated * query).astype(low)

    later_end = later_of(spot, grad_conv, decay)
    laters = [passed(later_end, "z", -k) for k in range(1, depth)]
    later = laters[0]
    for k in range(1, depth - 1):
        later = later + jnp.exp(-decay * (k * block)) * laters[k]
    slope_end = after(slope_end, normed_two_all)
    slopes = [passed(slope_end, "z", k) for k in range(1, depth)]
    slope = slopes[0]
    for k in range(1, depth - 1):
        slope = slope + jnp.exp(-decay * (k * block)) * (slopes[k] + (k * block) * states[k])

    low_taps = [taps[:, g * channels : (g + 1) * channels] for g in range(3)]

    def short_back(grad_short, weights):
        head = jnp.roll(grad_short[:, :, :, :2].astype(low), -1, axis=1)
        ahead = passed(head, "z", -1)
        whole = jnp.concatenate([grad_short, jnp.where(closing, ahead, head).astype(wide)], axis=3)
        result = (
            weights[0] * whole[:, :, :, :-2]
            + weights[1] * whole[:, :, :, 1:-1]
            + weights[2] * whole[:, :, :, 2:]
        )
        return result.astype(low).reshape(-1, grad_short.shape[-1])

    grad_mixed_query = short_back(grad_query, low_taps[0])
    query_mine = scatter_tile(after(dot_w(normed_all, grad_mixed_query), down_term))

    grad_product, grad_residue, grad_decay = backward_of(
        spot, product, grad_conv, decay, residue, start, slope, later
    )
    grad_product = grad_product.astype(wide)
    grad_pair = jnp.concatenate([grad_product * values, grad_product * keys], axis=-1)
    grad_mixed_pair = short_back(grad_pair, jnp.concatenate(low_taps[1:], axis=1))
    grad_mixed_pair = after(grad_mixed_pair, gate_mine)
    pair_mine = scatter_tile(dot_w(normed_all, grad_mixed_pair))
    grad_mixed = jnp.concatenate([grad_mixed_query, grad_mixed_pair], axis=1)
    grad_normed = scatter_tokens(dot_t(grad_mixed, w_in, low), batch)
    grad_normed = after(grad_normed, down_mine)
    grad_hidden, grad_norm_gain = norm_back(hidden, scale_one, norm_gain, grad_normed)
    grad_tokens = (grad_hidden + grad_middle).astype(low)

    feed_active = after(active, grad_mixed_pair)
    feed = scatter_tokens(dot(feed_active, w_down, low), batch)
    feed = after(feed, query_mine)
    output = (mask * (middle + feed)).astype(low)
    up_mine = after(up_mine, grad_conv)
    gated_late, mix_late = after((gated_own, mix_parts), grad_gated)
    grad_out_weight = out_owner([dot_w(gated_late, m) for m in mix_late])
    grad_up_weight = column_owner(up_mine, 1)
    grad_gate_weight = column_owner(gate_mine, 1)
    grad_down = row_owner(down_mine)
    grad_in_weight = jnp.concatenate(
        [column_owner(query_mine, 1), column_owner(pair_mine, 2)], axis=1
    )

    query_late, pair_late, extended_late = after((grad_query, grad_pair, extended), grad_mixed_pair)
    grad_taps = []
    for g, part in enumerate((query_late, pair_late[..., :channels], pair_late[..., channels:])):
        own = extended_late[..., g * channels : (g + 1) * channels]
        grad_taps += [
            jnp.sum(part * own[:, :, :, 2 - j : local + 2 - j], axis=(0, 1, 2, 3)) for j in range(3)
        ]
    gains = jnp.stack([grad_norm_gain, grad_feed_gain]).reshape(-1, channels)
    small = jnp.concatenate([grad_residue, grad_decay, jnp.stack(grad_taps)], axis=0)
    count = small.shape[0]
    small = sum_axis(sum_axis(jnp.concatenate([small, gains], axis=0), "c"), "z")
    small = gather_slots(gather_slots(small, "x"), "y")
    gains = jnp.sum(small[:, :, count:], axis=(0, 1)).reshape(2, width)
    small = all_channels(small[:, :, :count])
    poles = decay.shape[0]
    grad_conv_taps = jnp.concatenate(
        [small[2 * poles + 3 * g : 2 * poles + 3 * g + 3] for g in range(3)], axis=1
    )
    return (
        output,
        grad_tokens,
        gains[0],
        grad_in_weight,
        grad_conv_taps,
        small[:poles].T,
        small[poles : 2 * poles].T,
        grad_out_weight,
        gains[1],
        grad_gate_weight,
        grad_up_weight,
        grad_down,
    )


def solution(mesh):
    pairs, blocks = mesh.shape["dp"], mesh.shape["seq"]
    devices = mesh.devices.reshape(pairs // cores, cores, depth, blocks // depth)
    inner = Mesh(devices, ("y", "c", "z", "x"))
    dp, seq = ("y", "c"), ("z", "x")
    tokens, rows = P(dp, seq, None), P(seq, None)
    return jax.shard_map(
        body,
        mesh=inner,
        in_specs=(
            tokens,
            P(dp),
            P(),
            rows,
            P(),
            P(),
            P(),
            rows,
            P(),
            rows,
            rows,
            rows,
            tokens,
        ),
        out_specs=(tokens, tokens, P(), rows, P(), P(), P(), rows, P(), rows, rows, rows),
        check_vma=False,
    )
```

```python
import functools

import jax
import jax.numpy as jnp
from jax import lax
from jax.experimental import pallas as pl
from jax.experimental.pallas import tpu as pltpu
from jax.sharding import Mesh, PartitionSpec as P

epsilon = 1e-06
low = jnp.bfloat16
wide = jnp.float32
tile = 8
depth = 4
cores = 2


def turned(value, axis, by):
    length = lax.axis_size(axis)
    return lax.ppermute(value, axis, [(i, (i + by) % length) for i in range(length)])


def passed(value, axis, by):
    length = lax.axis_size(axis)
    pairs = [(i, i + by) for i in range(length) if 0 <= i + by < length]
    return lax.ppermute(value, axis, pairs)


def swap_slots(slots):
    ycount, spread = lax.axis_size("y"), lax.axis_size("x")
    result = []
    for dy in range(ycount):
        line = []
        for dx in range(spread):
            sy, sx = (ycount - dy) % ycount, (spread - dx) % spread
            if sy == 0 and sx == 0:
                line.append(slots[0][0])
                continue
            pairs = [
                (i * spread + j, (i + sy) % ycount * spread + (j + sx) % spread)
                for i in range(ycount)
                for j in range(spread)
            ]
            line.append(lax.ppermute(slots[sy][sx], ("y", "x"), pairs))
        result.append(line)
    return result


class Line:
    def __init__(self):
        self.last = ()

    def run(self, work, *values):
        values = lax.optimization_barrier((values, self.last))[0]
        result = work(*values)
        self.last = jax.tree.leaves(result)
        return result


def moved(value, axis, sign):
    return [turned(value, axis, sign * d) for d in range(1, lax.axis_size(axis))]


class Gather:
    def __init__(self, first, second):
        self.held = (first, second)
        self.got = (moved(first, "x", -1), moved(second, "y", -1))

    def turn(self, line):
        self.held = line.run(
            lambda held, got: tuple(jnp.stack([h] + g) for h, g in zip(held, got)), self.held, self.got
        )
        self.got = (moved(self.held[0], "y", -1), moved(self.held[1], "x", -1))

    def end(self, line):
        def work(held, got):
            first = jnp.stack([held[0]] + got[0])
            second = jnp.swapaxes(jnp.stack([held[1]] + got[1]), 0, 1)
            return jnp.stack([first, second]).reshape(-1, first.shape[-1])

        return line.run(work, self.held, self.got)


def split_sum(partial):
    grid = partial.reshape(2, lax.axis_size("y"), lax.axis_size("x"), -1, partial.shape[-1])
    first = [grid[0][:, d].astype(low) for d in range(grid.shape[2])]
    second = [grid[1][d].astype(low) for d in range(grid.shape[1])]
    return first, second


def add_up(parts, got):
    total = parts[0].astype(wide)
    for g in got:
        total = total + g.astype(wide)
    return total


class Scatter:
    def __init__(self, parts):
        self.parts = parts
        self.send("x", "y")

    def send(self, *axes):
        self.got = [
            [turned(p, axis, d + 1) for d, p in enumerate(part[1:])]
            for part, axis in zip(self.parts, axes)
        ]

    def turn(self, line):
        def work(parts, got):
            result = []
            for part, g in zip(parts, got):
                total = add_up(part, g).astype(low)
                result.append([total[d] for d in range(total.shape[0])])
            return result

        self.parts = line.run(work, self.parts, self.got)
        self.send("y", "x")

    def rest(self):
        return self.parts, self.got

    @staticmethod
    def sum(parts, got):
        return jnp.stack([add_up(part, g) for part, g in zip(parts, got)])


def pick_kernel(count, part, stride, start_ref, source, *refs):
    targets, sems = refs[:-1], refs[-1]
    copies = []
    for d, target in enumerate(targets):
        for k in range(count):
            at = pl.multiple_of((k * stride + start_ref[d]) * part, part)
            copies.append(
                pltpu.make_async_copy(
                    source.at[:, pl.ds(at, part)],
                    target.at[:, k * part : (k + 1) * part],
                    sems.at[d * count + k],
                )
            )
    for copy in copies:
        copy.start()
    for copy in copies:
        copy.wait()


def column_pieces(weight, groups):
    spread, ycount = lax.axis_size("x"), lax.axis_size("y")
    rows = weight.shape[0]
    count = groups * depth
    part = weight.shape[1] // (count * spread * ycount)
    starts = [
        (lax.axis_index("x") + d) % spread * ycount + lax.axis_index("y") for d in range(spread)
    ]
    if part % 128 == 0:
        return pl.pallas_call(
            functools.partial(pick_kernel, count, part, spread * ycount),
            out_shape=[jax.ShapeDtypeStruct((rows, count * part), weight.dtype)] * spread,
            grid_spec=pltpu.PrefetchScalarGridSpec(
                num_scalar_prefetch=1,
                in_specs=[pl.BlockSpec(memory_space=pl.ANY)],
                out_specs=[pl.BlockSpec(memory_space=pltpu.VMEM)] * spread,
                scratch_shapes=[pltpu.SemaphoreType.DMA((count * spread,))],
            ),
            cost_estimate=pl.CostEstimate(
                flops=0, transcendentals=0, bytes_accessed=4 * rows * count * part * spread
            ),
        )(jnp.stack(starts).astype(jnp.int32), weight)
    return [
        jnp.concatenate(
            [
                lax.dynamic_slice_in_dim(weight, (k * spread * ycount + start) * part, part, 1)
                for k in range(count)
            ],
            axis=1,
        )
        for start in starts
    ]


def column_moves(pieces):
    spread, ccount = lax.axis_size("x"), lax.axis_size("c")
    share = spread // ccount
    got = [pieces[0]]
    for d in range(1, spread):
        pairs = [
            (i // share * spread + i, i // share * spread + (i + d) % spread) for i in range(spread)
        ]
        got.append(lax.ppermute(pieces[d], ("c", "x"), pairs))
    return got


def column_block(got):
    spread, ccount = lax.axis_size("x"), lax.axis_size("c")
    share = spread // ccount
    place, core = lax.axis_index("x"), lax.axis_index("c")
    got = jnp.stack(got)
    return jnp.concatenate(
        [
            lax.dynamic_index_in_dim(got, (place - core * share - j) % spread, 0, False)
            for j in range(share)
        ]
    )


def row_block(weight):
    ycount, ccount = lax.axis_size("y"), lax.axis_size("c")
    part = weight.shape[0] // (ycount * ccount)
    pair = lax.axis_index("y") * ccount + lax.axis_index("c")
    return lax.dynamic_slice_in_dim(weight, pair * part, part, 0)


def core_halves(value):
    ccount = lax.axis_size("c")
    width = value.shape[1] // ccount
    core = lax.axis_index("c")
    return [
        lax.dynamic_slice_in_dim(value, (core + d) % ccount * width, width, 1)
        for d in range(ccount)
    ]


def out_block(weight):
    part = weight.shape[0] // lax.axis_size("y")
    rows = lax.dynamic_slice_in_dim(weight, lax.axis_index("y") * part, part, 0)
    return core_halves(rows)[0]


def by_z(slots):
    held = in_order(jnp.stack(slots), "z")
    return held.reshape(2, -1, held.shape[-1])


def z_slots(mine):
    mine = mine.reshape(depth, -1, mine.shape[-1]).astype(low)
    place = lax.axis_index("z")
    return [
        lax.dynamic_index_in_dim(mine, (place + d) % depth, 0, False) for d in range(depth)
    ]


def gather_tile(block):
    return lax.all_gather(block, ("z", "c"), axis=0, tiled=True)


def scatter_tile(term):
    return lax.psum_scatter(term, ("z", "c"), scatter_dimension=0, tiled=True)


def owner_parts(mine):
    spread, ccount = lax.axis_size("x"), lax.axis_size("c")
    share = spread // ccount
    place, core = lax.axis_index("x"), lax.axis_index("c")
    parts = mine.reshape(share, -1, mine.shape[-1])
    return [
        lax.dynamic_index_in_dim(
            parts, jnp.clip((place + d) % spread - core * share, 0, share - 1), 0, False
        )
        for d in range(spread)
    ]


def owner_moves(parts):
    spread, ccount = lax.axis_size("x"), lax.axis_size("c")
    share = spread // ccount
    got = [parts[0]]
    for d in range(1, spread):
        pairs = [
            ((i + d) % spread // share * spread + i, i // share * spread + (i + d) % spread)
            for i in range(spread)
        ]
        got.append(lax.ppermute(parts[d], ("c", "x"), pairs))
    return got


def owner_held(got):
    spread, ccount = lax.axis_size("x"), lax.axis_size("c")
    share = spread // ccount
    place, core = lax.axis_index("x"), lax.axis_index("c")
    got = jnp.stack(got)
    return jnp.stack(
        [
            lax.dynamic_index_in_dim(got, (place - core * share - j) % spread, 0, False)
            for j in range(share)
        ]
    )


def owner_ranks(slots):
    spread, ccount, ycount = lax.axis_size("x"), lax.axis_size("c"), lax.axis_size("y")
    share = spread // ccount
    core, yplace = lax.axis_index("c"), lax.axis_index("y")
    flat = slots.reshape((-1,) + slots.shape[3:])
    ranks = []
    for i in range(spread):
        for k in range(ycount):
            slot = (i // share - core) % ccount * ycount + (k - yplace) % ycount
            ranks.append(lax.dynamic_index_in_dim(flat, slot * share + i % share, 0, False))
    return ranks


def owner_whole(ranks, count):
    part = ranks[0].shape[1] // count
    pieces = []
    for at in range(count):
        pieces += [r[:, at * part : (at + 1) * part].astype(wide) for r in ranks]
    return jnp.concatenate(pieces, axis=1)


def in_order(slots, axis):
    length = lax.axis_size(axis)
    place = lax.axis_index(axis)
    return jnp.stack(
        [lax.dynamic_index_in_dim(slots, (j - place) % length, 0, False) for j in range(length)]
    )


def rank_rows(values, axis):
    spread, ycount = lax.axis_size("x"), lax.axis_size("y")
    part = values.shape[axis] // (depth * spread * ycount)
    place = lax.axis_index("x") * ycount + lax.axis_index("y")
    return jnp.concatenate(
        [
            lax.dynamic_slice_in_dim(values, (k * spread * ycount + place) * part, part, axis)
            for k in range(depth)
        ],
        axis=axis,
    )


def all_channels(slots):
    whole = in_order(slots, "y")
    whole = in_order(jnp.swapaxes(whole, 0, 1), "x")
    spread, ycount, rows = whole.shape[:3]
    whole = whole.reshape(spread, ycount, rows, depth, -1)
    return jnp.transpose(whole, (2, 3, 0, 1, 4)).reshape(rows, -1)


def fill(source, target, place):
    groups, parts, inner, length = source.shape[:4]
    for j in range(parts):
        slot = lax.rem(j + parts - place, parts)
        for g in range(groups):
            for b in range(inner):
                target[g * inner + b, j * length : (j + 1) * length, :] = source[g, slot, b].astype(
                    wide
                )


def empty(source, target, place):
    groups, parts, inner, length = target.shape[:4]
    for j in range(parts):
        slot = lax.rem(j + parts - place, parts)
        for g in range(groups):
            for b in range(inner):
                target[g, slot, b] = source[g * inner + b, j * length : (j + 1) * length, :].astype(
                    low
                )


def halves(ref):
    return [ref[k * tile : (k + 1) * tile, :] for k in range(ref.shape[0] // tile)]


def row_of(ref, seq, at):
    return ref[seq, pl.ds(at, tile, stride=0), :]


def states_kernel(place_ref, signal_ref, decay_ref, state_ref, slope_ref, held):
    fill(signal_ref, held, place_ref[0])
    seqs, length, lanes = held.shape
    keep = [jnp.exp(-d) for d in halves(decay_ref)]
    count = len(keep)
    zero = jnp.zeros((tile, lanes), wide)

    def step(i, carry):
        state, slope = [list(v) for v in carry]
        for k in range(tile):
            for n in range(seqs):
                new = row_of(held, n, i * tile + k)
                for h in range(count):
                    at = n * count + h
                    slope[at] = keep[h] * (slope[at] + state[at])
                    state[at] = keep[h] * state[at] + new
        return tuple(state), tuple(slope)

    start = tuple(zero for _ in range(seqs * count))
    state, slope = lax.fori_loop(0, length // tile, step, (start, start))
    for n in range(seqs):
        for h in range(count):
            state_ref[n, h * tile : (h + 1) * tile, :] = state[n * count + h]
            slope_ref[n, h * tile : (h + 1) * tile, :] = slope[n * count + h]


def forward_kernel(place_ref, signal_ref, decay_ref, residue_ref, start_ref, out_ref, held, terms, made):
    fill(signal_ref, held, place_ref[0])
    seqs, length, lanes = held.shape
    keep = [jnp.exp(-d) for d in halves(decay_ref)]
    weigh = halves(residue_ref)
    count = len(keep)

    def step(i, carry):
        state = list(carry)
        for k in range(tile):
            for n in range(seqs):
                new = row_of(held, n, i * tile + k)
                total = None
                for h in range(count):
                    at = n * count + h
                    state[at] = keep[h] * state[at] + new
                    term = weigh[h] * state[at]
                    total = term if total is None else total + term
                terms[n, k * tile : (k + 1) * tile, :] = total
        for n in range(seqs):
            result = terms[n, pl.ds(0, tile, stride=tile), :]
            for p in range(1, tile):
                result = result + terms[n, pl.ds(p, tile, stride=tile), :]
            made[n, pl.ds(i * tile, tile), :] = result
        return tuple(state)

    start = tuple(
        start_ref[n, h * tile : (h + 1) * tile, :] for n in range(seqs) for h in range(count)
    )
    lax.fori_loop(0, length // tile, step, start)
    empty(made, out_ref, place_ref[0])


def later_kernel(place_ref, signal_ref, decay_ref, state_ref, held):
    fill(signal_ref, held, place_ref[0])
    seqs, length, lanes = held.shape
    keep = [jnp.exp(-d) for d in halves(decay_ref)]
    count = len(keep)

    def step(i, carry):
        state = list(carry)
        base = length - tile - i * tile
        for k in range(tile - 1, -1, -1):
            for n in range(seqs):
                new = row_of(held, n, base + k)
                for h in range(count):
                    at = n * count + h
                    state[at] = keep[h] * state[at] + new
        return tuple(state)

    zero = jnp.zeros((tile, lanes), wide)
    state = lax.fori_loop(0, length // tile, step, tuple(zero for _ in range(seqs * count)))
    for n in range(seqs):
        for h in range(count):
            state_ref[n, h * tile : (h + 1) * tile, :] = state[n * count + h]


def backward_kernel(
    place_ref,
    signal_ref,
    grad_ref,
    decay_ref,
    residue_ref,
    start_ref,
    slope_ref,
    end_ref,
    out_ref,
    residue_grad_ref,
    decay_grad_ref,
    held,
    grads,
    terms,
    made,
):
    fill(signal_ref, held, place_ref[0])
    fill(grad_ref, grads, place_ref[0])
    seqs, length, lanes = held.shape
    keep = [jnp.exp(-d) for d in halves(decay_ref)]
    weigh = halves(residue_ref)
    count = len(keep)
    zero = jnp.zeros((tile, lanes), wide)

    def ahead(i, carry):
        state, slope, first, second = [list(v) for v in carry]
        for k in range(tile):
            for n in range(seqs):
                new = row_of(held, n, i * tile + k)
                back = row_of(grads, n, i * tile + k)
                for h in range(count):
                    at = n * count + h
                    slope[at] = keep[h] * (slope[at] + state[at])
                    state[at] = keep[h] * state[at] + new
                    first[at] = first[at] + back * state[at]
                    second[at] = second[at] + back * slope[at]
        return tuple(state), tuple(slope), tuple(first), tuple(second)

    def load(ref):
        return tuple(
            ref[n, h * tile : (h + 1) * tile, :] for n in range(seqs) for h in range(count)
        )

    none = tuple(zero for _ in range(seqs * count))
    _, _, first, second = lax.fori_loop(
        0, length // tile, ahead, (load(start_ref), load(slope_ref), none, none)
    )
    for h in range(count):
        sum_first, sum_second = first[h], second[h]
        for n in range(1, seqs):
            sum_first = sum_first + first[n * count + h]
            sum_second = sum_second + second[n * count + h]
        residue_grad_ref[h * tile : (h + 1) * tile, :] = sum_first
        decay_grad_ref[h * tile : (h + 1) * tile, :] = -weigh[h] * sum_second

    def back_step(i, carry):
        state = list(carry)
        base = length - tile - i * tile
        for k in range(tile - 1, -1, -1):
            for n in range(seqs):
                new = row_of(grads, n, base + k)
                total = None
                for h in range(count):
                    at = n * count + h
                    state[at] = keep[h] * state[at] + new
                    term = weigh[h] * state[at]
                    total = term if total is None else total + term
                terms[n, k * tile : (k + 1) * tile, :] = total
        for n in range(seqs):
            result = terms[n, pl.ds(0, tile, stride=tile), :]
            for p in range(1, tile):
                result = result + terms[n, pl.ds(p, tile, stride=tile), :]
            made[n, pl.ds(base, tile), :] = result
        return tuple(state)

    lax.fori_loop(0, length // tile, back_step, load(end_ref))
    empty(made, out_ref, place_ref[0])


def conv_call(kernel, place, arrays, results, scratch, flops):
    channels = arrays[0].shape[-1]
    lanes = min(channels, 128)

    def spec(shape):
        lead = len(shape) - 1
        return pl.BlockSpec(shape[:-1] + (lanes,), lambda i, *_: (0,) * lead + (i,))

    return pl.pallas_call(
        kernel,
        out_shape=results,
        grid_spec=pltpu.PrefetchScalarGridSpec(
            num_scalar_prefetch=1,
            grid=(channels // lanes,),
            in_specs=[spec(a.shape) for a in arrays],
            out_specs=[spec(r.shape) for r in results],
            scratch_shapes=[pltpu.VMEM(s + (lanes,), wide) for s in scratch],
        ),
        compiler_params=pltpu.CompilerParams(
            dimension_semantics=("arbitrary",), vmem_limit_bytes=48 << 20
        ),
        cost_estimate=pl.CostEstimate(
            flops=flops, transcendentals=0, bytes_accessed=sum(a.size * 4 for a in arrays)
        ),
    )(place, *arrays)


def sizes(signal, poles):
    groups, parts, inner, length, channels = signal.shape
    return groups * inner, parts * length, channels, signal.size * poles


def states_of(place, signal, decay):
    seqs, length, channels, work = sizes(signal, decay.shape[0])
    shape = jax.ShapeDtypeStruct((seqs, decay.shape[0], channels), wide)
    return conv_call(
        states_kernel, place, [signal, decay], [shape, shape], [(seqs, length)], 4 * work
    )


def forward_of(place, signal, decay, residue, start):
    seqs, length, channels, work = sizes(signal, decay.shape[0])
    return conv_call(
        forward_kernel,
        place,
        [signal, decay, residue, start],
        [jax.ShapeDtypeStruct(signal.shape, low)],
        [(seqs, length), (seqs, tile * tile), (seqs, length)],
        4 * work,
    )[0]


def later_of(place, signal, decay):
    seqs, length, channels, work = sizes(signal, decay.shape[0])
    shape = jax.ShapeDtypeStruct((seqs, decay.shape[0], channels), wide)
    return conv_call(later_kernel, place, [signal, decay], [shape], [(seqs, length)], 2 * work)[0]


def backward_of(place, signal, grad, decay, residue, start, slope, end):
    seqs, length, channels, work = sizes(signal, decay.shape[0])
    shape = jax.ShapeDtypeStruct(decay.shape, wide)
    return conv_call(
        backward_kernel,
        place,
        [signal, grad, decay, residue, start, slope, end],
        [jax.ShapeDtypeStruct(signal.shape, low), shape, shape],
        [(seqs, length), (seqs, length), (seqs, tile * tile), (seqs, length)],
        12 * work,
    )


def rms_scale(values):
    return lax.rsqrt(jnp.mean(values * values, axis=-1, keepdims=True) + epsilon)


def norm_back(values, scale, gain, grad_normed):
    grad_gain = jnp.sum(grad_normed * values * scale, axis=(0, 1))
    scaled = grad_normed * gain
    grad_values = scale * scaled - values * scale * scale * scale * jnp.mean(
        scaled * values, axis=-1, keepdims=True
    )
    return (grad_values, grad_gain)


def dot(a, b, kind=wide):
    return jnp.dot(a, b, preferred_element_type=wide).astype(kind)


def dot_t(a, b, kind=wide):
    return lax.dot_general(a, b, (((1,), (1,)), ((), ())), preferred_element_type=wide).astype(kind)


def dot_w(a, b):
    return lax.dot_general(a, b, (((0,), (0,)), ((), ())), preferred_element_type=wide).astype(low)


def body(
    tokens,
    lengths,
    norm_gain,
    in_weight,
    conv_taps,
    filter_residue,
    filter_decay,
    out_weight,
    feed_gain,
    gate_weight,
    up_weight,
    down_weight,
    cotangent,
):
    spread, ycount = lax.axis_size("x"), lax.axis_size("y")
    batch, local, width = tokens.shape
    place = lax.axis_index("z") * spread + lax.axis_index("x")
    position = place * local + jnp.arange(local)
    mask = (position[None, :] < lengths[:, None]).astype(wide)[..., None]
    block = spread * local

    count = 3 * depth
    line = Line()
    run = line.run

    def stacked(value, got):
        return jnp.stack([value] + got)

    block_out = run(out_block, out_weight)
    out_got = moved(block_out, "z", -1)
    in_got = column_moves(run(lambda w: column_pieces(w, 3), in_weight))

    def norm_one(values, gain):
        values = values.astype(wide)
        scale = rms_scale(values)
        normed = (values * scale * gain).astype(low)
        return normed[: batch // 2], normed[batch // 2 :], scale

    first, second, scale_one = run(norm_one, tokens, norm_gain)
    normed_move = Gather(first, second)
    w_in = gather_tile(run(column_block, in_got))
    normed_move.turn(line)
    w_down = gather_tile(run(row_block, down_weight))
    held = run(lambda own, got: by_z([own] + got), block_out, out_got)
    out_move = Gather(held[:1], held[1:])
    gate_got = column_moves(run(lambda w: column_pieces(w, 1), gate_weight))
    normed_all = normed_move.end(line)
    out_move.turn(line)
    w_gate = gather_tile(run(column_block, gate_got))
    up_got = column_moves(run(lambda w: column_pieces(w, 1), up_weight))

    channels = w_in.shape[1] // 3
    half = channels // 2
    grid = (2 * ycount, spread, batch // 2, local)

    def rank_values(all_taps, all_decay, all_residue):
        return (
            jnp.concatenate(
                [rank_rows(all_taps[:, g * width : (g + 1) * width], 1) for g in range(3)], axis=1
            ),
            rank_rows(all_decay, 0).T,
            rank_rows(all_residue, 0).T,
        )

    taps, decay, residue = run(rank_values, conv_taps, filter_decay, filter_residue)
    opening = (lax.axis_index("x") + jnp.arange(spread)) % spread == 0
    opening = opening[None, :, None, None, None]
    closing = (lax.axis_index("x") + jnp.arange(spread)) % spread == spread - 1
    closing = closing[None, :, None, None, None]

    def project(v, w):
        value = dot(v, w, low).reshape(grid + (3 * channels,))
        return value, jnp.roll(value[:, :, :, local - 2 :], 1, axis=1)

    mixed, tail = run(project, normed_all, w_in)
    behind = passed(tail, "z", 1)

    def feed_grad(values):
        values = (values.astype(wide) * mask).astype(low)
        return values[: batch // 2], values[batch // 2 :]

    feed_move = Gather(*run(feed_grad, cotangent))
    w_up = gather_tile(run(column_block, up_got))
    out_own = out_move.end(line)
    w_out = [out_own] + moved(out_own, "c", -1)

    def extend(value, ends, before, g):
        at = slice(g * channels, (g + 1) * channels)
        return jnp.concatenate(
            [jnp.where(opening, before[..., at], ends[..., at]), value[..., at]], axis=3
        ).astype(wide)

    def short_of(value, ends, before, weights, g):
        longer = extend(value, ends, before, g)
        own = weights[:, g * channels : (g + 1) * channels]
        return own[0] * longer[:, :, :, 2:] + own[1] * longer[:, :, :, 1:-1] + own[2] * longer[:, :, :, :-2]

    spot = lax.axis_index("x").astype(jnp.int32).reshape(1)

    def multiply(value, ends, before, weights, rates):
        keys, values = (short_of(value, ends, before, weights, g) for g in (1, 2))
        product = (keys * values).astype(low)
        return (product,) + tuple(states_of(spot, product, rates))

    product, state_end, slope_end = run(multiply, mixed, tail, behind, taps, decay)
    states = [passed(state_end, "z", k) for k in range(1, depth)]
    feed_move.turn(line)

    def combine(parts, rates):
        total = parts[0]
        for k in range(1, depth - 1):
            total = total + jnp.exp(-rates * (k * block)) * parts[k]
        return total

    def convolve(parts, value, ends, before, weights, signal, rates, amounts):
        start = combine(parts, rates)
        result = forward_of(spot, signal, rates, amounts, start)
        query = short_of(value, ends, before, weights, 0)
        gated = (query * result.astype(wide)).astype(low)
        slots = gated.reshape(2, ycount, spread, -1, channels)
        return (
            start,
            result,
            [[slots[:, k, i].reshape(-1, channels) for i in range(spread)] for k in range(ycount)],
        )

    start, convolved, gated = run(
        convolve, states, mixed, tail, behind, taps, product, decay, residue
    )
    gated_got = swap_slots(gated)
    grad_feed_all = feed_move.end(line)

    def mix(got, weights, values, gain):
        own = jnp.concatenate(
            [g[:, h * half : (h + 1) * half] for h in range(2) for row in got for g in row], axis=1
        )
        mixer = in_order(jnp.stack([dot(own, w) for w in weights]), "c")
        mixer = jnp.concatenate([m for m in mixer], axis=1).reshape(batch, local, width)
        middle = values.astype(wide) + mixer
        scale = rms_scale(middle)
        normed = (middle * scale * gain).astype(low)
        return own, middle, scale, normed[: batch // 2], normed[batch // 2 :]

    gated_own, middle, scale_two, first, second = run(mix, gated_got, w_out, tokens, feed_gain)

    two_move = Gather(first, second)
    grad_active = run(dot_t, grad_feed_all, w_down)
    two_move.turn(line)
    slopes = [passed(slope_end, "z", k) for k in range(1, depth)]
    normed_two_all = two_move.end(line)

    def open_gate(v, w, back):
        value = dot(v, w)
        return value, (back * value * jax.nn.sigmoid(value)).astype(low)

    gate, grad_upper = run(open_gate, normed_two_all, w_gate, grad_active)
    up_term = run(dot_w, normed_two_all, grad_upper)
    up_mine = scatter_tile(up_term)

    def activate(v, w, value, back):
        upper = dot(v, w)
        sigma = jax.nn.sigmoid(value)
        return (
            (value * sigma * upper).astype(low),
            (back * upper * sigma * (1.0 + value * (1.0 - sigma))).astype(low),
        )

    active, grad_gate = run(activate, normed_two_all, w_up, gate, grad_active)
    two_back = Scatter(
        run(
            lambda a, b, wa, wb: split_sum((dot_t(a, wa) + dot_t(b, wb)).astype(low)),
            grad_gate,
            grad_upper,
            w_gate,
            w_up,
        )
    )
    gate_mine = scatter_tile(run(dot_w, normed_two_all, grad_gate))
    down_mine = scatter_tile(run(dot_w, active, grad_feed_all))
    two_back.turn(line)

    def middle_back(rest, values, scale, gain, back, weights):
        grad_normed = Scatter.sum(*rest).reshape(batch, local, width)
        result, grad_gain = norm_back(values, scale, gain, grad_normed)
        result = result + back.astype(wide) * mask
        parts = core_halves(result.astype(low).reshape(-1, width))
        own = sum(dot_t(m, w) for m, w in zip(parts, weights)).astype(low)
        slots = own.reshape(-1, 2, ycount, spread, half)
        return (
            result,
            grad_gain,
            parts,
            [
                [slots[:, :, k, i].reshape(-1, channels) for i in range(spread)]
                for k in range(ycount)
            ],
        )

    grad_middle, grad_feed_gain, mix_parts, grad_slots = run(
        middle_back, two_back.rest(), middle, scale_two, feed_gain, cotangent, w_out
    )
    grad_got = swap_slots(grad_slots)
    out_terms = run(lambda g, parts: [dot_w(g, m) for m in parts], gated_own, mix_parts)
    out_terms_got = [turned(t, "c", d + 1) for d, t in enumerate(out_terms[1:])]

    def conv_grads(got, result, value, ends, before, weights, rates):
        grad = jnp.stack([jnp.stack(row) for row in got])
        grad = grad.reshape(ycount, spread, 2, batch // 2, local, channels)
        grad = jnp.moveaxis(grad, 2, 0).reshape(grid + (channels,)).astype(wide)
        grad_query = (grad * result.astype(wide)).astype(wide)
        grad_conv = (grad * short_of(value, ends, before, weights, 0)).astype(low)
        return (
            grad_query,
            jnp.roll(grad_query[:, :, :, :2].astype(low), -1, axis=1),
            grad_conv,
            later_of(spot, grad_conv, rates),
        )

    grad_query, query_head, grad_conv, later_end = run(
        conv_grads, grad_got, convolved, mixed, tail, behind, taps, decay
    )
    laters = [passed(later_end, "z", -k) for k in range(1, depth)]
    query_ahead = passed(query_head, "z", -1)
    feed_back = Scatter(run(lambda a, w: split_sum(dot(a, w, low)), active, w_down))

    def short_back(grad_short, head, ahead, weights):
        whole = jnp.concatenate([grad_short, jnp.where(closing, ahead, head).astype(wide)], axis=3)
        result = (
            weights[0] * whole[:, :, :, :-2]
            + weights[1] * whole[:, :, :, 1:-1]
            + weights[2] * whole[:, :, :, 2:]
        )
        return result.astype(low).reshape(-1, grad_short.shape[-1])

    def query_back(grad, head, ahead, weights, v):
        result = short_back(grad, head, ahead, weights[:, :channels])
        return result, dot_w(v, result)

    grad_mixed_query, query_term = run(
        query_back, grad_query, query_head, query_ahead, taps, normed_all
    )
    query_mine = scatter_tile(query_term)

    def conv_back(signal, grad, rates, amounts, begin, parts, ended, ends_later, value, ends, before, weights):
        slope = parts[0]
        for k in range(1, depth - 1):
            slope = slope + jnp.exp(-rates * (k * block)) * (parts[k] + (k * block) * ended[k])
        later = combine(ends_later, rates)
        grad_product, grad_residue, grad_decay = backward_of(
            spot, signal, grad, rates, amounts, begin, slope, later
        )
        grad_product = grad_product.astype(wide)
        keys, values = (short_of(value, ends, before, weights, g) for g in (1, 2))
        pair = jnp.concatenate([grad_product * values, grad_product * keys], axis=-1)
        return pair, jnp.roll(pair[:, :, :, :2].astype(low), -1, axis=1), grad_residue, grad_decay

    grad_pair, pair_head, grad_residue, grad_decay = run(
        conv_back,
        product,
        grad_conv,
        decay,
        residue,
        start,
        slopes,
        states,
        laters,
        mixed,
        tail,
        behind,
        taps,
    )
    pair_ahead = passed(pair_head, "z", -1)
    feed_back.turn(line)

    def pair_back(grad, head, ahead, weights, v):
        result = short_back(grad, head, ahead, weights[:, channels:])
        return result, dot_w(v, result)

    grad_mixed_pair, pair_term = run(
        pair_back, grad_pair, pair_head, pair_ahead, taps, normed_all
    )
    pair_mine = scatter_tile(pair_term)
    one_back = Scatter(
        run(
            lambda a, b, w: split_sum(dot_t(jnp.concatenate([a, b], axis=1), w, low)),
            grad_mixed_query,
            grad_mixed_pair,
            w_in,
        )
    )

    out_back_parts = run(
        lambda own, got: split_sum(add_up([own], got)), out_terms[0], out_terms_got
    )
    parts = run(lambda a, b: owner_parts(jnp.concatenate([a, b], axis=1)), up_mine, gate_mine)
    both_got = owner_moves(parts)
    output = run(
        lambda rest, values: (
            mask * (values + Scatter.sum(*rest).reshape(batch, local, width))
        ).astype(low),
        feed_back.rest(),
        middle,
    )
    one_back.turn(line)
    out_back = Scatter(out_back_parts)

    def tap_sums(query, pair, value, ends, before):
        sums = []
        for g, part in enumerate((query, pair[..., :channels], pair[..., channels:])):
            own = extend(value, ends, before, g)
            sums += [
                jnp.sum(part * own[:, :, :, 2 - j : local + 2 - j], axis=(0, 1, 2, 3))
                for j in range(3)
            ]
        return jnp.stack(sums)

    grad_taps = run(tap_sums, grad_query, grad_pair, mixed, tail, behind)
    both_held = run(owner_held, both_got)
    both_got = moved(both_held, "y", -1)

    def tokens_back(rest, values, scale, gain, back, small):
        values = values.astype(wide)
        grad_normed = Scatter.sum(*rest).reshape(batch, local, width)
        result, grad_gain = norm_back(values, scale, gain, grad_normed)
        gains = jnp.stack([grad_gain, small[0]]).reshape(-1, channels)
        return (result + back).astype(low), jnp.concatenate(list(small[1:]) + [gains], axis=0)

    grad_tokens, small = run(
        tokens_back,
        one_back.rest(),
        tokens,
        scale_one,
        norm_gain,
        grad_middle,
        (grad_feed_gain, grad_residue, grad_decay, grad_taps),
    )
    small_got = moved(small, "c", 1)
    out_back.turn(line)
    both_held = run(stacked, both_held, both_got)
    both_got = moved(both_held, "c", -1)
    small = run(lambda v, got: v + sum(got), small, small_got)
    small_got = moved(small, "z", 1)
    down_got = moved(run(lambda v: v + 0, down_mine), "y", -1)
    out_slots = run(
        lambda rest: z_slots(Scatter.sum(*rest).reshape(channels, -1)), out_back.rest()
    )
    out_got = [turned(p, "z", d + 1) for d, p in enumerate(out_slots[1:])]
    small = run(lambda v, got: v + sum(got), small, small_got)
    small_got = moved(small, "x", -1)

    def both_whole(own, got):
        ranks = owner_ranks(jnp.stack([own] + got))
        middle_at = ranks[0].shape[1] // 2
        return (
            owner_whole([r[:, :middle_at] for r in ranks], depth),
            owner_whole([r[:, middle_at:] for r in ranks], depth),
        )

    grad_up_weight, grad_gate_weight = run(both_whole, both_held, both_got)
    down_held = run(stacked, down_mine, down_got)
    down_got = moved(down_held, "c", -1)
    out_held = run(lambda own, got: add_up([own], got).astype(low), out_slots[0], out_got)
    out_got = moved(out_held, "y", -1)
    small = run(stacked, small, small_got)
    small_got = moved(small, "y", -1)

    def down_whole(own, got):
        whole = in_order(jnp.swapaxes(in_order(jnp.stack([own] + got), "c"), 0, 1), "y")
        return whole.reshape(-1, width).astype(wide)

    grad_down = run(down_whole, down_held, down_got)
    out_held = run(stacked, out_held, out_got)
    out_got = moved(out_held, "c", -1)
    poles = decay.shape[0]

    def small_whole(own, got):
        slots = jnp.stack([own] + got)
        rows = 2 * poles + 9
        gains = jnp.sum(slots[:, :, rows:], axis=(0, 1)).reshape(2, width)
        whole = all_channels(slots[:, :, :rows])
        grad_conv_taps = jnp.concatenate(
            [whole[2 * poles + 3 * g : 2 * poles + 3 * g + 3] for g in range(3)], axis=1
        )
        return gains[0], gains[1], grad_conv_taps, whole[:poles].T, whole[poles : 2 * poles].T

    grad_norm_gain, feed_gain_sum, grad_conv_taps, residue_sum, decay_sum = run(
        small_whole, small, small_got
    )
    parts = run(
        lambda a, b: owner_parts(jnp.concatenate([a, b], axis=1)), query_mine, pair_mine
    )
    in_got = owner_moves(parts)

    def out_whole(own, got):
        whole = in_order(jnp.stack([own] + got), "c")
        whole = in_order(jnp.swapaxes(whole, 0, 1), "y")
        ys, cs, rows, columns = whole.shape
        return jnp.swapaxes(whole, 1, 2).reshape(ys * rows, cs * columns).astype(wide)

    grad_out_weight = run(out_whole, out_held, out_got)
    in_held = run(owner_held, in_got)
    in_held = run(stacked, in_held, moved(in_held, "y", -1))
    grad_in_weight = run(
        lambda own, got: owner_whole(owner_ranks(jnp.stack([own] + got)), count),
        in_held,
        moved(in_held, "c", -1),
    )
    return (
        output,
        grad_tokens,
        grad_norm_gain,
        grad_in_weight,
        grad_conv_taps,
        residue_sum,
        decay_sum,
        grad_out_weight,
        feed_gain_sum,
        grad_gate_weight,
        grad_up_weight,
        grad_down,
    )


def solution(mesh):
    pairs, blocks = mesh.shape["dp"], mesh.shape["seq"]
    devices = mesh.devices.reshape(pairs // cores, cores, depth, blocks // depth)
    inner = Mesh(devices, ("y", "c", "z", "x"))
    dp, seq = ("y", "c"), ("z", "x")
    tokens, rows = P(dp, seq, None), P(seq, None)
    return jax.shard_map(
        body,
        mesh=inner,
        in_specs=(
            tokens,
            P(dp),
            P(),
            rows,
            P(),
            P(),
            P(),
            rows,
            P(),
            rows,
            rows,
            rows,
            tokens,
        ),
        out_specs=(tokens, tokens, P(), rows, P(), P(), P(), rows, P(), rows, rows, rows),
        check_vma=False,
    )
```

```python
import functools

import jax
import jax.numpy as jnp
from jax import lax
from jax.experimental import pallas as pl
from jax.experimental.pallas import tpu as pltpu
from jax.sharding import Mesh, PartitionSpec as P

epsilon = 1e-06
low = jnp.bfloat16
wide = jnp.float32
tile = 8
depth = 4
cores = 2


def turned(value, axis, by):
    length = lax.axis_size(axis)
    return lax.ppermute(value, axis, [(i, (i + by) % length) for i in range(length)])


def passed(value, axis, by):
    length = lax.axis_size(axis)
    pairs = [(i, i + by) for i in range(length) if 0 <= i + by < length]
    return lax.ppermute(value, axis, pairs)


def swap_slots(slots):
    ycount, spread = lax.axis_size("y"), lax.axis_size("x")
    result = []
    for dy in range(ycount):
        line = []
        for dx in range(spread):
            sy, sx = (ycount - dy) % ycount, (spread - dx) % spread
            if sy == 0 and sx == 0:
                line.append(slots[0][0])
                continue
            pairs = [
                (i * spread + j, (i + sy) % ycount * spread + (j + sx) % spread)
                for i in range(ycount)
                for j in range(spread)
            ]
            line.append(lax.ppermute(slots[sy][sx], ("y", "x"), pairs))
        result.append(line)
    return result


class Line:
    def __init__(self, token):
        self.token = token

    def run(self, work, *values):
        values, token = lax.optimization_barrier((values, self.token))
        result, self.token = lax.optimization_barrier((work(*values), token))
        return result

    def finish(self, work, *values):
        values, token = lax.optimization_barrier((values, self.token))
        return work(token, *values)


def moved(value, axis, sign):
    return [turned(value, axis, sign * d) for d in range(1, lax.axis_size(axis))]


class Gather:
    def __init__(self, first, second):
        self.held = (first, second)
        self.got = (moved(first, "x", -1), moved(second, "y", -1))

    def turn(self, line):
        self.held = line.run(
            lambda held, got: tuple(jnp.stack([h] + g) for h, g in zip(held, got)), self.held, self.got
        )
        self.got = (moved(self.held[0], "y", -1), moved(self.held[1], "x", -1))

    def end(self, line):
        def work(held, got):
            first = jnp.stack([held[0]] + got[0])
            second = jnp.swapaxes(jnp.stack([held[1]] + got[1]), 0, 1)
            return jnp.stack([first, second]).reshape(-1, first.shape[-1])

        return line.run(work, self.held, self.got)


def split_sum(partial):
    grid = partial.reshape(2, lax.axis_size("y"), lax.axis_size("x"), -1, partial.shape[-1])
    first = [grid[0][:, d].astype(low) for d in range(grid.shape[2])]
    second = [grid[1][d].astype(low) for d in range(grid.shape[1])]
    return first, second


def add_up(parts, got):
    total = parts[0].astype(wide)
    for g in got:
        total = total + g.astype(wide)
    return total


class Scatter:
    def __init__(self, parts):
        self.parts = parts
        self.send("x", "y")

    def send(self, *axes):
        self.got = [
            [turned(p, axis, d + 1) for d, p in enumerate(part[1:])]
            for part, axis in zip(self.parts, axes)
        ]

    def turn(self, line):
        def work(parts, got):
            result = []
            for part, g in zip(parts, got):
                total = add_up(part, g).astype(low)
                result.append([total[d] for d in range(total.shape[0])])
            return result

        self.parts = line.run(work, self.parts, self.got)
        self.send("y", "x")

    def rest(self):
        return self.parts, self.got

    @staticmethod
    def sum(parts, got):
        return jnp.stack([add_up(part, g) for part, g in zip(parts, got)])


def pick_kernel(count, part, stride, start_ref, source, *refs):
    targets, sems = refs[:-1], refs[-1]
    copies = []
    for d, target in enumerate(targets):
        for k in range(count):
            at = pl.multiple_of((k * stride + start_ref[d]) * part, part)
            copies.append(
                pltpu.make_async_copy(
                    source.at[:, pl.ds(at, part)],
                    target.at[:, k * part : (k + 1) * part],
                    sems.at[d * count + k],
                )
            )
    for copy in copies:
        copy.start()
    for copy in copies:
        copy.wait()


def column_pieces(weight, groups):
    spread, ycount = lax.axis_size("x"), lax.axis_size("y")
    rows = weight.shape[0]
    count = groups * depth
    part = weight.shape[1] // (count * spread * ycount)
    starts = [
        (lax.axis_index("x") + d) % spread * ycount + lax.axis_index("y") for d in range(spread)
    ]
    if part % 128 == 0:
        return pl.pallas_call(
            functools.partial(pick_kernel, count, part, spread * ycount),
            out_shape=[jax.ShapeDtypeStruct((rows, count * part), weight.dtype)] * spread,
            grid_spec=pltpu.PrefetchScalarGridSpec(
                num_scalar_prefetch=1,
                in_specs=[pl.BlockSpec(memory_space=pl.ANY)],
                out_specs=[pl.BlockSpec(memory_space=pltpu.VMEM)] * spread,
                scratch_shapes=[pltpu.SemaphoreType.DMA((count * spread,))],
            ),
            cost_estimate=pl.CostEstimate(
                flops=0, transcendentals=0, bytes_accessed=4 * rows * count * part * spread
            ),
        )(jnp.stack(starts).astype(jnp.int32), weight)
    return [
        jnp.concatenate(
            [
                lax.dynamic_slice_in_dim(weight, (k * spread * ycount + start) * part, part, 1)
                for k in range(count)
            ],
            axis=1,
        )
        for start in starts
    ]


def column_moves(pieces):
    spread, ccount = lax.axis_size("x"), lax.axis_size("c")
    share = spread // ccount
    got = [pieces[0]]
    for d in range(1, spread):
        pairs = [
            (i // share * spread + i, i // share * spread + (i + d) % spread) for i in range(spread)
        ]
        got.append(lax.ppermute(pieces[d], ("c", "x"), pairs))
    return got


def column_block(got):
    spread, ccount = lax.axis_size("x"), lax.axis_size("c")
    share = spread // ccount
    place, core = lax.axis_index("x"), lax.axis_index("c")
    got = jnp.stack(got)
    return jnp.concatenate(
        [
            lax.dynamic_index_in_dim(got, (place - core * share - j) % spread, 0, False)
            for j in range(share)
        ]
    )


def row_block(weight):
    ycount, ccount = lax.axis_size("y"), lax.axis_size("c")
    part = weight.shape[0] // (ycount * ccount)
    pair = lax.axis_index("y") * ccount + lax.axis_index("c")
    return lax.dynamic_slice_in_dim(weight, pair * part, part, 0)


def core_halves(value):
    ccount = lax.axis_size("c")
    width = value.shape[1] // ccount
    core = lax.axis_index("c")
    return [
        lax.dynamic_slice_in_dim(value, (core + d) % ccount * width, width, 1)
        for d in range(ccount)
    ]


def out_block(weight):
    part = weight.shape[0] // lax.axis_size("y")
    rows = lax.dynamic_slice_in_dim(weight, lax.axis_index("y") * part, part, 0)
    return core_halves(rows)[0]


def by_z(slots):
    held = in_order(jnp.stack(slots), "z")
    return held.reshape(2, -1, held.shape[-1])


def z_slots(mine):
    mine = mine.reshape(depth, -1, mine.shape[-1]).astype(low)
    place = lax.axis_index("z")
    return [
        lax.dynamic_index_in_dim(mine, (place + d) % depth, 0, False) for d in range(depth)
    ]


def gather_tile(block):
    return lax.all_gather(block, ("z", "c"), axis=0, tiled=True)


def scatter_tile(term):
    return lax.psum_scatter(term, ("z", "c"), scatter_dimension=0, tiled=True)


def owner_parts(mine):
    spread, ccount = lax.axis_size("x"), lax.axis_size("c")
    share = spread // ccount
    place, core = lax.axis_index("x"), lax.axis_index("c")
    parts = mine.reshape(share, -1, mine.shape[-1])
    return [
        lax.dynamic_index_in_dim(
            parts, jnp.clip((place + d) % spread - core * share, 0, share - 1), 0, False
        )
        for d in range(spread)
    ]


def owner_moves(parts):
    spread, ccount = lax.axis_size("x"), lax.axis_size("c")
    share = spread // ccount
    got = [parts[0]]
    for d in range(1, spread):
        pairs = [
            ((i + d) % spread // share * spread + i, i // share * spread + (i + d) % spread)
            for i in range(spread)
        ]
        got.append(lax.ppermute(parts[d], ("c", "x"), pairs))
    return got


def owner_held(got):
    spread, ccount = lax.axis_size("x"), lax.axis_size("c")
    share = spread // ccount
    place, core = lax.axis_index("x"), lax.axis_index("c")
    got = jnp.stack(got)
    return jnp.stack(
        [
            lax.dynamic_index_in_dim(got, (place - core * share - j) % spread, 0, False)
            for j in range(share)
        ]
    )


def owner_ranks(slots, core):
    spread, ccount, ycount = lax.axis_size("x"), lax.axis_size("c"), lax.axis_size("y")
    share = spread // ccount
    yplace = lax.axis_index("y")
    flat = slots.reshape((-1,) + slots.shape[3:])
    ranks = []
    for i in range(spread):
        for k in range(ycount):
            slot = (i // share - core) % ccount * ycount + (k - yplace) % ycount
            ranks.append(lax.dynamic_index_in_dim(flat, slot * share + i % share, 0, False))
    return ranks


def owner_whole(ranks, count):
    part = ranks[0].shape[1] // count
    pieces = []
    for at in range(count):
        pieces += [r[:, at * part : (at + 1) * part].astype(wide) for r in ranks]
    return jnp.concatenate(pieces, axis=1)


def in_order(slots, axis):
    length = lax.axis_size(axis)
    place = lax.axis_index(axis)
    return jnp.stack(
        [lax.dynamic_index_in_dim(slots, (j - place) % length, 0, False) for j in range(length)]
    )


def rank_rows(values, axis):
    spread, ycount = lax.axis_size("x"), lax.axis_size("y")
    part = values.shape[axis] // (depth * spread * ycount)
    place = lax.axis_index("x") * ycount + lax.axis_index("y")
    return jnp.concatenate(
        [
            lax.dynamic_slice_in_dim(values, (k * spread * ycount + place) * part, part, axis)
            for k in range(depth)
        ],
        axis=axis,
    )


def all_channels(slots):
    whole = in_order(slots, "y")
    whole = in_order(jnp.swapaxes(whole, 0, 1), "x")
    spread, ycount, rows = whole.shape[:3]
    whole = whole.reshape(spread, ycount, rows, depth, -1)
    return jnp.transpose(whole, (2, 3, 0, 1, 4)).reshape(rows, -1)


def fill(source, target, place):
    groups, parts, inner, length = source.shape[:4]
    for j in range(parts):
        slot = lax.rem(j + parts - place, parts)
        for g in range(groups):
            for b in range(inner):
                target[g * inner + b, j * length : (j + 1) * length, :] = source[g, slot, b].astype(
                    wide
                )


def empty(source, target, place):
    groups, parts, inner, length = target.shape[:4]
    for j in range(parts):
        slot = lax.rem(j + parts - place, parts)
        for g in range(groups):
            for b in range(inner):
                target[g, slot, b] = source[g * inner + b, j * length : (j + 1) * length, :].astype(
                    low
                )


def halves(ref):
    return [ref[k * tile : (k + 1) * tile, :] for k in range(ref.shape[0] // tile)]


def row_of(ref, seq, at):
    return ref[seq, pl.ds(at, tile, stride=0), :]


def states_kernel(place_ref, signal_ref, decay_ref, state_ref, held):
    fill(signal_ref, held, place_ref[0])
    seqs, length, lanes = held.shape
    keep = [jnp.exp(-d) for d in halves(decay_ref)]
    count = len(keep)

    def step(i, carry):
        state = list(carry)
        for k in range(tile):
            for n in range(seqs):
                new = row_of(held, n, i * tile + k)
                for h in range(count):
                    at = n * count + h
                    state[at] = keep[h] * state[at] + new
        return tuple(state)

    zero = jnp.zeros((tile, lanes), wide)
    state = lax.fori_loop(0, length // tile, step, tuple(zero for _ in range(seqs * count)))
    for n in range(seqs):
        for h in range(count):
            state_ref[n, h * tile : (h + 1) * tile, :] = state[n * count + h]


def forward_kernel(place_ref, signal_ref, decay_ref, residue_ref, start_ref, out_ref, held, terms, made):
    fill(signal_ref, held, place_ref[0])
    seqs, length, lanes = held.shape
    keep = [jnp.exp(-d) for d in halves(decay_ref)]
    weigh = halves(residue_ref)
    count = len(keep)

    def step(i, carry):
        state = list(carry)
        for k in range(tile):
            for n in range(seqs):
                new = row_of(held, n, i * tile + k)
                total = None
                for h in range(count):
                    at = n * count + h
                    state[at] = keep[h] * state[at] + new
                    term = weigh[h] * state[at]
                    total = term if total is None else total + term
                terms[n, k * tile : (k + 1) * tile, :] = total
        for n in range(seqs):
            result = terms[n, pl.ds(0, tile, stride=tile), :]
            for p in range(1, tile):
                result = result + terms[n, pl.ds(p, tile, stride=tile), :]
            made[n, pl.ds(i * tile, tile), :] = result
        return tuple(state)

    start = tuple(
        start_ref[n, h * tile : (h + 1) * tile, :] for n in range(seqs) for h in range(count)
    )
    lax.fori_loop(0, length // tile, step, start)
    empty(made, out_ref, place_ref[0])


def later_kernel(place_ref, signal_ref, decay_ref, state_ref, held):
    fill(signal_ref, held, place_ref[0])
    seqs, length, lanes = held.shape
    keep = [jnp.exp(-d) for d in halves(decay_ref)]
    count = len(keep)

    def step(i, carry):
        state = list(carry)
        base = length - tile - i * tile
        for k in range(tile - 1, -1, -1):
            for n in range(seqs):
                new = row_of(held, n, base + k)
                for h in range(count):
                    at = n * count + h
                    state[at] = keep[h] * state[at] + new
        return tuple(state)

    zero = jnp.zeros((tile, lanes), wide)
    state = lax.fori_loop(0, length // tile, step, tuple(zero for _ in range(seqs * count)))
    for n in range(seqs):
        for h in range(count):
            state_ref[n, h * tile : (h + 1) * tile, :] = state[n * count + h]


def backward_kernel(
    place_ref,
    signal_ref,
    grad_ref,
    decay_ref,
    residue_ref,
    start_ref,
    end_ref,
    out_ref,
    residue_grad_ref,
    decay_grad_ref,
    held,
    grads,
    terms,
    made,
    later,
):
    fill(signal_ref, held, place_ref[0])
    fill(grad_ref, grads, place_ref[0])
    seqs, length, lanes = held.shape
    keep = [jnp.exp(-d) for d in halves(decay_ref)]
    weigh = halves(residue_ref)
    count = len(keep)
    group = later.shape[0]
    zero = jnp.zeros((tile, lanes), wide)
    none = tuple(zero for _ in range(group * count))
    sum_first = [zero] * count
    sum_second = [zero] * count
    for base_seq in range(0, seqs, group):

        def load(ref):
            return tuple(
                ref[base_seq + n, h * tile : (h + 1) * tile, :]
                for n in range(group)
                for h in range(count)
            )

        def back_step(i, carry):
            state, first = [list(v) for v in carry]
            base = length - tile - i * tile
            for k in range(tile - 1, -1, -1):
                for n in range(group):
                    back = row_of(grads, base_seq + n, base + k)
                    new = row_of(held, base_seq + n, base + k)
                    total = None
                    for h in range(count):
                        at = n * count + h
                        state[at] = keep[h] * state[at] + back
                        first[at] = first[at] + new * state[at]
                        later[n, pl.ds(((base + k) * count + h) * tile, tile), :] = state[at]
                        term = weigh[h] * state[at]
                        total = term if total is None else total + term
                    terms[n, k * tile : (k + 1) * tile, :] = total
            for n in range(group):
                result = terms[n, pl.ds(0, tile, stride=tile), :]
                for p in range(1, tile):
                    result = result + terms[n, pl.ds(p, tile, stride=tile), :]
                made[base_seq + n, pl.ds(base, tile), :] = result
            return tuple(state), tuple(first)

        _, first = lax.fori_loop(0, length // tile, back_step, (load(end_ref), none))

        def ahead(i, carry):
            state, second = [list(v) for v in carry]
            for k in range(tile):
                for n in range(group):
                    new = row_of(held, base_seq + n, i * tile + k)
                    for h in range(count):
                        at = n * count + h
                        state[at] = keep[h] * state[at] + new
                        other = later[n, pl.ds(((i * tile + k) * count + h) * tile, tile), :]
                        second[at] = second[at] + state[at] * other
            return tuple(state), tuple(second)

        _, second = lax.fori_loop(0, length // tile, ahead, (load(start_ref), none))
        for n in range(group):
            for h in range(count):
                at = n * count + h
                sum_first[h] = sum_first[h] + first[at]
                sum_second[h] = sum_second[h] + (second[at] - first[at])
    for h in range(count):
        residue_grad_ref[h * tile : (h + 1) * tile, :] = sum_first[h]
        decay_grad_ref[h * tile : (h + 1) * tile, :] = -weigh[h] * sum_second[h]
    empty(made, out_ref, place_ref[0])


def conv_call(kernel, place, arrays, results, scratch, flops):
    channels = arrays[0].shape[-1]
    lanes = min(channels, 128)

    def spec(shape):
        lead = len(shape) - 1
        return pl.BlockSpec(shape[:-1] + (lanes,), lambda i, *_: (0,) * lead + (i,))

    return pl.pallas_call(
        kernel,
        out_shape=results,
        grid_spec=pltpu.PrefetchScalarGridSpec(
            num_scalar_prefetch=1,
            grid=(channels // lanes,),
            in_specs=[spec(a.shape) for a in arrays],
            out_specs=[spec(r.shape) for r in results],
            scratch_shapes=[pltpu.VMEM(s + (lanes,), wide) for s in scratch],
        ),
        compiler_params=pltpu.CompilerParams(
            dimension_semantics=("arbitrary",), vmem_limit_bytes=56 << 20
        ),
        cost_estimate=pl.CostEstimate(
            flops=flops, transcendentals=0, bytes_accessed=sum(a.size * 4 for a in arrays)
        ),
    )(place, *arrays)


def sizes(signal, poles):
    groups, parts, inner, length, channels = signal.shape
    return groups * inner, parts * length, channels, signal.size * poles


def states_of(place, signal, decay):
    seqs, length, channels, work = sizes(signal, decay.shape[0])
    shape = jax.ShapeDtypeStruct((seqs, decay.shape[0], channels), wide)
    return conv_call(states_kernel, place, [signal, decay], [shape], [(seqs, length)], 2 * work)[0]


def forward_of(place, signal, decay, residue, start):
    seqs, length, channels, work = sizes(signal, decay.shape[0])
    return conv_call(
        forward_kernel,
        place,
        [signal, decay, residue, start],
        [jax.ShapeDtypeStruct(signal.shape, low)],
        [(seqs, length), (seqs, tile * tile), (seqs, length)],
        4 * work,
    )[0]


def later_of(place, signal, decay):
    seqs, length, channels, work = sizes(signal, decay.shape[0])
    shape = jax.ShapeDtypeStruct((seqs, decay.shape[0], channels), wide)
    return conv_call(later_kernel, place, [signal, decay], [shape], [(seqs, length)], 2 * work)[0]


def backward_of(place, signal, grad, decay, residue, start, end):
    poles = decay.shape[0]
    seqs, length, channels, work = sizes(signal, poles)
    shape = jax.ShapeDtypeStruct(decay.shape, wide)
    group = min(seqs, 4)
    return conv_call(
        backward_kernel,
        place,
        [signal, grad, decay, residue, start, end],
        [jax.ShapeDtypeStruct(signal.shape, low), shape, shape],
        [
            (seqs, length),
            (seqs, length),
            (group, tile * tile),
            (seqs, length),
            (group, length * poles),
        ],
        12 * work,
    )


def rms_scale(values):
    return lax.rsqrt(jnp.mean(values * values, axis=-1, keepdims=True) + epsilon)


def norm_back(values, scale, gain, grad_normed):
    grad_gain = jnp.sum(grad_normed * values * scale, axis=(0, 1))
    scaled = grad_normed * gain
    grad_values = scale * scaled - values * scale * scale * scale * jnp.mean(
        scaled * values, axis=-1, keepdims=True
    )
    return (grad_values, grad_gain)


def dot(a, b, kind=wide):
    return jnp.dot(a, b, preferred_element_type=wide).astype(kind)


def dot_t(a, b, kind=wide):
    return lax.dot_general(a, b, (((1,), (1,)), ((), ())), preferred_element_type=wide).astype(kind)


def dot_w(a, b):
    return lax.dot_general(a, b, (((0,), (0,)), ((), ())), preferred_element_type=wide).astype(low)


def body(
    tokens,
    lengths,
    norm_gain,
    in_weight,
    conv_taps,
    filter_residue,
    filter_decay,
    out_weight,
    feed_gain,
    gate_weight,
    up_weight,
    down_weight,
    cotangent,
):
    spread, ycount = lax.axis_size("x"), lax.axis_size("y")
    batch, local, width = tokens.shape
    place = lax.axis_index("z") * spread + lax.axis_index("x")
    position = place * local + jnp.arange(local)
    mask = (position[None, :] < lengths[:, None]).astype(wide)[..., None]
    block = spread * local

    count = 3 * depth
    line = Line(lax.axis_index("c"))
    run = line.run

    def stacked(value, got):
        return jnp.stack([value] + got)

    block_out = run(out_block, out_weight)
    out_got = moved(block_out, "z", -1)
    in_got = column_moves(run(lambda w: column_pieces(w, 3), in_weight))

    def norm_one(values, gain):
        values = values.astype(wide)
        scale = rms_scale(values)
        normed = (values * scale * gain).astype(low)
        return normed[: batch // 2], normed[batch // 2 :], scale

    first, second, scale_one = run(norm_one, tokens, norm_gain)
    normed_move = Gather(first, second)
    w_in = gather_tile(run(column_block, in_got))
    held = run(lambda own, got: by_z([own] + got), block_out, out_got)
    normed_move.turn(line)
    w_down = gather_tile(run(row_block, down_weight))
    out_move = Gather(held[:1], held[1:])
    gate_got = column_moves(run(lambda w: column_pieces(w, 1), gate_weight))
    normed_all = normed_move.end(line)
    out_move.turn(line)
    w_gate = gather_tile(run(column_block, gate_got))
    up_got = column_moves(run(lambda w: column_pieces(w, 1), up_weight))

    channels = w_in.shape[1] // 3
    half = channels // 2
    grid = (2 * ycount, spread, batch // 2, local)

    def rank_values(all_taps, all_decay, all_residue):
        return (
            jnp.concatenate(
                [rank_rows(all_taps[:, g * width : (g + 1) * width], 1) for g in range(3)], axis=1
            ),
            rank_rows(all_decay, 0).T,
            rank_rows(all_residue, 0).T,
        )

    taps, decay, residue = run(rank_values, conv_taps, filter_decay, filter_residue)
    opening = (lax.axis_index("x") + jnp.arange(spread)) % spread == 0
    opening = opening[None, :, None, None, None]
    closing = (lax.axis_index("x") + jnp.arange(spread)) % spread == spread - 1
    closing = closing[None, :, None, None, None]

    def project(v, w):
        value = dot(v, w, low).reshape(grid + (3 * channels,))
        return value, jnp.roll(value[:, :, :, local - 2 :], 1, axis=1)

    mixed, tail = run(project, normed_all, w_in)
    behind = passed(tail, "z", 1)

    def feed_grad(values):
        values = (values.astype(wide) * mask).astype(low)
        return values[: batch // 2], values[batch // 2 :]

    feed_move = Gather(*run(feed_grad, cotangent))
    w_up = gather_tile(run(column_block, up_got))
    out_own = out_move.end(line)
    w_out = [out_own] + moved(out_own, "c", -1)

    def extend(value, ends, before, g):
        at = slice(g * channels, (g + 1) * channels)
        return jnp.concatenate(
            [jnp.where(opening, before[..., at], ends[..., at]), value[..., at]], axis=3
        ).astype(wide)

    def short_of(value, ends, before, weights, g):
        longer = extend(value, ends, before, g)
        own = weights[:, g * channels : (g + 1) * channels]
        return own[0] * longer[:, :, :, 2:] + own[1] * longer[:, :, :, 1:-1] + own[2] * longer[:, :, :, :-2]

    spot = lax.axis_index("x").astype(jnp.int32).reshape(1)

    def multiply(value, ends, before, weights, rates):
        keys, values = (short_of(value, ends, before, weights, g) for g in (1, 2))
        product = (keys * values).astype(low)
        return product, states_of(spot, product, rates)

    product, state_end = run(multiply, mixed, tail, behind, taps, decay)
    states = [passed(state_end, "z", k) for k in range(1, depth)]
    feed_move.turn(line)

    def combine(parts, rates):
        total = parts[0]
        for k in range(1, depth - 1):
            total = total + jnp.exp(-rates * (k * block)) * parts[k]
        return total

    def convolve(parts, value, ends, before, weights, signal, rates, amounts):
        start = combine(parts, rates)
        result = forward_of(spot, signal, rates, amounts, start)
        query = short_of(value, ends, before, weights, 0)
        gated = (query * result.astype(wide)).astype(low)
        slots = gated.reshape(2, ycount, spread, -1, channels)
        return (
            start,
            result,
            [[slots[:, k, i].reshape(-1, channels) for i in range(spread)] for k in range(ycount)],
        )

    start, convolved, gated = run(
        convolve, states, mixed, tail, behind, taps, product, decay, residue
    )
    gated_got = swap_slots(gated)
    grad_feed_all = feed_move.end(line)

    def mix(got, weights, values, gain):
        own = jnp.concatenate(
            [g[:, h * half : (h + 1) * half] for h in range(2) for row in got for g in row], axis=1
        )
        mixer = in_order(jnp.stack([dot(own, w) for w in weights]), "c")
        mixer = jnp.concatenate([m for m in mixer], axis=1).reshape(batch, local, width)
        middle = values.astype(wide) + mixer
        scale = rms_scale(middle)
        normed = (middle * scale * gain).astype(low)
        return own, middle, scale, normed[: batch // 2], normed[batch // 2 :]

    gated_own, middle, scale_two, first, second = run(mix, gated_got, w_out, tokens, feed_gain)

    two_move = Gather(first, second)
    grad_active = run(dot_t, grad_feed_all, w_down)
    two_move.turn(line)
    normed_two_all = two_move.end(line)

    def open_gate(v, w, back):
        value = dot(v, w)
        return value, (back * value * jax.nn.sigmoid(value)).astype(low)

    gate, grad_upper = run(open_gate, normed_two_all, w_gate, grad_active)
    up_term = run(dot_w, normed_two_all, grad_upper)
    up_mine = scatter_tile(up_term)

    def activate(v, w, value, back):
        upper = dot(v, w)
        sigma = jax.nn.sigmoid(value)
        return (
            (value * sigma * upper).astype(low),
            (back * upper * sigma * (1.0 + value * (1.0 - sigma))).astype(low),
        )

    active, grad_gate = run(activate, normed_two_all, w_up, gate, grad_active)
    two_back = Scatter(
        run(
            lambda a, b, wa, wb: split_sum((dot_t(a, wa) + dot_t(b, wb)).astype(low)),
            grad_gate,
            grad_upper,
            w_gate,
            w_up,
        )
    )
    gate_mine = scatter_tile(run(dot_w, normed_two_all, grad_gate))
    down_mine = scatter_tile(run(dot_w, active, grad_feed_all))
    two_back.turn(line)

    def middle_back(rest, values, scale, gain, back, weights):
        grad_normed = Scatter.sum(*rest).reshape(batch, local, width)
        result, grad_gain = norm_back(values, scale, gain, grad_normed)
        result = result + back.astype(wide) * mask
        parts = core_halves(result.astype(low).reshape(-1, width))
        own = sum(dot_t(m, w) for m, w in zip(parts, weights)).astype(low)
        ranks = ycount * spread

        def slot(at):
            pieces = [
                own[:, (h * ranks + at) * half : (h * ranks + at + 1) * half] for h in range(2)
            ]
            return jnp.concatenate(pieces, axis=1)

        slots = [[slot(k * spread + i) for i in range(spread)] for k in range(ycount)]
        return result, grad_gain, parts, slots

    grad_middle, grad_feed_gain, mix_parts, grad_slots = run(
        middle_back, two_back.rest(), middle, scale_two, feed_gain, cotangent, w_out
    )
    grad_got = swap_slots(grad_slots)
    out_terms = run(lambda g, parts: [dot_w(g, m) for m in parts], gated_own, mix_parts)
    out_terms_got = [turned(t, "c", d + 1) for d, t in enumerate(out_terms[1:])]

    def conv_grads(got, result, value, ends, before, weights, rates):
        grad = jnp.stack([jnp.stack(row) for row in got])
        grad = grad.reshape(ycount, spread, 2, batch // 2, local, channels)
        grad = jnp.moveaxis(grad, 2, 0).reshape(grid + (channels,)).astype(wide)
        grad_query = (grad * result.astype(wide)).astype(wide)
        grad_conv = (grad * short_of(value, ends, before, weights, 0)).astype(low)
        return (
            grad_query,
            jnp.roll(grad_query[:, :, :, :2].astype(low), -1, axis=1),
            grad_conv,
            later_of(spot, grad_conv, rates),
        )

    grad_query, query_head, grad_conv, later_end = run(
        conv_grads, grad_got, convolved, mixed, tail, behind, taps, decay
    )
    laters = [passed(later_end, "z", -k) for k in range(1, depth)]
    query_ahead = passed(query_head, "z", -1)
    feed_back = Scatter(run(lambda a, w: split_sum(dot(a, w, low)), active, w_down))

    def short_back(grad_short, head, ahead, weights):
        whole = jnp.concatenate([grad_short, jnp.where(closing, ahead, head).astype(wide)], axis=3)
        result = (
            weights[0] * whole[:, :, :, :-2]
            + weights[1] * whole[:, :, :, 1:-1]
            + weights[2] * whole[:, :, :, 2:]
        )
        return result.astype(low).reshape(-1, grad_short.shape[-1])

    def query_back(grad, head, ahead, weights, v):
        result = short_back(grad, head, ahead, weights[:, :channels])
        return result, dot_w(v, result)

    up_parts_got = owner_moves(run(owner_parts, up_mine))
    grad_mixed_query, query_term = run(
        query_back, grad_query, query_head, query_ahead, taps, normed_all
    )
    query_mine = scatter_tile(query_term)

    up_held = run(owner_held, up_parts_got)
    up_got = moved(up_held, "y", -1)

    def conv_back(signal, grad, rates, amounts, begin, ends_later, value, ends, before, weights):
        later = combine(ends_later, rates)
        grad_product, grad_residue, grad_decay = backward_of(
            spot, signal, grad, rates, amounts, begin, later
        )
        grad_product = grad_product.astype(wide)
        keys, values = (short_of(value, ends, before, weights, g) for g in (1, 2))
        pair = jnp.concatenate([grad_product * values, grad_product * keys], axis=-1)
        return pair, jnp.roll(pair[:, :, :, :2].astype(low), -1, axis=1), grad_residue, grad_decay

    grad_pair, pair_head, grad_residue, grad_decay = run(
        conv_back,
        product,
        grad_conv,
        decay,
        residue,
        start,
        laters,
        mixed,
        tail,
        behind,
        taps,
    )
    pair_ahead = passed(pair_head, "z", -1)
    feed_back.turn(line)
    up_held = run(stacked, up_held, up_got)
    up_got = moved(up_held, "c", -1)

    def pair_back(grad, head, ahead, weights, v):
        result = short_back(grad, head, ahead, weights[:, channels:])
        return result, dot_w(v, result)

    grad_mixed_pair, pair_term = run(
        pair_back, grad_pair, pair_head, pair_ahead, taps, normed_all
    )
    pair_mine = scatter_tile(pair_term)
    one_back = Scatter(
        run(
            lambda a, b, w: split_sum(dot_t(jnp.concatenate([a, b], axis=1), w, low)),
            grad_mixed_query,
            grad_mixed_pair,
            w_in,
        )
    )

    output = run(
        lambda rest, values: (
            mask * (values + Scatter.sum(*rest).reshape(batch, local, width))
        ).astype(low),
        feed_back.rest(),
        middle,
    )
    out_back_parts = run(
        lambda own, got: split_sum(add_up([own], got)), out_terms[0], out_terms_got
    )

    def column_whole(own, got):
        return owner_whole(owner_ranks(jnp.stack([own] + got), lax.axis_index("c")), depth)

    grad_up_weight = run(column_whole, up_held, up_got)
    one_back.turn(line)
    gate_got = owner_moves(run(owner_parts, gate_mine))
    out_back = Scatter(out_back_parts)

    def tap_sums(query, pair, value, ends, before):
        sums = []
        for g, part in enumerate((query, pair[..., :channels], pair[..., channels:])):
            own = extend(value, ends, before, g)
            sums += [
                jnp.sum(part * own[:, :, :, 2 - j : local + 2 - j], axis=(0, 1, 2, 3))
                for j in range(3)
            ]
        return jnp.stack(sums)

    grad_taps = run(tap_sums, grad_query, grad_pair, mixed, tail, behind)

    def tokens_back(rest, values, scale, gain, back, small):
        values = values.astype(wide)
        grad_normed = Scatter.sum(*rest).reshape(batch, local, width)
        result, grad_gain = norm_back(values, scale, gain, grad_normed)
        gains = jnp.stack([grad_gain, small[0]]).reshape(-1, channels)
        return (result + back).astype(low), jnp.concatenate(list(small[1:]) + [gains], axis=0)

    grad_tokens, small = run(
        tokens_back,
        one_back.rest(),
        tokens,
        scale_one,
        norm_gain,
        grad_middle,
        (grad_feed_gain, grad_residue, grad_decay, grad_taps),
    )
    small_got = moved(small, "c", 1)
    gate_held = run(owner_held, gate_got)
    gate_got = moved(gate_held, "y", -1)
    out_back.turn(line)
    small = run(lambda v, got: v + sum(got), small, small_got)
    small_got = moved(small, "z", 1)
    gate_held = run(stacked, gate_held, gate_got)
    gate_got = moved(gate_held, "c", -1)
    out_slots = run(
        lambda rest: z_slots(Scatter.sum(*rest).reshape(channels, -1)), out_back.rest()
    )
    out_got = [turned(p, "z", d + 1) for d, p in enumerate(out_slots[1:])]
    small = run(lambda v, got: v + sum(got), small, small_got)
    small_got = moved(small, "x", -1)
    down_held = run(lambda v: v.reshape(1, -1, width), down_mine)
    down_got = moved(down_held, "y", -1)
    parts = run(
        lambda a, b: owner_parts(jnp.concatenate([a, b], axis=1)), query_mine, pair_mine
    )
    in_got = owner_moves(parts)
    grad_gate_weight = run(column_whole, gate_held, gate_got)
    out_held = run(lambda own, got: add_up([own], got).astype(low), out_slots[0], out_got)
    out_got = moved(out_held, "y", -1)
    in_held = run(owner_held, in_got)
    in_got = moved(in_held, "y", -1)
    small = run(stacked, small, small_got)
    small_got = moved(small, "y", -1)
    down_held = run(lambda own, got: jnp.concatenate([own] + got), down_held, down_got)
    down_got = moved(down_held, "c", -1)
    out_held = run(stacked, out_held, out_got)
    out_got = moved(out_held, "c", -1)
    in_held = run(stacked, in_held, in_got)
    in_got = moved(in_held, "c", -1)
    poles = decay.shape[0]

    def small_whole(own, got):
        slots = jnp.stack([own] + got)
        rows = 2 * poles + 9
        gains = jnp.sum(slots[:, :, rows:], axis=(0, 1)).reshape(2, width)
        whole = all_channels(slots[:, :, :rows])
        grad_conv_taps = jnp.concatenate(
            [whole[2 * poles + 3 * g : 2 * poles + 3 * g + 3] for g in range(3)], axis=1
        )
        return gains[0], gains[1], grad_conv_taps, whole[:poles].T, whole[poles : 2 * poles].T

    grad_norm_gain, feed_gain_sum, grad_conv_taps, residue_sum, decay_sum = run(
        small_whole, small, small_got
    )

    def down_whole(own, got):
        whole = in_order(jnp.swapaxes(in_order(jnp.stack([own] + got), "c"), 0, 1), "y")
        return whole.reshape(-1, width).astype(wide)

    grad_down = run(down_whole, down_held, down_got)

    def out_whole(own, got):
        whole = in_order(jnp.stack([own] + got), "c")
        whole = in_order(jnp.swapaxes(whole, 0, 1), "y")
        ys, cs, rows, columns = whole.shape
        return jnp.swapaxes(whole, 1, 2).reshape(ys * rows, cs * columns).astype(wide)

    grad_out_weight = run(out_whole, out_held, out_got)
    grad_in_weight = line.finish(
        lambda core, own, got: owner_whole(owner_ranks(jnp.stack([own] + got), core), count),
        in_held,
        in_got,
    )
    return (
        output,
        grad_tokens,
        grad_norm_gain,
        grad_in_weight,
        grad_conv_taps,
        residue_sum,
        decay_sum,
        grad_out_weight,
        feed_gain_sum,
        grad_gate_weight,
        grad_up_weight,
        grad_down,
    )


def solution(mesh):
    pairs, blocks = mesh.shape["dp"], mesh.shape["seq"]
    devices = mesh.devices.reshape(pairs // cores, cores, depth, blocks // depth)
    inner = Mesh(devices, ("y", "c", "z", "x"))
    dp, seq = ("y", "c"), ("z", "x")
    tokens, rows = P(dp, seq, None), P(seq, None)
    return jax.shard_map(
        body,
        mesh=inner,
        in_specs=(
            tokens,
            P(dp),
            P(),
            rows,
            P(),
            P(),
            P(),
            rows,
            P(),
            rows,
            rows,
            rows,
            tokens,
        ),
        out_specs=(tokens, tokens, P(), rows, P(), P(), P(), rows, P(), rows, rows, rows),
        check_vma=False,
    )
```

```python
import functools

import jax
import jax.numpy as jnp
from jax import lax
from jax.experimental import pallas as pl
from jax.experimental.pallas import tpu as pltpu
from jax.sharding import Mesh, PartitionSpec as P

epsilon = 1e-06
low = jnp.bfloat16
wide = jnp.float32
tile = 8
depth = 4
cores = 2


def turned(value, axis, by):
    length = lax.axis_size(axis)
    return lax.ppermute(value, axis, [(i, (i + by) % length) for i in range(length)])


def passed(value, axis, by):
    length = lax.axis_size(axis)
    pairs = [(i, i + by) for i in range(length) if 0 <= i + by < length]
    return lax.ppermute(value, axis, pairs)


def swap_slots(slots):
    ycount, spread = lax.axis_size("y"), lax.axis_size("x")
    result = []
    for dy in range(ycount):
        line = []
        for dx in range(spread):
            sy, sx = (ycount - dy) % ycount, (spread - dx) % spread
            if sy == 0 and sx == 0:
                line.append(slots[0][0])
                continue
            pairs = [
                (i * spread + j, (i + sy) % ycount * spread + (j + sx) % spread)
                for i in range(ycount)
                for j in range(spread)
            ]
            line.append(lax.ppermute(slots[sy][sx], ("y", "x"), pairs))
        result.append(line)
    return result


class Line:
    def __init__(self, token):
        self.token = token

    def run(self, work, *values):
        values, token = lax.optimization_barrier((values, self.token))
        result, self.token = lax.optimization_barrier((work(*values), token))
        return result

    def finish(self, work, *values):
        values, token = lax.optimization_barrier((values, self.token))
        return work(token, *values)


def moved(value, axis, sign):
    return [turned(value, axis, sign * d) for d in range(1, lax.axis_size(axis))]


class Gather:
    def __init__(self, first, second):
        self.held = (first, second)
        self.got = (moved(first, "x", -1), moved(second, "y", -1))

    def turn(self, line):
        self.held = line.run(
            lambda held, got: tuple(jnp.stack([h] + g) for h, g in zip(held, got)), self.held, self.got
        )
        self.got = (moved(self.held[0], "y", -1), moved(self.held[1], "x", -1))

    def end(self, line):
        def work(held, got):
            first = jnp.stack([held[0]] + got[0])
            second = jnp.swapaxes(jnp.stack([held[1]] + got[1]), 0, 1)
            return jnp.stack([first, second]).reshape(-1, first.shape[-1])

        return line.run(work, self.held, self.got)


def split_sum(partial):
    grid = partial.reshape(2, lax.axis_size("y"), lax.axis_size("x"), -1, partial.shape[-1])
    first = [grid[0][:, d].astype(low) for d in range(grid.shape[2])]
    second = [grid[1][d].astype(low) for d in range(grid.shape[1])]
    return first, second


def add_up(parts, got):
    total = parts[0].astype(wide)
    for g in got:
        total = total + g.astype(wide)
    return total


class Scatter:
    def __init__(self, parts):
        self.parts = parts
        self.send("x", "y")

    def send(self, *axes):
        self.got = [
            [turned(p, axis, d + 1) for d, p in enumerate(part[1:])]
            for part, axis in zip(self.parts, axes)
        ]

    def turn(self, line):
        def work(parts, got):
            result = []
            for part, g in zip(parts, got):
                total = add_up(part, g).astype(low)
                result.append([total[d] for d in range(total.shape[0])])
            return result

        self.parts = line.run(work, self.parts, self.got)
        self.send("y", "x")

    def rest(self):
        return self.parts, self.got

    @staticmethod
    def sum(parts, got):
        return jnp.stack([add_up(part, g) for part, g in zip(parts, got)])


def pick_kernel(count, part, stride, start_ref, source, *refs):
    targets, sems = refs[:-1], refs[-1]
    copies = []
    for d, target in enumerate(targets):
        for k in range(count):
            at = pl.multiple_of((k * stride + start_ref[d]) * part, part)
            copies.append(
                pltpu.make_async_copy(
                    source.at[:, pl.ds(at, part)],
                    target.at[:, k * part : (k + 1) * part],
                    sems.at[d * count + k],
                )
            )
    for copy in copies:
        copy.start()
    for copy in copies:
        copy.wait()


def column_pieces(weight, groups):
    spread, ycount = lax.axis_size("x"), lax.axis_size("y")
    rows = weight.shape[0]
    count = groups * depth
    part = weight.shape[1] // (count * spread * ycount)
    starts = [
        (lax.axis_index("x") + d) % spread * ycount + lax.axis_index("y") for d in range(spread)
    ]
    if part % 128 == 0:
        return pl.pallas_call(
            functools.partial(pick_kernel, count, part, spread * ycount),
            out_shape=[jax.ShapeDtypeStruct((rows, count * part), weight.dtype)] * spread,
            grid_spec=pltpu.PrefetchScalarGridSpec(
                num_scalar_prefetch=1,
                in_specs=[pl.BlockSpec(memory_space=pl.ANY)],
                out_specs=[pl.BlockSpec(memory_space=pltpu.VMEM)] * spread,
                scratch_shapes=[pltpu.SemaphoreType.DMA((count * spread,))],
            ),
            cost_estimate=pl.CostEstimate(
                flops=0, transcendentals=0, bytes_accessed=4 * rows * count * part * spread
            ),
        )(jnp.stack(starts).astype(jnp.int32), weight)
    return [
        jnp.concatenate(
            [
                lax.dynamic_slice_in_dim(weight, (k * spread * ycount + start) * part, part, 1)
                for k in range(count)
            ],
            axis=1,
        )
        for start in starts
    ]


def column_moves(pieces):
    spread, ccount = lax.axis_size("x"), lax.axis_size("c")
    share = spread // ccount
    got = [pieces[0]]
    for d in range(1, spread):
        pairs = [
            (i // share * spread + i, i // share * spread + (i + d) % spread) for i in range(spread)
        ]
        got.append(lax.ppermute(pieces[d], ("c", "x"), pairs))
    return got


def column_block(got):
    spread, ccount = lax.axis_size("x"), lax.axis_size("c")
    share = spread // ccount
    place, core = lax.axis_index("x"), lax.axis_index("c")
    got = jnp.stack(got)
    return jnp.concatenate(
        [
            lax.dynamic_index_in_dim(got, (place - core * share - j) % spread, 0, False)
            for j in range(share)
        ]
    )


def row_block(weight):
    ycount, ccount = lax.axis_size("y"), lax.axis_size("c")
    part = weight.shape[0] // (ycount * ccount)
    pair = lax.axis_index("y") * ccount + lax.axis_index("c")
    return lax.dynamic_slice_in_dim(weight, pair * part, part, 0)


def core_halves(value):
    ccount = lax.axis_size("c")
    width = value.shape[1] // ccount
    core = lax.axis_index("c")
    return [
        lax.dynamic_slice_in_dim(value, (core + d) % ccount * width, width, 1)
        for d in range(ccount)
    ]


def out_block(weight):
    part = weight.shape[0] // lax.axis_size("y")
    rows = lax.dynamic_slice_in_dim(weight, lax.axis_index("y") * part, part, 0)
    return core_halves(rows)[0]


def by_z(slots):
    held = in_order(jnp.stack(slots), "z")
    return held.reshape(2, -1, held.shape[-1])


def gather_tile(block):
    return lax.all_gather(block, ("z", "c"), axis=0, tiled=True)


def scatter_tile(term):
    return lax.psum_scatter(term, ("z", "c"), scatter_dimension=0, tiled=True)


def owner_parts(mine):
    spread, ccount = lax.axis_size("x"), lax.axis_size("c")
    share = spread // ccount
    place, core = lax.axis_index("x"), lax.axis_index("c")
    parts = mine.reshape(share, -1, mine.shape[-1])
    return [
        lax.dynamic_index_in_dim(
            parts, jnp.clip((place + d) % spread - core * share, 0, share - 1), 0, False
        )
        for d in range(spread)
    ]


def owner_moves(parts):
    spread, ccount = lax.axis_size("x"), lax.axis_size("c")
    share = spread // ccount
    got = [parts[0]]
    for d in range(1, spread):
        pairs = [
            ((i + d) % spread // share * spread + i, i // share * spread + (i + d) % spread)
            for i in range(spread)
        ]
        got.append(lax.ppermute(parts[d], ("c", "x"), pairs))
    return got


def owner_held(got):
    spread, ccount = lax.axis_size("x"), lax.axis_size("c")
    share = spread // ccount
    place, core = lax.axis_index("x"), lax.axis_index("c")
    got = jnp.stack(got)
    return jnp.stack(
        [
            lax.dynamic_index_in_dim(got, (place - core * share - j) % spread, 0, False)
            for j in range(share)
        ]
    )


def assemble_kernel(count, width, order_ref, *refs):
    sources, target = refs[:-1], refs[-1]
    part = width // count
    ranks = order_ref.shape[0] // 2
    for r in range(ranks):
        core, slot = order_ref[2 * r], order_ref[2 * r + 1]
        value = sources[0][slot]
        for c in range(1, len(sources)):
            value = jnp.where(core == c, sources[c][slot], value)
        value = value.astype(wide)
        for at in range(count):
            start = (at * ranks + r) * part
            target[:, start : start + part] = value[:, at * part : (at + 1) * part]


def owner_whole(core, sources, count):
    spread, ccount, ycount = lax.axis_size("x"), lax.axis_size("c"), lax.axis_size("y")
    share = spread // ccount
    yplace = lax.axis_index("y")
    order = []
    for i in range(spread):
        for k in range(ycount):
            order += [(i // share - core) % ccount, (k - yplace) % ycount * share + i % share]
    sources = [v.reshape((-1,) + v.shape[2:]) for v in sources]
    held, rows, width = sources[0].shape
    block = min(rows, 64)
    return pl.pallas_call(
        functools.partial(assemble_kernel, count, width),
        out_shape=jax.ShapeDtypeStruct((rows, width * spread * ycount), wide),
        grid_spec=pltpu.PrefetchScalarGridSpec(
            num_scalar_prefetch=1,
            grid=(rows // block,),
            in_specs=[pl.BlockSpec((held, block, width), lambda i, order: (0, i, 0))]
            * len(sources),
            out_specs=pl.BlockSpec((block, width * spread * ycount), lambda i, order: (i, 0)),
        ),
        compiler_params=pltpu.CompilerParams(vmem_limit_bytes=56 << 20),
        cost_estimate=pl.CostEstimate(
            flops=0, transcendentals=0, bytes_accessed=6 * rows * width * spread * ycount
        ),
    )(jnp.stack(order).astype(jnp.int32), *sources)


def in_order(slots, axis):
    length = lax.axis_size(axis)
    place = lax.axis_index(axis)
    return jnp.stack(
        [lax.dynamic_index_in_dim(slots, (j - place) % length, 0, False) for j in range(length)]
    )


def rank_rows(values, axis):
    spread, ycount = lax.axis_size("x"), lax.axis_size("y")
    part = values.shape[axis] // (depth * spread * ycount)
    place = lax.axis_index("x") * ycount + lax.axis_index("y")
    return jnp.concatenate(
        [
            lax.dynamic_slice_in_dim(values, (k * spread * ycount + place) * part, part, axis)
            for k in range(depth)
        ],
        axis=axis,
    )


def all_channels(slots):
    whole = in_order(slots, "y")
    whole = in_order(jnp.swapaxes(whole, 0, 1), "x")
    spread, ycount, rows = whole.shape[:3]
    whole = whole.reshape(spread, ycount, rows, depth, -1)
    return jnp.transpose(whole, (2, 3, 0, 1, 4)).reshape(rows, -1)


def fill(source, target, place):
    groups, parts, inner, length = source.shape[:4]
    for j in range(parts):
        slot = lax.rem(j + parts - place, parts)
        for g in range(groups):
            for b in range(inner):
                target[g * inner + b, j * length : (j + 1) * length, :] = source[g, slot, b].astype(
                    wide
                )


def empty(source, target, place):
    groups, parts, inner, length = target.shape[:4]
    for j in range(parts):
        slot = lax.rem(j + parts - place, parts)
        for g in range(groups):
            for b in range(inner):
                target[g, slot, b] = source[g * inner + b, j * length : (j + 1) * length, :].astype(
                    low
                )


def halves(ref):
    return [ref[k * tile : (k + 1) * tile, :] for k in range(ref.shape[0] // tile)]


def row_of(ref, seq, at):
    return ref[seq, pl.ds(at, tile, stride=0), :]


def states_kernel(place_ref, signal_ref, decay_ref, state_ref, held):
    fill(signal_ref, held, place_ref[0])
    seqs, length, lanes = held.shape
    keep = [jnp.exp(-d) for d in halves(decay_ref)]
    count = len(keep)

    def step(i, carry):
        state = list(carry)
        for k in range(tile):
            for n in range(seqs):
                new = row_of(held, n, i * tile + k)
                for h in range(count):
                    at = n * count + h
                    state[at] = keep[h] * state[at] + new
        return tuple(state)

    zero = jnp.zeros((tile, lanes), wide)
    state = lax.fori_loop(0, length // tile, step, tuple(zero for _ in range(seqs * count)))
    for n in range(seqs):
        for h in range(count):
            state_ref[n, h * tile : (h + 1) * tile, :] = state[n * count + h]


def forward_kernel(place_ref, signal_ref, decay_ref, residue_ref, start_ref, out_ref, held, terms, made):
    fill(signal_ref, held, place_ref[0])
    seqs, length, lanes = held.shape
    keep = [jnp.exp(-d) for d in halves(decay_ref)]
    weigh = halves(residue_ref)
    count = len(keep)

    def step(i, carry):
        state = list(carry)
        for k in range(tile):
            for n in range(seqs):
                new = row_of(held, n, i * tile + k)
                total = None
                for h in range(count):
                    at = n * count + h
                    state[at] = keep[h] * state[at] + new
                    term = weigh[h] * state[at]
                    total = term if total is None else total + term
                terms[n, k * tile : (k + 1) * tile, :] = total
        for n in range(seqs):
            result = terms[n, pl.ds(0, tile, stride=tile), :]
            for p in range(1, tile):
                result = result + terms[n, pl.ds(p, tile, stride=tile), :]
            made[n, pl.ds(i * tile, tile), :] = result
        return tuple(state)

    start = tuple(
        start_ref[n, h * tile : (h + 1) * tile, :] for n in range(seqs) for h in range(count)
    )
    lax.fori_loop(0, length // tile, step, start)
    empty(made, out_ref, place_ref[0])


def later_kernel(place_ref, signal_ref, decay_ref, state_ref, held):
    fill(signal_ref, held, place_ref[0])
    seqs, length, lanes = held.shape
    keep = [jnp.exp(-d) for d in halves(decay_ref)]
    count = len(keep)

    def step(i, carry):
        state = list(carry)
        base = length - tile - i * tile
        for k in range(tile - 1, -1, -1):
            for n in range(seqs):
                new = row_of(held, n, base + k)
                for h in range(count):
                    at = n * count + h
                    state[at] = keep[h] * state[at] + new
        return tuple(state)

    zero = jnp.zeros((tile, lanes), wide)
    state = lax.fori_loop(0, length // tile, step, tuple(zero for _ in range(seqs * count)))
    for n in range(seqs):
        for h in range(count):
            state_ref[n, h * tile : (h + 1) * tile, :] = state[n * count + h]


def backward_kernel(
    place_ref,
    signal_ref,
    grad_ref,
    decay_ref,
    residue_ref,
    start_ref,
    end_ref,
    out_ref,
    residue_grad_ref,
    decay_grad_ref,
    held,
    grads,
    terms,
    made,
    later,
):
    fill(signal_ref, held, place_ref[0])
    fill(grad_ref, grads, place_ref[0])
    seqs, length, lanes = held.shape
    keep = [jnp.exp(-d) for d in halves(decay_ref)]
    weigh = halves(residue_ref)
    count = len(keep)
    group = later.shape[0]
    zero = jnp.zeros((tile, lanes), wide)
    none = tuple(zero for _ in range(group * count))
    sum_first = [zero] * count
    sum_second = [zero] * count
    for base_seq in range(0, seqs, group):

        def load(ref):
            return tuple(
                ref[base_seq + n, h * tile : (h + 1) * tile, :]
                for n in range(group)
                for h in range(count)
            )

        def back_step(i, carry):
            state, first = [list(v) for v in carry]
            base = length - tile - i * tile
            for k in range(tile - 1, -1, -1):
                for n in range(group):
                    back = row_of(grads, base_seq + n, base + k)
                    new = row_of(held, base_seq + n, base + k)
                    total = None
                    for h in range(count):
                        at = n * count + h
                        state[at] = keep[h] * state[at] + back
                        first[at] = first[at] + new * state[at]
                        later[n, pl.ds(((base + k) * count + h) * tile, tile), :] = state[at]
                        term = weigh[h] * state[at]
                        total = term if total is None else total + term
                    terms[n, k * tile : (k + 1) * tile, :] = total
            for n in range(group):
                result = terms[n, pl.ds(0, tile, stride=tile), :]
                for p in range(1, tile):
                    result = result + terms[n, pl.ds(p, tile, stride=tile), :]
                made[base_seq + n, pl.ds(base, tile), :] = result
            return tuple(state), tuple(first)

        _, first = lax.fori_loop(0, length // tile, back_step, (load(end_ref), none))

        def ahead(i, carry):
            state, second = [list(v) for v in carry]
            for k in range(tile):
                for n in range(group):
                    new = row_of(held, base_seq + n, i * tile + k)
                    for h in range(count):
                        at = n * count + h
                        state[at] = keep[h] * state[at] + new
                        other = later[n, pl.ds(((i * tile + k) * count + h) * tile, tile), :]
                        second[at] = second[at] + state[at] * other
            return tuple(state), tuple(second)

        _, second = lax.fori_loop(0, length // tile, ahead, (load(start_ref), none))
        for n in range(group):
            for h in range(count):
                at = n * count + h
                sum_first[h] = sum_first[h] + first[at]
                sum_second[h] = sum_second[h] + (second[at] - first[at])
    for h in range(count):
        residue_grad_ref[h * tile : (h + 1) * tile, :] = sum_first[h]
        decay_grad_ref[h * tile : (h + 1) * tile, :] = -weigh[h] * sum_second[h]
    empty(made, out_ref, place_ref[0])


def conv_call(kernel, place, arrays, results, scratch, flops):
    channels = arrays[0].shape[-1]
    lanes = min(channels, 128)

    def spec(shape):
        lead = len(shape) - 1
        return pl.BlockSpec(shape[:-1] + (lanes,), lambda i, *_: (0,) * lead + (i,))

    return pl.pallas_call(
        kernel,
        out_shape=results,
        grid_spec=pltpu.PrefetchScalarGridSpec(
            num_scalar_prefetch=1,
            grid=(channels // lanes,),
            in_specs=[spec(a.shape) for a in arrays],
            out_specs=[spec(r.shape) for r in results],
            scratch_shapes=[pltpu.VMEM(s + (lanes,), wide) for s in scratch],
        ),
        compiler_params=pltpu.CompilerParams(
            dimension_semantics=("arbitrary",), vmem_limit_bytes=56 << 20
        ),
        cost_estimate=pl.CostEstimate(
            flops=flops, transcendentals=0, bytes_accessed=sum(a.size * 4 for a in arrays)
        ),
    )(place, *arrays)


def sizes(signal, poles):
    groups, parts, inner, length, channels = signal.shape
    return groups * inner, parts * length, channels, signal.size * poles


def states_of(place, signal, decay):
    seqs, length, channels, work = sizes(signal, decay.shape[0])
    shape = jax.ShapeDtypeStruct((seqs, decay.shape[0], channels), wide)
    return conv_call(states_kernel, place, [signal, decay], [shape], [(seqs, length)], 2 * work)[0]


def forward_of(place, signal, decay, residue, start):
    seqs, length, channels, work = sizes(signal, decay.shape[0])
    return conv_call(
        forward_kernel,
        place,
        [signal, decay, residue, start],
        [jax.ShapeDtypeStruct(signal.shape, low)],
        [(seqs, length), (seqs, tile * tile), (seqs, length)],
        4 * work,
    )[0]


def later_of(place, signal, decay):
    seqs, length, channels, work = sizes(signal, decay.shape[0])
    shape = jax.ShapeDtypeStruct((seqs, decay.shape[0], channels), wide)
    return conv_call(later_kernel, place, [signal, decay], [shape], [(seqs, length)], 2 * work)[0]


def backward_of(place, signal, grad, decay, residue, start, end):
    poles = decay.shape[0]
    seqs, length, channels, work = sizes(signal, poles)
    shape = jax.ShapeDtypeStruct(decay.shape, wide)
    group = min(seqs, 4)
    return conv_call(
        backward_kernel,
        place,
        [signal, grad, decay, residue, start, end],
        [jax.ShapeDtypeStruct(signal.shape, low), shape, shape],
        [
            (seqs, length),
            (seqs, length),
            (group, tile * tile),
            (seqs, length),
            (group, length * poles),
        ],
        12 * work,
    )


def rms_scale(values):
    return lax.rsqrt(jnp.mean(values * values, axis=-1, keepdims=True) + epsilon)


def norm_back(values, scale, gain, grad_normed):
    grad_gain = jnp.sum(grad_normed * values * scale, axis=(0, 1))
    scaled = grad_normed * gain
    grad_values = scale * scaled - values * scale * scale * scale * jnp.mean(
        scaled * values, axis=-1, keepdims=True
    )
    return (grad_values, grad_gain)


def dot(a, b, kind=wide):
    return jnp.dot(a, b, preferred_element_type=wide).astype(kind)


def dot_t(a, b, kind=wide):
    return lax.dot_general(a, b, (((1,), (1,)), ((), ())), preferred_element_type=wide).astype(kind)


def dot_w(a, b):
    return lax.dot_general(a, b, (((0,), (0,)), ((), ())), preferred_element_type=wide).astype(low)


def body(
    tokens,
    lengths,
    norm_gain,
    in_weight,
    conv_taps,
    filter_residue,
    filter_decay,
    out_weight,
    feed_gain,
    gate_weight,
    up_weight,
    down_weight,
    cotangent,
):
    spread, ycount = lax.axis_size("x"), lax.axis_size("y")
    batch, local, width = tokens.shape
    place = lax.axis_index("z") * spread + lax.axis_index("x")
    position = place * local + jnp.arange(local)
    mask = (position[None, :] < lengths[:, None]).astype(wide)[..., None]
    block = spread * local

    count = 3 * depth
    extra = 8
    line = Line(lax.axis_index("c"))
    run = line.run

    def stacked(value, got):
        return jnp.stack([value] + got)

    in_got = column_moves(run(lambda w: column_pieces(w, 3), in_weight))
    block_out = run(out_block, out_weight)
    out_got = moved(block_out, "z", -1)
    last = [(i * spread + spread - 1, (i + 1) * spread) for i in range(depth - 1)]

    def norm_one(values, gain):
        values = values.astype(wide)
        scale = rms_scale(values)
        normed = (values * scale * gain).astype(low)
        return normed, normed[:, local - 2 :], scale

    normed, ending, scale_one = run(norm_one, tokens, norm_gain)
    before = lax.ppermute(ending, ("z", "x"), last)
    w_in = gather_tile(run(column_block, in_got))

    def lengthen(values, rows):
        rest = jnp.zeros((batch, extra - 2, width), values.dtype)
        values = jnp.concatenate([values, rows, rest], axis=1)
        return values[: batch // 2], values[batch // 2 :]

    normed_move = Gather(*run(lengthen, normed, before))
    held = run(lambda own, got: by_z([own] + got), block_out, out_got)
    normed_move.turn(line)
    w_down = gather_tile(run(row_block, down_weight))
    gate_got = column_moves(run(lambda w: column_pieces(w, 1), gate_weight))
    normed_all = normed_move.end(line)
    out_move = Gather(held[:1], held[1:])

    channels = w_in.shape[1] // 3
    half = channels // 2
    grid = (2 * ycount, spread, batch // 2, local)

    def rank_values(all_taps, all_decay, all_residue):
        return (
            jnp.concatenate(
                [rank_rows(all_taps[:, g * width : (g + 1) * width], 1) for g in range(3)], axis=1
            ),
            rank_rows(all_decay, 0).T,
            rank_rows(all_residue, 0).T,
        )

    taps, decay, residue = run(rank_values, conv_taps, filter_decay, filter_residue)
    opening = (lax.axis_index("x") + jnp.arange(spread)) % spread == 0
    opening = opening[None, :, None, None, None]
    closing = (lax.axis_index("x") + jnp.arange(spread)) % spread == spread - 1
    closing = closing[None, :, None, None, None]

    def project(v, w):
        return dot(v, w, low).reshape(grid[:3] + (local + extra, 3 * channels))

    mixed = run(project, normed_all, w_in)
    out_move.turn(line)
    w_gate = gather_tile(run(column_block, gate_got))
    up_got = column_moves(run(lambda w: column_pieces(w, 1), up_weight))

    def extend(value, g):
        own = value[..., g * channels : (g + 1) * channels]
        earlier = jnp.roll(own[:, :, :, local - 2 : local], 1, axis=1)
        earlier = jnp.where(opening, own[:, :, :, local : local + 2], earlier)
        return jnp.concatenate([earlier, own[:, :, :, :local]], axis=3).astype(wide)

    def short_of(value, weights, g):
        longer = extend(value, g)
        own = weights[:, g * channels : (g + 1) * channels]
        return own[0] * longer[:, :, :, 2:] + own[1] * longer[:, :, :, 1:-1] + own[2] * longer[:, :, :, :-2]

    spot = lax.axis_index("x").astype(jnp.int32).reshape(1)

    def multiply(value, weights, rates):
        keys, values = (short_of(value, weights, g) for g in (1, 2))
        product = (keys * values).astype(low)
        return product, states_of(spot, product, rates)

    product, state_end = run(multiply, mixed, taps, decay)
    states = [passed(state_end, "z", k) for k in range(1, depth)]
    w_up = gather_tile(run(column_block, up_got))
    out_own = out_move.end(line)
    w_out = [out_own] + moved(out_own, "c", -1)

    def feed_grad(values):
        values = (values.astype(wide) * mask).astype(low)
        return values[: batch // 2], values[batch // 2 :]

    feed_move = Gather(*run(feed_grad, cotangent))

    def combine(parts, rates):
        total = parts[0]
        for k in range(1, depth - 1):
            total = total + jnp.exp(-rates * (k * block)) * parts[k]
        return total

    def convolve(parts, value, weights, signal, rates, amounts):
        start = combine(parts, rates)
        result = forward_of(spot, signal, rates, amounts, start)
        query = short_of(value, weights, 0)
        gated = (query * result.astype(wide)).astype(low)
        slots = gated.reshape(2, ycount, spread, -1, channels)
        return (
            start,
            result,
            gated.reshape(-1, channels),
            [[slots[:, k, i].reshape(-1, channels) for i in range(spread)] for k in range(ycount)],
        )

    start, convolved, gated_all, gated = run(
        convolve, states, mixed, taps, product, decay, residue
    )
    gated_got = swap_slots(gated)
    feed_move.turn(line)

    def mix(got, weights, values, gain):
        own = jnp.concatenate(
            [g[:, h * half : (h + 1) * half] for h in range(2) for row in got for g in row], axis=1
        )
        mixer = in_order(jnp.stack([dot(own, w) for w in weights]), "c")
        mixer = jnp.concatenate([m for m in mixer], axis=1).reshape(batch, local, width)
        middle = values.astype(wide) + mixer
        scale = rms_scale(middle)
        normed = (middle * scale * gain).astype(low)
        return middle, scale, normed[: batch // 2], normed[batch // 2 :]

    middle, scale_two, first, second = run(mix, gated_got, w_out, tokens, feed_gain)

    two_move = Gather(first, second)
    grad_feed_all = feed_move.end(line)
    grad_active = run(dot_t, grad_feed_all, w_down)
    two_move.turn(line)
    normed_two_all = two_move.end(line)

    def open_gate(v, w, back):
        value = dot(v, w)
        return value, (back * value * jax.nn.sigmoid(value)).astype(low)

    gate, grad_upper = run(open_gate, normed_two_all, w_gate, grad_active)
    up_term = run(dot_w, normed_two_all, grad_upper)
    up_mine = scatter_tile(up_term)

    def activate(v, w, value, back):
        upper = dot(v, w)
        sigma = jax.nn.sigmoid(value)
        return (
            (value * sigma * upper).astype(low),
            (back * upper * sigma * (1.0 + value * (1.0 - sigma))).astype(low),
        )

    active, grad_gate = run(activate, normed_two_all, w_up, gate, grad_active)
    two_back = Scatter(
        run(
            lambda a, b, wa, wb: split_sum((dot_t(a, wa) + dot_t(b, wb)).astype(low)),
            grad_gate,
            grad_upper,
            w_gate,
            w_up,
        )
    )
    gate_mine = scatter_tile(run(dot_w, normed_two_all, grad_gate))
    down_mine = scatter_tile(run(dot_w, active, grad_feed_all))
    two_back.turn(line)

    def middle_back(rest, values, scale, gain, back, weights):
        grad_normed = Scatter.sum(*rest).reshape(batch, local, width)
        result, grad_gain = norm_back(values, scale, gain, grad_normed)
        result = result + back.astype(wide) * mask
        parts = core_halves(result.astype(low).reshape(-1, width))
        own = sum(dot_t(m, w) for m, w in zip(parts, weights)).astype(low)
        ranks = ycount * spread

        def slot(at):
            pieces = [
                own[:, (h * ranks + at) * half : (h * ranks + at + 1) * half] for h in range(2)
            ]
            return jnp.concatenate(pieces, axis=1)

        slots = [[slot(k * spread + i) for i in range(spread)] for k in range(ycount)]
        rounded = result.astype(low)
        return result, grad_gain, rounded[: batch // 2], rounded[batch // 2 :], slots

    grad_middle, grad_feed_gain, first, second, grad_slots = run(
        middle_back, two_back.rest(), middle, scale_two, feed_gain, cotangent, w_out
    )
    grad_got = swap_slots(grad_slots)
    mix_move = Gather(first, second)

    def conv_grads(got, result, value, weights, rates):
        grad = jnp.stack([jnp.stack(row) for row in got])
        grad = grad.reshape(ycount, spread, 2, batch // 2, local, channels)
        grad = jnp.moveaxis(grad, 2, 0).reshape(grid + (channels,)).astype(wide)
        grad_query = grad * result.astype(wide)
        grad_conv = (grad * short_of(value, weights, 0)).astype(low)
        return grad_query, grad_conv, later_of(spot, grad_conv, rates)

    grad_query, grad_conv, later_end = run(conv_grads, grad_got, convolved, mixed, taps, decay)
    laters = [passed(later_end, "z", -k) for k in range(1, depth)]
    mix_move.turn(line)

    def short_back(grad, weights):
        head = jnp.roll(grad[:, :, :, :2], -1, axis=1)
        whole = jnp.concatenate([grad, jnp.where(closing, 0.0, head)], axis=3)
        result = (
            weights[0] * whole[:, :, :, :-2]
            + weights[1] * whole[:, :, :, 1:-1]
            + weights[2] * whole[:, :, :, 2:]
        )
        one, two = grad[:, :, :, :1], grad[:, :, :, 1:2]
        earlier = jnp.concatenate([weights[2] * one, weights[1] * one + weights[2] * two], axis=3)
        rest = jnp.zeros(grad.shape[:3] + (extra - 2, grad.shape[-1]), wide)
        result = jnp.concatenate([result, jnp.where(opening, earlier, 0.0), rest], axis=3)
        return result.astype(low).reshape(-1, grad.shape[-1])

    def query_back(grad, weights, v):
        result = short_back(grad, weights[:, :channels])
        return result, dot_w(v, result)

    grad_mixed_query, query_term = run(query_back, grad_query, taps, normed_all)
    query_mine = scatter_tile(query_term)
    up_parts_got = owner_moves(run(owner_parts, up_mine))

    def conv_back(signal, grad, rates, amounts, begin, ends_later, value, weights):
        later = combine(ends_later, rates)
        grad_product, grad_residue, grad_decay = backward_of(
            spot, signal, grad, rates, amounts, begin, later
        )
        grad_product = grad_product.astype(wide)
        keys, values = (short_of(value, weights, g) for g in (1, 2))
        pair = jnp.concatenate([grad_product * values, grad_product * keys], axis=-1)
        return pair, grad_residue, grad_decay

    grad_pair, grad_residue, grad_decay = run(
        conv_back, product, grad_conv, decay, residue, start, laters, mixed, taps
    )

    def pair_back(grad, weights, v):
        result = short_back(grad, weights[:, channels:])
        return result, dot_w(v, result)

    grad_mixed_pair, pair_term = run(pair_back, grad_pair, taps, normed_all)
    pair_mine = scatter_tile(pair_term)
    up_held = run(owner_held, up_parts_got)
    up_got = moved(up_held, "y", -1)
    grad_mix_all = mix_move.end(line)
    out_mine = scatter_tile(run(dot_w, gated_all, grad_mix_all))
    one_back = Scatter(
        run(
            lambda a, b, w: split_sum(dot_t(jnp.concatenate([a, b], axis=1), w, low)),
            grad_mixed_query,
            grad_mixed_pair,
            w_in,
        )
    )

    feed_parts = run(lambda a, w: split_sum(dot(a, w, low)), active, w_down)
    up_held = run(stacked, up_held, up_got)
    up_got = moved(up_held, "c", -1)
    one_back.turn(line)
    feed_back = Scatter(feed_parts)
    gate_got = owner_moves(run(owner_parts, gate_mine))

    def tap_sums(query, pair, value):
        sums = []
        for g, part in enumerate((query, pair[..., :channels], pair[..., channels:])):
            own = extend(value, g)
            sums += [
                jnp.sum(part * own[:, :, :, 2 - j : local + 2 - j], axis=(0, 1, 2, 3))
                for j in range(3)
            ]
        return jnp.stack(sums)

    grad_taps = run(tap_sums, grad_query, grad_pair, mixed)

    def normed_sum(rest):
        value = Scatter.sum(*rest).reshape(batch, local + extra, width)
        return value[:, :local], value[:, local : local + 2].astype(low)

    grad_normed, grad_before = run(normed_sum, one_back.rest())
    grad_after = lax.ppermute(grad_before, ("z", "x"), [(j, i) for i, j in last])

    def column_whole(own, got):
        return owner_whole(lax.axis_index("c"), [own] + got, depth)

    grad_up_weight = run(column_whole, up_held, up_got)
    gate_held = run(owner_held, gate_got)
    gate_got = moved(gate_held, "y", -1)
    feed_back.turn(line)

    def tokens_back(grad, extension, values, scale, gain, back, small):
        values = values.astype(wide)
        grad = jnp.concatenate(
            [grad[:, : local - 2], grad[:, local - 2 :] + extension.astype(wide)], axis=1
        )
        result, grad_gain = norm_back(values, scale, gain, grad)
        gains = jnp.stack([grad_gain, small[0]]).reshape(-1, channels)
        return (result + back).astype(low), jnp.concatenate(list(small[1:]) + [gains], axis=0)

    grad_tokens, small = run(
        tokens_back,
        grad_normed,
        grad_after,
        tokens,
        scale_one,
        norm_gain,
        grad_middle,
        (grad_feed_gain, grad_residue, grad_decay, grad_taps),
    )
    small_got = moved(small, "c", 1)
    gate_held = run(stacked, gate_held, gate_got)
    gate_got = moved(gate_held, "c", -1)
    small = run(lambda v, got: v + sum(got), small, small_got)
    small_got = moved(small, "z", 1)
    output = run(
        lambda rest, values: (
            mask * (values + Scatter.sum(*rest).reshape(batch, local, width))
        ).astype(low),
        feed_back.rest(),
        middle,
    )
    down_rows = down_mine.shape[0]
    rows_held = run(lambda a, b: jnp.concatenate([a, b])[None], down_mine, out_mine)
    rows_got = moved(rows_held, "y", -1)
    grad_gate_weight = run(column_whole, gate_held, gate_got)
    small = run(lambda v, got: v + sum(got), small, small_got)
    small_got = moved(small, "x", -1)
    parts = run(
        lambda a, b: owner_parts(jnp.concatenate([a, b], axis=1)), query_mine, pair_mine
    )
    in_got = owner_moves(parts)
    rows_held = run(lambda own, got: jnp.concatenate([own] + got), rows_held, rows_got)
    rows_got = moved(rows_held, "c", -1)
    small = run(stacked, small, small_got)
    small_got = moved(small, "y", -1)
    in_held = run(owner_held, in_got)
    in_got = moved(in_held, "y", -1)

    def rows_whole(own, got):
        whole = in_order(jnp.swapaxes(in_order(jnp.stack([own] + got), "c"), 0, 1), "y")
        return (
            whole[:, :, :down_rows].reshape(-1, width).astype(wide),
            whole[:, :, down_rows:].reshape(-1, width).astype(wide),
        )

    grad_down, grad_out_weight = run(rows_whole, rows_held, rows_got)
    in_held = run(stacked, in_held, in_got)
    in_got = moved(in_held, "c", -1)
    poles = decay.shape[0]

    def small_whole(own, got):
        slots = jnp.stack([own] + got)
        rows = 2 * poles + 9
        gains = jnp.sum(slots[:, :, rows:], axis=(0, 1)).reshape(2, width)
        whole = all_channels(slots[:, :, :rows])
        grad_conv_taps = jnp.concatenate(
            [whole[2 * poles + 3 * g : 2 * poles + 3 * g + 3] for g in range(3)], axis=1
        )
        return gains[0], gains[1], grad_conv_taps, whole[:poles].T, whole[poles : 2 * poles].T

    grad_norm_gain, feed_gain_sum, grad_conv_taps, residue_sum, decay_sum = run(
        small_whole, small, small_got
    )
    grad_in_weight = line.finish(
        lambda core, own, got: owner_whole(core, [own] + got, count), in_held, in_got
    )
    return (
        output,
        grad_tokens,
        grad_norm_gain,
        grad_in_weight,
        grad_conv_taps,
        residue_sum,
        decay_sum,
        grad_out_weight,
        feed_gain_sum,
        grad_gate_weight,
        grad_up_weight,
        grad_down,
    )


def solution(mesh):
    pairs, blocks = mesh.shape["dp"], mesh.shape["seq"]
    devices = mesh.devices.reshape(pairs // cores, cores, depth, blocks // depth)
    inner = Mesh(devices, ("y", "c", "z", "x"))
    dp, seq = ("y", "c"), ("z", "x")
    tokens, rows = P(dp, seq, None), P(seq, None)
    return jax.shard_map(
        body,
        mesh=inner,
        in_specs=(
            tokens,
            P(dp),
            P(),
            rows,
            P(),
            P(),
            P(),
            rows,
            P(),
            rows,
            rows,
            rows,
            tokens,
        ),
        out_specs=(tokens, tokens, P(), rows, P(), P(), P(), rows, P(), rows, rows, rows),
        check_vma=False,
    )
```

```python
import functools

import jax
import jax.numpy as jnp
from jax import lax
from jax.experimental import pallas as pl
from jax.experimental.pallas import tpu as pltpu
from jax.sharding import Mesh, PartitionSpec as P

epsilon = 1e-06
low = jnp.bfloat16
wide = jnp.float32
tile = 8
depth = 4
cores = 2


def turned(value, axis, by):
    length = lax.axis_size(axis)
    return lax.ppermute(value, axis, [(i, (i + by) % length) for i in range(length)])


def passed(value, axis, by):
    length = lax.axis_size(axis)
    pairs = [(i, i + by) for i in range(length) if 0 <= i + by < length]
    return lax.ppermute(value, axis, pairs)


def swap_slots(slots):
    ycount, spread = lax.axis_size("y"), lax.axis_size("x")
    result = []
    for dy in range(ycount):
        line = []
        for dx in range(spread):
            sy, sx = (ycount - dy) % ycount, (spread - dx) % spread
            if sy == 0 and sx == 0:
                line.append(slots[0][0])
                continue
            pairs = [
                (i * spread + j, (i + sy) % ycount * spread + (j + sx) % spread)
                for i in range(ycount)
                for j in range(spread)
            ]
            line.append(lax.ppermute(slots[sy][sx], ("y", "x"), pairs))
        result.append(line)
    return result


class Line:
    def __init__(self, token):
        self.token = token

    def run(self, work, *values):
        values, token = lax.optimization_barrier((values, self.token))
        result, self.token = lax.optimization_barrier((work(*values), token))
        return result

    def finish(self, work, *values):
        values, token = lax.optimization_barrier((values, self.token))
        return work(token, *values)


def moved(value, axis, sign):
    return [turned(value, axis, sign * d) for d in range(1, lax.axis_size(axis))]


class Gather:
    def __init__(self, first, second):
        self.held = (first, second)
        self.got = (moved(first, "x", -1), moved(second, "y", -1))

    def turn(self, line):
        self.held = line.run(
            lambda held, got: tuple(jnp.stack([h] + g) for h, g in zip(held, got)), self.held, self.got
        )
        self.got = (moved(self.held[0], "y", -1), moved(self.held[1], "x", -1))

    def end(self, line):
        def work(held, got):
            first = jnp.stack([held[0]] + got[0])
            second = jnp.swapaxes(jnp.stack([held[1]] + got[1]), 0, 1)
            return jnp.stack([first, second]).reshape(-1, first.shape[-1])

        return line.run(work, self.held, self.got)


def split_sum(partial):
    grid = partial.reshape(2, lax.axis_size("y"), lax.axis_size("x"), -1, partial.shape[-1])
    first = [grid[0][:, d].astype(low) for d in range(grid.shape[2])]
    second = [grid[1][d].astype(low) for d in range(grid.shape[1])]
    return first, second


def add_up(parts, got):
    total = parts[0].astype(wide)
    for g in got:
        total = total + g.astype(wide)
    return total


class Scatter:
    def __init__(self, parts):
        self.parts = parts
        self.send("x", "y")

    def send(self, *axes):
        self.got = [
            [turned(p, axis, d + 1) for d, p in enumerate(part[1:])]
            for part, axis in zip(self.parts, axes)
        ]

    def turn(self, line):
        def work(parts, got):
            result = []
            for part, g in zip(parts, got):
                total = add_up(part, g).astype(low)
                result.append([total[d] for d in range(total.shape[0])])
            return result

        self.parts = line.run(work, self.parts, self.got)
        self.send("y", "x")

    def rest(self):
        return self.parts, self.got

    @staticmethod
    def sum(parts, got):
        return jnp.stack([add_up(part, g) for part, g in zip(parts, got)])


def pick_kernel(count, part, stride, start_ref, source, *refs):
    targets, sems = refs[:-1], refs[-1]
    copies = []
    for d, target in enumerate(targets):
        for k in range(count):
            at = pl.multiple_of((k * stride + start_ref[d]) * part, part)
            copies.append(
                pltpu.make_async_copy(
                    source.at[:, pl.ds(at, part)],
                    target.at[:, k * part : (k + 1) * part],
                    sems.at[d * count + k],
                )
            )
    for copy in copies:
        copy.start()
    for copy in copies:
        copy.wait()


def column_pieces(weight, groups):
    spread, ycount = lax.axis_size("x"), lax.axis_size("y")
    rows = weight.shape[0]
    count = groups * depth
    part = weight.shape[1] // (count * spread * ycount)
    starts = [
        (lax.axis_index("x") + d) % spread * ycount + lax.axis_index("y") for d in range(spread)
    ]
    if part % 128 == 0:
        return pl.pallas_call(
            functools.partial(pick_kernel, count, part, spread * ycount),
            out_shape=[jax.ShapeDtypeStruct((rows, count * part), weight.dtype)] * spread,
            grid_spec=pltpu.PrefetchScalarGridSpec(
                num_scalar_prefetch=1,
                in_specs=[pl.BlockSpec(memory_space=pl.ANY)],
                out_specs=[pl.BlockSpec(memory_space=pltpu.VMEM)] * spread,
                scratch_shapes=[pltpu.SemaphoreType.DMA((count * spread,))],
            ),
            cost_estimate=pl.CostEstimate(
                flops=0, transcendentals=0, bytes_accessed=4 * rows * count * part * spread
            ),
        )(jnp.stack(starts).astype(jnp.int32), weight)
    return [
        jnp.concatenate(
            [
                lax.dynamic_slice_in_dim(weight, (k * spread * ycount + start) * part, part, 1)
                for k in range(count)
            ],
            axis=1,
        )
        for start in starts
    ]


def column_moves(pieces):
    spread, ccount = lax.axis_size("x"), lax.axis_size("c")
    share = spread // ccount
    got = [pieces[0]]
    for d in range(1, spread):
        pairs = [
            (i // share * spread + i, i // share * spread + (i + d) % spread) for i in range(spread)
        ]
        got.append(lax.ppermute(pieces[d], ("c", "x"), pairs))
    return got


def column_block(got):
    spread, ccount = lax.axis_size("x"), lax.axis_size("c")
    share = spread // ccount
    place, core = lax.axis_index("x"), lax.axis_index("c")
    got = jnp.stack(got)
    return jnp.concatenate(
        [
            lax.dynamic_index_in_dim(got, (place - core * share - j) % spread, 0, False)
            for j in range(share)
        ]
    )


def row_block(weight):
    ycount, ccount = lax.axis_size("y"), lax.axis_size("c")
    part = weight.shape[0] // (ycount * ccount)
    pair = lax.axis_index("y") * ccount + lax.axis_index("c")
    return lax.dynamic_slice_in_dim(weight, pair * part, part, 0)


def core_halves(value):
    ccount = lax.axis_size("c")
    width = value.shape[1] // ccount
    core = lax.axis_index("c")
    return [
        lax.dynamic_slice_in_dim(value, (core + d) % ccount * width, width, 1)
        for d in range(ccount)
    ]


def out_block(weight):
    part = weight.shape[0] // lax.axis_size("y")
    rows = lax.dynamic_slice_in_dim(weight, lax.axis_index("y") * part, part, 0)
    return core_halves(rows)[0]


def by_z(slots):
    held = in_order(jnp.stack(slots), "z")
    return held.reshape(2, -1, held.shape[-1])


def gather_tile(block):
    return lax.all_gather(block, ("z", "c"), axis=0, tiled=True)


def scatter_tile(term):
    return lax.psum_scatter(term, ("z", "c"), scatter_dimension=0, tiled=True)


def owner_parts(mine):
    spread, ccount = lax.axis_size("x"), lax.axis_size("c")
    share = spread // ccount
    place, core = lax.axis_index("x"), lax.axis_index("c")
    parts = mine.reshape(share, -1, mine.shape[-1])
    return [
        lax.dynamic_index_in_dim(
            parts, jnp.clip((place + d) % spread - core * share, 0, share - 1), 0, False
        )
        for d in range(spread)
    ]


def owner_moves(parts):
    spread, ccount = lax.axis_size("x"), lax.axis_size("c")
    share = spread // ccount
    got = [parts[0]]
    for d in range(1, spread):
        pairs = [
            ((i + d) % spread // share * spread + i, i // share * spread + (i + d) % spread)
            for i in range(spread)
        ]
        got.append(lax.ppermute(parts[d], ("c", "x"), pairs))
    return got


def owner_held(got):
    spread, ccount = lax.axis_size("x"), lax.axis_size("c")
    share = spread // ccount
    place, core = lax.axis_index("x"), lax.axis_index("c")
    got = jnp.stack(got)
    return jnp.stack(
        [
            lax.dynamic_index_in_dim(got, (place - core * share - j) % spread, 0, False)
            for j in range(share)
        ]
    )


def assemble_kernel(count, width, order_ref, *refs):
    sources, target = refs[:-1], refs[-1]
    part = width // count
    ranks = order_ref.shape[0] // 2
    for r in range(ranks):
        core, slot = order_ref[2 * r], order_ref[2 * r + 1]
        value = sources[0][slot]
        for c in range(1, len(sources)):
            value = jnp.where(core == c, sources[c][slot], value)
        value = value.astype(wide)
        for at in range(count):
            start = (at * ranks + r) * part
            target[:, start : start + part] = value[:, at * part : (at + 1) * part]


def owner_whole(core, sources, count):
    spread, ccount, ycount = lax.axis_size("x"), lax.axis_size("c"), lax.axis_size("y")
    share = spread // ccount
    yplace = lax.axis_index("y")
    order = []
    for i in range(spread):
        for k in range(ycount):
            order += [(i // share - core) % ccount, (k - yplace) % ycount * share + i % share]
    sources = [v.reshape((-1,) + v.shape[2:]) for v in sources]
    held, rows, width = sources[0].shape
    block = min(rows, 64)
    return pl.pallas_call(
        functools.partial(assemble_kernel, count, width),
        out_shape=jax.ShapeDtypeStruct((rows, width * spread * ycount), wide),
        grid_spec=pltpu.PrefetchScalarGridSpec(
            num_scalar_prefetch=1,
            grid=(rows // block,),
            in_specs=[pl.BlockSpec((held, block, width), lambda i, order: (0, i, 0))]
            * len(sources),
            out_specs=pl.BlockSpec((block, width * spread * ycount), lambda i, order: (i, 0)),
        ),
        compiler_params=pltpu.CompilerParams(vmem_limit_bytes=56 << 20),
        cost_estimate=pl.CostEstimate(
            flops=0, transcendentals=0, bytes_accessed=6 * rows * width * spread * ycount
        ),
    )(jnp.stack(order).astype(jnp.int32), *sources)


def in_order(slots, axis):
    length = lax.axis_size(axis)
    place = lax.axis_index(axis)
    return jnp.stack(
        [lax.dynamic_index_in_dim(slots, (j - place) % length, 0, False) for j in range(length)]
    )


def rank_rows(values, axis):
    spread, ycount = lax.axis_size("x"), lax.axis_size("y")
    part = values.shape[axis] // (depth * spread * ycount)
    place = lax.axis_index("x") * ycount + lax.axis_index("y")
    return jnp.concatenate(
        [
            lax.dynamic_slice_in_dim(values, (k * spread * ycount + place) * part, part, axis)
            for k in range(depth)
        ],
        axis=axis,
    )


def all_channels(slots):
    whole = in_order(slots, "y")
    whole = in_order(jnp.swapaxes(whole, 0, 1), "x")
    spread, ycount, rows = whole.shape[:3]
    whole = whole.reshape(spread, ycount, rows, depth, -1)
    return jnp.transpose(whole, (2, 3, 0, 1, 4)).reshape(rows, -1)


def fill(source, target, place):
    groups, parts, inner, length = source.shape[:4]
    for j in range(parts):
        slot = lax.rem(j + parts - place, parts)
        for g in range(groups):
            for b in range(inner):
                target[g * inner + b, j * length : (j + 1) * length, :] = source[g, slot, b].astype(
                    wide
                )


def empty(source, target, place):
    groups, parts, inner, length = target.shape[:4]
    for j in range(parts):
        slot = lax.rem(j + parts - place, parts)
        for g in range(groups):
            for b in range(inner):
                target[g, slot, b] = source[g * inner + b, j * length : (j + 1) * length, :].astype(
                    low
                )


def halves(ref):
    return [ref[k * tile : (k + 1) * tile, :] for k in range(ref.shape[0] // tile)]


def row_of(ref, seq, at):
    return ref[seq, pl.ds(at, tile, stride=0), :]


def states_kernel(place_ref, signal_ref, decay_ref, state_ref, held):
    fill(signal_ref, held, place_ref[0])
    seqs, length, lanes = held.shape
    keep = [jnp.exp(-d) for d in halves(decay_ref)]
    count = len(keep)

    def step(i, carry):
        state = list(carry)
        for k in range(tile):
            for n in range(seqs):
                new = row_of(held, n, i * tile + k)
                for h in range(count):
                    at = n * count + h
                    state[at] = keep[h] * state[at] + new
        return tuple(state)

    zero = jnp.zeros((tile, lanes), wide)
    state = lax.fori_loop(0, length // tile, step, tuple(zero for _ in range(seqs * count)))
    for n in range(seqs):
        for h in range(count):
            state_ref[n, h * tile : (h + 1) * tile, :] = state[n * count + h]


def forward_kernel(place_ref, signal_ref, decay_ref, residue_ref, start_ref, out_ref, held, terms, made):
    fill(signal_ref, held, place_ref[0])
    seqs, length, lanes = held.shape
    keep = [jnp.exp(-d) for d in halves(decay_ref)]
    weigh = halves(residue_ref)
    count = len(keep)

    def step(i, carry):
        state = list(carry)
        for k in range(tile):
            for n in range(seqs):
                new = row_of(held, n, i * tile + k)
                total = None
                for h in range(count):
                    at = n * count + h
                    state[at] = keep[h] * state[at] + new
                    term = weigh[h] * state[at]
                    total = term if total is None else total + term
                terms[n, k * tile : (k + 1) * tile, :] = total
        for n in range(seqs):
            result = terms[n, pl.ds(0, tile, stride=tile), :]
            for p in range(1, tile):
                result = result + terms[n, pl.ds(p, tile, stride=tile), :]
            made[n, pl.ds(i * tile, tile), :] = result
        return tuple(state)

    start = tuple(
        start_ref[n, h * tile : (h + 1) * tile, :] for n in range(seqs) for h in range(count)
    )
    lax.fori_loop(0, length // tile, step, start)
    empty(made, out_ref, place_ref[0])


def later_kernel(place_ref, signal_ref, decay_ref, state_ref, held):
    fill(signal_ref, held, place_ref[0])
    seqs, length, lanes = held.shape
    keep = [jnp.exp(-d) for d in halves(decay_ref)]
    count = len(keep)

    def step(i, carry):
        state = list(carry)
        base = length - tile - i * tile
        for k in range(tile - 1, -1, -1):
            for n in range(seqs):
                new = row_of(held, n, base + k)
                for h in range(count):
                    at = n * count + h
                    state[at] = keep[h] * state[at] + new
        return tuple(state)

    zero = jnp.zeros((tile, lanes), wide)
    state = lax.fori_loop(0, length // tile, step, tuple(zero for _ in range(seqs * count)))
    for n in range(seqs):
        for h in range(count):
            state_ref[n, h * tile : (h + 1) * tile, :] = state[n * count + h]


def backward_kernel(
    place_ref,
    signal_ref,
    grad_ref,
    decay_ref,
    residue_ref,
    start_ref,
    end_ref,
    out_ref,
    residue_grad_ref,
    decay_grad_ref,
    held,
    grads,
    terms,
    made,
    later,
):
    fill(signal_ref, held, place_ref[0])
    fill(grad_ref, grads, place_ref[0])
    seqs, length, lanes = held.shape
    keep = [jnp.exp(-d) for d in halves(decay_ref)]
    weigh = halves(residue_ref)
    count = len(keep)
    group = later.shape[0]
    zero = jnp.zeros((tile, lanes), wide)
    none = tuple(zero for _ in range(group * count))
    sum_first = [zero] * count
    sum_second = [zero] * count
    for base_seq in range(0, seqs, group):

        def load(ref):
            return tuple(
                ref[base_seq + n, h * tile : (h + 1) * tile, :]
                for n in range(group)
                for h in range(count)
            )

        def back_step(i, carry):
            state, first = [list(v) for v in carry]
            base = length - tile - i * tile
            for k in range(tile - 1, -1, -1):
                for n in range(group):
                    back = row_of(grads, base_seq + n, base + k)
                    new = row_of(held, base_seq + n, base + k)
                    total = None
                    for h in range(count):
                        at = n * count + h
                        state[at] = keep[h] * state[at] + back
                        first[at] = first[at] + new * state[at]
                        later[n, pl.ds(((base + k) * count + h) * tile, tile), :] = state[at]
                        term = weigh[h] * state[at]
                        total = term if total is None else total + term
                    terms[n, k * tile : (k + 1) * tile, :] = total
            for n in range(group):
                result = terms[n, pl.ds(0, tile, stride=tile), :]
                for p in range(1, tile):
                    result = result + terms[n, pl.ds(p, tile, stride=tile), :]
                made[base_seq + n, pl.ds(base, tile), :] = result
            return tuple(state), tuple(first)

        _, first = lax.fori_loop(0, length // tile, back_step, (load(end_ref), none))

        def ahead(i, carry):
            state, second = [list(v) for v in carry]
            for k in range(tile):
                for n in range(group):
                    new = row_of(held, base_seq + n, i * tile + k)
                    for h in range(count):
                        at = n * count + h
                        state[at] = keep[h] * state[at] + new
                        other = later[n, pl.ds(((i * tile + k) * count + h) * tile, tile), :]
                        second[at] = second[at] + state[at] * other
            return tuple(state), tuple(second)

        _, second = lax.fori_loop(0, length // tile, ahead, (load(start_ref), none))
        for n in range(group):
            for h in range(count):
                at = n * count + h
                sum_first[h] = sum_first[h] + first[at]
                sum_second[h] = sum_second[h] + (second[at] - first[at])
    for h in range(count):
        residue_grad_ref[h * tile : (h + 1) * tile, :] = sum_first[h]
        decay_grad_ref[h * tile : (h + 1) * tile, :] = -weigh[h] * sum_second[h]
    empty(made, out_ref, place_ref[0])


def conv_call(kernel, place, arrays, results, scratch, flops):
    channels = arrays[0].shape[-1]
    lanes = min(channels, 128)

    def spec(shape):
        lead = len(shape) - 1
        return pl.BlockSpec(shape[:-1] + (lanes,), lambda i, *_: (0,) * lead + (i,))

    return pl.pallas_call(
        kernel,
        out_shape=results,
        grid_spec=pltpu.PrefetchScalarGridSpec(
            num_scalar_prefetch=1,
            grid=(channels // lanes,),
            in_specs=[spec(a.shape) for a in arrays],
            out_specs=[spec(r.shape) for r in results],
            scratch_shapes=[pltpu.VMEM(s + (lanes,), wide) for s in scratch],
        ),
        compiler_params=pltpu.CompilerParams(
            dimension_semantics=("arbitrary",), vmem_limit_bytes=56 << 20
        ),
        cost_estimate=pl.CostEstimate(
            flops=flops, transcendentals=0, bytes_accessed=sum(a.size * 4 for a in arrays)
        ),
    )(place, *arrays)


def sizes(signal, poles):
    groups, parts, inner, length, channels = signal.shape
    return groups * inner, parts * length, channels, signal.size * poles


def states_of(place, signal, decay):
    seqs, length, channels, work = sizes(signal, decay.shape[0])
    shape = jax.ShapeDtypeStruct((seqs, decay.shape[0], channels), wide)
    return conv_call(states_kernel, place, [signal, decay], [shape], [(seqs, length)], 2 * work)[0]


def forward_of(place, signal, decay, residue, start):
    seqs, length, channels, work = sizes(signal, decay.shape[0])
    return conv_call(
        forward_kernel,
        place,
        [signal, decay, residue, start],
        [jax.ShapeDtypeStruct(signal.shape, low)],
        [(seqs, length), (seqs, tile * tile), (seqs, length)],
        4 * work,
    )[0]


def later_of(place, signal, decay):
    seqs, length, channels, work = sizes(signal, decay.shape[0])
    shape = jax.ShapeDtypeStruct((seqs, decay.shape[0], channels), wide)
    return conv_call(later_kernel, place, [signal, decay], [shape], [(seqs, length)], 2 * work)[0]


def backward_of(place, signal, grad, decay, residue, start, end):
    poles = decay.shape[0]
    seqs, length, channels, work = sizes(signal, poles)
    shape = jax.ShapeDtypeStruct(decay.shape, wide)
    group = min(seqs, 4)
    return conv_call(
        backward_kernel,
        place,
        [signal, grad, decay, residue, start, end],
        [jax.ShapeDtypeStruct(signal.shape, low), shape, shape],
        [
            (seqs, length),
            (seqs, length),
            (group, tile * tile),
            (seqs, length),
            (group, length * poles),
        ],
        12 * work,
    )


def rms_scale(values):
    return lax.rsqrt(jnp.mean(values * values, axis=-1, keepdims=True) + epsilon)


def norm_back(values, scale, gain, grad_normed):
    grad_gain = jnp.sum(grad_normed * values * scale, axis=(0, 1))
    scaled = grad_normed * gain
    grad_values = scale * scaled - values * scale * scale * scale * jnp.mean(
        scaled * values, axis=-1, keepdims=True
    )
    return (grad_values, grad_gain)


def dot(a, b, kind=wide):
    return jnp.dot(a, b, preferred_element_type=wide).astype(kind)


def dot_t(a, b, kind=wide):
    return lax.dot_general(a, b, (((1,), (1,)), ((), ())), preferred_element_type=wide).astype(kind)


def dot_w(a, b):
    return lax.dot_general(a, b, (((0,), (0,)), ((), ())), preferred_element_type=wide).astype(low)


def body(
    tokens,
    lengths,
    norm_gain,
    in_weight,
    conv_taps,
    filter_residue,
    filter_decay,
    out_weight,
    feed_gain,
    gate_weight,
    up_weight,
    down_weight,
    cotangent,
):
    spread, ycount = lax.axis_size("x"), lax.axis_size("y")
    batch, local, width = tokens.shape
    place = lax.axis_index("z") * spread + lax.axis_index("x")
    position = place * local + jnp.arange(local)
    mask = (position[None, :] < lengths[:, None]).astype(wide)[..., None]
    block = spread * local

    count = 3 * depth
    extra = 8
    line = Line(lax.axis_index("c"))
    run = line.run

    def stacked(value, got):
        return jnp.stack([value] + got)

    in_got = column_moves(run(lambda w: column_pieces(w, 3), in_weight))
    block_out = run(out_block, out_weight)
    out_got = moved(block_out, "z", -1)
    last = [(i * spread + spread - 1, (i + 1) * spread) for i in range(depth - 1)]

    def norm_one(values, gain):
        values = values.astype(wide)
        scale = rms_scale(values)
        normed = (values * scale * gain).astype(low)
        return normed, normed[:, local - 2 :], scale

    normed, ending, scale_one = run(norm_one, tokens, norm_gain)
    before = lax.ppermute(ending, ("z", "x"), last)
    w_in = gather_tile(run(column_block, in_got))

    def lengthen(values, rows):
        rest = jnp.zeros((batch, extra - 2, width), values.dtype)
        values = jnp.concatenate([values, rows, rest], axis=1)
        return values[: batch // 2], values[batch // 2 :]

    normed_move = Gather(*run(lengthen, normed, before))
    held = run(lambda own, got: by_z([own] + got), block_out, out_got)
    normed_move.turn(line)
    w_down = gather_tile(run(row_block, down_weight))
    out_move = Gather(held[:1], held[1:])
    gate_got = column_moves(run(lambda w: column_pieces(w, 1), gate_weight))
    normed_all = normed_move.end(line)

    channels = w_in.shape[1] // 3
    half = channels // 2
    grid = (2 * ycount, spread, batch // 2, local)

    def rank_values(all_taps, all_decay, all_residue):
        return (
            jnp.concatenate(
                [rank_rows(all_taps[:, g * width : (g + 1) * width], 1) for g in range(3)], axis=1
            ),
            rank_rows(all_decay, 0).T,
            rank_rows(all_residue, 0).T,
        )

    taps, decay, residue = run(rank_values, conv_taps, filter_decay, filter_residue)
    opening = (lax.axis_index("x") + jnp.arange(spread)) % spread == 0
    opening = opening[None, :, None, None, None]
    closing = (lax.axis_index("x") + jnp.arange(spread)) % spread == spread - 1
    closing = closing[None, :, None, None, None]

    def project(v, w):
        return dot(v, w, low).reshape(grid[:3] + (local + extra, 3 * channels))

    out_move.turn(line)
    mixed = run(project, normed_all, w_in)

    def extend(value, g):
        own = value[..., g * channels : (g + 1) * channels]
        earlier = jnp.roll(own[:, :, :, local - 2 : local], 1, axis=1)
        earlier = jnp.where(opening, own[:, :, :, local : local + 2], earlier)
        return jnp.concatenate([earlier, own[:, :, :, :local]], axis=3).astype(wide)

    def short_of(value, weights, g):
        longer = extend(value, g)
        own = weights[:, g * channels : (g + 1) * channels]
        return own[0] * longer[:, :, :, 2:] + own[1] * longer[:, :, :, 1:-1] + own[2] * longer[:, :, :, :-2]

    spot = lax.axis_index("x").astype(jnp.int32).reshape(1)

    def multiply(value, weights, rates):
        keys, values = (short_of(value, weights, g) for g in (1, 2))
        product = (keys * values).astype(low)
        return product, states_of(spot, product, rates)

    product, state_end = run(multiply, mixed, taps, decay)
    states = [passed(state_end, "z", k) for k in range(1, depth)]
    w_gate = gather_tile(run(column_block, gate_got))

    def feed_grad(values):
        values = (values.astype(wide) * mask).astype(low)
        return values[: batch // 2], values[batch // 2 :]

    feed_move = Gather(*run(feed_grad, cotangent))
    up_pieces = run(lambda w: column_pieces(w, 1), up_weight)
    out_own = out_move.end(line)
    w_out = [out_own] + moved(out_own, "c", -1)
    feed_move.turn(line)

    def combine(parts, rates):
        total = parts[0]
        for k in range(1, depth - 1):
            total = total + jnp.exp(-rates * (k * block)) * parts[k]
        return total

    def convolve(parts, value, weights, signal, rates, amounts):
        start = combine(parts, rates)
        result = forward_of(spot, signal, rates, amounts, start)
        query = short_of(value, weights, 0)
        gated = (query * result.astype(wide)).astype(low)
        slots = gated.reshape(2, ycount, spread, -1, channels)
        return (
            start,
            result,
            gated.reshape(-1, channels),
            [[slots[:, k, i].reshape(-1, channels) for i in range(spread)] for k in range(ycount)],
        )

    start, convolved, gated_all, gated = run(
        convolve, states, mixed, taps, product, decay, residue
    )
    gated_got = swap_slots(gated)
    up_got = column_moves(up_pieces)
    grad_feed_all = feed_move.end(line)
    w_up = gather_tile(run(column_block, up_got))
    grad_active = run(dot_t, grad_feed_all, w_down)

    def mix(got, weights, values, gain):
        own = jnp.concatenate(
            [g[:, h * half : (h + 1) * half] for h in range(2) for row in got for g in row], axis=1
        )
        mixer = in_order(jnp.stack([dot(own, w) for w in weights]), "c")
        mixer = jnp.concatenate([m for m in mixer], axis=1).reshape(batch, local, width)
        middle = values.astype(wide) + mixer
        scale = rms_scale(middle)
        normed = (middle * scale * gain).astype(low)
        return middle, scale, normed[: batch // 2], normed[batch // 2 :]

    middle, scale_two, first, second = run(mix, gated_got, w_out, tokens, feed_gain)

    two_move = Gather(first, second)
    two_move.turn(line)
    normed_two_all = two_move.end(line)

    def open_gate(v, w, back):
        value = dot(v, w)
        return value, (back * value * jax.nn.sigmoid(value)).astype(low)

    gate, grad_upper = run(open_gate, normed_two_all, w_gate, grad_active)
    up_term = run(dot_w, normed_two_all, grad_upper)
    up_mine = scatter_tile(up_term)

    def activate(v, w, value, back):
        upper = dot(v, w)
        sigma = jax.nn.sigmoid(value)
        return (
            (value * sigma * upper).astype(low),
            (back * upper * sigma * (1.0 + value * (1.0 - sigma))).astype(low),
        )

    active, grad_gate = run(activate, normed_two_all, w_up, gate, grad_active)
    two_back = Scatter(
        run(
            lambda a, b, wa, wb: split_sum((dot_t(a, wa) + dot_t(b, wb)).astype(low)),
            grad_gate,
            grad_upper,
            w_gate,
            w_up,
        )
    )
    gate_mine = scatter_tile(run(dot_w, normed_two_all, grad_gate))
    two_back.turn(line)
    feed_parts = run(lambda a, w: split_sum(dot(a, w, low)), active, w_down)

    def middle_back(rest, values, scale, gain, back, weights):
        grad_normed = Scatter.sum(*rest).reshape(batch, local, width)
        result, grad_gain = norm_back(values, scale, gain, grad_normed)
        result = result + back.astype(wide) * mask
        parts = core_halves(result.astype(low).reshape(-1, width))
        own = sum(dot_t(m, w) for m, w in zip(parts, weights)).astype(low)
        ranks = ycount * spread

        def slot(at):
            pieces = [
                own[:, (h * ranks + at) * half : (h * ranks + at + 1) * half] for h in range(2)
            ]
            return jnp.concatenate(pieces, axis=1)

        slots = [[slot(k * spread + i) for i in range(spread)] for k in range(ycount)]
        rounded = result.astype(low)
        return result, grad_gain, rounded[: batch // 2], rounded[batch // 2 :], slots

    grad_middle, grad_feed_gain, first, second, grad_slots = run(
        middle_back, two_back.rest(), middle, scale_two, feed_gain, cotangent, w_out
    )
    grad_got = swap_slots(grad_slots)
    down_mine = scatter_tile(run(dot_w, active, grad_feed_all))
    mix_move = Gather(first, second)

    def conv_grads(got, result, value, weights, rates):
        grad = jnp.stack([jnp.stack(row) for row in got])
        grad = grad.reshape(ycount, spread, 2, batch // 2, local, channels)
        grad = jnp.moveaxis(grad, 2, 0).reshape(grid + (channels,)).astype(wide)
        grad_query = grad * result.astype(wide)
        grad_conv = (grad * short_of(value, weights, 0)).astype(low)
        return grad_query, grad_conv, later_of(spot, grad_conv, rates)

    grad_query, grad_conv, later_end = run(conv_grads, grad_got, convolved, mixed, taps, decay)
    laters = [passed(later_end, "z", -k) for k in range(1, depth)]
    mix_move.turn(line)

    def short_back(grad, weights):
        head = jnp.roll(grad[:, :, :, :2], -1, axis=1)
        whole = jnp.concatenate([grad, jnp.where(closing, 0.0, head)], axis=3)
        result = (
            weights[0] * whole[:, :, :, :-2]
            + weights[1] * whole[:, :, :, 1:-1]
            + weights[2] * whole[:, :, :, 2:]
        )
        one, two = grad[:, :, :, :1], grad[:, :, :, 1:2]
        earlier = jnp.concatenate([weights[2] * one, weights[1] * one + weights[2] * two], axis=3)
        rest = jnp.zeros(grad.shape[:3] + (extra - 2, grad.shape[-1]), wide)
        result = jnp.concatenate([result, jnp.where(opening, earlier, 0.0), rest], axis=3)
        return result.astype(low).reshape(-1, grad.shape[-1])

    feed_back = Scatter(feed_parts)
    up_parts_got = owner_moves(run(owner_parts, up_mine))

    def conv_back(signal, grad, rates, amounts, begin, ends_later, value, weights):
        later = combine(ends_later, rates)
        grad_product, grad_residue, grad_decay = backward_of(
            spot, signal, grad, rates, amounts, begin, later
        )
        grad_product = grad_product.astype(wide)
        keys, values = (short_of(value, weights, g) for g in (1, 2))
        pair = jnp.concatenate([grad_product * values, grad_product * keys], axis=-1)
        return pair, grad_residue, grad_decay

    grad_pair, grad_residue, grad_decay = run(
        conv_back, product, grad_conv, decay, residue, start, laters, mixed, taps
    )

    grad_mix_all = mix_move.end(line)
    feed_back.turn(line)

    def in_back(query, pair, weights, v):
        result = jnp.concatenate(
            [
                short_back(query, weights[:, :channels]),
                short_back(pair, weights[:, channels:]),
            ],
            axis=1,
        )
        return result, dot_w(v, result)

    grad_mixed, in_term = run(in_back, grad_query, grad_pair, taps, normed_all)
    in_mine = scatter_tile(in_term)
    one_back = Scatter(run(lambda a, w: split_sum(dot_t(a, w, low)), grad_mixed, w_in))
    out_mine = scatter_tile(run(dot_w, gated_all, grad_mix_all))
    up_held = run(owner_held, up_parts_got)
    up_got = moved(up_held, "y", -1)

    output = run(
        lambda rest, values: (
            mask * (values + Scatter.sum(*rest).reshape(batch, local, width))
        ).astype(low),
        feed_back.rest(),
        middle,
    )
    up_held = run(stacked, up_held, up_got)
    up_got = moved(up_held, "c", -1)
    one_back.turn(line)
    gate_got = owner_moves(run(owner_parts, gate_mine))

    def tap_sums(query, pair, value):
        sums = []
        for g, part in enumerate((query, pair[..., :channels], pair[..., channels:])):
            own = extend(value, g)
            sums += [
                jnp.sum(part * own[:, :, :, 2 - j : local + 2 - j], axis=(0, 1, 2, 3))
                for j in range(3)
            ]
        return jnp.stack(sums)

    grad_taps = run(tap_sums, grad_query, grad_pair, mixed)

    def normed_sum(rest):
        value = Scatter.sum(*rest).reshape(batch, local + extra, width)
        return value[:, :local], value[:, local : local + 2].astype(low)

    grad_normed, grad_before = run(normed_sum, one_back.rest())
    grad_after = lax.ppermute(grad_before, ("z", "x"), [(j, i) for i, j in last])

    def column_whole(own, got):
        return owner_whole(lax.axis_index("c"), [own] + got, depth)

    gate_held = run(owner_held, gate_got)
    gate_got = moved(gate_held, "y", -1)
    grad_up_weight = run(column_whole, up_held, up_got)
    down_held = run(lambda v: v[None], down_mine)
    down_got = moved(down_held, "y", -1)

    def tokens_back(grad, extension, values, scale, gain, back, small):
        values = values.astype(wide)
        grad = jnp.concatenate(
            [grad[:, : local - 2], grad[:, local - 2 :] + extension.astype(wide)], axis=1
        )
        result, grad_gain = norm_back(values, scale, gain, grad)
        gains = jnp.stack([grad_gain, small[0]]).reshape(-1, channels)
        return (result + back).astype(low), jnp.concatenate(list(small[1:]) + [gains], axis=0)

    grad_tokens, small = run(
        tokens_back,
        grad_normed,
        grad_after,
        tokens,
        scale_one,
        norm_gain,
        grad_middle,
        (grad_feed_gain, grad_residue, grad_decay, grad_taps),
    )
    small_got = moved(small, "c", 1)
    gate_held = run(stacked, gate_held, gate_got)
    gate_got = moved(gate_held, "c", -1)
    small = run(lambda v, got: v + sum(got), small, small_got)
    small_got = moved(small, "z", 1)
    down_held = run(lambda own, got: jnp.concatenate([own] + got), down_held, down_got)
    down_got = moved(down_held, "c", -1)
    grad_gate_weight = run(column_whole, gate_held, gate_got)
    small = run(lambda v, got: v + sum(got), small, small_got)
    small_got = moved(small, "x", -1)
    in_got = owner_moves(run(owner_parts, in_mine))

    def rows_whole(own, got):
        whole = in_order(jnp.swapaxes(in_order(jnp.stack([own] + got), "c"), 0, 1), "y")
        return whole.reshape(-1, width).astype(wide)

    grad_down = run(rows_whole, down_held, down_got)
    small = run(stacked, small, small_got)
    small_got = moved(small, "y", -1)
    in_held = run(owner_held, in_got)
    in_got = moved(in_held, "y", -1)
    poles = decay.shape[0]

    def small_whole(own, got):
        slots = jnp.stack([own] + got)
        rows = 2 * poles + 9
        gains = jnp.sum(slots[:, :, rows:], axis=(0, 1)).reshape(2, width)
        whole = all_channels(slots[:, :, :rows])
        grad_conv_taps = jnp.concatenate(
            [whole[2 * poles + 3 * g : 2 * poles + 3 * g + 3] for g in range(3)], axis=1
        )
        return gains[0], gains[1], grad_conv_taps, whole[:poles].T, whole[poles : 2 * poles].T

    grad_norm_gain, feed_gain_sum, grad_conv_taps, residue_sum, decay_sum = run(
        small_whole, small, small_got
    )
    in_held = run(stacked, in_held, in_got)
    in_got = moved(in_held, "c", -1)
    out_held = run(lambda v: v[None], out_mine)
    out_got = moved(out_held, "y", -1)
    out_held = run(lambda own, got: jnp.concatenate([own] + got), out_held, out_got)
    out_got = moved(out_held, "c", -1)
    grad_in_weight = run(
        lambda own, got: owner_whole(lax.axis_index("c"), [own] + got, count), in_held, in_got
    )

    def out_whole(core, own, got):
        ccount = lax.axis_size("c")
        slots = jnp.stack([own] + got)
        slots = jnp.stack(
            [lax.dynamic_index_in_dim(slots, (j - core) % ccount, 0, False) for j in range(ccount)]
        )
        whole = in_order(jnp.swapaxes(slots, 0, 1), "y")
        return whole.reshape(-1, width).astype(wide)

    grad_out_weight = line.finish(out_whole, out_held, out_got)
    return (
        output,
        grad_tokens,
        grad_norm_gain,
        grad_in_weight,
        grad_conv_taps,
        residue_sum,
        decay_sum,
        grad_out_weight,
        feed_gain_sum,
        grad_gate_weight,
        grad_up_weight,
        grad_down,
    )


def solution(mesh):
    pairs, blocks = mesh.shape["dp"], mesh.shape["seq"]
    devices = mesh.devices.reshape(pairs // cores, cores, depth, blocks // depth)
    inner = Mesh(devices, ("y", "c", "z", "x"))
    dp, seq = ("y", "c"), ("z", "x")
    tokens, rows = P(dp, seq, None), P(seq, None)
    return jax.shard_map(
        body,
        mesh=inner,
        in_specs=(
            tokens,
            P(dp),
            P(),
            rows,
            P(),
            P(),
            P(),
            rows,
            P(),
            rows,
            rows,
            rows,
            tokens,
        ),
        out_specs=(tokens, tokens, P(), rows, P(), P(), P(), rows, P(), rows, rows, rows),
        check_vma=False,
    )
```

```python
import functools

import jax
import jax.numpy as jnp
from jax import lax
from jax.experimental import pallas as pl
from jax.experimental.pallas import tpu as pltpu
from jax.sharding import Mesh, PartitionSpec as P

epsilon = 1e-06
low = jnp.bfloat16
wide = jnp.float32
tile = 8
depth = 4
cores = 2


def turned(value, axis, by):
    length = lax.axis_size(axis)
    return lax.ppermute(value, axis, [(i, (i + by) % length) for i in range(length)])


def passed(value, axis, by):
    length = lax.axis_size(axis)
    pairs = [(i, i + by) for i in range(length) if 0 <= i + by < length]
    return lax.ppermute(value, axis, pairs)


def swap_slots(slots):
    ycount, spread = lax.axis_size("y"), lax.axis_size("x")
    result = []
    for dy in range(ycount):
        line = []
        for dx in range(spread):
            sy, sx = (ycount - dy) % ycount, (spread - dx) % spread
            if sy == 0 and sx == 0:
                line.append(slots[0][0])
                continue
            pairs = [
                (i * spread + j, (i + sy) % ycount * spread + (j + sx) % spread)
                for i in range(ycount)
                for j in range(spread)
            ]
            line.append(lax.ppermute(slots[sy][sx], ("y", "x"), pairs))
        result.append(line)
    return result


class Line:
    def __init__(self, token):
        self.token = token

    def run(self, work, *values):
        values, token = lax.optimization_barrier((values, self.token))
        result, self.token = lax.optimization_barrier((work(*values), token))
        return result

    def finish(self, work, *values):
        values, token = lax.optimization_barrier((values, self.token))
        return work(token, *values)


def moved(value, axis, sign):
    return [turned(value, axis, sign * d) for d in range(1, lax.axis_size(axis))]


class Gather:
    def __init__(self, first, second):
        self.held = (first, second)
        self.got = (moved(first, "x", -1), moved(second, "y", -1))

    def turn(self, line):
        self.held = line.run(
            lambda held, got: tuple(jnp.stack([h] + g) for h, g in zip(held, got)), self.held, self.got
        )
        self.got = (moved(self.held[0], "y", -1), moved(self.held[1], "x", -1))

    def end(self, line):
        def work(held, got):
            first = jnp.stack([held[0]] + got[0])
            second = jnp.swapaxes(jnp.stack([held[1]] + got[1]), 0, 1)
            return jnp.stack([first, second]).reshape(-1, first.shape[-1])

        return line.run(work, self.held, self.got)


def split_sum(partial):
    grid = partial.reshape(2, lax.axis_size("y"), lax.axis_size("x"), -1, partial.shape[-1])
    first = [grid[0][:, d].astype(low) for d in range(grid.shape[2])]
    second = [grid[1][d].astype(low) for d in range(grid.shape[1])]
    return first, second


def add_up(parts, got):
    total = parts[0].astype(wide)
    for g in got:
        total = total + g.astype(wide)
    return total


class Scatter:
    def __init__(self, parts):
        self.parts = parts
        self.send("x", "y")

    def send(self, *axes):
        self.got = [
            [turned(p, axis, d + 1) for d, p in enumerate(part[1:])]
            for part, axis in zip(self.parts, axes)
        ]

    def turn(self, line):
        def work(parts, got):
            result = []
            for part, g in zip(parts, got):
                total = add_up(part, g).astype(low)
                result.append([total[d] for d in range(total.shape[0])])
            return result

        self.parts = line.run(work, self.parts, self.got)
        self.send("y", "x")

    def rest(self):
        return self.parts, self.got

    @staticmethod
    def sum(parts, got):
        return jnp.stack([add_up(part, g) for part, g in zip(parts, got)])


def pick_kernel(count, part, stride, start_ref, source, *refs):
    targets, sems = refs[:-1], refs[-1]
    copies = []
    for d, target in enumerate(targets):
        for k in range(count):
            at = pl.multiple_of((k * stride + start_ref[d]) * part, part)
            copies.append(
                pltpu.make_async_copy(
                    source.at[:, pl.ds(at, part)],
                    target.at[:, k * part : (k + 1) * part],
                    sems.at[d * count + k],
                )
            )
    for copy in copies:
        copy.start()
    for copy in copies:
        copy.wait()


def column_pieces(weight, groups):
    spread, ycount = lax.axis_size("x"), lax.axis_size("y")
    rows = weight.shape[0]
    count = groups * depth
    part = weight.shape[1] // (count * spread * ycount)
    starts = [
        (lax.axis_index("x") + d) % spread * ycount + lax.axis_index("y") for d in range(spread)
    ]
    if part % 128 == 0:
        return pl.pallas_call(
            functools.partial(pick_kernel, count, part, spread * ycount),
            out_shape=[jax.ShapeDtypeStruct((rows, count * part), weight.dtype)] * spread,
            grid_spec=pltpu.PrefetchScalarGridSpec(
                num_scalar_prefetch=1,
                in_specs=[pl.BlockSpec(memory_space=pl.ANY)],
                out_specs=[pl.BlockSpec(memory_space=pltpu.VMEM)] * spread,
                scratch_shapes=[pltpu.SemaphoreType.DMA((count * spread,))],
            ),
            cost_estimate=pl.CostEstimate(
                flops=0, transcendentals=0, bytes_accessed=4 * rows * count * part * spread
            ),
        )(jnp.stack(starts).astype(jnp.int32), weight)
    return [
        jnp.concatenate(
            [
                lax.dynamic_slice_in_dim(weight, (k * spread * ycount + start) * part, part, 1)
                for k in range(count)
            ],
            axis=1,
        )
        for start in starts
    ]


def column_moves(pieces):
    spread, ccount = lax.axis_size("x"), lax.axis_size("c")
    share = spread // ccount
    got = [pieces[0]]
    for d in range(1, spread):
        pairs = [
            (i // share * spread + i, i // share * spread + (i + d) % spread) for i in range(spread)
        ]
        got.append(lax.ppermute(pieces[d], ("c", "x"), pairs))
    return got


def column_block(got):
    spread, ccount = lax.axis_size("x"), lax.axis_size("c")
    share = spread // ccount
    place, core = lax.axis_index("x"), lax.axis_index("c")
    got = jnp.stack(got)
    return jnp.concatenate(
        [
            lax.dynamic_index_in_dim(got, (place - core * share - j) % spread, 0, False)
            for j in range(share)
        ]
    )


def row_block(weight):
    ycount, ccount = lax.axis_size("y"), lax.axis_size("c")
    part = weight.shape[0] // (ycount * ccount)
    pair = lax.axis_index("y") * ccount + lax.axis_index("c")
    return lax.dynamic_slice_in_dim(weight, pair * part, part, 0)


def core_halves(value):
    ccount = lax.axis_size("c")
    width = value.shape[1] // ccount
    core = lax.axis_index("c")
    return [
        lax.dynamic_slice_in_dim(value, (core + d) % ccount * width, width, 1)
        for d in range(ccount)
    ]


def out_block(weight):
    part = weight.shape[0] // lax.axis_size("y")
    rows = lax.dynamic_slice_in_dim(weight, lax.axis_index("y") * part, part, 0)
    return core_halves(rows)[0]


def by_z(slots):
    held = in_order(jnp.stack(slots), "z")
    return held.reshape(2, -1, held.shape[-1])


def gather_tile(block):
    return lax.all_gather(block, ("z", "c"), axis=0, tiled=True)


def scatter_tile(term):
    return lax.psum_scatter(term, ("z", "c"), scatter_dimension=0, tiled=True)


def owner_parts(mine):
    spread, ccount = lax.axis_size("x"), lax.axis_size("c")
    share = spread // ccount
    place, core = lax.axis_index("x"), lax.axis_index("c")
    parts = mine.reshape(share, -1, mine.shape[-1])
    return [
        lax.dynamic_index_in_dim(
            parts, jnp.clip((place + d) % spread - core * share, 0, share - 1), 0, False
        )
        for d in range(spread)
    ]


def owner_moves(parts):
    spread, ccount = lax.axis_size("x"), lax.axis_size("c")
    share = spread // ccount
    got = [parts[0]]
    for d in range(1, spread):
        pairs = [
            ((i + d) % spread // share * spread + i, i // share * spread + (i + d) % spread)
            for i in range(spread)
        ]
        got.append(lax.ppermute(parts[d], ("c", "x"), pairs))
    return got


def owner_held(got):
    spread, ccount = lax.axis_size("x"), lax.axis_size("c")
    share = spread // ccount
    place, core = lax.axis_index("x"), lax.axis_index("c")
    got = jnp.stack(got)
    return jnp.stack(
        [
            lax.dynamic_index_in_dim(got, (place - core * share - j) % spread, 0, False)
            for j in range(share)
        ]
    )


def assemble_kernel(count, width, order_ref, *refs):
    sources, target = refs[:-1], refs[-1]
    part = width // count
    ranks = order_ref.shape[0] // 2
    for r in range(ranks):
        core, slot = order_ref[2 * r], order_ref[2 * r + 1]
        value = sources[0][slot]
        for c in range(1, len(sources)):
            value = jnp.where(core == c, sources[c][slot], value)
        value = value.astype(wide)
        for at in range(count):
            start = (at * ranks + r) * part
            target[:, start : start + part] = value[:, at * part : (at + 1) * part]


def owner_whole(core, sources, count):
    spread, ccount, ycount = lax.axis_size("x"), lax.axis_size("c"), lax.axis_size("y")
    share = spread // ccount
    yplace = lax.axis_index("y")
    order = []
    for i in range(spread):
        for k in range(ycount):
            order += [(i // share - core) % ccount, (k - yplace) % ycount * share + i % share]
    sources = [v.reshape((-1,) + v.shape[2:]) for v in sources]
    held, rows, width = sources[0].shape
    block = min(rows, 64)
    return pl.pallas_call(
        functools.partial(assemble_kernel, count, width),
        out_shape=jax.ShapeDtypeStruct((rows, width * spread * ycount), wide),
        grid_spec=pltpu.PrefetchScalarGridSpec(
            num_scalar_prefetch=1,
            grid=(rows // block,),
            in_specs=[pl.BlockSpec((held, block, width), lambda i, order: (0, i, 0))]
            * len(sources),
            out_specs=pl.BlockSpec((block, width * spread * ycount), lambda i, order: (i, 0)),
        ),
        compiler_params=pltpu.CompilerParams(vmem_limit_bytes=56 << 20),
        cost_estimate=pl.CostEstimate(
            flops=0, transcendentals=0, bytes_accessed=6 * rows * width * spread * ycount
        ),
    )(jnp.stack(order).astype(jnp.int32), *sources)


def in_order(slots, axis):
    length = lax.axis_size(axis)
    place = lax.axis_index(axis)
    return jnp.stack(
        [lax.dynamic_index_in_dim(slots, (j - place) % length, 0, False) for j in range(length)]
    )


def rank_rows(values, axis):
    spread, ycount = lax.axis_size("x"), lax.axis_size("y")
    part = values.shape[axis] // (depth * spread * ycount)
    place = lax.axis_index("x") * ycount + lax.axis_index("y")
    return jnp.concatenate(
        [
            lax.dynamic_slice_in_dim(values, (k * spread * ycount + place) * part, part, axis)
            for k in range(depth)
        ],
        axis=axis,
    )


def all_channels(slots):
    whole = in_order(slots, "y")
    whole = in_order(jnp.swapaxes(whole, 0, 1), "x")
    spread, ycount, rows = whole.shape[:3]
    whole = whole.reshape(spread, ycount, rows, depth, -1)
    return jnp.transpose(whole, (2, 3, 0, 1, 4)).reshape(rows, -1)


def fill(source, target, place):
    groups, parts, inner, length = source.shape[:4]
    for j in range(parts):
        slot = lax.rem(j + parts - place, parts)
        for g in range(groups):
            for b in range(inner):
                target[g * inner + b, j * length : (j + 1) * length, :] = source[g, slot, b].astype(
                    wide
                )


def empty(source, target, place):
    groups, parts, inner, length = target.shape[:4]
    for j in range(parts):
        slot = lax.rem(j + parts - place, parts)
        for g in range(groups):
            for b in range(inner):
                target[g, slot, b] = source[g * inner + b, j * length : (j + 1) * length, :].astype(
                    low
                )


def halves(ref):
    return [ref[k * tile : (k + 1) * tile, :] for k in range(ref.shape[0] // tile)]


def row_of(ref, seq, at):
    return ref[seq, pl.ds(at, tile, stride=0), :]


def states_kernel(place_ref, signal_ref, decay_ref, state_ref, held):
    fill(signal_ref, held, place_ref[0])
    seqs, length, lanes = held.shape
    keep = [jnp.exp(-d) for d in halves(decay_ref)]
    count = len(keep)

    def step(i, carry):
        state = list(carry)
        for k in range(tile):
            for n in range(seqs):
                new = row_of(held, n, i * tile + k)
                for h in range(count):
                    at = n * count + h
                    state[at] = keep[h] * state[at] + new
        return tuple(state)

    zero = jnp.zeros((tile, lanes), wide)
    state = lax.fori_loop(0, length // tile, step, tuple(zero for _ in range(seqs * count)))
    for n in range(seqs):
        for h in range(count):
            state_ref[n, h * tile : (h + 1) * tile, :] = state[n * count + h]


def forward_kernel(place_ref, signal_ref, decay_ref, residue_ref, start_ref, out_ref, held, terms, made):
    fill(signal_ref, held, place_ref[0])
    seqs, length, lanes = held.shape
    keep = [jnp.exp(-d) for d in halves(decay_ref)]
    weigh = halves(residue_ref)
    count = len(keep)

    def step(i, carry):
        state = list(carry)
        for k in range(tile):
            for n in range(seqs):
                new = row_of(held, n, i * tile + k)
                total = None
                for h in range(count):
                    at = n * count + h
                    state[at] = keep[h] * state[at] + new
                    term = weigh[h] * state[at]
                    total = term if total is None else total + term
                terms[n, k * tile : (k + 1) * tile, :] = total
        for n in range(seqs):
            result = terms[n, pl.ds(0, tile, stride=tile), :]
            for p in range(1, tile):
                result = result + terms[n, pl.ds(p, tile, stride=tile), :]
            made[n, pl.ds(i * tile, tile), :] = result
        return tuple(state)

    start = tuple(
        start_ref[n, h * tile : (h + 1) * tile, :] for n in range(seqs) for h in range(count)
    )
    lax.fori_loop(0, length // tile, step, start)
    empty(made, out_ref, place_ref[0])


def later_kernel(place_ref, signal_ref, decay_ref, state_ref, held):
    fill(signal_ref, held, place_ref[0])
    seqs, length, lanes = held.shape
    keep = [jnp.exp(-d) for d in halves(decay_ref)]
    count = len(keep)

    def step(i, carry):
        state = list(carry)
        base = length - tile - i * tile
        for k in range(tile - 1, -1, -1):
            for n in range(seqs):
                new = row_of(held, n, base + k)
                for h in range(count):
                    at = n * count + h
                    state[at] = keep[h] * state[at] + new
        return tuple(state)

    zero = jnp.zeros((tile, lanes), wide)
    state = lax.fori_loop(0, length // tile, step, tuple(zero for _ in range(seqs * count)))
    for n in range(seqs):
        for h in range(count):
            state_ref[n, h * tile : (h + 1) * tile, :] = state[n * count + h]


def backward_kernel(
    place_ref,
    signal_ref,
    grad_ref,
    decay_ref,
    residue_ref,
    start_ref,
    end_ref,
    out_ref,
    residue_grad_ref,
    decay_grad_ref,
    held,
    grads,
    terms,
    made,
    later,
):
    fill(signal_ref, held, place_ref[0])
    fill(grad_ref, grads, place_ref[0])
    seqs, length, lanes = held.shape
    keep = [jnp.exp(-d) for d in halves(decay_ref)]
    weigh = halves(residue_ref)
    count = len(keep)
    group = later.shape[0]
    zero = jnp.zeros((tile, lanes), wide)
    none = tuple(zero for _ in range(group * count))
    sum_first = [zero] * count
    sum_second = [zero] * count
    for base_seq in range(0, seqs, group):

        def load(ref):
            return tuple(
                ref[base_seq + n, h * tile : (h + 1) * tile, :]
                for n in range(group)
                for h in range(count)
            )

        def back_step(i, carry):
            state, first = [list(v) for v in carry]
            base = length - tile - i * tile
            for k in range(tile - 1, -1, -1):
                for n in range(group):
                    back = row_of(grads, base_seq + n, base + k)
                    new = row_of(held, base_seq + n, base + k)
                    total = None
                    for h in range(count):
                        at = n * count + h
                        state[at] = keep[h] * state[at] + back
                        first[at] = first[at] + new * state[at]
                        later[n, pl.ds(((base + k) * count + h) * tile, tile), :] = state[at]
                        term = weigh[h] * state[at]
                        total = term if total is None else total + term
                    terms[n, k * tile : (k + 1) * tile, :] = total
            for n in range(group):
                result = terms[n, pl.ds(0, tile, stride=tile), :]
                for p in range(1, tile):
                    result = result + terms[n, pl.ds(p, tile, stride=tile), :]
                made[base_seq + n, pl.ds(base, tile), :] = result
            return tuple(state), tuple(first)

        _, first = lax.fori_loop(0, length // tile, back_step, (load(end_ref), none))

        def ahead(i, carry):
            state, second = [list(v) for v in carry]
            for k in range(tile):
                for n in range(group):
                    new = row_of(held, base_seq + n, i * tile + k)
                    for h in range(count):
                        at = n * count + h
                        state[at] = keep[h] * state[at] + new
                        other = later[n, pl.ds(((i * tile + k) * count + h) * tile, tile), :]
                        second[at] = second[at] + state[at] * other
            return tuple(state), tuple(second)

        _, second = lax.fori_loop(0, length // tile, ahead, (load(start_ref), none))
        for n in range(group):
            for h in range(count):
                at = n * count + h
                sum_first[h] = sum_first[h] + first[at]
                sum_second[h] = sum_second[h] + (second[at] - first[at])
    for h in range(count):
        residue_grad_ref[h * tile : (h + 1) * tile, :] = sum_first[h]
        decay_grad_ref[h * tile : (h + 1) * tile, :] = -weigh[h] * sum_second[h]
    empty(made, out_ref, place_ref[0])


def conv_call(kernel, place, arrays, results, scratch, flops):
    channels = arrays[0].shape[-1]
    lanes = min(channels, 128)

    def spec(shape):
        lead = len(shape) - 1
        return pl.BlockSpec(shape[:-1] + (lanes,), lambda i, *_: (0,) * lead + (i,))

    return pl.pallas_call(
        kernel,
        out_shape=results,
        grid_spec=pltpu.PrefetchScalarGridSpec(
            num_scalar_prefetch=1,
            grid=(channels // lanes,),
            in_specs=[spec(a.shape) for a in arrays],
            out_specs=[spec(r.shape) for r in results],
            scratch_shapes=[pltpu.VMEM(s + (lanes,), wide) for s in scratch],
        ),
        compiler_params=pltpu.CompilerParams(
            dimension_semantics=("arbitrary",), vmem_limit_bytes=56 << 20
        ),
        cost_estimate=pl.CostEstimate(
            flops=flops, transcendentals=0, bytes_accessed=sum(a.size * 4 for a in arrays)
        ),
    )(place, *arrays)


def sizes(signal, poles):
    groups, parts, inner, length, channels = signal.shape
    return groups * inner, parts * length, channels, signal.size * poles


def states_of(place, signal, decay):
    seqs, length, channels, work = sizes(signal, decay.shape[0])
    shape = jax.ShapeDtypeStruct((seqs, decay.shape[0], channels), wide)
    return conv_call(states_kernel, place, [signal, decay], [shape], [(seqs, length)], 2 * work)[0]


def forward_of(place, signal, decay, residue, start):
    seqs, length, channels, work = sizes(signal, decay.shape[0])
    return conv_call(
        forward_kernel,
        place,
        [signal, decay, residue, start],
        [jax.ShapeDtypeStruct(signal.shape, low)],
        [(seqs, length), (seqs, tile * tile), (seqs, length)],
        4 * work,
    )[0]


def later_of(place, signal, decay):
    seqs, length, channels, work = sizes(signal, decay.shape[0])
    shape = jax.ShapeDtypeStruct((seqs, decay.shape[0], channels), wide)
    return conv_call(later_kernel, place, [signal, decay], [shape], [(seqs, length)], 2 * work)[0]


def backward_of(place, signal, grad, decay, residue, start, end):
    poles = decay.shape[0]
    seqs, length, channels, work = sizes(signal, poles)
    shape = jax.ShapeDtypeStruct(decay.shape, wide)
    group = min(seqs, 4)
    return conv_call(
        backward_kernel,
        place,
        [signal, grad, decay, residue, start, end],
        [jax.ShapeDtypeStruct(signal.shape, low), shape, shape],
        [
            (seqs, length),
            (seqs, length),
            (group, tile * tile),
            (seqs, length),
            (group, length * poles),
        ],
        12 * work,
    )


def rms_scale(values):
    return lax.rsqrt(jnp.mean(values * values, axis=-1, keepdims=True) + epsilon)


def norm_back(values, scale, gain, grad_normed):
    grad_gain = jnp.sum(grad_normed * values * scale, axis=(0, 1))
    scaled = grad_normed * gain
    grad_values = scale * scaled - values * scale * scale * scale * jnp.mean(
        scaled * values, axis=-1, keepdims=True
    )
    return (grad_values, grad_gain)


def dot(a, b, kind=wide):
    return jnp.dot(a, b, preferred_element_type=wide).astype(kind)


def dot_t(a, b, kind=wide):
    return lax.dot_general(a, b, (((1,), (1,)), ((), ())), preferred_element_type=wide).astype(kind)


def dot_w(a, b):
    return lax.dot_general(a, b, (((0,), (0,)), ((), ())), preferred_element_type=wide).astype(low)


def body(
    tokens,
    lengths,
    norm_gain,
    in_weight,
    conv_taps,
    filter_residue,
    filter_decay,
    out_weight,
    feed_gain,
    gate_weight,
    up_weight,
    down_weight,
    cotangent,
):
    spread, ycount = lax.axis_size("x"), lax.axis_size("y")
    batch, local, width = tokens.shape
    place = lax.axis_index("z") * spread + lax.axis_index("x")
    position = place * local + jnp.arange(local)
    mask = (position[None, :] < lengths[:, None]).astype(wide)[..., None]
    block = spread * local

    count = 3 * depth
    extra = 8
    line = Line(lax.axis_index("c"))
    run = line.run

    def stacked(value, got):
        return jnp.stack([value] + got)

    in_got = column_moves(run(lambda w: column_pieces(w, 3), in_weight))
    block_out = run(out_block, out_weight)
    out_got = moved(block_out, "z", -1)
    last = [(i * spread + spread - 1, (i + 1) * spread) for i in range(depth - 1)]

    def norm_one(values, gain):
        values = values.astype(wide)
        scale = rms_scale(values)
        normed = (values * scale * gain).astype(low)
        return normed, normed[:, local - 2 :], scale

    normed, ending, scale_one = run(norm_one, tokens, norm_gain)
    before = lax.ppermute(ending, ("z", "x"), last)
    w_in = gather_tile(run(column_block, in_got))

    def lengthen(values, rows):
        rest = jnp.zeros((batch, extra - 2, width), values.dtype)
        values = jnp.concatenate([values, rows, rest], axis=1)
        return values[: batch // 2], values[batch // 2 :]

    normed_move = Gather(*run(lengthen, normed, before))
    normed_move.turn(line)
    w_down = gather_tile(run(row_block, down_weight))
    gate_got = column_moves(run(lambda w: column_pieces(w, 1), gate_weight))
    held = run(lambda own, got: by_z([own] + got), block_out, out_got)
    normed_all = normed_move.end(line)
    out_move = Gather(held[:1], held[1:])

    channels = w_in.shape[1] // 3
    half = channels // 2
    grid = (2 * ycount, spread, batch // 2, local)

    def rank_values(all_taps, all_decay, all_residue):
        return (
            jnp.concatenate(
                [rank_rows(all_taps[:, g * width : (g + 1) * width], 1) for g in range(3)], axis=1
            ),
            rank_rows(all_decay, 0).T,
            rank_rows(all_residue, 0).T,
        )

    taps, decay, residue = run(rank_values, conv_taps, filter_decay, filter_residue)
    opening = (lax.axis_index("x") + jnp.arange(spread)) % spread == 0
    opening = opening[None, :, None, None, None]
    closing = (lax.axis_index("x") + jnp.arange(spread)) % spread == spread - 1
    closing = closing[None, :, None, None, None]

    def project(v, w):
        return dot(v, w, low).reshape(grid[:3] + (local + extra, 3 * channels))

    mixed = run(project, normed_all, w_in)

    def extend(value, g):
        own = value[..., g * channels : (g + 1) * channels]
        earlier = jnp.roll(own[:, :, :, local - 2 : local], 1, axis=1)
        earlier = jnp.where(opening, own[:, :, :, local : local + 2], earlier)
        return jnp.concatenate([earlier, own[:, :, :, :local]], axis=3).astype(wide)

    def short_of(value, weights, g):
        longer = extend(value, g)
        own = weights[:, g * channels : (g + 1) * channels]
        return own[0] * longer[:, :, :, 2:] + own[1] * longer[:, :, :, 1:-1] + own[2] * longer[:, :, :, :-2]

    spot = lax.axis_index("x").astype(jnp.int32).reshape(1)

    def multiply(value, weights, rates):
        keys, values = (short_of(value, weights, g) for g in (1, 2))
        product = (keys * values).astype(low)
        return product, states_of(spot, product, rates)

    product, state_end = run(multiply, mixed, taps, decay)
    states = [passed(state_end, "z", k) for k in range(1, depth)]
    w_gate = gather_tile(run(column_block, gate_got))
    out_move.turn(line)

    def feed_grad(values):
        values = (values.astype(wide) * mask).astype(low)
        return values[: batch // 2], values[batch // 2 :]

    feed_move = Gather(*run(feed_grad, cotangent))
    up_got = column_moves(run(lambda w: column_pieces(w, 1), up_weight))
    out_own = out_move.end(line)
    w_out = [out_own] + moved(out_own, "c", -1)
    feed_move.turn(line)

    def combine(parts, rates):
        total = parts[0]
        for k in range(1, depth - 1):
            total = total + jnp.exp(-rates * (k * block)) * parts[k]
        return total

    def convolve(parts, value, weights, signal, rates, amounts):
        start = combine(parts, rates)
        result = forward_of(spot, signal, rates, amounts, start)
        query = short_of(value, weights, 0)
        gated = (query * result.astype(wide)).astype(low)
        slots = gated.reshape(2, ycount, spread, -1, channels)
        return (
            start,
            result,
            gated.reshape(-1, channels),
            [[slots[:, k, i].reshape(-1, channels) for i in range(spread)] for k in range(ycount)],
        )

    start, convolved, gated_all, gated = run(
        convolve, states, mixed, taps, product, decay, residue
    )
    gated_got = swap_slots(gated)
    w_up = gather_tile(run(column_block, up_got))
    grad_feed_all = feed_move.end(line)

    def mix(got, weights, values, gain):
        own = jnp.concatenate(
            [g[:, h * half : (h + 1) * half] for h in range(2) for row in got for g in row], axis=1
        )
        mixer = in_order(jnp.stack([dot(own, w) for w in weights]), "c")
        mixer = jnp.concatenate([m for m in mixer], axis=1).reshape(batch, local, width)
        middle = values.astype(wide) + mixer
        scale = rms_scale(middle)
        normed = (middle * scale * gain).astype(low)
        return middle, scale, normed[: batch // 2], normed[batch // 2 :]

    middle, scale_two, first, second = run(mix, gated_got, w_out, tokens, feed_gain)

    two_move = Gather(first, second)
    grad_active = run(dot_t, grad_feed_all, w_down)
    two_move.turn(line)
    normed_two_all = two_move.end(line)

    def open_gate(v, w, back):
        value = dot(v, w)
        return value, (back * value * jax.nn.sigmoid(value)).astype(low)

    gate, grad_upper = run(open_gate, normed_two_all, w_gate, grad_active)
    up_term = run(dot_w, normed_two_all, grad_upper)
    up_mine = scatter_tile(up_term)

    def activate(v, w, value, back):
        upper = dot(v, w)
        sigma = jax.nn.sigmoid(value)
        return (
            (value * sigma * upper).astype(low),
            (back * upper * sigma * (1.0 + value * (1.0 - sigma))).astype(low),
        )

    active, grad_gate = run(activate, normed_two_all, w_up, gate, grad_active)
    two_back = Scatter(
        run(
            lambda a, b, wa, wb: split_sum((dot_t(a, wa) + dot_t(b, wb)).astype(low)),
            grad_gate,
            grad_upper,
            w_gate,
            w_up,
        )
    )
    gate_mine = scatter_tile(run(dot_w, normed_two_all, grad_gate))
    two_back.turn(line)
    feed_parts = run(lambda a, w: split_sum(dot(a, w, low)), active, w_down)

    def middle_back(rest, values, scale, gain, back, weights):
        grad_normed = Scatter.sum(*rest).reshape(batch, local, width)
        result, grad_gain = norm_back(values, scale, gain, grad_normed)
        result = result + back.astype(wide) * mask
        parts = core_halves(result.astype(low).reshape(-1, width))
        own = sum(dot_t(m, w) for m, w in zip(parts, weights)).astype(low)
        ranks = ycount * spread

        def slot(at):
            pieces = [
                own[:, (h * ranks + at) * half : (h * ranks + at + 1) * half] for h in range(2)
            ]
            return jnp.concatenate(pieces, axis=1)

        slots = [[slot(k * spread + i) for i in range(spread)] for k in range(ycount)]
        rounded = result.astype(low)
        return result, grad_gain, rounded[: batch // 2], rounded[batch // 2 :], slots

    grad_middle, grad_feed_gain, first, second, grad_slots = run(
        middle_back, two_back.rest(), middle, scale_two, feed_gain, cotangent, w_out
    )
    grad_got = swap_slots(grad_slots)
    down_mine = scatter_tile(run(dot_w, active, grad_feed_all))
    mix_move = Gather(first, second)

    def conv_grads(got, result, value, weights, rates):
        grad = jnp.stack([jnp.stack(row) for row in got])
        grad = grad.reshape(ycount, spread, 2, batch // 2, local, channels)
        grad = jnp.moveaxis(grad, 2, 0).reshape(grid + (channels,)).astype(wide)
        grad_query = grad * result.astype(wide)
        grad_conv = (grad * short_of(value, weights, 0)).astype(low)
        return grad_query, grad_conv, later_of(spot, grad_conv, rates)

    grad_query, grad_conv, later_end = run(conv_grads, grad_got, convolved, mixed, taps, decay)
    laters = [passed(later_end, "z", -k) for k in range(1, depth)]
    mix_move.turn(line)

    def short_back(grad, weights):
        head = jnp.roll(grad[:, :, :, :2], -1, axis=1)
        whole = jnp.concatenate([grad, jnp.where(closing, 0.0, head)], axis=3)
        result = (
            weights[0] * whole[:, :, :, :-2]
            + weights[1] * whole[:, :, :, 1:-1]
            + weights[2] * whole[:, :, :, 2:]
        )
        one, two = grad[:, :, :, :1], grad[:, :, :, 1:2]
        earlier = jnp.concatenate([weights[2] * one, weights[1] * one + weights[2] * two], axis=3)
        rest = jnp.zeros(grad.shape[:3] + (extra - 2, grad.shape[-1]), wide)
        result = jnp.concatenate([result, jnp.where(opening, earlier, 0.0), rest], axis=3)
        return result.astype(low).reshape(-1, grad.shape[-1])

    feed_back = Scatter(feed_parts)
    up_parts_got = owner_moves(run(owner_parts, up_mine))

    def conv_back(signal, grad, rates, amounts, begin, ends_later, value, weights):
        later = combine(ends_later, rates)
        grad_product, grad_residue, grad_decay = backward_of(
            spot, signal, grad, rates, amounts, begin, later
        )
        grad_product = grad_product.astype(wide)
        keys, values = (short_of(value, weights, g) for g in (1, 2))
        pair = jnp.concatenate([grad_product * values, grad_product * keys], axis=-1)
        return pair, grad_residue, grad_decay

    grad_pair, grad_residue, grad_decay = run(
        conv_back, product, grad_conv, decay, residue, start, laters, mixed, taps
    )

    up_held = run(owner_held, up_parts_got)
    up_got = moved(up_held, "y", -1)
    grad_mix_all = mix_move.end(line)
    feed_back.turn(line)

    def in_back(query, pair, weights, v):
        result = jnp.concatenate(
            [
                short_back(query, weights[:, :channels]),
                short_back(pair, weights[:, channels:]),
            ],
            axis=1,
        )
        return result, dot_w(v, result)

    grad_mixed, in_term = run(in_back, grad_query, grad_pair, taps, normed_all)
    in_mine = scatter_tile(in_term)
    gate_got = owner_moves(run(owner_parts, gate_mine))
    one_back = Scatter(run(lambda a, w: split_sum(dot_t(a, w, low)), grad_mixed, w_in))
    up_held = run(stacked, up_held, up_got)
    up_got = moved(up_held, "c", -1)
    out_mine = scatter_tile(run(dot_w, gated_all, grad_mix_all))
    gate_held = run(owner_held, gate_got)
    gate_got = moved(gate_held, "y", -1)

    output = run(
        lambda rest, values: (
            mask * (values + Scatter.sum(*rest).reshape(batch, local, width))
        ).astype(low),
        feed_back.rest(),
        middle,
    )

    def tap_sums(query, pair, value):
        sums = []
        for g, part in enumerate((query, pair[..., :channels], pair[..., channels:])):
            own = extend(value, g)
            sums += [
                jnp.sum(part * own[:, :, :, 2 - j : local + 2 - j], axis=(0, 1, 2, 3))
                for j in range(3)
            ]
        return jnp.stack(sums)

    grad_taps = run(tap_sums, grad_query, grad_pair, mixed)

    def normed_sum(rest):
        value = Scatter.sum(*rest).reshape(batch, local + extra, width)
        return value[:, :local], value[:, local : local + 2].astype(low)

    def column_whole(own, got):
        return owner_whole(lax.axis_index("c"), [own] + got, depth)

    grad_up_weight = run(column_whole, up_held, up_got)
    one_back.turn(line)
    down_held = run(lambda v: v[None], down_mine)
    down_got = moved(down_held, "y", -1)
    gate_held = run(stacked, gate_held, gate_got)
    gate_got = moved(gate_held, "c", -1)
    grad_normed, grad_before = run(normed_sum, one_back.rest())
    grad_after = lax.ppermute(grad_before, ("z", "x"), [(j, i) for i, j in last])
    grad_gate_weight = run(column_whole, gate_held, gate_got)

    def tokens_back(grad, extension, values, scale, gain, back, small):
        values = values.astype(wide)
        grad = jnp.concatenate(
            [grad[:, : local - 2], grad[:, local - 2 :] + extension.astype(wide)], axis=1
        )
        result, grad_gain = norm_back(values, scale, gain, grad)
        gains = jnp.stack([grad_gain, small[0]]).reshape(-1, channels)
        return (result + back).astype(low), jnp.concatenate(list(small[1:]) + [gains], axis=0)

    grad_tokens, small = run(
        tokens_back,
        grad_normed,
        grad_after,
        tokens,
        scale_one,
        norm_gain,
        grad_middle,
        (grad_feed_gain, grad_residue, grad_decay, grad_taps),
    )
    small_got = moved(small, "c", 1)
    down_held = run(lambda own, got: jnp.concatenate([own] + got), down_held, down_got)
    down_got = moved(down_held, "c", -1)
    small = run(lambda v, got: v + sum(got), small, small_got)
    small_got = moved(small, "z", 1)
    in_got = owner_moves(run(owner_parts, in_mine))

    def rows_whole(own, got):
        whole = in_order(jnp.swapaxes(in_order(jnp.stack([own] + got), "c"), 0, 1), "y")
        return whole.reshape(-1, width).astype(wide)

    grad_down = run(rows_whole, down_held, down_got)
    in_held = run(owner_held, in_got)
    in_got = moved(in_held, "y", -1)
    small = run(lambda v, got: v + sum(got), small, small_got)
    small_got = moved(small, "x", -1)
    small = run(stacked, small, small_got)
    small_got = moved(small, "y", -1)
    out_held = run(lambda v: v[None], out_mine)
    out_got = moved(out_held, "y", -1)
    in_held = run(stacked, in_held, in_got)
    in_got = moved(in_held, "c", -1)
    poles = decay.shape[0]

    def small_whole(own, got):
        slots = jnp.stack([own] + got)
        rows = 2 * poles + 9
        gains = jnp.sum(slots[:, :, rows:], axis=(0, 1)).reshape(2, width)
        whole = all_channels(slots[:, :, :rows])
        grad_conv_taps = jnp.concatenate(
            [whole[2 * poles + 3 * g : 2 * poles + 3 * g + 3] for g in range(3)], axis=1
        )
        return gains[0], gains[1], grad_conv_taps, whole[:poles].T, whole[poles : 2 * poles].T

    grad_norm_gain, feed_gain_sum, grad_conv_taps, residue_sum, decay_sum = run(
        small_whole, small, small_got
    )
    out_held = run(lambda own, got: jnp.concatenate([own] + got), out_held, out_got)
    out_got = moved(out_held, "c", -1)
    grad_in_weight = run(
        lambda own, got: owner_whole(lax.axis_index("c"), [own] + got, count), in_held, in_got
    )

    def out_whole(core, own, got):
        ccount = lax.axis_size("c")
        slots = jnp.stack([own] + got)
        slots = jnp.stack(
            [lax.dynamic_index_in_dim(slots, (j - core) % ccount, 0, False) for j in range(ccount)]
        )
        whole = in_order(jnp.swapaxes(slots, 0, 1), "y")
        return whole.reshape(-1, width).astype(wide)

    grad_out_weight = line.finish(out_whole, out_held, out_got)
    return (
        output,
        grad_tokens,
        grad_norm_gain,
        grad_in_weight,
        grad_conv_taps,
        residue_sum,
        decay_sum,
        grad_out_weight,
        feed_gain_sum,
        grad_gate_weight,
        grad_up_weight,
        grad_down,
    )


def solution(mesh):
    pairs, blocks = mesh.shape["dp"], mesh.shape["seq"]
    devices = mesh.devices.reshape(pairs // cores, cores, depth, blocks // depth)
    inner = Mesh(devices, ("y", "c", "z", "x"))
    dp, seq = ("y", "c"), ("z", "x")
    tokens, rows = P(dp, seq, None), P(seq, None)
    return jax.shard_map(
        body,
        mesh=inner,
        in_specs=(
            tokens,
            P(dp),
            P(),
            rows,
            P(),
            P(),
            P(),
            rows,
            P(),
            rows,
            rows,
            rows,
            tokens,
        ),
        out_specs=(tokens, tokens, P(), rows, P(), P(), P(), rows, P(), rows, rows, rows),
        check_vma=False,
    )
```

```python
import functools

import jax
import jax.numpy as jnp
from jax import lax
from jax.experimental import pallas as pl
from jax.experimental.pallas import tpu as pltpu
from jax.sharding import Mesh, PartitionSpec as P

epsilon = 1e-06
low = jnp.bfloat16
wide = jnp.float32
tile = 8
depth = 4
cores = 2


def turned(value, axis, by):
    length = lax.axis_size(axis)
    return lax.ppermute(value, axis, [(i, (i + by) % length) for i in range(length)])


def passed(value, axis, by):
    length = lax.axis_size(axis)
    pairs = [(i, i + by) for i in range(length) if 0 <= i + by < length]
    return lax.ppermute(value, axis, pairs)


def swap_slots(slots):
    ycount, spread = lax.axis_size("y"), lax.axis_size("x")
    result = []
    for dy in range(ycount):
        line = []
        for dx in range(spread):
            sy, sx = (ycount - dy) % ycount, (spread - dx) % spread
            if sy == 0 and sx == 0:
                line.append(slots[0][0])
                continue
            pairs = [
                (i * spread + j, (i + sy) % ycount * spread + (j + sx) % spread)
                for i in range(ycount)
                for j in range(spread)
            ]
            line.append(lax.ppermute(slots[sy][sx], ("y", "x"), pairs))
        result.append(line)
    return result


class Line:
    def __init__(self, token):
        self.token = token

    def run(self, work, *values):
        values, token = lax.optimization_barrier((values, self.token))
        result, self.token = lax.optimization_barrier((work(*values), token))
        return result

    def finish(self, work, *values):
        values, token = lax.optimization_barrier((values, self.token))
        return work(token, *values)


def moved(value, axis, sign):
    return [turned(value, axis, sign * d) for d in range(1, lax.axis_size(axis))]


class Gather:
    def __init__(self, first, second):
        self.held = (first, second)
        self.got = (moved(first, "x", -1), moved(second, "y", -1))

    def turn(self, line):
        self.held = line.run(
            lambda held, got: tuple(jnp.stack([h] + g) for h, g in zip(held, got)), self.held, self.got
        )
        self.got = (moved(self.held[0], "y", -1), moved(self.held[1], "x", -1))

    def end(self, line):
        def work(held, got):
            first = jnp.stack([held[0]] + got[0])
            second = jnp.swapaxes(jnp.stack([held[1]] + got[1]), 0, 1)
            return jnp.stack([first, second]).reshape(-1, first.shape[-1])

        return line.run(work, self.held, self.got)


def split_sum(partial):
    grid = partial.reshape(2, lax.axis_size("y"), lax.axis_size("x"), -1, partial.shape[-1])
    first = [grid[0][:, d].astype(low) for d in range(grid.shape[2])]
    second = [grid[1][d].astype(low) for d in range(grid.shape[1])]
    return first, second


def add_up(parts, got):
    total = parts[0].astype(wide)
    for g in got:
        total = total + g.astype(wide)
    return total


class Scatter:
    def __init__(self, parts):
        self.parts = parts
        self.send("x", "y")

    def send(self, *axes):
        self.got = [
            [turned(p, axis, d + 1) for d, p in enumerate(part[1:])]
            for part, axis in zip(self.parts, axes)
        ]

    def turn(self, line):
        def work(parts, got):
            result = []
            for part, g in zip(parts, got):
                total = add_up(part, g).astype(low)
                result.append([total[d] for d in range(total.shape[0])])
            return result

        self.parts = line.run(work, self.parts, self.got)
        self.send("y", "x")

    def rest(self):
        return self.parts, self.got

    @staticmethod
    def sum(parts, got):
        return jnp.stack([add_up(part, g) for part, g in zip(parts, got)])


def pick_kernel(count, part, stride, start_ref, source, *refs):
    targets, sems = refs[:-1], refs[-1]
    copies = []
    for d, target in enumerate(targets):
        for k in range(count):
            at = pl.multiple_of((k * stride + start_ref[d]) * part, part)
            copies.append(
                pltpu.make_async_copy(
                    source.at[:, pl.ds(at, part)],
                    target.at[:, k * part : (k + 1) * part],
                    sems.at[d * count + k],
                )
            )
    for copy in copies:
        copy.start()
    for copy in copies:
        copy.wait()


def column_pieces(weight, groups):
    spread, ycount = lax.axis_size("x"), lax.axis_size("y")
    rows = weight.shape[0]
    count = groups * depth
    part = weight.shape[1] // (count * spread * ycount)
    starts = [
        (lax.axis_index("x") + d) % spread * ycount + lax.axis_index("y") for d in range(spread)
    ]
    if part % 128 == 0:
        return pl.pallas_call(
            functools.partial(pick_kernel, count, part, spread * ycount),
            out_shape=[jax.ShapeDtypeStruct((rows, count * part), weight.dtype)] * spread,
            grid_spec=pltpu.PrefetchScalarGridSpec(
                num_scalar_prefetch=1,
                in_specs=[pl.BlockSpec(memory_space=pl.ANY)],
                out_specs=[pl.BlockSpec(memory_space=pltpu.VMEM)] * spread,
                scratch_shapes=[pltpu.SemaphoreType.DMA((count * spread,))],
            ),
            cost_estimate=pl.CostEstimate(
                flops=0, transcendentals=0, bytes_accessed=4 * rows * count * part * spread
            ),
        )(jnp.stack(starts).astype(jnp.int32), weight)
    return [
        jnp.concatenate(
            [
                lax.dynamic_slice_in_dim(weight, (k * spread * ycount + start) * part, part, 1)
                for k in range(count)
            ],
            axis=1,
        )
        for start in starts
    ]


def column_moves(pieces):
    spread, ccount = lax.axis_size("x"), lax.axis_size("c")
    share = spread // ccount
    got = [pieces[0]]
    for d in range(1, spread):
        pairs = [
            (i // share * spread + i, i // share * spread + (i + d) % spread) for i in range(spread)
        ]
        got.append(lax.ppermute(pieces[d], ("c", "x"), pairs))
    return got


def column_block(got):
    spread, ccount = lax.axis_size("x"), lax.axis_size("c")
    share = spread // ccount
    place, core = lax.axis_index("x"), lax.axis_index("c")
    got = jnp.stack(got)
    return jnp.concatenate(
        [
            lax.dynamic_index_in_dim(got, (place - core * share - j) % spread, 0, False)
            for j in range(share)
        ]
    )


def row_block(weight):
    ycount, ccount = lax.axis_size("y"), lax.axis_size("c")
    part = weight.shape[0] // (ycount * ccount)
    pair = lax.axis_index("y") * ccount + lax.axis_index("c")
    return lax.dynamic_slice_in_dim(weight, pair * part, part, 0)


def core_halves(value):
    ccount = lax.axis_size("c")
    width = value.shape[1] // ccount
    core = lax.axis_index("c")
    return [
        lax.dynamic_slice_in_dim(value, (core + d) % ccount * width, width, 1)
        for d in range(ccount)
    ]


def out_block(weight):
    part = weight.shape[0] // lax.axis_size("y")
    rows = lax.dynamic_slice_in_dim(weight, lax.axis_index("y") * part, part, 0)
    return core_halves(rows)[0]


def by_z(slots):
    held = in_order(jnp.stack(slots), "z")
    return held.reshape(2, -1, held.shape[-1])


def gather_tile(block):
    return lax.all_gather(block, ("z", "c"), axis=0, tiled=True)


def scatter_tile(term):
    return lax.psum_scatter(term, ("z", "c"), scatter_dimension=0, tiled=True)


def owner_parts(mine):
    spread, ccount = lax.axis_size("x"), lax.axis_size("c")
    share = spread // ccount
    place, core = lax.axis_index("x"), lax.axis_index("c")
    parts = mine.reshape(share, -1, mine.shape[-1])
    return [
        lax.dynamic_index_in_dim(
            parts, jnp.clip((place + d) % spread - core * share, 0, share - 1), 0, False
        )
        for d in range(spread)
    ]


def owner_moves(parts):
    spread, ccount = lax.axis_size("x"), lax.axis_size("c")
    share = spread // ccount
    got = [parts[0]]
    for d in range(1, spread):
        pairs = [
            ((i + d) % spread // share * spread + i, i // share * spread + (i + d) % spread)
            for i in range(spread)
        ]
        got.append(lax.ppermute(parts[d], ("c", "x"), pairs))
    return got


def owner_held(got):
    spread, ccount = lax.axis_size("x"), lax.axis_size("c")
    share = spread // ccount
    place, core = lax.axis_index("x"), lax.axis_index("c")
    got = jnp.stack(got)
    return jnp.stack(
        [
            lax.dynamic_index_in_dim(got, (place - core * share - j) % spread, 0, False)
            for j in range(share)
        ]
    )


def assemble_kernel(count, width, order_ref, *refs):
    sources, target = refs[:-1], refs[-1]
    part = width // count
    ranks = order_ref.shape[0] // 2
    for r in range(ranks):
        core, slot = order_ref[2 * r], order_ref[2 * r + 1]
        value = sources[0][slot]
        for c in range(1, len(sources)):
            value = jnp.where(core == c, sources[c][slot], value)
        value = value.astype(wide)
        for at in range(count):
            start = (at * ranks + r) * part
            target[:, start : start + part] = value[:, at * part : (at + 1) * part]


def owner_whole(core, sources, count):
    spread, ccount, ycount = lax.axis_size("x"), lax.axis_size("c"), lax.axis_size("y")
    share = spread // ccount
    yplace = lax.axis_index("y")
    order = []
    for i in range(spread):
        for k in range(ycount):
            order += [(i // share - core) % ccount, (k - yplace) % ycount * share + i % share]
    sources = [v.reshape((-1,) + v.shape[2:]) for v in sources]
    held, rows, width = sources[0].shape
    block = min(rows, 64)
    return pl.pallas_call(
        functools.partial(assemble_kernel, count, width),
        out_shape=jax.ShapeDtypeStruct((rows, width * spread * ycount), wide),
        grid_spec=pltpu.PrefetchScalarGridSpec(
            num_scalar_prefetch=1,
            grid=(rows // block,),
            in_specs=[pl.BlockSpec((held, block, width), lambda i, order: (0, i, 0))]
            * len(sources),
            out_specs=pl.BlockSpec((block, width * spread * ycount), lambda i, order: (i, 0)),
        ),
        compiler_params=pltpu.CompilerParams(vmem_limit_bytes=56 << 20),
        cost_estimate=pl.CostEstimate(
            flops=0, transcendentals=0, bytes_accessed=6 * rows * width * spread * ycount
        ),
    )(jnp.stack(order).astype(jnp.int32), *sources)


def in_order(slots, axis):
    length = lax.axis_size(axis)
    place = lax.axis_index(axis)
    return jnp.stack(
        [lax.dynamic_index_in_dim(slots, (j - place) % length, 0, False) for j in range(length)]
    )


def rank_rows(values, axis):
    spread, ycount = lax.axis_size("x"), lax.axis_size("y")
    part = values.shape[axis] // (depth * spread * ycount)
    place = lax.axis_index("x") * ycount + lax.axis_index("y")
    return jnp.concatenate(
        [
            lax.dynamic_slice_in_dim(values, (k * spread * ycount + place) * part, part, axis)
            for k in range(depth)
        ],
        axis=axis,
    )


def all_channels(slots):
    whole = in_order(slots, "y")
    whole = in_order(jnp.swapaxes(whole, 0, 1), "x")
    spread, ycount, rows = whole.shape[:3]
    whole = whole.reshape(spread, ycount, rows, depth, -1)
    return jnp.transpose(whole, (2, 3, 0, 1, 4)).reshape(rows, -1)


def fill(source, target, place):
    groups, parts, inner, length = source.shape[:4]
    for j in range(parts):
        slot = lax.rem(j + parts - place, parts)
        for g in range(groups):
            for b in range(inner):
                target[g * inner + b, j * length : (j + 1) * length, :] = source[g, slot, b].astype(
                    wide
                )


def empty(source, target, place):
    groups, parts, inner, length = target.shape[:4]
    for j in range(parts):
        slot = lax.rem(j + parts - place, parts)
        for g in range(groups):
            for b in range(inner):
                target[g, slot, b] = source[g * inner + b, j * length : (j + 1) * length, :].astype(
                    low
                )


def halves(ref):
    return [ref[k * tile : (k + 1) * tile, :] for k in range(ref.shape[0] // tile)]


def row_of(ref, seq, at):
    return ref[seq, pl.ds(at, tile, stride=0), :]


def states_kernel(place_ref, signal_ref, decay_ref, state_ref, held):
    fill(signal_ref, held, place_ref[0])
    seqs, length, lanes = held.shape
    keep = [jnp.exp(-d) for d in halves(decay_ref)]
    count = len(keep)

    def step(i, carry):
        state = list(carry)
        for k in range(tile):
            for n in range(seqs):
                new = row_of(held, n, i * tile + k)
                for h in range(count):
                    at = n * count + h
                    state[at] = keep[h] * state[at] + new
        return tuple(state)

    zero = jnp.zeros((tile, lanes), wide)
    state = lax.fori_loop(0, length // tile, step, tuple(zero for _ in range(seqs * count)))
    for n in range(seqs):
        for h in range(count):
            state_ref[n, h * tile : (h + 1) * tile, :] = state[n * count + h]


def forward_kernel(place_ref, signal_ref, decay_ref, residue_ref, start_ref, out_ref, held, terms, made):
    fill(signal_ref, held, place_ref[0])
    seqs, length, lanes = held.shape
    keep = [jnp.exp(-d) for d in halves(decay_ref)]
    weigh = halves(residue_ref)
    count = len(keep)

    def step(i, carry):
        state = list(carry)
        for k in range(tile):
            for n in range(seqs):
                new = row_of(held, n, i * tile + k)
                total = None
                for h in range(count):
                    at = n * count + h
                    state[at] = keep[h] * state[at] + new
                    term = weigh[h] * state[at]
                    total = term if total is None else total + term
                terms[n, k * tile : (k + 1) * tile, :] = total
        for n in range(seqs):
            result = terms[n, pl.ds(0, tile, stride=tile), :]
            for p in range(1, tile):
                result = result + terms[n, pl.ds(p, tile, stride=tile), :]
            made[n, pl.ds(i * tile, tile), :] = result
        return tuple(state)

    start = tuple(
        start_ref[n, h * tile : (h + 1) * tile, :] for n in range(seqs) for h in range(count)
    )
    lax.fori_loop(0, length // tile, step, start)
    empty(made, out_ref, place_ref[0])


def later_kernel(place_ref, signal_ref, decay_ref, state_ref, held):
    fill(signal_ref, held, place_ref[0])
    seqs, length, lanes = held.shape
    keep = [jnp.exp(-d) for d in halves(decay_ref)]
    count = len(keep)

    def step(i, carry):
        state = list(carry)
        base = length - tile - i * tile
        for k in range(tile - 1, -1, -1):
            for n in range(seqs):
                new = row_of(held, n, base + k)
                for h in range(count):
                    at = n * count + h
                    state[at] = keep[h] * state[at] + new
        return tuple(state)

    zero = jnp.zeros((tile, lanes), wide)
    state = lax.fori_loop(0, length // tile, step, tuple(zero for _ in range(seqs * count)))
    for n in range(seqs):
        for h in range(count):
            state_ref[n, h * tile : (h + 1) * tile, :] = state[n * count + h]


def backward_kernel(
    place_ref,
    signal_ref,
    grad_ref,
    decay_ref,
    residue_ref,
    start_ref,
    end_ref,
    out_ref,
    residue_grad_ref,
    decay_grad_ref,
    held,
    grads,
    terms,
    made,
    later,
):
    fill(signal_ref, held, place_ref[0])
    fill(grad_ref, grads, place_ref[0])
    seqs, length, lanes = held.shape
    keep = [jnp.exp(-d) for d in halves(decay_ref)]
    weigh = halves(residue_ref)
    count = len(keep)
    group = later.shape[0]
    zero = jnp.zeros((tile, lanes), wide)
    none = tuple(zero for _ in range(group * count))
    sum_first = [zero] * count
    sum_second = [zero] * count
    for base_seq in range(0, seqs, group):

        def load(ref):
            return tuple(
                ref[base_seq + n, h * tile : (h + 1) * tile, :]
                for n in range(group)
                for h in range(count)
            )

        def back_step(i, carry):
            state, first = [list(v) for v in carry]
            base = length - tile - i * tile
            for k in range(tile - 1, -1, -1):
                for n in range(group):
                    back = row_of(grads, base_seq + n, base + k)
                    new = row_of(held, base_seq + n, base + k)
                    total = None
                    for h in range(count):
                        at = n * count + h
                        state[at] = keep[h] * state[at] + back
                        first[at] = first[at] + new * state[at]
                        later[n, pl.ds(((base + k) * count + h) * tile, tile), :] = state[at]
                        term = weigh[h] * state[at]
                        total = term if total is None else total + term
                    terms[n, k * tile : (k + 1) * tile, :] = total
            for n in range(group):
                result = terms[n, pl.ds(0, tile, stride=tile), :]
                for p in range(1, tile):
                    result = result + terms[n, pl.ds(p, tile, stride=tile), :]
                made[base_seq + n, pl.ds(base, tile), :] = result
            return tuple(state), tuple(first)

        _, first = lax.fori_loop(0, length // tile, back_step, (load(end_ref), none))

        def ahead(i, carry):
            state, second = [list(v) for v in carry]
            for k in range(tile):
                for n in range(group):
                    new = row_of(held, base_seq + n, i * tile + k)
                    for h in range(count):
                        at = n * count + h
                        state[at] = keep[h] * state[at] + new
                        other = later[n, pl.ds(((i * tile + k) * count + h) * tile, tile), :]
                        second[at] = second[at] + state[at] * other
            return tuple(state), tuple(second)

        _, second = lax.fori_loop(0, length // tile, ahead, (load(start_ref), none))
        for n in range(group):
            for h in range(count):
                at = n * count + h
                sum_first[h] = sum_first[h] + first[at]
                sum_second[h] = sum_second[h] + (second[at] - first[at])
    for h in range(count):
        residue_grad_ref[h * tile : (h + 1) * tile, :] = sum_first[h]
        decay_grad_ref[h * tile : (h + 1) * tile, :] = -weigh[h] * sum_second[h]
    empty(made, out_ref, place_ref[0])


def conv_call(kernel, place, arrays, results, scratch, flops):
    channels = arrays[0].shape[-1]
    lanes = min(channels, 128)

    def spec(shape):
        lead = len(shape) - 1
        return pl.BlockSpec(shape[:-1] + (lanes,), lambda i, *_: (0,) * lead + (i,))

    return pl.pallas_call(
        kernel,
        out_shape=results,
        grid_spec=pltpu.PrefetchScalarGridSpec(
            num_scalar_prefetch=1,
            grid=(channels // lanes,),
            in_specs=[spec(a.shape) for a in arrays],
            out_specs=[spec(r.shape) for r in results],
            scratch_shapes=[pltpu.VMEM(s + (lanes,), wide) for s in scratch],
        ),
        compiler_params=pltpu.CompilerParams(
            dimension_semantics=("arbitrary",), vmem_limit_bytes=56 << 20
        ),
        cost_estimate=pl.CostEstimate(
            flops=flops, transcendentals=0, bytes_accessed=sum(a.size * 4 for a in arrays)
        ),
    )(place, *arrays)


def sizes(signal, poles):
    groups, parts, inner, length, channels = signal.shape
    return groups * inner, parts * length, channels, signal.size * poles


def states_of(place, signal, decay):
    seqs, length, channels, work = sizes(signal, decay.shape[0])
    shape = jax.ShapeDtypeStruct((seqs, decay.shape[0], channels), wide)
    return conv_call(states_kernel, place, [signal, decay], [shape], [(seqs, length)], 2 * work)[0]


def forward_of(place, signal, decay, residue, start):
    seqs, length, channels, work = sizes(signal, decay.shape[0])
    return conv_call(
        forward_kernel,
        place,
        [signal, decay, residue, start],
        [jax.ShapeDtypeStruct(signal.shape, low)],
        [(seqs, length), (seqs, tile * tile), (seqs, length)],
        4 * work,
    )[0]


def later_of(place, signal, decay):
    seqs, length, channels, work = sizes(signal, decay.shape[0])
    shape = jax.ShapeDtypeStruct((seqs, decay.shape[0], channels), wide)
    return conv_call(later_kernel, place, [signal, decay], [shape], [(seqs, length)], 2 * work)[0]


def backward_of(place, signal, grad, decay, residue, start, end):
    poles = decay.shape[0]
    seqs, length, channels, work = sizes(signal, poles)
    shape = jax.ShapeDtypeStruct(decay.shape, wide)
    group = min(seqs, 4)
    return conv_call(
        backward_kernel,
        place,
        [signal, grad, decay, residue, start, end],
        [jax.ShapeDtypeStruct(signal.shape, low), shape, shape],
        [
            (seqs, length),
            (seqs, length),
            (group, tile * tile),
            (seqs, length),
            (group, length * poles),
        ],
        12 * work,
    )


def rms_scale(values):
    return lax.rsqrt(jnp.mean(values * values, axis=-1, keepdims=True) + epsilon)


def norm_back(values, scale, gain, grad_normed):
    grad_gain = jnp.sum(grad_normed * values * scale, axis=(0, 1))
    scaled = grad_normed * gain
    grad_values = scale * scaled - values * scale * scale * scale * jnp.mean(
        scaled * values, axis=-1, keepdims=True
    )
    return (grad_values, grad_gain)


def dot(a, b, kind=wide):
    return jnp.dot(a, b, preferred_element_type=wide).astype(kind)


def dot_t(a, b, kind=wide):
    return lax.dot_general(a, b, (((1,), (1,)), ((), ())), preferred_element_type=wide).astype(kind)


def dot_w(a, b):
    return lax.dot_general(a, b, (((0,), (0,)), ((), ())), preferred_element_type=wide).astype(low)


def body(
    tokens,
    lengths,
    norm_gain,
    in_weight,
    conv_taps,
    filter_residue,
    filter_decay,
    out_weight,
    feed_gain,
    gate_weight,
    up_weight,
    down_weight,
    cotangent,
):
    spread, ycount = lax.axis_size("x"), lax.axis_size("y")
    batch, local, width = tokens.shape
    place = lax.axis_index("z") * spread + lax.axis_index("x")
    position = place * local + jnp.arange(local)
    mask = (position[None, :] < lengths[:, None]).astype(wide)[..., None]
    block = spread * local

    count = 3 * depth
    extra = 8
    line = Line(lax.axis_index("c"))
    run = line.run

    def stacked(value, got):
        return jnp.stack([value] + got)

    in_got = column_moves(run(lambda w: column_pieces(w, 3), in_weight))
    last = [(i * spread + spread - 1, (i + 1) * spread) for i in range(depth - 1)]

    def norm_one(values, gain):
        values = values.astype(wide)
        scale = rms_scale(values)
        normed = (values * scale * gain).astype(low)
        return normed, normed[:, local - 2 :], scale

    normed, ending, scale_one = run(norm_one, tokens, norm_gain)
    before = lax.ppermute(ending, ("z", "x"), last)
    w_in = gather_tile(run(column_block, in_got))

    def lengthen(values, rows):
        rest = jnp.zeros((batch, extra - 2, width), values.dtype)
        values = jnp.concatenate([values, rows, rest], axis=1)
        return values[: batch // 2], values[batch // 2 :]

    normed_move = Gather(*run(lengthen, normed, before))
    normed_move.turn(line)
    w_down = gather_tile(run(row_block, down_weight))
    gate_got = column_moves(run(lambda w: column_pieces(w, 1), gate_weight))

    def feed_grad(values):
        values = (values.astype(wide) * mask).astype(low)
        return values[: batch // 2], values[batch // 2 :]

    feed_move = Gather(*run(feed_grad, cotangent))
    normed_all = normed_move.end(line)
    feed_move.turn(line)
    block_out = run(out_block, out_weight)
    out_got = moved(block_out, "z", -1)

    channels = w_in.shape[1] // 3
    half = channels // 2
    grid = (2 * ycount, spread, batch // 2, local)

    def rank_values(all_taps, all_decay, all_residue):
        return (
            jnp.concatenate(
                [rank_rows(all_taps[:, g * width : (g + 1) * width], 1) for g in range(3)], axis=1
            ),
            rank_rows(all_decay, 0).T,
            rank_rows(all_residue, 0).T,
        )

    taps, decay, residue = run(rank_values, conv_taps, filter_decay, filter_residue)
    opening = (lax.axis_index("x") + jnp.arange(spread)) % spread == 0
    opening = opening[None, :, None, None, None]
    closing = (lax.axis_index("x") + jnp.arange(spread)) % spread == spread - 1
    closing = closing[None, :, None, None, None]

    def project(v, w):
        return dot(v, w, low).reshape(grid[:3] + (local + extra, 3 * channels))

    mixed = run(project, normed_all, w_in)

    def extend(value, g):
        own = value[..., g * channels : (g + 1) * channels]
        earlier = jnp.roll(own[:, :, :, local - 2 : local], 1, axis=1)
        earlier = jnp.where(opening, own[:, :, :, local : local + 2], earlier)
        return jnp.concatenate([earlier, own[:, :, :, :local]], axis=3).astype(wide)

    def short_of(value, weights, g):
        longer = extend(value, g)
        own = weights[:, g * channels : (g + 1) * channels]
        return own[0] * longer[:, :, :, 2:] + own[1] * longer[:, :, :, 1:-1] + own[2] * longer[:, :, :, :-2]

    spot = lax.axis_index("x").astype(jnp.int32).reshape(1)

    def multiply(value, weights, rates):
        keys, values = (short_of(value, weights, g) for g in (1, 2))
        product = (keys * values).astype(low)
        return product, states_of(spot, product, rates)

    product, state_end = run(multiply, mixed, taps, decay)
    states = [passed(state_end, "z", k) for k in range(1, depth)]
    w_gate = gather_tile(run(column_block, gate_got))
    grad_feed_all = feed_move.end(line)
    held = run(lambda own, got: by_z([own] + got), block_out, out_got)
    out_move = Gather(held[:1], held[1:])
    up_got = column_moves(run(lambda w: column_pieces(w, 1), up_weight))
    out_move.turn(line)

    def combine(parts, rates):
        total = parts[0]
        for k in range(1, depth - 1):
            total = total + jnp.exp(-rates * (k * block)) * parts[k]
        return total

    def convolve(parts, value, weights, signal, rates, amounts):
        start = combine(parts, rates)
        result = forward_of(spot, signal, rates, amounts, start)
        query = short_of(value, weights, 0)
        gated = (query * result.astype(wide)).astype(low)
        slots = gated.reshape(2, ycount, spread, -1, channels)
        return (
            start,
            result,
            gated.reshape(-1, channels),
            [[slots[:, k, i].reshape(-1, channels) for i in range(spread)] for k in range(ycount)],
        )

    start, convolved, gated_all, gated = run(
        convolve, states, mixed, taps, product, decay, residue
    )
    gated_got = swap_slots(gated)
    w_up = gather_tile(run(column_block, up_got))
    out_own = out_move.end(line)
    w_out = [out_own] + moved(out_own, "c", -1)

    def mix(got, weights, values, gain):
        own = jnp.concatenate(
            [g[:, h * half : (h + 1) * half] for h in range(2) for row in got for g in row], axis=1
        )
        mixer = in_order(jnp.stack([dot(own, w) for w in weights]), "c")
        mixer = jnp.concatenate([m for m in mixer], axis=1).reshape(batch, local, width)
        middle = values.astype(wide) + mixer
        scale = rms_scale(middle)
        normed = (middle * scale * gain).astype(low)
        return middle, scale, normed[: batch // 2], normed[batch // 2 :]

    middle, scale_two, first, second = run(mix, gated_got, w_out, tokens, feed_gain)

    two_move = Gather(first, second)
    grad_active = run(dot_t, grad_feed_all, w_down)
    two_move.turn(line)
    normed_two_all = two_move.end(line)

    def open_gate(v, w, back):
        value = dot(v, w)
        return value, (back * value * jax.nn.sigmoid(value)).astype(low)

    gate, grad_upper = run(open_gate, normed_two_all, w_gate, grad_active)
    up_term = run(dot_w, normed_two_all, grad_upper)
    up_mine = scatter_tile(up_term)

    def activate(v, w, value, back):
        upper = dot(v, w)
        sigma = jax.nn.sigmoid(value)
        return (
            (value * sigma * upper).astype(low),
            (back * upper * sigma * (1.0 + value * (1.0 - sigma))).astype(low),
        )

    active, grad_gate = run(activate, normed_two_all, w_up, gate, grad_active)
    two_back = Scatter(
        run(
            lambda a, b, wa, wb: split_sum((dot_t(a, wa) + dot_t(b, wb)).astype(low)),
            grad_gate,
            grad_upper,
            w_gate,
            w_up,
        )
    )
    gate_mine = scatter_tile(run(dot_w, normed_two_all, grad_gate))
    two_back.turn(line)
    feed_parts = run(lambda a, w: split_sum(dot(a, w, low)), active, w_down)

    def middle_back(rest, values, scale, gain, back, weights):
        grad_normed = Scatter.sum(*rest).reshape(batch, local, width)
        result, grad_gain = norm_back(values, scale, gain, grad_normed)
        result = result + back.astype(wide) * mask
        parts = core_halves(result.astype(low).reshape(-1, width))
        own = sum(dot_t(m, w) for m, w in zip(parts, weights)).astype(low)
        ranks = ycount * spread

        def slot(at):
            pieces = [
                own[:, (h * ranks + at) * half : (h * ranks + at + 1) * half] for h in range(2)
            ]
            return jnp.concatenate(pieces, axis=1)

        slots = [[slot(k * spread + i) for i in range(spread)] for k in range(ycount)]
        rounded = result.astype(low)
        return result, grad_gain, rounded[: batch // 2], rounded[batch // 2 :], slots

    grad_middle, grad_feed_gain, first, second, grad_slots = run(
        middle_back, two_back.rest(), middle, scale_two, feed_gain, cotangent, w_out
    )
    grad_got = swap_slots(grad_slots)
    down_mine = scatter_tile(run(dot_w, active, grad_feed_all))
    mix_move = Gather(first, second)

    def conv_grads(got, result, value, weights, rates):
        grad = jnp.stack([jnp.stack(row) for row in got])
        grad = grad.reshape(ycount, spread, 2, batch // 2, local, channels)
        grad = jnp.moveaxis(grad, 2, 0).reshape(grid + (channels,)).astype(wide)
        grad_query = grad * result.astype(wide)
        grad_conv = (grad * short_of(value, weights, 0)).astype(low)
        return grad_query, grad_conv, later_of(spot, grad_conv, rates)

    grad_query, grad_conv, later_end = run(conv_grads, grad_got, convolved, mixed, taps, decay)
    laters = [passed(later_end, "z", -k) for k in range(1, depth)]
    mix_move.turn(line)

    def short_back(grad, weights):
        head = jnp.roll(grad[:, :, :, :2], -1, axis=1)
        whole = jnp.concatenate([grad, jnp.where(closing, 0.0, head)], axis=3)
        result = (
            weights[0] * whole[:, :, :, :-2]
            + weights[1] * whole[:, :, :, 1:-1]
            + weights[2] * whole[:, :, :, 2:]
        )
        one, two = grad[:, :, :, :1], grad[:, :, :, 1:2]
        earlier = jnp.concatenate([weights[2] * one, weights[1] * one + weights[2] * two], axis=3)
        rest = jnp.zeros(grad.shape[:3] + (extra - 2, grad.shape[-1]), wide)
        result = jnp.concatenate([result, jnp.where(opening, earlier, 0.0), rest], axis=3)
        return result.astype(low).reshape(-1, grad.shape[-1])

    feed_back = Scatter(feed_parts)
    up_parts_got = owner_moves(run(owner_parts, up_mine))

    def conv_back(signal, grad, rates, amounts, begin, ends_later, value, weights):
        later = combine(ends_later, rates)
        grad_product, grad_residue, grad_decay = backward_of(
            spot, signal, grad, rates, amounts, begin, later
        )
        grad_product = grad_product.astype(wide)
        keys, values = (short_of(value, weights, g) for g in (1, 2))
        pair = jnp.concatenate([grad_product * values, grad_product * keys], axis=-1)
        return pair, grad_residue, grad_decay

    grad_pair, grad_residue, grad_decay = run(
        conv_back, product, grad_conv, decay, residue, start, laters, mixed, taps
    )

    up_held = run(owner_held, up_parts_got)
    up_got = moved(up_held, "y", -1)

    def in_back(query, pair, weights, v):
        result = jnp.concatenate(
            [
                short_back(query, weights[:, :channels]),
                short_back(pair, weights[:, channels:]),
            ],
            axis=1,
        )
        return result, dot_w(v, result)

    grad_mixed, in_term = run(in_back, grad_query, grad_pair, taps, normed_all)
    in_mine = scatter_tile(in_term)
    one_back = Scatter(run(lambda a, w: split_sum(dot_t(a, w, low)), grad_mixed, w_in))
    grad_mix_all = mix_move.end(line)
    out_mine = scatter_tile(run(dot_w, gated_all, grad_mix_all))
    gate_got = owner_moves(run(owner_parts, gate_mine))
    feed_back.turn(line)
    up_held = run(stacked, up_held, up_got)
    up_got = moved(up_held, "c", -1)

    def tap_sums(query, pair, value):
        sums = []
        for g, part in enumerate((query, pair[..., :channels], pair[..., channels:])):
            own = extend(value, g)
            sums += [
                jnp.sum(part * own[:, :, :, 2 - j : local + 2 - j], axis=(0, 1, 2, 3))
                for j in range(3)
            ]
        return jnp.stack(sums)

    grad_taps = run(tap_sums, grad_query, grad_pair, mixed)
    gate_held = run(owner_held, gate_got)
    gate_got = moved(gate_held, "y", -1)

    def normed_sum(rest):
        value = Scatter.sum(*rest).reshape(batch, local + extra, width)
        return value[:, :local], value[:, local : local + 2].astype(low)

    def column_whole(own, got):
        return owner_whole(lax.axis_index("c"), [own] + got, depth)

    grad_up_weight = run(column_whole, up_held, up_got)
    one_back.turn(line)
    output = run(
        lambda rest, values: (
            mask * (values + Scatter.sum(*rest).reshape(batch, local, width))
        ).astype(low),
        feed_back.rest(),
        middle,
    )
    down_held = run(lambda v: v[None], down_mine)
    down_got = moved(down_held, "y", -1)
    gate_held = run(stacked, gate_held, gate_got)
    gate_got = moved(gate_held, "c", -1)
    grad_normed, grad_before = run(normed_sum, one_back.rest())
    grad_after = lax.ppermute(grad_before, ("z", "x"), [(j, i) for i, j in last])
    grad_gate_weight = run(column_whole, gate_held, gate_got)

    def tokens_back(grad, extension, values, scale, gain, back, small):
        values = values.astype(wide)
        grad = jnp.concatenate(
            [grad[:, : local - 2], grad[:, local - 2 :] + extension.astype(wide)], axis=1
        )
        result, grad_gain = norm_back(values, scale, gain, grad)
        gains = jnp.stack([grad_gain, small[0]]).reshape(-1, channels)
        return (result + back).astype(low), jnp.concatenate(list(small[1:]) + [gains], axis=0)

    grad_tokens, small = run(
        tokens_back,
        grad_normed,
        grad_after,
        tokens,
        scale_one,
        norm_gain,
        grad_middle,
        (grad_feed_gain, grad_residue, grad_decay, grad_taps),
    )
    small_got = moved(small, "c", 1)
    down_held = run(lambda own, got: jnp.concatenate([own] + got), down_held, down_got)
    down_got = moved(down_held, "c", -1)
    small = run(lambda v, got: v + sum(got), small, small_got)
    small_got = moved(small, "z", 1)
    in_got = owner_moves(run(owner_parts, in_mine))

    def rows_whole(own, got):
        whole = in_order(jnp.swapaxes(in_order(jnp.stack([own] + got), "c"), 0, 1), "y")
        return whole.reshape(-1, width).astype(wide)

    grad_down = run(rows_whole, down_held, down_got)
    in_held = run(owner_held, in_got)
    in_got = moved(in_held, "y", -1)
    out_held = run(lambda v: v[None], out_mine)
    out_got = moved(out_held, "y", -1)
    small = run(lambda v, got: v + sum(got), small, small_got)
    small_got = moved(small, "x", -1)
    small = run(stacked, small, small_got)
    small_got = moved(small, "y", -1)
    in_held = run(stacked, in_held, in_got)
    in_got = moved(in_held, "c", -1)
    poles = decay.shape[0]

    def small_whole(own, got):
        slots = jnp.stack([own] + got)
        rows = 2 * poles + 9
        gains = jnp.sum(slots[:, :, rows:], axis=(0, 1)).reshape(2, width)
        whole = all_channels(slots[:, :, :rows])
        grad_conv_taps = jnp.concatenate(
            [whole[2 * poles + 3 * g : 2 * poles + 3 * g + 3] for g in range(3)], axis=1
        )
        return gains[0], gains[1], grad_conv_taps, whole[:poles].T, whole[poles : 2 * poles].T

    grad_norm_gain, feed_gain_sum, grad_conv_taps, residue_sum, decay_sum = run(
        small_whole, small, small_got
    )
    out_held = run(lambda own, got: jnp.concatenate([own] + got), out_held, out_got)
    out_got = moved(out_held, "c", -1)
    grad_in_weight = run(
        lambda own, got: owner_whole(lax.axis_index("c"), [own] + got, count), in_held, in_got
    )

    def out_whole(core, own, got):
        ccount = lax.axis_size("c")
        slots = jnp.stack([own] + got)
        slots = jnp.stack(
            [lax.dynamic_index_in_dim(slots, (j - core) % ccount, 0, False) for j in range(ccount)]
        )
        whole = in_order(jnp.swapaxes(slots, 0, 1), "y")
        return whole.reshape(-1, width).astype(wide)

    grad_out_weight = line.finish(out_whole, out_held, out_got)
    return (
        output,
        grad_tokens,
        grad_norm_gain,
        grad_in_weight,
        grad_conv_taps,
        residue_sum,
        decay_sum,
        grad_out_weight,
        feed_gain_sum,
        grad_gate_weight,
        grad_up_weight,
        grad_down,
    )


def solution(mesh):
    pairs, blocks = mesh.shape["dp"], mesh.shape["seq"]
    devices = mesh.devices.reshape(pairs // cores, cores, depth, blocks // depth)
    inner = Mesh(devices, ("y", "c", "z", "x"))
    dp, seq = ("y", "c"), ("z", "x")
    tokens, rows = P(dp, seq, None), P(seq, None)
    return jax.shard_map(
        body,
        mesh=inner,
        in_specs=(
            tokens,
            P(dp),
            P(),
            rows,
            P(),
            P(),
            P(),
            rows,
            P(),
            rows,
            rows,
            rows,
            tokens,
        ),
        out_specs=(tokens, tokens, P(), rows, P(), P(), P(), rows, P(), rows, rows, rows),
        check_vma=False,
    )
```

```python
import functools

import jax
import jax.numpy as jnp
from jax import lax
from jax.experimental import pallas as pl
from jax.experimental.pallas import tpu as pltpu
from jax.sharding import Mesh, PartitionSpec as P

epsilon = 1e-06
low = jnp.bfloat16
wide = jnp.float32
tile = 8
depth = 4
cores = 2


def turned(value, axis, by):
    length = lax.axis_size(axis)
    return lax.ppermute(value, axis, [(i, (i + by) % length) for i in range(length)])


def passed(value, axis, by):
    length = lax.axis_size(axis)
    pairs = [(i, i + by) for i in range(length) if 0 <= i + by < length]
    return lax.ppermute(value, axis, pairs)


def swap_slots(slots):
    ycount, spread = lax.axis_size("y"), lax.axis_size("x")
    result = []
    for dy in range(ycount):
        line = []
        for dx in range(spread):
            sy, sx = (ycount - dy) % ycount, (spread - dx) % spread
            if sy == 0 and sx == 0:
                line.append(slots[0][0])
                continue
            pairs = [
                (i * spread + j, (i + sy) % ycount * spread + (j + sx) % spread)
                for i in range(ycount)
                for j in range(spread)
            ]
            line.append(lax.ppermute(slots[sy][sx], ("y", "x"), pairs))
        result.append(line)
    return result


class Line:
    def __init__(self, token):
        self.token = token

    def run(self, work, *values):
        values, token = lax.optimization_barrier((values, self.token))
        result, self.token = lax.optimization_barrier((work(*values), token))
        return result

    def finish(self, work, *values):
        values, token = lax.optimization_barrier((values, self.token))
        return work(token, *values)


def moved(value, axis, sign):
    return [turned(value, axis, sign * d) for d in range(1, lax.axis_size(axis))]


class Gather:
    def __init__(self, first, second):
        self.held = (first, second)
        self.got = (moved(first, "x", -1), moved(second, "y", -1))

    def turn(self, line):
        self.held = line.run(
            lambda held, got: tuple(jnp.stack([h] + g) for h, g in zip(held, got)), self.held, self.got
        )
        self.got = (moved(self.held[0], "y", -1), moved(self.held[1], "x", -1))

    def end(self, line):
        def work(held, got):
            first = jnp.stack([held[0]] + got[0])
            second = jnp.swapaxes(jnp.stack([held[1]] + got[1]), 0, 1)
            return jnp.stack([first, second]).reshape(-1, first.shape[-1])

        return line.run(work, self.held, self.got)


def split_sum(partial):
    grid = partial.reshape(2, lax.axis_size("y"), lax.axis_size("x"), -1, partial.shape[-1])
    first = [grid[0][:, d].astype(low) for d in range(grid.shape[2])]
    second = [grid[1][d].astype(low) for d in range(grid.shape[1])]
    return first, second


def add_up(parts, got):
    total = parts[0].astype(wide)
    for g in got:
        total = total + g.astype(wide)
    return total


class Scatter:
    def __init__(self, parts):
        self.parts = parts
        self.send("x", "y")

    def send(self, *axes):
        self.got = [
            [turned(p, axis, d + 1) for d, p in enumerate(part[1:])]
            for part, axis in zip(self.parts, axes)
        ]

    def turn(self, line):
        def work(parts, got):
            result = []
            for part, g in zip(parts, got):
                total = add_up(part, g).astype(low)
                result.append([total[d] for d in range(total.shape[0])])
            return result

        self.parts = line.run(work, self.parts, self.got)
        self.send("y", "x")

    def rest(self):
        return self.parts, self.got

    @staticmethod
    def sum(parts, got):
        return jnp.stack([add_up(part, g) for part, g in zip(parts, got)])


def pick_kernel(count, part, stride, start_ref, source, *refs):
    targets, sems = refs[:-1], refs[-1]
    copies = []
    for d, target in enumerate(targets):
        for k in range(count):
            at = pl.multiple_of((k * stride + start_ref[d]) * part, part)
            copies.append(
                pltpu.make_async_copy(
                    source.at[:, pl.ds(at, part)],
                    target.at[:, k * part : (k + 1) * part],
                    sems.at[d * count + k],
                )
            )
    for copy in copies:
        copy.start()
    for copy in copies:
        copy.wait()


def column_pieces(weight, groups):
    spread, ycount = lax.axis_size("x"), lax.axis_size("y")
    rows = weight.shape[0]
    count = groups * depth
    part = weight.shape[1] // (count * spread * ycount)
    starts = [
        (lax.axis_index("x") + d) % spread * ycount + lax.axis_index("y") for d in range(spread)
    ]
    if part % 128 == 0:
        return pl.pallas_call(
            functools.partial(pick_kernel, count, part, spread * ycount),
            out_shape=[jax.ShapeDtypeStruct((rows, count * part), weight.dtype)] * spread,
            grid_spec=pltpu.PrefetchScalarGridSpec(
                num_scalar_prefetch=1,
                in_specs=[pl.BlockSpec(memory_space=pl.ANY)],
                out_specs=[pl.BlockSpec(memory_space=pltpu.VMEM)] * spread,
                scratch_shapes=[pltpu.SemaphoreType.DMA((count * spread,))],
            ),
            cost_estimate=pl.CostEstimate(
                flops=0, transcendentals=0, bytes_accessed=4 * rows * count * part * spread
            ),
        )(jnp.stack(starts).astype(jnp.int32), weight)
    return [
        jnp.concatenate(
            [
                lax.dynamic_slice_in_dim(weight, (k * spread * ycount + start) * part, part, 1)
                for k in range(count)
            ],
            axis=1,
        )
        for start in starts
    ]


def column_moves(pieces):
    spread, ccount = lax.axis_size("x"), lax.axis_size("c")
    share = spread // ccount
    got = [pieces[0]]
    for d in range(1, spread):
        pairs = [
            (i // share * spread + i, i // share * spread + (i + d) % spread) for i in range(spread)
        ]
        got.append(lax.ppermute(pieces[d], ("c", "x"), pairs))
    return got


def column_block(got):
    spread, ccount = lax.axis_size("x"), lax.axis_size("c")
    share = spread // ccount
    place, core = lax.axis_index("x"), lax.axis_index("c")
    got = jnp.stack(got)
    return jnp.concatenate(
        [
            lax.dynamic_index_in_dim(got, (place - core * share - j) % spread, 0, False)
            for j in range(share)
        ]
    )


def row_block(weight):
    ycount, ccount = lax.axis_size("y"), lax.axis_size("c")
    part = weight.shape[0] // (ycount * ccount)
    pair = lax.axis_index("y") * ccount + lax.axis_index("c")
    return lax.dynamic_slice_in_dim(weight, pair * part, part, 0)


def core_halves(value):
    ccount = lax.axis_size("c")
    width = value.shape[1] // ccount
    core = lax.axis_index("c")
    return [
        lax.dynamic_slice_in_dim(value, (core + d) % ccount * width, width, 1)
        for d in range(ccount)
    ]


def out_block(weight):
    part = weight.shape[0] // lax.axis_size("y")
    rows = lax.dynamic_slice_in_dim(weight, lax.axis_index("y") * part, part, 0)
    return core_halves(rows)[0]


def gather_tile(block):
    return lax.all_gather(block, ("z", "c"), axis=0, tiled=True)


def scatter_tile(term):
    return lax.psum_scatter(term, ("z", "c"), scatter_dimension=0, tiled=True)


def owner_parts(mine):
    spread, ccount = lax.axis_size("x"), lax.axis_size("c")
    share = spread // ccount
    place, core = lax.axis_index("x"), lax.axis_index("c")
    parts = mine.reshape(share, -1, mine.shape[-1])
    return [
        lax.dynamic_index_in_dim(
            parts, jnp.clip((place + d) % spread - core * share, 0, share - 1), 0, False
        )
        for d in range(spread)
    ]


def owner_moves(parts):
    spread, ccount = lax.axis_size("x"), lax.axis_size("c")
    share = spread // ccount
    got = [parts[0]]
    for d in range(1, spread):
        pairs = [
            ((i + d) % spread // share * spread + i, i // share * spread + (i + d) % spread)
            for i in range(spread)
        ]
        got.append(lax.ppermute(parts[d], ("c", "x"), pairs))
    return got


def owner_held(got):
    spread, ccount = lax.axis_size("x"), lax.axis_size("c")
    share = spread // ccount
    place, core = lax.axis_index("x"), lax.axis_index("c")
    got = jnp.stack(got)
    return jnp.stack(
        [
            lax.dynamic_index_in_dim(got, (place - core * share - j) % spread, 0, False)
            for j in range(share)
        ]
    )


def assemble_kernel(count, width, order_ref, *refs):
    sources, target = refs[:-1], refs[-1]
    part = width // count
    ranks = order_ref.shape[0] // 2
    for r in range(ranks):
        core, slot = order_ref[2 * r], order_ref[2 * r + 1]
        value = sources[0][slot]
        for c in range(1, len(sources)):
            value = jnp.where(core == c, sources[c][slot], value)
        value = value.astype(wide)
        for at in range(count):
            start = (at * ranks + r) * part
            target[:, start : start + part] = value[:, at * part : (at + 1) * part]


def owner_whole(core, sources, count):
    spread, ccount, ycount = lax.axis_size("x"), lax.axis_size("c"), lax.axis_size("y")
    share = spread // ccount
    yplace = lax.axis_index("y")
    order = []
    for i in range(spread):
        for k in range(ycount):
            order += [(i // share - core) % ccount, (k - yplace) % ycount * share + i % share]
    sources = [v.reshape((-1,) + v.shape[2:]) for v in sources]
    held, rows, width = sources[0].shape
    block = min(rows, 64)
    return pl.pallas_call(
        functools.partial(assemble_kernel, count, width),
        out_shape=jax.ShapeDtypeStruct((rows, width * spread * ycount), wide),
        grid_spec=pltpu.PrefetchScalarGridSpec(
            num_scalar_prefetch=1,
            grid=(rows // block,),
            in_specs=[pl.BlockSpec((held, block, width), lambda i, order: (0, i, 0))]
            * len(sources),
            out_specs=pl.BlockSpec((block, width * spread * ycount), lambda i, order: (i, 0)),
        ),
        compiler_params=pltpu.CompilerParams(vmem_limit_bytes=56 << 20),
        cost_estimate=pl.CostEstimate(
            flops=0, transcendentals=0, bytes_accessed=6 * rows * width * spread * ycount
        ),
    )(jnp.stack(order).astype(jnp.int32), *sources)


def in_order(slots, axis):
    length = lax.axis_size(axis)
    place = lax.axis_index(axis)
    return jnp.stack(
        [lax.dynamic_index_in_dim(slots, (j - place) % length, 0, False) for j in range(length)]
    )


def rank_rows(values, axis):
    spread, ycount = lax.axis_size("x"), lax.axis_size("y")
    part = values.shape[axis] // (depth * spread * ycount)
    place = lax.axis_index("x") * ycount + lax.axis_index("y")
    return jnp.concatenate(
        [
            lax.dynamic_slice_in_dim(values, (k * spread * ycount + place) * part, part, axis)
            for k in range(depth)
        ],
        axis=axis,
    )


def all_channels(slots):
    whole = in_order(slots, "y")
    whole = in_order(jnp.swapaxes(whole, 0, 1), "x")
    spread, ycount, rows = whole.shape[:3]
    whole = whole.reshape(spread, ycount, rows, depth, -1)
    return jnp.transpose(whole, (2, 3, 0, 1, 4)).reshape(rows, -1)


def fill(source, target, place):
    groups, parts, inner, length = source.shape[:4]
    for j in range(parts):
        slot = lax.rem(j + parts - place, parts)
        for g in range(groups):
            for b in range(inner):
                target[g * inner + b, j * length : (j + 1) * length, :] = source[g, slot, b].astype(
                    wide
                )


def empty(source, target, place):
    groups, parts, inner, length = target.shape[:4]
    for j in range(parts):
        slot = lax.rem(j + parts - place, parts)
        for g in range(groups):
            for b in range(inner):
                target[g, slot, b] = source[g * inner + b, j * length : (j + 1) * length, :].astype(
                    low
                )


def halves(ref):
    return [ref[k * tile : (k + 1) * tile, :] for k in range(ref.shape[0] // tile)]


def row_of(ref, seq, at):
    return ref[seq, pl.ds(at, tile, stride=0), :]


def states_kernel(place_ref, signal_ref, decay_ref, state_ref, held):
    fill(signal_ref, held, place_ref[0])
    seqs, length, lanes = held.shape
    keep = [jnp.exp(-d) for d in halves(decay_ref)]
    count = len(keep)

    def step(i, carry):
        state = list(carry)
        for k in range(tile):
            for n in range(seqs):
                new = row_of(held, n, i * tile + k)
                for h in range(count):
                    at = n * count + h
                    state[at] = keep[h] * state[at] + new
        return tuple(state)

    zero = jnp.zeros((tile, lanes), wide)
    state = lax.fori_loop(0, length // tile, step, tuple(zero for _ in range(seqs * count)))
    for n in range(seqs):
        for h in range(count):
            state_ref[n, h * tile : (h + 1) * tile, :] = state[n * count + h]


def forward_kernel(place_ref, signal_ref, decay_ref, residue_ref, start_ref, out_ref, held, terms, made):
    fill(signal_ref, held, place_ref[0])
    seqs, length, lanes = held.shape
    keep = [jnp.exp(-d) for d in halves(decay_ref)]
    weigh = halves(residue_ref)
    count = len(keep)

    def step(i, carry):
        state = list(carry)
        for k in range(tile):
            for n in range(seqs):
                new = row_of(held, n, i * tile + k)
                total = None
                for h in range(count):
                    at = n * count + h
                    state[at] = keep[h] * state[at] + new
                    term = weigh[h] * state[at]
                    total = term if total is None else total + term
                terms[n, k * tile : (k + 1) * tile, :] = total
        for n in range(seqs):
            result = terms[n, pl.ds(0, tile, stride=tile), :]
            for p in range(1, tile):
                result = result + terms[n, pl.ds(p, tile, stride=tile), :]
            made[n, pl.ds(i * tile, tile), :] = result
        return tuple(state)

    start = tuple(
        start_ref[n, h * tile : (h + 1) * tile, :] for n in range(seqs) for h in range(count)
    )
    lax.fori_loop(0, length // tile, step, start)
    empty(made, out_ref, place_ref[0])


def later_kernel(place_ref, signal_ref, decay_ref, state_ref, held):
    fill(signal_ref, held, place_ref[0])
    seqs, length, lanes = held.shape
    keep = [jnp.exp(-d) for d in halves(decay_ref)]
    count = len(keep)

    def step(i, carry):
        state = list(carry)
        base = length - tile - i * tile
        for k in range(tile - 1, -1, -1):
            for n in range(seqs):
                new = row_of(held, n, base + k)
                for h in range(count):
                    at = n * count + h
                    state[at] = keep[h] * state[at] + new
        return tuple(state)

    zero = jnp.zeros((tile, lanes), wide)
    state = lax.fori_loop(0, length // tile, step, tuple(zero for _ in range(seqs * count)))
    for n in range(seqs):
        for h in range(count):
            state_ref[n, h * tile : (h + 1) * tile, :] = state[n * count + h]


def backward_kernel(
    place_ref,
    signal_ref,
    grad_ref,
    decay_ref,
    residue_ref,
    start_ref,
    end_ref,
    out_ref,
    residue_grad_ref,
    decay_grad_ref,
    held,
    grads,
    terms,
    made,
    later,
):
    fill(signal_ref, held, place_ref[0])
    fill(grad_ref, grads, place_ref[0])
    seqs, length, lanes = held.shape
    keep = [jnp.exp(-d) for d in halves(decay_ref)]
    weigh = halves(residue_ref)
    count = len(keep)
    group = later.shape[0]
    zero = jnp.zeros((tile, lanes), wide)
    none = tuple(zero for _ in range(group * count))
    sum_first = [zero] * count
    sum_second = [zero] * count
    for base_seq in range(0, seqs, group):

        def load(ref):
            return tuple(
                ref[base_seq + n, h * tile : (h + 1) * tile, :]
                for n in range(group)
                for h in range(count)
            )

        def back_step(i, carry):
            state, first = [list(v) for v in carry]
            base = length - tile - i * tile
            for k in range(tile - 1, -1, -1):
                for n in range(group):
                    back = row_of(grads, base_seq + n, base + k)
                    new = row_of(held, base_seq + n, base + k)
                    total = None
                    for h in range(count):
                        at = n * count + h
                        state[at] = keep[h] * state[at] + back
                        first[at] = first[at] + new * state[at]
                        later[n, pl.ds(((base + k) * count + h) * tile, tile), :] = state[at]
                        term = weigh[h] * state[at]
                        total = term if total is None else total + term
                    terms[n, k * tile : (k + 1) * tile, :] = total
            for n in range(group):
                result = terms[n, pl.ds(0, tile, stride=tile), :]
                for p in range(1, tile):
                    result = result + terms[n, pl.ds(p, tile, stride=tile), :]
                made[base_seq + n, pl.ds(base, tile), :] = result
            return tuple(state), tuple(first)

        _, first = lax.fori_loop(0, length // tile, back_step, (load(end_ref), none))

        def ahead(i, carry):
            state, second = [list(v) for v in carry]
            for k in range(tile):
                for n in range(group):
                    new = row_of(held, base_seq + n, i * tile + k)
                    for h in range(count):
                        at = n * count + h
                        state[at] = keep[h] * state[at] + new
                        other = later[n, pl.ds(((i * tile + k) * count + h) * tile, tile), :]
                        second[at] = second[at] + state[at] * other
            return tuple(state), tuple(second)

        _, second = lax.fori_loop(0, length // tile, ahead, (load(start_ref), none))
        for n in range(group):
            for h in range(count):
                at = n * count + h
                sum_first[h] = sum_first[h] + first[at]
                sum_second[h] = sum_second[h] + (second[at] - first[at])
    for h in range(count):
        residue_grad_ref[h * tile : (h + 1) * tile, :] = sum_first[h]
        decay_grad_ref[h * tile : (h + 1) * tile, :] = -weigh[h] * sum_second[h]
    empty(made, out_ref, place_ref[0])


def conv_call(kernel, place, arrays, results, scratch, flops):
    channels = arrays[0].shape[-1]
    lanes = min(channels, 128)

    def spec(shape):
        lead = len(shape) - 1
        return pl.BlockSpec(shape[:-1] + (lanes,), lambda i, *_: (0,) * lead + (i,))

    return pl.pallas_call(
        kernel,
        out_shape=results,
        grid_spec=pltpu.PrefetchScalarGridSpec(
            num_scalar_prefetch=1,
            grid=(channels // lanes,),
            in_specs=[spec(a.shape) for a in arrays],
            out_specs=[spec(r.shape) for r in results],
            scratch_shapes=[pltpu.VMEM(s + (lanes,), wide) for s in scratch],
        ),
        compiler_params=pltpu.CompilerParams(
            dimension_semantics=("arbitrary",), vmem_limit_bytes=56 << 20
        ),
        cost_estimate=pl.CostEstimate(
            flops=flops, transcendentals=0, bytes_accessed=sum(a.size * 4 for a in arrays)
        ),
    )(place, *arrays)


def sizes(signal, poles):
    groups, parts, inner, length, channels = signal.shape
    return groups * inner, parts * length, channels, signal.size * poles


def states_of(place, signal, decay):
    seqs, length, channels, work = sizes(signal, decay.shape[0])
    shape = jax.ShapeDtypeStruct((seqs, decay.shape[0], channels), wide)
    return conv_call(states_kernel, place, [signal, decay], [shape], [(seqs, length)], 2 * work)[0]


def forward_of(place, signal, decay, residue, start):
    seqs, length, channels, work = sizes(signal, decay.shape[0])
    return conv_call(
        forward_kernel,
        place,
        [signal, decay, residue, start],
        [jax.ShapeDtypeStruct(signal.shape, low)],
        [(seqs, length), (seqs, tile * tile), (seqs, length)],
        4 * work,
    )[0]


def later_of(place, signal, decay):
    seqs, length, channels, work = sizes(signal, decay.shape[0])
    shape = jax.ShapeDtypeStruct((seqs, decay.shape[0], channels), wide)
    return conv_call(later_kernel, place, [signal, decay], [shape], [(seqs, length)], 2 * work)[0]


def backward_of(place, signal, grad, decay, residue, start, end):
    poles = decay.shape[0]
    seqs, length, channels, work = sizes(signal, poles)
    shape = jax.ShapeDtypeStruct(decay.shape, wide)
    group = min(seqs, 4)
    return conv_call(
        backward_kernel,
        place,
        [signal, grad, decay, residue, start, end],
        [jax.ShapeDtypeStruct(signal.shape, low), shape, shape],
        [
            (seqs, length),
            (seqs, length),
            (group, tile * tile),
            (seqs, length),
            (group, length * poles),
        ],
        12 * work,
    )


def rms_scale(values):
    return lax.rsqrt(jnp.mean(values * values, axis=-1, keepdims=True) + epsilon)


def norm_back(values, scale, gain, grad_normed):
    grad_gain = jnp.sum(grad_normed * values * scale, axis=(0, 1))
    scaled = grad_normed * gain
    grad_values = scale * scaled - values * scale * scale * scale * jnp.mean(
        scaled * values, axis=-1, keepdims=True
    )
    return (grad_values, grad_gain)


def dot(a, b, kind=wide):
    return jnp.dot(a, b, preferred_element_type=wide).astype(kind)


def dot_t(a, b, kind=wide):
    return lax.dot_general(a, b, (((1,), (1,)), ((), ())), preferred_element_type=wide).astype(kind)


def dot_w(a, b):
    return lax.dot_general(a, b, (((0,), (0,)), ((), ())), preferred_element_type=wide).astype(low)


def body(
    tokens,
    lengths,
    norm_gain,
    in_weight,
    conv_taps,
    filter_residue,
    filter_decay,
    out_weight,
    feed_gain,
    gate_weight,
    up_weight,
    down_weight,
    cotangent,
):
    spread, ycount = lax.axis_size("x"), lax.axis_size("y")
    batch, local, width = tokens.shape
    place = lax.axis_index("z") * spread + lax.axis_index("x")
    position = place * local + jnp.arange(local)
    mask = (position[None, :] < lengths[:, None]).astype(wide)[..., None]
    block = spread * local

    count = 3 * depth
    extra = 8
    line = Line(lax.axis_index("c"))
    run = line.run

    def stacked(value, got):
        return jnp.stack([value] + got)

    w_out = lax.all_gather(run(out_block, out_weight), "z", axis=0, tiled=True)
    in_got = column_moves(run(lambda w: column_pieces(w, 3), in_weight))
    last = [(i * spread + spread - 1, (i + 1) * spread) for i in range(depth - 1)]

    def norm_one(values, gain):
        values = values.astype(wide)
        scale = rms_scale(values)
        normed = (values * scale * gain).astype(low)
        return normed, normed[:, local - 2 :], scale

    normed, ending, scale_one = run(norm_one, tokens, norm_gain)
    before = lax.ppermute(ending, ("z", "x"), last)

    def lengthen(values, rows):
        rest = jnp.zeros((batch, extra - 2, width), values.dtype)
        values = jnp.concatenate([values, rows, rest], axis=1)
        return values[: batch // 2], values[batch // 2 :]

    normed_move = Gather(*run(lengthen, normed, before))
    gate_got = column_moves(run(lambda w: column_pieces(w, 1), gate_weight))
    in_block, w_out = run(lambda got, w: (column_block(got), w), in_got, w_out)
    w_in = gather_tile(in_block)
    normed_move.turn(line)
    w_down = gather_tile(run(row_block, down_weight))

    def feed_grad(values):
        values = (values.astype(wide) * mask).astype(low)
        return values[: batch // 2], values[batch // 2 :]

    feed_move = Gather(*run(feed_grad, cotangent))
    normed_all = normed_move.end(line)
    feed_move.turn(line)

    channels = w_in.shape[1] // 3
    half = channels // 2
    grid = (2 * ycount, spread, batch // 2, local)

    def rank_values(all_taps, all_decay, all_residue):
        return (
            jnp.concatenate(
                [rank_rows(all_taps[:, g * width : (g + 1) * width], 1) for g in range(3)], axis=1
            ),
            rank_rows(all_decay, 0).T,
            rank_rows(all_residue, 0).T,
        )

    taps, decay, residue = run(rank_values, conv_taps, filter_decay, filter_residue)
    opening = (lax.axis_index("x") + jnp.arange(spread)) % spread == 0
    opening = opening[None, :, None, None, None]
    closing = (lax.axis_index("x") + jnp.arange(spread)) % spread == spread - 1
    closing = closing[None, :, None, None, None]

    def project(v, w):
        return dot(v, w, low).reshape(grid[:3] + (local + extra, 3 * channels))

    mixed = run(project, normed_all, w_in)

    def extend(value, g):
        own = value[..., g * channels : (g + 1) * channels]
        earlier = jnp.roll(own[:, :, :, local - 2 : local], 1, axis=1)
        earlier = jnp.where(opening, own[:, :, :, local : local + 2], earlier)
        return jnp.concatenate([earlier, own[:, :, :, :local]], axis=3).astype(wide)

    def short_of(value, weights, g):
        longer = extend(value, g)
        own = weights[:, g * channels : (g + 1) * channels]
        return own[0] * longer[:, :, :, 2:] + own[1] * longer[:, :, :, 1:-1] + own[2] * longer[:, :, :, :-2]

    spot = lax.axis_index("x").astype(jnp.int32).reshape(1)

    def multiply(value, weights, rates):
        keys, values = (short_of(value, weights, g) for g in (1, 2))
        product = (keys * values).astype(low)
        return product, states_of(spot, product, rates)

    product, state_end = run(multiply, mixed, taps, decay)
    states = [passed(state_end, "z", k) for k in range(1, depth)]
    w_gate = gather_tile(run(column_block, gate_got))
    out_move = Gather(*run(lambda w: (w[None, : w.shape[0] // 2], w[None, w.shape[0] // 2 :]), w_out))
    grad_feed_all = feed_move.end(line)
    up_got = column_moves(run(lambda w: column_pieces(w, 1), up_weight))
    out_move.turn(line)

    def combine(parts, rates):
        total = parts[0]
        for k in range(1, depth - 1):
            total = total + jnp.exp(-rates * (k * block)) * parts[k]
        return total

    def convolve(parts, value, weights, signal, rates, amounts):
        start = combine(parts, rates)
        result = forward_of(spot, signal, rates, amounts, start)
        query = short_of(value, weights, 0)
        gated = (query * result.astype(wide)).astype(low)
        slots = gated.reshape(2, ycount, spread, -1, channels)
        return (
            start,
            result,
            gated.reshape(-1, channels),
            [[slots[:, k, i].reshape(-1, channels) for i in range(spread)] for k in range(ycount)],
        )

    start, convolved, gated_all, gated = run(
        convolve, states, mixed, taps, product, decay, residue
    )
    gated_got = swap_slots(gated)
    w_up = gather_tile(run(column_block, up_got))
    out_own = out_move.end(line)
    w_out = [out_own] + moved(out_own, "c", -1)

    def mix(got, weights, values, gain):
        own = jnp.concatenate(
            [g[:, h * half : (h + 1) * half] for h in range(2) for row in got for g in row], axis=1
        )
        mixer = in_order(jnp.stack([dot(own, w) for w in weights]), "c")
        mixer = jnp.concatenate([m for m in mixer], axis=1).reshape(batch, local, width)
        middle = values.astype(wide) + mixer
        scale = rms_scale(middle)
        normed = (middle * scale * gain).astype(low)
        return middle, scale, normed[: batch // 2], normed[batch // 2 :]

    middle, scale_two, first, second = run(mix, gated_got, w_out, tokens, feed_gain)

    two_move = Gather(first, second)
    grad_active = run(dot_t, grad_feed_all, w_down)
    two_move.turn(line)
    normed_two_all = two_move.end(line)

    def open_gate(v, w, back):
        value = dot(v, w)
        return value, (back * value * jax.nn.sigmoid(value)).astype(low)

    gate, grad_upper = run(open_gate, normed_two_all, w_gate, grad_active)
    up_term = run(dot_w, normed_two_all, grad_upper)
    up_mine = scatter_tile(up_term)

    def activate(v, w, value, back):
        upper = dot(v, w)
        sigma = jax.nn.sigmoid(value)
        return (
            (value * sigma * upper).astype(low),
            (back * upper * sigma * (1.0 + value * (1.0 - sigma))).astype(low),
        )

    active, grad_gate = run(activate, normed_two_all, w_up, gate, grad_active)
    two_back = Scatter(
        run(
            lambda a, b, wa, wb: split_sum((dot_t(a, wa) + dot_t(b, wb)).astype(low)),
            grad_gate,
            grad_upper,
            w_gate,
            w_up,
        )
    )
    gate_mine = scatter_tile(run(dot_w, normed_two_all, grad_gate))
    two_back.turn(line)

    def feed_slots(a, w):
        value = dot(a, w, low).reshape(2, ycount, spread, -1, width)
        return [[value[:, k, i] for i in range(spread)] for k in range(ycount)]

    feed_parts = run(feed_slots, active, w_down)

    def middle_back(rest, values, scale, gain, back, weights):
        grad_normed = Scatter.sum(*rest).reshape(batch, local, width)
        result, grad_gain = norm_back(values, scale, gain, grad_normed)
        result = result + back.astype(wide) * mask
        parts = core_halves(result.astype(low).reshape(-1, width))
        own = sum(dot_t(m, w) for m, w in zip(parts, weights)).astype(low)
        ranks = ycount * spread

        def slot(at):
            pieces = [
                own[:, (h * ranks + at) * half : (h * ranks + at + 1) * half] for h in range(2)
            ]
            return jnp.concatenate(pieces, axis=1)

        slots = [[slot(k * spread + i) for i in range(spread)] for k in range(ycount)]
        rounded = result.astype(low)
        return result, grad_gain, rounded.reshape(2, -1, width), slots

    grad_middle, grad_feed_gain, grad_mix, grad_slots = run(
        middle_back, two_back.rest(), middle, scale_two, feed_gain, cotangent, w_out
    )
    grad_got = swap_slots(grad_slots)
    down_mine = scatter_tile(run(dot_w, active, grad_feed_all))
    mix_got = swap_slots([[grad_mix] * spread] * ycount)

    def conv_grads(got, result, value, weights, rates):
        grad = jnp.stack([jnp.stack(row) for row in got])
        grad = grad.reshape(ycount, spread, 2, batch // 2, local, channels)
        grad = jnp.moveaxis(grad, 2, 0).reshape(grid + (channels,)).astype(wide)
        grad_query = grad * result.astype(wide)
        grad_conv = (grad * short_of(value, weights, 0)).astype(low)
        return grad_query, grad_conv, later_of(spot, grad_conv, rates)

    grad_query, grad_conv, later_end = run(conv_grads, grad_got, convolved, mixed, taps, decay)
    laters = [passed(later_end, "z", -k) for k in range(1, depth)]

    def short_back(grad, weights):
        head = jnp.roll(grad[:, :, :, :2], -1, axis=1)
        whole = jnp.concatenate([grad, jnp.where(closing, 0.0, head)], axis=3)
        result = (
            weights[0] * whole[:, :, :, :-2]
            + weights[1] * whole[:, :, :, 1:-1]
            + weights[2] * whole[:, :, :, 2:]
        )
        one, two = grad[:, :, :, :1], grad[:, :, :, 1:2]
        earlier = jnp.concatenate([weights[2] * one, weights[1] * one + weights[2] * two], axis=3)
        rest = jnp.zeros(grad.shape[:3] + (extra - 2, grad.shape[-1]), wide)
        result = jnp.concatenate([result, jnp.where(opening, earlier, 0.0), rest], axis=3)
        return result.astype(low).reshape(-1, grad.shape[-1])

    feed_got = swap_slots(feed_parts)
    up_parts_got = owner_moves(run(owner_parts, up_mine))

    def conv_back(signal, grad, rates, amounts, begin, ends_later, value, weights):
        later = combine(ends_later, rates)
        grad_product, grad_residue, grad_decay = backward_of(
            spot, signal, grad, rates, amounts, begin, later
        )
        grad_product = grad_product.astype(wide)
        keys, values = (short_of(value, weights, g) for g in (1, 2))
        pair = jnp.concatenate([grad_product * values, grad_product * keys], axis=-1)
        return pair, grad_residue, grad_decay

    grad_pair, grad_residue, grad_decay = run(
        conv_back, product, grad_conv, decay, residue, start, laters, mixed, taps
    )

    up_held = run(owner_held, up_parts_got)
    up_got = moved(up_held, "y", -1)

    def in_back(query, pair, weights, v):
        result = jnp.concatenate(
            [
                short_back(query, weights[:, :channels]),
                short_back(pair, weights[:, channels:]),
            ],
            axis=1,
        )
        return result, dot_w(v, result)

    grad_mixed, in_term = run(in_back, grad_query, grad_pair, taps, normed_all)
    in_mine = scatter_tile(in_term)
    one_back = Scatter(run(lambda a, w: split_sum(dot_t(a, w, low)), grad_mixed, w_in))
    grad_mix_all = run(
        lambda got: jnp.concatenate([g[h] for h in range(2) for row in got for g in row]), mix_got
    )
    out_mine = scatter_tile(run(dot_w, gated_all, grad_mix_all))
    gate_got = owner_moves(run(owner_parts, gate_mine))
    output = run(
        lambda got, values: (
            mask
            * (values + add_up(got[0][:1], got[0][1:] + sum(got[1:], [])).reshape(batch, local, width))
        ).astype(low),
        feed_got,
        middle,
    )
    up_held = run(stacked, up_held, up_got)
    up_got = moved(up_held, "c", -1)

    def tap_sums(query, pair, value):
        sums = []
        for g, part in enumerate((query, pair[..., :channels], pair[..., channels:])):
            own = extend(value, g)
            sums += [
                jnp.sum(part * own[:, :, :, 2 - j : local + 2 - j], axis=(0, 1, 2, 3))
                for j in range(3)
            ]
        return jnp.stack(sums)

    grad_taps = run(tap_sums, grad_query, grad_pair, mixed)
    gate_held = run(owner_held, gate_got)
    gate_got = moved(gate_held, "y", -1)

    def normed_sum(rest):
        value = Scatter.sum(*rest).reshape(batch, local + extra, width)
        return value[:, :local], value[:, local : local + 2].astype(low)

    def column_whole(own, got):
        return owner_whole(lax.axis_index("c"), [own] + got, depth)

    grad_up_weight = run(column_whole, up_held, up_got)
    one_back.turn(line)
    down_held = run(lambda v: v[None], down_mine)
    down_got = moved(down_held, "y", -1)
    gate_held = run(stacked, gate_held, gate_got)
    gate_got = moved(gate_held, "c", -1)
    in_got = owner_moves(run(owner_parts, in_mine))
    grad_normed, grad_before = run(normed_sum, one_back.rest())
    grad_after = lax.ppermute(grad_before, ("z", "x"), [(j, i) for i, j in last])
    grad_gate_weight = run(column_whole, gate_held, gate_got)

    def tokens_back(grad, extension, values, scale, gain, back, small):
        values = values.astype(wide)
        grad = jnp.concatenate(
            [grad[:, : local - 2], grad[:, local - 2 :] + extension.astype(wide)], axis=1
        )
        result, grad_gain = norm_back(values, scale, gain, grad)
        gains = jnp.stack([grad_gain, small[0]]).reshape(-1, channels)
        return (result + back).astype(low), jnp.concatenate(list(small[1:]) + [gains], axis=0)

    grad_tokens, small = run(
        tokens_back,
        grad_normed,
        grad_after,
        tokens,
        scale_one,
        norm_gain,
        grad_middle,
        (grad_feed_gain, grad_residue, grad_decay, grad_taps),
    )
    small_got = moved(small, "c", 1)
    in_held = run(owner_held, in_got)
    in_got = moved(in_held, "y", -1)
    down_held = run(lambda own, got: jnp.concatenate([own] + got), down_held, down_got)
    down_got = moved(down_held, "c", -1)
    small = run(lambda v, got: v + sum(got), small, small_got)
    small_got = moved(small, "z", 1)

    def rows_whole(own, got):
        whole = in_order(jnp.swapaxes(in_order(jnp.stack([own] + got), "c"), 0, 1), "y")
        return whole.reshape(-1, width).astype(wide)

    grad_down = run(rows_whole, down_held, down_got)
    out_held = run(lambda v: v[None], out_mine)
    out_got = moved(out_held, "y", -1)
    small = run(lambda v, got: v + sum(got), small, small_got)
    small_got = moved(small, "x", -1)
    small = run(stacked, small, small_got)
    small_got = moved(small, "y", -1)
    in_held = run(stacked, in_held, in_got)
    in_got = moved(in_held, "c", -1)
    poles = decay.shape[0]

    def small_whole(own, got):
        slots = jnp.stack([own] + got)
        rows = 2 * poles + 9
        gains = jnp.sum(slots[:, :, rows:], axis=(0, 1)).reshape(2, width)
        whole = all_channels(slots[:, :, :rows])
        grad_conv_taps = jnp.concatenate(
            [whole[2 * poles + 3 * g : 2 * poles + 3 * g + 3] for g in range(3)], axis=1
        )
        return gains[0], gains[1], grad_conv_taps, whole[:poles].T, whole[poles : 2 * poles].T

    grad_norm_gain, feed_gain_sum, grad_conv_taps, residue_sum, decay_sum = run(
        small_whole, small, small_got
    )
    out_held = run(lambda own, got: jnp.concatenate([own] + got), out_held, out_got)
    out_got = moved(out_held, "c", -1)
    grad_in_weight = run(
        lambda own, got: owner_whole(lax.axis_index("c"), [own] + got, count), in_held, in_got
    )

    def out_whole(core, own, got):
        ccount = lax.axis_size("c")
        slots = jnp.stack([own] + got)
        slots = jnp.stack(
            [lax.dynamic_index_in_dim(slots, (j - core) % ccount, 0, False) for j in range(ccount)]
        )
        whole = in_order(jnp.swapaxes(slots, 0, 1), "y")
        return whole.reshape(-1, width).astype(wide)

    grad_out_weight = line.finish(out_whole, out_held, out_got)
    return (
        output,
        grad_tokens,
        grad_norm_gain,
        grad_in_weight,
        grad_conv_taps,
        residue_sum,
        decay_sum,
        grad_out_weight,
        feed_gain_sum,
        grad_gate_weight,
        grad_up_weight,
        grad_down,
    )


def solution(mesh):
    pairs, blocks = mesh.shape["dp"], mesh.shape["seq"]
    devices = mesh.devices.reshape(pairs // cores, cores, depth, blocks // depth)
    inner = Mesh(devices, ("y", "c", "z", "x"))
    dp, seq = ("y", "c"), ("z", "x")
    tokens, rows = P(dp, seq, None), P(seq, None)
    return jax.shard_map(
        body,
        mesh=inner,
        in_specs=(
            tokens,
            P(dp),
            P(),
            rows,
            P(),
            P(),
            P(),
            rows,
            P(),
            rows,
            rows,
            rows,
            tokens,
        ),
        out_specs=(tokens, tokens, P(), rows, P(), P(), P(), rows, P(), rows, rows, rows),
        check_vma=False,
    )
```

```python
import functools

import jax
import jax.numpy as jnp
from jax import lax
from jax.experimental import pallas as pl
from jax.experimental.pallas import tpu as pltpu
from jax.sharding import Mesh, PartitionSpec as P

epsilon = 1e-06
low = jnp.bfloat16
wide = jnp.float32
tile = 8
depth = 4
cores = 2


def turned(value, axis, by):
    length = lax.axis_size(axis)
    return lax.ppermute(value, axis, [(i, (i + by) % length) for i in range(length)])


def passed(value, axis, by):
    length = lax.axis_size(axis)
    pairs = [(i, i + by) for i in range(length) if 0 <= i + by < length]
    return lax.ppermute(value, axis, pairs)


def swap_slots(slots):
    ycount, spread = lax.axis_size("y"), lax.axis_size("x")
    result = []
    for dy in range(ycount):
        line = []
        for dx in range(spread):
            sy, sx = (ycount - dy) % ycount, (spread - dx) % spread
            if sy == 0 and sx == 0:
                line.append(slots[0][0])
                continue
            pairs = [
                (i * spread + j, (i + sy) % ycount * spread + (j + sx) % spread)
                for i in range(ycount)
                for j in range(spread)
            ]
            line.append(lax.ppermute(slots[sy][sx], ("y", "x"), pairs))
        result.append(line)
    return result


class Line:
    def __init__(self, token):
        self.token = token

    def run(self, work, *values):
        values, token = lax.optimization_barrier((values, self.token))
        result, self.token = lax.optimization_barrier((work(*values), token))
        return result

    def finish(self, work, *values):
        values, token = lax.optimization_barrier((values, self.token))
        return work(token, *values)


def moved(value, axis, sign):
    return [turned(value, axis, sign * d) for d in range(1, lax.axis_size(axis))]


class Gather:
    def __init__(self, first, second):
        self.held = (first, second)
        self.got = (moved(first, "x", -1), moved(second, "y", -1))

    def turn(self, line):
        self.held = line.run(
            lambda held, got: tuple(jnp.stack([h] + g) for h, g in zip(held, got)), self.held, self.got
        )
        self.got = (moved(self.held[0], "y", -1), moved(self.held[1], "x", -1))

    def end(self, line):
        def work(held, got):
            first = jnp.stack([held[0]] + got[0])
            second = jnp.swapaxes(jnp.stack([held[1]] + got[1]), 0, 1)
            return jnp.stack([first, second]).reshape(-1, first.shape[-1])

        return line.run(work, self.held, self.got)


def split_sum(partial):
    grid = partial.reshape(2, lax.axis_size("y"), lax.axis_size("x"), -1, partial.shape[-1])
    first = [grid[0][:, d].astype(low) for d in range(grid.shape[2])]
    second = [grid[1][d].astype(low) for d in range(grid.shape[1])]
    return first, second


def add_up(parts, got):
    total = parts[0].astype(wide)
    for g in got:
        total = total + g.astype(wide)
    return total


class Scatter:
    def __init__(self, parts):
        self.parts = parts
        self.send("x", "y")

    def send(self, *axes):
        self.got = [
            [turned(p, axis, d + 1) for d, p in enumerate(part[1:])]
            for part, axis in zip(self.parts, axes)
        ]

    def turn(self, line):
        def work(parts, got):
            result = []
            for part, g in zip(parts, got):
                total = add_up(part, g).astype(low)
                result.append([total[d] for d in range(total.shape[0])])
            return result

        self.parts = line.run(work, self.parts, self.got)
        self.send("y", "x")

    def rest(self):
        return self.parts, self.got

    @staticmethod
    def sum(parts, got):
        return jnp.stack([add_up(part, g) for part, g in zip(parts, got)])


def pick_kernel(count, part, stride, start_ref, source, *refs):
    targets, sems = refs[:-1], refs[-1]
    copies = []
    for d, target in enumerate(targets):
        for k in range(count):
            at = pl.multiple_of((k * stride + start_ref[d]) * part, part)
            copies.append(
                pltpu.make_async_copy(
                    source.at[:, pl.ds(at, part)],
                    target.at[:, k * part : (k + 1) * part],
                    sems.at[d * count + k],
                )
            )
    for copy in copies:
        copy.start()
    for copy in copies:
        copy.wait()


def column_pieces(weight, groups):
    spread, ycount = lax.axis_size("x"), lax.axis_size("y")
    rows = weight.shape[0]
    count = groups * depth
    part = weight.shape[1] // (count * spread * ycount)
    starts = [
        (lax.axis_index("x") + d) % spread * ycount + lax.axis_index("y") for d in range(spread)
    ]
    if part % 128 == 0:
        return pl.pallas_call(
            functools.partial(pick_kernel, count, part, spread * ycount),
            out_shape=[jax.ShapeDtypeStruct((rows, count * part), weight.dtype)] * spread,
            grid_spec=pltpu.PrefetchScalarGridSpec(
                num_scalar_prefetch=1,
                in_specs=[pl.BlockSpec(memory_space=pl.ANY)],
                out_specs=[pl.BlockSpec(memory_space=pltpu.VMEM)] * spread,
                scratch_shapes=[pltpu.SemaphoreType.DMA((count * spread,))],
            ),
            cost_estimate=pl.CostEstimate(
                flops=0, transcendentals=0, bytes_accessed=4 * rows * count * part * spread
            ),
        )(jnp.stack(starts).astype(jnp.int32), weight)
    return [
        jnp.concatenate(
            [
                lax.dynamic_slice_in_dim(weight, (k * spread * ycount + start) * part, part, 1)
                for k in range(count)
            ],
            axis=1,
        )
        for start in starts
    ]


def column_moves(pieces):
    spread, ccount = lax.axis_size("x"), lax.axis_size("c")
    share = spread // ccount
    got = [pieces[0]]
    for d in range(1, spread):
        pairs = [
            (i // share * spread + i, i // share * spread + (i + d) % spread) for i in range(spread)
        ]
        got.append(lax.ppermute(pieces[d], ("c", "x"), pairs))
    return got


def column_block(got):
    spread, ccount = lax.axis_size("x"), lax.axis_size("c")
    share = spread // ccount
    place, core = lax.axis_index("x"), lax.axis_index("c")
    got = jnp.stack(got)
    return jnp.concatenate(
        [
            lax.dynamic_index_in_dim(got, (place - core * share - j) % spread, 0, False)
            for j in range(share)
        ]
    )


def row_block(weight):
    ycount, ccount = lax.axis_size("y"), lax.axis_size("c")
    part = weight.shape[0] // (ycount * ccount)
    pair = lax.axis_index("y") * ccount + lax.axis_index("c")
    return lax.dynamic_slice_in_dim(weight, pair * part, part, 0)


def core_halves(value):
    ccount = lax.axis_size("c")
    width = value.shape[1] // ccount
    core = lax.axis_index("c")
    return [
        lax.dynamic_slice_in_dim(value, (core + d) % ccount * width, width, 1)
        for d in range(ccount)
    ]


def out_block(weight):
    part = weight.shape[0] // lax.axis_size("y")
    rows = lax.dynamic_slice_in_dim(weight, lax.axis_index("y") * part, part, 0)
    return core_halves(rows)[0]


def gather_tile(block):
    return lax.all_gather(block, ("z", "c"), axis=0, tiled=True)


def scatter_tile(term):
    return lax.psum_scatter(term, ("z", "c"), scatter_dimension=0, tiled=True)


def owner_parts(mine):
    spread, ccount = lax.axis_size("x"), lax.axis_size("c")
    share = spread // ccount
    place, core = lax.axis_index("x"), lax.axis_index("c")
    parts = mine.reshape(share, -1, mine.shape[-1])
    return [
        lax.dynamic_index_in_dim(
            parts, jnp.clip((place + d) % spread - core * share, 0, share - 1), 0, False
        )
        for d in range(spread)
    ]


def owner_moves(parts):
    spread, ccount = lax.axis_size("x"), lax.axis_size("c")
    share = spread // ccount
    got = [parts[0]]
    for d in range(1, spread):
        pairs = [
            ((i + d) % spread // share * spread + i, i // share * spread + (i + d) % spread)
            for i in range(spread)
        ]
        got.append(lax.ppermute(parts[d], ("c", "x"), pairs))
    return got


def owner_held(got):
    spread, ccount = lax.axis_size("x"), lax.axis_size("c")
    share = spread // ccount
    place, core = lax.axis_index("x"), lax.axis_index("c")
    got = jnp.stack(got)
    return jnp.stack(
        [
            lax.dynamic_index_in_dim(got, (place - core * share - j) % spread, 0, False)
            for j in range(share)
        ]
    )


def assemble_kernel(count, width, order_ref, *refs):
    sources, target = refs[:-1], refs[-1]
    part = width // count
    ranks = order_ref.shape[0] // 2
    for r in range(ranks):
        core, slot = order_ref[2 * r], order_ref[2 * r + 1]
        value = sources[0][slot]
        for c in range(1, len(sources)):
            value = jnp.where(core == c, sources[c][slot], value)
        value = value.astype(wide)
        for at in range(count):
            start = (at * ranks + r) * part
            target[:, start : start + part] = value[:, at * part : (at + 1) * part]


def owner_whole(core, sources, count):
    spread, ccount, ycount = lax.axis_size("x"), lax.axis_size("c"), lax.axis_size("y")
    share = spread // ccount
    yplace = lax.axis_index("y")
    order = []
    for i in range(spread):
        for k in range(ycount):
            order += [(i // share - core) % ccount, (k - yplace) % ycount * share + i % share]
    sources = [v.reshape((-1,) + v.shape[2:]) for v in sources]
    held, rows, width = sources[0].shape
    block = min(rows, 64)
    return pl.pallas_call(
        functools.partial(assemble_kernel, count, width),
        out_shape=jax.ShapeDtypeStruct((rows, width * spread * ycount), wide),
        grid_spec=pltpu.PrefetchScalarGridSpec(
            num_scalar_prefetch=1,
            grid=(rows // block,),
            in_specs=[pl.BlockSpec((held, block, width), lambda i, order: (0, i, 0))]
            * len(sources),
            out_specs=pl.BlockSpec((block, width * spread * ycount), lambda i, order: (i, 0)),
        ),
        compiler_params=pltpu.CompilerParams(vmem_limit_bytes=56 << 20),
        cost_estimate=pl.CostEstimate(
            flops=0, transcendentals=0, bytes_accessed=6 * rows * width * spread * ycount
        ),
    )(jnp.stack(order).astype(jnp.int32), *sources)


def in_order(slots, axis):
    length = lax.axis_size(axis)
    place = lax.axis_index(axis)
    return jnp.stack(
        [lax.dynamic_index_in_dim(slots, (j - place) % length, 0, False) for j in range(length)]
    )


def rank_rows(values, axis):
    spread, ycount = lax.axis_size("x"), lax.axis_size("y")
    part = values.shape[axis] // (depth * spread * ycount)
    place = lax.axis_index("x") * ycount + lax.axis_index("y")
    return jnp.concatenate(
        [
            lax.dynamic_slice_in_dim(values, (k * spread * ycount + place) * part, part, axis)
            for k in range(depth)
        ],
        axis=axis,
    )


def all_channels(slots):
    whole = in_order(slots, "y")
    whole = in_order(jnp.swapaxes(whole, 0, 1), "x")
    spread, ycount, rows = whole.shape[:3]
    whole = whole.reshape(spread, ycount, rows, depth, -1)
    return jnp.transpose(whole, (2, 3, 0, 1, 4)).reshape(rows, -1)


def fill(source, target, place):
    groups, parts, inner, length = source.shape[:4]
    for j in range(parts):
        slot = lax.rem(j + parts - place, parts)
        for g in range(groups):
            for b in range(inner):
                target[g * inner + b, j * length : (j + 1) * length, :] = source[g, slot, b].astype(
                    wide
                )


def empty(source, target, place):
    groups, parts, inner, length = target.shape[:4]
    for j in range(parts):
        slot = lax.rem(j + parts - place, parts)
        for g in range(groups):
            for b in range(inner):
                target[g, slot, b] = source[g * inner + b, j * length : (j + 1) * length, :].astype(
                    low
                )


def halves(ref):
    return [ref[k * tile : (k + 1) * tile, :] for k in range(ref.shape[0] // tile)]


def row_of(ref, seq, at):
    return ref[seq, pl.ds(at, tile, stride=0), :]


def states_kernel(place_ref, signal_ref, decay_ref, state_ref, held):
    fill(signal_ref, held, place_ref[0])
    seqs, length, lanes = held.shape
    keep = [jnp.exp(-d) for d in halves(decay_ref)]
    count = len(keep)

    def step(i, carry):
        state = list(carry)
        for k in range(tile):
            for n in range(seqs):
                new = row_of(held, n, i * tile + k)
                for h in range(count):
                    at = n * count + h
                    state[at] = keep[h] * state[at] + new
        return tuple(state)

    zero = jnp.zeros((tile, lanes), wide)
    state = lax.fori_loop(0, length // tile, step, tuple(zero for _ in range(seqs * count)))
    for n in range(seqs):
        for h in range(count):
            state_ref[n, h * tile : (h + 1) * tile, :] = state[n * count + h]


def forward_kernel(place_ref, signal_ref, decay_ref, residue_ref, start_ref, out_ref, held, terms, made):
    fill(signal_ref, held, place_ref[0])
    seqs, length, lanes = held.shape
    keep = [jnp.exp(-d) for d in halves(decay_ref)]
    weigh = halves(residue_ref)
    count = len(keep)

    def step(i, carry):
        state = list(carry)
        for k in range(tile):
            for n in range(seqs):
                new = row_of(held, n, i * tile + k)
                total = None
                for h in range(count):
                    at = n * count + h
                    state[at] = keep[h] * state[at] + new
                    term = weigh[h] * state[at]
                    total = term if total is None else total + term
                terms[n, k * tile : (k + 1) * tile, :] = total
        for n in range(seqs):
            result = terms[n, pl.ds(0, tile, stride=tile), :]
            for p in range(1, tile):
                result = result + terms[n, pl.ds(p, tile, stride=tile), :]
            made[n, pl.ds(i * tile, tile), :] = result
        return tuple(state)

    start = tuple(
        start_ref[n, h * tile : (h + 1) * tile, :] for n in range(seqs) for h in range(count)
    )
    lax.fori_loop(0, length // tile, step, start)
    empty(made, out_ref, place_ref[0])


def later_kernel(place_ref, signal_ref, decay_ref, state_ref, held):
    fill(signal_ref, held, place_ref[0])
    seqs, length, lanes = held.shape
    keep = [jnp.exp(-d) for d in halves(decay_ref)]
    count = len(keep)

    def step(i, carry):
        state = list(carry)
        base = length - tile - i * tile
        for k in range(tile - 1, -1, -1):
            for n in range(seqs):
                new = row_of(held, n, base + k)
                for h in range(count):
                    at = n * count + h
                    state[at] = keep[h] * state[at] + new
        return tuple(state)

    zero = jnp.zeros((tile, lanes), wide)
    state = lax.fori_loop(0, length // tile, step, tuple(zero for _ in range(seqs * count)))
    for n in range(seqs):
        for h in range(count):
            state_ref[n, h * tile : (h + 1) * tile, :] = state[n * count + h]


def backward_kernel(
    place_ref,
    signal_ref,
    grad_ref,
    decay_ref,
    residue_ref,
    start_ref,
    end_ref,
    out_ref,
    residue_grad_ref,
    decay_grad_ref,
    held,
    grads,
    terms,
    made,
    later,
):
    fill(signal_ref, held, place_ref[0])
    fill(grad_ref, grads, place_ref[0])
    seqs, length, lanes = held.shape
    keep = [jnp.exp(-d) for d in halves(decay_ref)]
    weigh = halves(residue_ref)
    count = len(keep)
    group = later.shape[0]
    zero = jnp.zeros((tile, lanes), wide)
    none = tuple(zero for _ in range(group * count))
    sum_first = [zero] * count
    sum_second = [zero] * count
    for base_seq in range(0, seqs, group):

        def load(ref):
            return tuple(
                ref[base_seq + n, h * tile : (h + 1) * tile, :]
                for n in range(group)
                for h in range(count)
            )

        def back_step(i, carry):
            state, first = [list(v) for v in carry]
            base = length - tile - i * tile
            for k in range(tile - 1, -1, -1):
                for n in range(group):
                    back = row_of(grads, base_seq + n, base + k)
                    new = row_of(held, base_seq + n, base + k)
                    total = None
                    for h in range(count):
                        at = n * count + h
                        state[at] = keep[h] * state[at] + back
                        first[at] = first[at] + new * state[at]
                        later[n, pl.ds(((base + k) * count + h) * tile, tile), :] = state[at]
                        term = weigh[h] * state[at]
                        total = term if total is None else total + term
                    terms[n, k * tile : (k + 1) * tile, :] = total
            for n in range(group):
                result = terms[n, pl.ds(0, tile, stride=tile), :]
                for p in range(1, tile):
                    result = result + terms[n, pl.ds(p, tile, stride=tile), :]
                made[base_seq + n, pl.ds(base, tile), :] = result
            return tuple(state), tuple(first)

        _, first = lax.fori_loop(0, length // tile, back_step, (load(end_ref), none))

        def ahead(i, carry):
            state, second = [list(v) for v in carry]
            for k in range(tile):
                for n in range(group):
                    new = row_of(held, base_seq + n, i * tile + k)
                    for h in range(count):
                        at = n * count + h
                        state[at] = keep[h] * state[at] + new
                        other = later[n, pl.ds(((i * tile + k) * count + h) * tile, tile), :]
                        second[at] = second[at] + state[at] * other
            return tuple(state), tuple(second)

        _, second = lax.fori_loop(0, length // tile, ahead, (load(start_ref), none))
        for n in range(group):
            for h in range(count):
                at = n * count + h
                sum_first[h] = sum_first[h] + first[at]
                sum_second[h] = sum_second[h] + (second[at] - first[at])
    for h in range(count):
        residue_grad_ref[h * tile : (h + 1) * tile, :] = sum_first[h]
        decay_grad_ref[h * tile : (h + 1) * tile, :] = -weigh[h] * sum_second[h]
    empty(made, out_ref, place_ref[0])


def conv_call(kernel, place, arrays, results, scratch, flops):
    channels = arrays[0].shape[-1]
    lanes = min(channels, 128)

    def spec(shape):
        lead = len(shape) - 1
        return pl.BlockSpec(shape[:-1] + (lanes,), lambda i, *_: (0,) * lead + (i,))

    return pl.pallas_call(
        kernel,
        out_shape=results,
        grid_spec=pltpu.PrefetchScalarGridSpec(
            num_scalar_prefetch=1,
            grid=(channels // lanes,),
            in_specs=[spec(a.shape) for a in arrays],
            out_specs=[spec(r.shape) for r in results],
            scratch_shapes=[pltpu.VMEM(s + (lanes,), wide) for s in scratch],
        ),
        compiler_params=pltpu.CompilerParams(
            dimension_semantics=("arbitrary",), vmem_limit_bytes=56 << 20
        ),
        cost_estimate=pl.CostEstimate(
            flops=flops, transcendentals=0, bytes_accessed=sum(a.size * 4 for a in arrays)
        ),
    )(place, *arrays)


def sizes(signal, poles):
    groups, parts, inner, length, channels = signal.shape
    return groups * inner, parts * length, channels, signal.size * poles


def states_of(place, signal, decay):
    seqs, length, channels, work = sizes(signal, decay.shape[0])
    shape = jax.ShapeDtypeStruct((seqs, decay.shape[0], channels), wide)
    return conv_call(states_kernel, place, [signal, decay], [shape], [(seqs, length)], 2 * work)[0]


def forward_of(place, signal, decay, residue, start):
    seqs, length, channels, work = sizes(signal, decay.shape[0])
    return conv_call(
        forward_kernel,
        place,
        [signal, decay, residue, start],
        [jax.ShapeDtypeStruct(signal.shape, low)],
        [(seqs, length), (seqs, tile * tile), (seqs, length)],
        4 * work,
    )[0]


def later_of(place, signal, decay):
    seqs, length, channels, work = sizes(signal, decay.shape[0])
    shape = jax.ShapeDtypeStruct((seqs, decay.shape[0], channels), wide)
    return conv_call(later_kernel, place, [signal, decay], [shape], [(seqs, length)], 2 * work)[0]


def backward_of(place, signal, grad, decay, residue, start, end):
    poles = decay.shape[0]
    seqs, length, channels, work = sizes(signal, poles)
    shape = jax.ShapeDtypeStruct(decay.shape, wide)
    group = min(seqs, 4)
    return conv_call(
        backward_kernel,
        place,
        [signal, grad, decay, residue, start, end],
        [jax.ShapeDtypeStruct(signal.shape, low), shape, shape],
        [
            (seqs, length),
            (seqs, length),
            (group, tile * tile),
            (seqs, length),
            (group, length * poles),
        ],
        12 * work,
    )


def rms_scale(values):
    return lax.rsqrt(jnp.mean(values * values, axis=-1, keepdims=True) + epsilon)


def norm_back(values, scale, gain, grad_normed):
    grad_gain = jnp.sum(grad_normed * values * scale, axis=(0, 1))
    scaled = grad_normed * gain
    grad_values = scale * scaled - values * scale * scale * scale * jnp.mean(
        scaled * values, axis=-1, keepdims=True
    )
    return (grad_values, grad_gain)


def dot(a, b, kind=wide):
    return jnp.dot(a, b, preferred_element_type=wide).astype(kind)


def dot_t(a, b, kind=wide):
    return lax.dot_general(a, b, (((1,), (1,)), ((), ())), preferred_element_type=wide).astype(kind)


def dot_w(a, b):
    return lax.dot_general(a, b, (((0,), (0,)), ((), ())), preferred_element_type=wide).astype(low)


def body(
    tokens,
    lengths,
    norm_gain,
    in_weight,
    conv_taps,
    filter_residue,
    filter_decay,
    out_weight,
    feed_gain,
    gate_weight,
    up_weight,
    down_weight,
    cotangent,
):
    spread, ycount = lax.axis_size("x"), lax.axis_size("y")
    batch, local, width = tokens.shape
    place = lax.axis_index("z") * spread + lax.axis_index("x")
    position = place * local + jnp.arange(local)
    mask = (position[None, :] < lengths[:, None]).astype(wide)[..., None]
    block = spread * local

    count = 3 * depth
    extra = 8
    line = Line(lax.axis_index("c"))
    run = line.run

    def stacked(value, got):
        return jnp.stack([value] + got)

    w_out = lax.all_gather(run(out_block, out_weight), "z", axis=0, tiled=True)
    in_got = column_moves(run(lambda w: column_pieces(w, 3), in_weight))
    last = [(i * spread + spread - 1, (i + 1) * spread) for i in range(depth - 1)]

    def norm_one(values, gain):
        values = values.astype(wide)
        scale = rms_scale(values)
        normed = (values * scale * gain).astype(low)
        return normed, normed[:, local - 2 :], scale

    normed, ending, scale_one = run(norm_one, tokens, norm_gain)
    before = lax.ppermute(ending, ("z", "x"), last)

    def lengthen(values, rows):
        rest = jnp.zeros((batch, extra - 2, width), values.dtype)
        values = jnp.concatenate([values, rows, rest], axis=1)
        return values[: batch // 2], values[batch // 2 :]

    normed_move = Gather(*run(lengthen, normed, before))
    gate_got = column_moves(run(lambda w: column_pieces(w, 1), gate_weight))
    in_block, w_out = run(lambda got, w: (column_block(got), w), in_got, w_out)
    w_in = gather_tile(in_block)
    normed_move.turn(line)
    w_down = gather_tile(run(row_block, down_weight))

    def feed_grad(values):
        values = (values.astype(wide) * mask).astype(low)
        return values[: batch // 2], values[batch // 2 :]

    feed_move = Gather(*run(feed_grad, cotangent))
    up_got = column_moves(run(lambda w: column_pieces(w, 1), up_weight))
    normed_all = normed_move.end(line)
    feed_move.turn(line)

    channels = w_in.shape[1] // 3
    half = channels // 2
    grid = (2 * ycount, spread, batch // 2, local)

    def rank_values(all_taps, all_decay, all_residue):
        return (
            jnp.concatenate(
                [rank_rows(all_taps[:, g * width : (g + 1) * width], 1) for g in range(3)], axis=1
            ),
            rank_rows(all_decay, 0).T,
            rank_rows(all_residue, 0).T,
        )

    taps, decay, residue = run(rank_values, conv_taps, filter_decay, filter_residue)
    opening = (lax.axis_index("x") + jnp.arange(spread)) % spread == 0
    opening = opening[None, :, None, None, None]
    closing = (lax.axis_index("x") + jnp.arange(spread)) % spread == spread - 1
    closing = closing[None, :, None, None, None]

    def project(v, w):
        return dot(v, w, low).reshape(grid[:3] + (local + extra, 3 * channels))

    mixed = run(project, normed_all, w_in)

    def extend(value, g):
        own = value[..., g * channels : (g + 1) * channels]
        earlier = jnp.roll(own[:, :, :, local - 2 : local], 1, axis=1)
        earlier = jnp.where(opening, own[:, :, :, local : local + 2], earlier)
        return jnp.concatenate([earlier, own[:, :, :, :local]], axis=3).astype(wide)

    def short_of(value, weights, g):
        longer = extend(value, g)
        own = weights[:, g * channels : (g + 1) * channels]
        return own[0] * longer[:, :, :, 2:] + own[1] * longer[:, :, :, 1:-1] + own[2] * longer[:, :, :, :-2]

    spot = lax.axis_index("x").astype(jnp.int32).reshape(1)

    def multiply(value, weights, rates):
        keys, values = (short_of(value, weights, g) for g in (1, 2))
        product = (keys * values).astype(low)
        return product, states_of(spot, product, rates)

    product, state_end = run(multiply, mixed, taps, decay)
    states = [passed(state_end, "z", k) for k in range(1, depth)]
    both_blocks = run(lambda a, b: jnp.stack([column_block(a), column_block(b)]), gate_got, up_got)
    both = lax.all_gather(both_blocks, ("z", "c"), axis=1, tiled=True)
    out_move = Gather(*run(lambda w: (w[None, : w.shape[0] // 2], w[None, w.shape[0] // 2 :]), w_out))
    grad_feed_all = feed_move.end(line)
    out_move.turn(line)

    def combine(parts, rates):
        total = parts[0]
        for k in range(1, depth - 1):
            total = total + jnp.exp(-rates * (k * block)) * parts[k]
        return total

    def convolve(parts, value, weights, signal, rates, amounts):
        start = combine(parts, rates)
        result = forward_of(spot, signal, rates, amounts, start)
        query = short_of(value, weights, 0)
        gated = (query * result.astype(wide)).astype(low)
        slots = gated.reshape(2, ycount, spread, -1, channels)
        return (
            start,
            result,
            [[slots[:, k, i].reshape(-1, channels) for i in range(spread)] for k in range(ycount)],
        )

    start, convolved, gated = run(
        convolve, states, mixed, taps, product, decay, residue
    )
    gated_got = swap_slots(gated)
    out_own = out_move.end(line)
    w_out = [out_own] + moved(out_own, "c", -1)

    def mix(got, weights, values, gain):
        own = jnp.concatenate(
            [g[:, h * half : (h + 1) * half] for h in range(2) for row in got for g in row], axis=1
        )
        mixer = in_order(jnp.stack([dot(own, w) for w in weights]), "c")
        mixer = jnp.concatenate([m for m in mixer], axis=1).reshape(batch, local, width)
        middle = values.astype(wide) + mixer
        scale = rms_scale(middle)
        normed = (middle * scale * gain).astype(low)
        return middle, scale, normed[: batch // 2], normed[batch // 2 :]

    middle, scale_two, first, second = run(mix, gated_got, w_out, tokens, feed_gain)

    two_move = Gather(first, second)
    grad_active = run(dot_t, grad_feed_all, w_down)
    two_move.turn(line)
    normed_two_all = two_move.end(line)

    def open_gate(v, w, back):
        value = dot(v, w[0])
        return value, (back * value * jax.nn.sigmoid(value)).astype(low)

    gate, grad_upper = run(open_gate, normed_two_all, both, grad_active)
    up_term = run(dot_w, normed_two_all, grad_upper)
    up_mine = scatter_tile(up_term)

    def activate(v, w, value, back):
        upper = dot(v, w[1])
        sigma = jax.nn.sigmoid(value)
        return (
            (value * sigma * upper).astype(low),
            (back * upper * sigma * (1.0 + value * (1.0 - sigma))).astype(low),
        )

    active, grad_gate = run(activate, normed_two_all, both, gate, grad_active)
    two_back = Scatter(
        run(
            lambda a, b, w: split_sum((dot_t(a, w[0]) + dot_t(b, w[1])).astype(low)),
            grad_gate,
            grad_upper,
            both,
        )
    )
    gate_mine = scatter_tile(run(dot_w, normed_two_all, grad_gate))
    two_back.turn(line)

    def feed_slots(a, w):
        value = dot(a, w, low).reshape(2, ycount, spread, -1, width)
        return [[value[:, k, i] for i in range(spread)] for k in range(ycount)]

    feed_parts = run(feed_slots, active, w_down)

    def middle_back(rest, values, scale, gain, back, weights):
        grad_normed = Scatter.sum(*rest).reshape(batch, local, width)
        result, grad_gain = norm_back(values, scale, gain, grad_normed)
        result = result + back.astype(wide) * mask
        parts = core_halves(result.astype(low).reshape(-1, width))
        own = sum(dot_t(m, w) for m, w in zip(parts, weights)).astype(low)
        ranks = ycount * spread

        def slot(at):
            pieces = [
                own[:, (h * ranks + at) * half : (h * ranks + at + 1) * half] for h in range(2)
            ]
            return jnp.concatenate(pieces, axis=1)

        slots = [[slot(k * spread + i) for i in range(spread)] for k in range(ycount)]
        rounded = result.astype(low)
        return result, grad_gain, rounded.reshape(-1, width), slots

    grad_middle, grad_feed_gain, grad_mix, grad_slots = run(
        middle_back, two_back.rest(), middle, scale_two, feed_gain, cotangent, w_out
    )
    grad_got = swap_slots(grad_slots)
    down_mine = scatter_tile(run(dot_w, active, grad_feed_all))
    mix_got = swap_slots([[grad_mix] * spread] * ycount)

    def conv_grads(got, result, value, weights, rates):
        grad = jnp.stack([jnp.stack(row) for row in got])
        grad = grad.reshape(ycount, spread, 2, batch // 2, local, channels)
        grad = jnp.moveaxis(grad, 2, 0).reshape(grid + (channels,)).astype(wide)
        grad_query = grad * result.astype(wide)
        grad_conv = (grad * short_of(value, weights, 0)).astype(low)
        return grad_query, grad_conv, later_of(spot, grad_conv, rates)

    grad_query, grad_conv, later_end = run(conv_grads, grad_got, convolved, mixed, taps, decay)
    laters = [passed(later_end, "z", -k) for k in range(1, depth)]

    def short_back(grad, weights):
        head = jnp.roll(grad[:, :, :, :2], -1, axis=1)
        whole = jnp.concatenate([grad, jnp.where(closing, 0.0, head)], axis=3)
        result = (
            weights[0] * whole[:, :, :, :-2]
            + weights[1] * whole[:, :, :, 1:-1]
            + weights[2] * whole[:, :, :, 2:]
        )
        one, two = grad[:, :, :, :1], grad[:, :, :, 1:2]
        earlier = jnp.concatenate([weights[2] * one, weights[1] * one + weights[2] * two], axis=3)
        rest = jnp.zeros(grad.shape[:3] + (extra - 2, grad.shape[-1]), wide)
        result = jnp.concatenate([result, jnp.where(opening, earlier, 0.0), rest], axis=3)
        return result.astype(low).reshape(-1, grad.shape[-1])

    feed_got = swap_slots(feed_parts)
    up_parts_got = owner_moves(run(owner_parts, up_mine))

    def conv_back(signal, grad, rates, amounts, begin, ends_later, value, weights):
        later = combine(ends_later, rates)
        grad_product, grad_residue, grad_decay = backward_of(
            spot, signal, grad, rates, amounts, begin, later
        )
        grad_product = grad_product.astype(wide)
        keys, values = (short_of(value, weights, g) for g in (1, 2))
        pair = jnp.concatenate([grad_product * values, grad_product * keys], axis=-1)
        return pair, grad_residue, grad_decay

    grad_pair, grad_residue, grad_decay = run(
        conv_back, product, grad_conv, decay, residue, start, laters, mixed, taps
    )

    up_held = run(owner_held, up_parts_got)
    up_got = moved(up_held, "y", -1)

    def in_back(query, pair, weights, v):
        result = jnp.concatenate(
            [
                short_back(query, weights[:, :channels]),
                short_back(pair, weights[:, channels:]),
            ],
            axis=1,
        )
        return result, dot_w(v, result)

    grad_mixed, in_term = run(in_back, grad_query, grad_pair, taps, normed_all)
    in_mine = scatter_tile(in_term)
    one_back = Scatter(run(lambda a, w: split_sum(dot_t(a, w, low)), grad_mixed, w_in))
    grad_mix_all, gated_all = run(
        lambda got, own: (
            jnp.concatenate([g for row in got for g in row]),
            jnp.concatenate([g for row in own for g in row]),
        ),
        mix_got,
        gated,
    )
    out_mine = scatter_tile(run(dot_w, gated_all, grad_mix_all))
    gate_got = owner_moves(run(owner_parts, gate_mine))
    up_held = run(stacked, up_held, up_got)
    up_got = moved(up_held, "c", -1)

    def tap_sums(query, pair, value):
        sums = []
        for g, part in enumerate((query, pair[..., :channels], pair[..., channels:])):
            own = extend(value, g)
            sums += [
                jnp.sum(part * own[:, :, :, 2 - j : local + 2 - j], axis=(0, 1, 2, 3))
                for j in range(3)
            ]
        return jnp.stack(sums)

    grad_taps = run(tap_sums, grad_query, grad_pair, mixed)
    one_back.turn(line)
    gate_held = run(owner_held, gate_got)
    gate_got = moved(gate_held, "y", -1)

    def column_whole(own, got):
        return owner_whole(lax.axis_index("c"), [own] + got, depth)

    grad_up_weight = run(column_whole, up_held, up_got)
    output = run(
        lambda got, values: (
            mask
            * (values + add_up(got[0][:1], got[0][1:] + sum(got[1:], [])).reshape(batch, local, width))
        ).astype(low),
        feed_got,
        middle,
    )

    def normed_sum(rest):
        value = Scatter.sum(*rest).reshape(batch, local + extra, width)
        return value[:, :local], value[:, local : local + 2].astype(low)

    grad_normed, grad_before = run(normed_sum, one_back.rest())
    grad_after = lax.ppermute(grad_before, ("z", "x"), [(j, i) for i, j in last])
    down_held = run(lambda v: v[None], down_mine)
    down_got = moved(down_held, "y", -1)
    gate_held = run(stacked, gate_held, gate_got)
    gate_got = moved(gate_held, "c", -1)
    in_got = owner_moves(run(owner_parts, in_mine))

    def tokens_back(grad, extension, values, scale, gain, back, small):
        values = values.astype(wide)
        grad = jnp.concatenate(
            [grad[:, : local - 2], grad[:, local - 2 :] + extension.astype(wide)], axis=1
        )
        result, grad_gain = norm_back(values, scale, gain, grad)
        gains = jnp.stack([grad_gain, small[0]]).reshape(-1, channels)
        return (result + back).astype(low), jnp.concatenate(list(small[1:]) + [gains], axis=0)

    grad_tokens, small = run(
        tokens_back,
        grad_normed,
        grad_after,
        tokens,
        scale_one,
        norm_gain,
        grad_middle,
        (grad_feed_gain, grad_residue, grad_decay, grad_taps),
    )
    small_got = moved(small, "c", 1)
    grad_gate_weight = run(column_whole, gate_held, gate_got)
    in_held = run(owner_held, in_got)
    in_got = moved(in_held, "y", -1)
    down_held = run(lambda own, got: jnp.concatenate([own] + got), down_held, down_got)
    down_got = moved(down_held, "c", -1)
    small = run(lambda v, got: v + sum(got), small, small_got)
    small_got = moved(small, "z", 1)

    def rows_whole(own, got):
        whole = in_order(jnp.swapaxes(in_order(jnp.stack([own] + got), "c"), 0, 1), "y")
        return whole.reshape(-1, width).astype(wide)

    grad_down = run(rows_whole, down_held, down_got)
    small = run(lambda v, got: v + sum(got), small, small_got)
    small_got = moved(small, "x", -1)
    in_held = run(stacked, in_held, in_got)
    in_got = moved(in_held, "c", -1)
    out_held = run(lambda v: v[None], out_mine)
    out_got = moved(out_held, "y", -1)
    small = run(stacked, small, small_got)
    small_got = moved(small, "y", -1)
    grad_in_weight = run(
        lambda own, got: owner_whole(lax.axis_index("c"), [own] + got, count), in_held, in_got
    )
    out_held = run(lambda own, got: jnp.concatenate([own] + got), out_held, out_got)
    out_got = moved(out_held, "c", -1)
    poles = decay.shape[0]

    def small_whole(own, got):
        slots = jnp.stack([own] + got)
        rows = 2 * poles + 9
        gains = jnp.sum(slots[:, :, rows:], axis=(0, 1)).reshape(2, width)
        whole = all_channels(slots[:, :, :rows])
        grad_conv_taps = jnp.concatenate(
            [whole[2 * poles + 3 * g : 2 * poles + 3 * g + 3] for g in range(3)], axis=1
        )
        return gains[0], gains[1], grad_conv_taps, whole[:poles].T, whole[poles : 2 * poles].T

    grad_norm_gain, feed_gain_sum, grad_conv_taps, residue_sum, decay_sum = run(
        small_whole, small, small_got
    )

    def out_whole(core, own, got):
        ccount = lax.axis_size("c")
        slots = jnp.stack([own] + got)
        slots = jnp.stack(
            [lax.dynamic_index_in_dim(slots, (j - core) % ccount, 0, False) for j in range(ccount)]
        )
        whole = in_order(jnp.swapaxes(slots, 0, 1), "y")
        return whole.reshape(-1, width).astype(wide)

    grad_out_weight = line.finish(out_whole, out_held, out_got)
    return (
        output,
        grad_tokens,
        grad_norm_gain,
        grad_in_weight,
        grad_conv_taps,
        residue_sum,
        decay_sum,
        grad_out_weight,
        feed_gain_sum,
        grad_gate_weight,
        grad_up_weight,
        grad_down,
    )


def solution(mesh):
    pairs, blocks = mesh.shape["dp"], mesh.shape["seq"]
    devices = mesh.devices.reshape(pairs // cores, cores, depth, blocks // depth)
    inner = Mesh(devices, ("y", "c", "z", "x"))
    dp, seq = ("y", "c"), ("z", "x")
    tokens, rows = P(dp, seq, None), P(seq, None)
    return jax.shard_map(
        body,
        mesh=inner,
        in_specs=(
            tokens,
            P(dp),
            P(),
            rows,
            P(),
            P(),
            P(),
            rows,
            P(),
            rows,
            rows,
            rows,
            tokens,
        ),
        out_specs=(tokens, tokens, P(), rows, P(), P(), P(), rows, P(), rows, rows, rows),
        check_vma=False,
    )
```

```python
import functools

import jax
import jax.numpy as jnp
from jax import lax
from jax.experimental import pallas as pl
from jax.experimental.pallas import tpu as pltpu
from jax.sharding import Mesh, PartitionSpec as P

epsilon = 1e-06
low = jnp.bfloat16
wide = jnp.float32
tile = 8
depth = 4
cores = 2


def turned(value, axis, by):
    length = lax.axis_size(axis)
    return lax.ppermute(value, axis, [(i, (i + by) % length) for i in range(length)])


def passed(value, axis, by):
    length = lax.axis_size(axis)
    pairs = [(i, i + by) for i in range(length) if 0 <= i + by < length]
    return lax.ppermute(value, axis, pairs)


def swap_slots(slots):
    ycount, spread = lax.axis_size("y"), lax.axis_size("x")
    result = []
    for dy in range(ycount):
        line = []
        for dx in range(spread):
            sy, sx = (ycount - dy) % ycount, (spread - dx) % spread
            if sy == 0 and sx == 0:
                line.append(slots[0][0])
                continue
            pairs = [
                (i * spread + j, (i + sy) % ycount * spread + (j + sx) % spread)
                for i in range(ycount)
                for j in range(spread)
            ]
            line.append(lax.ppermute(slots[sy][sx], ("y", "x"), pairs))
        result.append(line)
    return result


class Line:
    def __init__(self, token):
        self.token = token

    def run(self, work, *values):
        values, token = lax.optimization_barrier((values, self.token))
        result, self.token = lax.optimization_barrier((work(*values), token))
        return result

    def finish(self, work, *values):
        values, token = lax.optimization_barrier((values, self.token))
        return work(token, *values)


def moved(value, axis, sign):
    return [turned(value, axis, sign * d) for d in range(1, lax.axis_size(axis))]


class Gather:
    def __init__(self, first, second):
        self.held = (first, second)
        self.got = (moved(first, "x", -1), moved(second, "y", -1))

    def turn(self, line):
        self.held = line.run(
            lambda held, got: tuple(jnp.stack([h] + g) for h, g in zip(held, got)), self.held, self.got
        )
        self.got = (moved(self.held[0], "y", -1), moved(self.held[1], "x", -1))

    def end(self, line):
        def work(held, got):
            first = jnp.stack([held[0]] + got[0])
            second = jnp.swapaxes(jnp.stack([held[1]] + got[1]), 0, 1)
            return jnp.stack([first, second]).reshape(-1, first.shape[-1])

        return line.run(work, self.held, self.got)


def split_sum(partial):
    grid = partial.reshape(2, lax.axis_size("y"), lax.axis_size("x"), -1, partial.shape[-1])
    first = [grid[0][:, d].astype(low) for d in range(grid.shape[2])]
    second = [grid[1][d].astype(low) for d in range(grid.shape[1])]
    return first, second


def add_up(parts, got):
    total = parts[0].astype(wide)
    for g in got:
        total = total + g.astype(wide)
    return total


class Scatter:
    def __init__(self, parts):
        self.parts = parts
        self.send("x", "y")

    def send(self, *axes):
        self.got = [
            [turned(p, axis, d + 1) for d, p in enumerate(part[1:])]
            for part, axis in zip(self.parts, axes)
        ]

    def turn(self, line):
        def work(parts, got):
            result = []
            for part, g in zip(parts, got):
                total = add_up(part, g).astype(low)
                result.append([total[d] for d in range(total.shape[0])])
            return result

        self.parts = line.run(work, self.parts, self.got)
        self.send("y", "x")

    def rest(self):
        return self.parts, self.got

    @staticmethod
    def sum(parts, got):
        return jnp.stack([add_up(part, g) for part, g in zip(parts, got)])


def pick_kernel(count, part, stride, start_ref, source, *refs):
    targets, sems = refs[:-1], refs[-1]
    copies = []
    for d, target in enumerate(targets):
        for k in range(count):
            at = pl.multiple_of((k * stride + start_ref[d]) * part, part)
            copies.append(
                pltpu.make_async_copy(
                    source.at[:, pl.ds(at, part)],
                    target.at[:, k * part : (k + 1) * part],
                    sems.at[d * count + k],
                )
            )
    for copy in copies:
        copy.start()
    for copy in copies:
        copy.wait()


def column_pieces(weight, groups):
    spread, ycount = lax.axis_size("x"), lax.axis_size("y")
    rows = weight.shape[0]
    count = groups * depth
    part = weight.shape[1] // (count * spread * ycount)
    starts = [
        (lax.axis_index("x") + d) % spread * ycount + lax.axis_index("y") for d in range(spread)
    ]
    if part % 128 == 0:
        return pl.pallas_call(
            functools.partial(pick_kernel, count, part, spread * ycount),
            out_shape=[jax.ShapeDtypeStruct((rows, count * part), weight.dtype)] * spread,
            grid_spec=pltpu.PrefetchScalarGridSpec(
                num_scalar_prefetch=1,
                in_specs=[pl.BlockSpec(memory_space=pl.ANY)],
                out_specs=[pl.BlockSpec(memory_space=pltpu.VMEM)] * spread,
                scratch_shapes=[pltpu.SemaphoreType.DMA((count * spread,))],
            ),
            cost_estimate=pl.CostEstimate(
                flops=0, transcendentals=0, bytes_accessed=4 * rows * count * part * spread
            ),
        )(jnp.stack(starts).astype(jnp.int32), weight)
    return [
        jnp.concatenate(
            [
                lax.dynamic_slice_in_dim(weight, (k * spread * ycount + start) * part, part, 1)
                for k in range(count)
            ],
            axis=1,
        )
        for start in starts
    ]


def column_moves(pieces):
    spread, ccount = lax.axis_size("x"), lax.axis_size("c")
    share = spread // ccount
    got = [pieces[0]]
    for d in range(1, spread):
        pairs = [
            (i // share * spread + i, i // share * spread + (i + d) % spread) for i in range(spread)
        ]
        got.append(lax.ppermute(pieces[d], ("c", "x"), pairs))
    return got


def column_block(got):
    spread, ccount = lax.axis_size("x"), lax.axis_size("c")
    share = spread // ccount
    place, core = lax.axis_index("x"), lax.axis_index("c")
    got = jnp.stack(got)
    return jnp.concatenate(
        [
            lax.dynamic_index_in_dim(got, (place - core * share - j) % spread, 0, False)
            for j in range(share)
        ]
    )


def row_block(weight):
    ycount, ccount = lax.axis_size("y"), lax.axis_size("c")
    part = weight.shape[0] // (ycount * ccount)
    pair = lax.axis_index("y") * ccount + lax.axis_index("c")
    return lax.dynamic_slice_in_dim(weight, pair * part, part, 0)


def core_halves(value):
    ccount = lax.axis_size("c")
    width = value.shape[1] // ccount
    core = lax.axis_index("c")
    return [
        lax.dynamic_slice_in_dim(value, (core + d) % ccount * width, width, 1)
        for d in range(ccount)
    ]


def out_block(weight):
    part = weight.shape[0] // lax.axis_size("y")
    rows = lax.dynamic_slice_in_dim(weight, lax.axis_index("y") * part, part, 0)
    return core_halves(rows)[0]


def gather_tile(block):
    return lax.all_gather(block, ("z", "c"), axis=0, tiled=True)


def scatter_tile(term):
    return lax.psum_scatter(term, ("z", "c"), scatter_dimension=0, tiled=True)


def owner_parts(mine):
    spread, ccount = lax.axis_size("x"), lax.axis_size("c")
    share = spread // ccount
    place, core = lax.axis_index("x"), lax.axis_index("c")
    parts = mine.reshape(share, -1, mine.shape[-1])
    return [
        lax.dynamic_index_in_dim(
            parts, jnp.clip((place + d) % spread - core * share, 0, share - 1), 0, False
        )
        for d in range(spread)
    ]


def owner_moves(parts):
    spread, ccount = lax.axis_size("x"), lax.axis_size("c")
    share = spread // ccount
    got = [parts[0]]
    for d in range(1, spread):
        pairs = [
            ((i + d) % spread // share * spread + i, i // share * spread + (i + d) % spread)
            for i in range(spread)
        ]
        got.append(lax.ppermute(parts[d], ("c", "x"), pairs))
    return got


def owner_held(got):
    spread, ccount = lax.axis_size("x"), lax.axis_size("c")
    share = spread // ccount
    place, core = lax.axis_index("x"), lax.axis_index("c")
    got = jnp.stack(got)
    return jnp.stack(
        [
            lax.dynamic_index_in_dim(got, (place - core * share - j) % spread, 0, False)
            for j in range(share)
        ]
    )


def assemble_kernel(count, width, order_ref, *refs):
    sources, target = refs[:-1], refs[-1]
    part = width // count
    ranks = order_ref.shape[0] // 2
    for r in range(ranks):
        core, slot = order_ref[2 * r], order_ref[2 * r + 1]
        value = sources[0][slot]
        for c in range(1, len(sources)):
            value = jnp.where(core == c, sources[c][slot], value)
        value = value.astype(wide)
        for at in range(count):
            start = (at * ranks + r) * part
            target[:, start : start + part] = value[:, at * part : (at + 1) * part]


def owner_whole(core, sources, count):
    spread, ccount, ycount = lax.axis_size("x"), lax.axis_size("c"), lax.axis_size("y")
    share = spread // ccount
    yplace = lax.axis_index("y")
    order = []
    for i in range(spread):
        for k in range(ycount):
            order += [(i // share - core) % ccount, (k - yplace) % ycount * share + i % share]
    sources = [v.reshape((-1,) + v.shape[2:]) for v in sources]
    held, rows, width = sources[0].shape
    block = min(rows, 64)
    return pl.pallas_call(
        functools.partial(assemble_kernel, count, width),
        out_shape=jax.ShapeDtypeStruct((rows, width * spread * ycount), wide),
        grid_spec=pltpu.PrefetchScalarGridSpec(
            num_scalar_prefetch=1,
            grid=(rows // block,),
            in_specs=[pl.BlockSpec((held, block, width), lambda i, order: (0, i, 0))]
            * len(sources),
            out_specs=pl.BlockSpec((block, width * spread * ycount), lambda i, order: (i, 0)),
        ),
        compiler_params=pltpu.CompilerParams(vmem_limit_bytes=56 << 20),
        cost_estimate=pl.CostEstimate(
            flops=0, transcendentals=0, bytes_accessed=6 * rows * width * spread * ycount
        ),
    )(jnp.stack(order).astype(jnp.int32), *sources)


def in_order(slots, axis):
    length = lax.axis_size(axis)
    place = lax.axis_index(axis)
    return jnp.stack(
        [lax.dynamic_index_in_dim(slots, (j - place) % length, 0, False) for j in range(length)]
    )


def rank_rows(values, axis):
    spread, ycount = lax.axis_size("x"), lax.axis_size("y")
    part = values.shape[axis] // (depth * spread * ycount)
    place = lax.axis_index("x") * ycount + lax.axis_index("y")
    return jnp.concatenate(
        [
            lax.dynamic_slice_in_dim(values, (k * spread * ycount + place) * part, part, axis)
            for k in range(depth)
        ],
        axis=axis,
    )


def all_channels(slots):
    whole = in_order(slots, "y")
    whole = in_order(jnp.swapaxes(whole, 0, 1), "x")
    spread, ycount, rows = whole.shape[:3]
    whole = whole.reshape(spread, ycount, rows, depth, -1)
    return jnp.transpose(whole, (2, 3, 0, 1, 4)).reshape(rows, -1)


def fill(source, target, place):
    groups, parts, inner, length = source.shape[:4]
    for j in range(parts):
        slot = lax.rem(j + parts - place, parts)
        for g in range(groups):
            for b in range(inner):
                target[g * inner + b, j * length : (j + 1) * length, :] = source[g, slot, b].astype(
                    wide
                )


def empty(source, target, place):
    groups, parts, inner, length = target.shape[:4]
    for j in range(parts):
        slot = lax.rem(j + parts - place, parts)
        for g in range(groups):
            for b in range(inner):
                target[g, slot, b] = source[g * inner + b, j * length : (j + 1) * length, :].astype(
                    low
                )


def halves(ref):
    return [ref[k * tile : (k + 1) * tile, :] for k in range(ref.shape[0] // tile)]


def row_of(ref, seq, at):
    return ref[seq, pl.ds(at, tile, stride=0), :]


def states_kernel(place_ref, signal_ref, decay_ref, state_ref, held):
    fill(signal_ref, held, place_ref[0])
    seqs, length, lanes = held.shape
    keep = [jnp.exp(-d) for d in halves(decay_ref)]
    count = len(keep)

    def step(i, carry):
        state = list(carry)
        for k in range(tile):
            for n in range(seqs):
                new = row_of(held, n, i * tile + k)
                for h in range(count):
                    at = n * count + h
                    state[at] = keep[h] * state[at] + new
        return tuple(state)

    zero = jnp.zeros((tile, lanes), wide)
    state = lax.fori_loop(0, length // tile, step, tuple(zero for _ in range(seqs * count)))
    for n in range(seqs):
        for h in range(count):
            state_ref[n, h * tile : (h + 1) * tile, :] = state[n * count + h]


def forward_kernel(place_ref, signal_ref, decay_ref, residue_ref, start_ref, out_ref, held, terms, made):
    fill(signal_ref, held, place_ref[0])
    seqs, length, lanes = held.shape
    keep = [jnp.exp(-d) for d in halves(decay_ref)]
    weigh = halves(residue_ref)
    count = len(keep)

    def step(i, carry):
        state = list(carry)
        for k in range(tile):
            for n in range(seqs):
                new = row_of(held, n, i * tile + k)
                total = None
                for h in range(count):
                    at = n * count + h
                    state[at] = keep[h] * state[at] + new
                    term = weigh[h] * state[at]
                    total = term if total is None else total + term
                terms[n, k * tile : (k + 1) * tile, :] = total
        for n in range(seqs):
            result = terms[n, pl.ds(0, tile, stride=tile), :]
            for p in range(1, tile):
                result = result + terms[n, pl.ds(p, tile, stride=tile), :]
            made[n, pl.ds(i * tile, tile), :] = result
        return tuple(state)

    start = tuple(
        start_ref[n, h * tile : (h + 1) * tile, :] for n in range(seqs) for h in range(count)
    )
    lax.fori_loop(0, length // tile, step, start)
    empty(made, out_ref, place_ref[0])


def later_kernel(place_ref, signal_ref, decay_ref, state_ref, held):
    fill(signal_ref, held, place_ref[0])
    seqs, length, lanes = held.shape
    keep = [jnp.exp(-d) for d in halves(decay_ref)]
    count = len(keep)

    def step(i, carry):
        state = list(carry)
        base = length - tile - i * tile
        for k in range(tile - 1, -1, -1):
            for n in range(seqs):
                new = row_of(held, n, base + k)
                for h in range(count):
                    at = n * count + h
                    state[at] = keep[h] * state[at] + new
        return tuple(state)

    zero = jnp.zeros((tile, lanes), wide)
    state = lax.fori_loop(0, length // tile, step, tuple(zero for _ in range(seqs * count)))
    for n in range(seqs):
        for h in range(count):
            state_ref[n, h * tile : (h + 1) * tile, :] = state[n * count + h]


def backward_kernel(
    place_ref,
    signal_ref,
    grad_ref,
    decay_ref,
    residue_ref,
    start_ref,
    end_ref,
    out_ref,
    residue_grad_ref,
    decay_grad_ref,
    held,
    grads,
    terms,
    made,
    later,
):
    fill(signal_ref, held, place_ref[0])
    fill(grad_ref, grads, place_ref[0])
    seqs, length, lanes = held.shape
    keep = [jnp.exp(-d) for d in halves(decay_ref)]
    weigh = halves(residue_ref)
    count = len(keep)
    group = later.shape[0]
    zero = jnp.zeros((tile, lanes), wide)
    none = tuple(zero for _ in range(group * count))
    sum_first = [zero] * count
    sum_second = [zero] * count
    for base_seq in range(0, seqs, group):

        def load(ref):
            return tuple(
                ref[base_seq + n, h * tile : (h + 1) * tile, :]
                for n in range(group)
                for h in range(count)
            )

        def back_step(i, carry):
            state, first = [list(v) for v in carry]
            base = length - tile - i * tile
            for k in range(tile - 1, -1, -1):
                for n in range(group):
                    back = row_of(grads, base_seq + n, base + k)
                    new = row_of(held, base_seq + n, base + k)
                    total = None
                    for h in range(count):
                        at = n * count + h
                        state[at] = keep[h] * state[at] + back
                        first[at] = first[at] + new * state[at]
                        later[n, pl.ds(((base + k) * count + h) * tile, tile), :] = state[at]
                        term = weigh[h] * state[at]
                        total = term if total is None else total + term
                    terms[n, k * tile : (k + 1) * tile, :] = total
            for n in range(group):
                result = terms[n, pl.ds(0, tile, stride=tile), :]
                for p in range(1, tile):
                    result = result + terms[n, pl.ds(p, tile, stride=tile), :]
                made[base_seq + n, pl.ds(base, tile), :] = result
            return tuple(state), tuple(first)

        _, first = lax.fori_loop(0, length // tile, back_step, (load(end_ref), none))

        def ahead(i, carry):
            state, second = [list(v) for v in carry]
            for k in range(tile):
                for n in range(group):
                    new = row_of(held, base_seq + n, i * tile + k)
                    for h in range(count):
                        at = n * count + h
                        state[at] = keep[h] * state[at] + new
                        other = later[n, pl.ds(((i * tile + k) * count + h) * tile, tile), :]
                        second[at] = second[at] + state[at] * other
            return tuple(state), tuple(second)

        _, second = lax.fori_loop(0, length // tile, ahead, (load(start_ref), none))
        for n in range(group):
            for h in range(count):
                at = n * count + h
                sum_first[h] = sum_first[h] + first[at]
                sum_second[h] = sum_second[h] + (second[at] - first[at])
    for h in range(count):
        residue_grad_ref[h * tile : (h + 1) * tile, :] = sum_first[h]
        decay_grad_ref[h * tile : (h + 1) * tile, :] = -weigh[h] * sum_second[h]
    empty(made, out_ref, place_ref[0])


def conv_call(kernel, place, arrays, results, scratch, flops):
    channels = arrays[0].shape[-1]
    lanes = min(channels, 128)

    def spec(shape):
        lead = len(shape) - 1
        return pl.BlockSpec(shape[:-1] + (lanes,), lambda i, *_: (0,) * lead + (i,))

    return pl.pallas_call(
        kernel,
        out_shape=results,
        grid_spec=pltpu.PrefetchScalarGridSpec(
            num_scalar_prefetch=1,
            grid=(channels // lanes,),
            in_specs=[spec(a.shape) for a in arrays],
            out_specs=[spec(r.shape) for r in results],
            scratch_shapes=[pltpu.VMEM(s + (lanes,), wide) for s in scratch],
        ),
        compiler_params=pltpu.CompilerParams(
            dimension_semantics=("arbitrary",), vmem_limit_bytes=56 << 20
        ),
        cost_estimate=pl.CostEstimate(
            flops=flops, transcendentals=0, bytes_accessed=sum(a.size * 4 for a in arrays)
        ),
    )(place, *arrays)


def sizes(signal, poles):
    groups, parts, inner, length, channels = signal.shape
    return groups * inner, parts * length, channels, signal.size * poles


def states_of(place, signal, decay):
    seqs, length, channels, work = sizes(signal, decay.shape[0])
    shape = jax.ShapeDtypeStruct((seqs, decay.shape[0], channels), wide)
    return conv_call(states_kernel, place, [signal, decay], [shape], [(seqs, length)], 2 * work)[0]


def forward_of(place, signal, decay, residue, start):
    seqs, length, channels, work = sizes(signal, decay.shape[0])
    return conv_call(
        forward_kernel,
        place,
        [signal, decay, residue, start],
        [jax.ShapeDtypeStruct(signal.shape, low)],
        [(seqs, length), (seqs, tile * tile), (seqs, length)],
        4 * work,
    )[0]


def later_of(place, signal, decay):
    seqs, length, channels, work = sizes(signal, decay.shape[0])
    shape = jax.ShapeDtypeStruct((seqs, decay.shape[0], channels), wide)
    return conv_call(later_kernel, place, [signal, decay], [shape], [(seqs, length)], 2 * work)[0]


def backward_of(place, signal, grad, decay, residue, start, end):
    poles = decay.shape[0]
    seqs, length, channels, work = sizes(signal, poles)
    shape = jax.ShapeDtypeStruct(decay.shape, wide)
    group = min(seqs, 4)
    return conv_call(
        backward_kernel,
        place,
        [signal, grad, decay, residue, start, end],
        [jax.ShapeDtypeStruct(signal.shape, low), shape, shape],
        [
            (seqs, length),
            (seqs, length),
            (group, tile * tile),
            (seqs, length),
            (group, length * poles),
        ],
        12 * work,
    )


def rms_scale(values):
    return lax.rsqrt(jnp.mean(values * values, axis=-1, keepdims=True) + epsilon)


def norm_back(values, scale, gain, grad_normed):
    grad_gain = jnp.sum(grad_normed * values * scale, axis=(0, 1))
    scaled = grad_normed * gain
    grad_values = scale * scaled - values * scale * scale * scale * jnp.mean(
        scaled * values, axis=-1, keepdims=True
    )
    return (grad_values, grad_gain)


def dot(a, b, kind=wide):
    return jnp.dot(a, b, preferred_element_type=wide).astype(kind)


def dot_t(a, b, kind=wide):
    return lax.dot_general(a, b, (((1,), (1,)), ((), ())), preferred_element_type=wide).astype(kind)


def dot_w(a, b):
    return lax.dot_general(a, b, (((0,), (0,)), ((), ())), preferred_element_type=wide).astype(low)


def body(
    tokens,
    lengths,
    norm_gain,
    in_weight,
    conv_taps,
    filter_residue,
    filter_decay,
    out_weight,
    feed_gain,
    gate_weight,
    up_weight,
    down_weight,
    cotangent,
):
    spread, ycount = lax.axis_size("x"), lax.axis_size("y")
    batch, local, width = tokens.shape
    place = lax.axis_index("z") * spread + lax.axis_index("x")
    position = place * local + jnp.arange(local)
    mask = (position[None, :] < lengths[:, None]).astype(wide)[..., None]
    block = spread * local

    count = 3 * depth
    extra = 8
    line = Line(lax.axis_index("c"))
    run = line.run

    def stacked(value, got):
        return jnp.stack([value] + got)

    w_out = lax.all_gather(run(out_block, out_weight), "z", axis=0, tiled=True)
    in_got = column_moves(run(lambda w: column_pieces(w, 3), in_weight))
    last = [(i * spread + spread - 1, (i + 1) * spread) for i in range(depth - 1)]

    def norm_one(values, gain):
        values = values.astype(wide)
        scale = rms_scale(values)
        normed = (values * scale * gain).astype(low)
        return normed, normed[:, local - 2 :], scale

    normed, ending, scale_one = run(norm_one, tokens, norm_gain)
    before = lax.ppermute(ending, ("z", "x"), last)

    def lengthen(values, rows):
        rest = jnp.zeros((batch, extra - 2, width), values.dtype)
        values = jnp.concatenate([values, rows, rest], axis=1)
        return values[: batch // 2], values[batch // 2 :]

    normed_move = Gather(*run(lengthen, normed, before))
    gate_got = column_moves(run(lambda w: column_pieces(w, 1), gate_weight))
    in_block, w_out = run(lambda got, w: (column_block(got), w), in_got, w_out)
    w_in = gather_tile(in_block)
    normed_move.turn(line)
    w_down = gather_tile(run(row_block, down_weight))

    def feed_grad(values):
        values = (values.astype(wide) * mask).astype(low)
        return values[: batch // 2], values[batch // 2 :]

    feed_move = Gather(*run(feed_grad, cotangent))
    up_got = column_moves(run(lambda w: column_pieces(w, 1), up_weight))
    normed_all = normed_move.end(line)
    feed_move.turn(line)

    channels = w_in.shape[1] // 3
    half = channels // 2
    grid = (2 * ycount, spread, batch // 2, local)

    def rank_values(all_taps, all_decay, all_residue):
        return (
            jnp.concatenate(
                [rank_rows(all_taps[:, g * width : (g + 1) * width], 1) for g in range(3)], axis=1
            ),
            rank_rows(all_decay, 0).T,
            rank_rows(all_residue, 0).T,
        )

    taps, decay, residue = run(rank_values, conv_taps, filter_decay, filter_residue)
    opening = (lax.axis_index("x") + jnp.arange(spread)) % spread == 0
    opening = opening[None, :, None, None, None]
    closing = (lax.axis_index("x") + jnp.arange(spread)) % spread == spread - 1
    closing = closing[None, :, None, None, None]

    def project(v, w):
        return dot(v, w, low).reshape(grid[:3] + (local + extra, 3 * channels))

    mixed = run(project, normed_all, w_in)

    def extend(value, g):
        own = value[..., g * channels : (g + 1) * channels]
        earlier = jnp.roll(own[:, :, :, local - 2 : local], 1, axis=1)
        earlier = jnp.where(opening, own[:, :, :, local : local + 2], earlier)
        return jnp.concatenate([earlier, own[:, :, :, :local]], axis=3).astype(wide)

    def short_of(value, weights, g):
        longer = extend(value, g)
        own = weights[:, g * channels : (g + 1) * channels]
        return own[0] * longer[:, :, :, 2:] + own[1] * longer[:, :, :, 1:-1] + own[2] * longer[:, :, :, :-2]

    spot = lax.axis_index("x").astype(jnp.int32).reshape(1)

    def multiply(value, weights, rates):
        keys, values = (short_of(value, weights, g) for g in (1, 2))
        product = (keys * values).astype(low)
        return product, states_of(spot, product, rates)

    product, state_end = run(multiply, mixed, taps, decay)
    states = [passed(state_end, "z", k) for k in range(1, depth)]
    w_gate = gather_tile(run(column_block, gate_got))
    out_move = Gather(*run(lambda w: (w[None, : w.shape[0] // 2], w[None, w.shape[0] // 2 :]), w_out))
    grad_feed_all = feed_move.end(line)
    out_move.turn(line)

    def combine(parts, rates):
        total = parts[0]
        for k in range(1, depth - 1):
            total = total + jnp.exp(-rates * (k * block)) * parts[k]
        return total

    def convolve(parts, value, weights, signal, rates, amounts):
        start = combine(parts, rates)
        result = forward_of(spot, signal, rates, amounts, start)
        query = short_of(value, weights, 0)
        gated = (query * result.astype(wide)).astype(low)
        slots = gated.reshape(2, ycount, spread, -1, channels)
        return (
            start,
            result,
            gated.reshape(-1, channels),
            [[slots[:, k, i].reshape(-1, channels) for i in range(spread)] for k in range(ycount)],
        )

    start, convolved, gated_all, gated = run(
        convolve, states, mixed, taps, product, decay, residue
    )
    gated_got = swap_slots(gated)
    w_up = gather_tile(run(column_block, up_got))
    out_own = out_move.end(line)
    w_out = [out_own] + moved(out_own, "c", -1)

    def mix(got, weights, values, gain):
        own = jnp.concatenate(
            [g[:, h * half : (h + 1) * half] for h in range(2) for row in got for g in row], axis=1
        )
        mixer = in_order(jnp.stack([dot(own, w) for w in weights]), "c")
        mixer = jnp.concatenate([m for m in mixer], axis=1).reshape(batch, local, width)
        middle = values.astype(wide) + mixer
        scale = rms_scale(middle)
        normed = (middle * scale * gain).astype(low)
        return middle, scale, normed[: batch // 2], normed[batch // 2 :]

    middle, scale_two, first, second = run(mix, gated_got, w_out, tokens, feed_gain)

    two_move = Gather(first, second)
    grad_active = run(dot_t, grad_feed_all, w_down)
    two_move.turn(line)
    normed_two_all = two_move.end(line)

    def open_gate(v, w, back):
        value = dot(v, w)
        return value, (back * value * jax.nn.sigmoid(value)).astype(low)

    gate, grad_upper = run(open_gate, normed_two_all, w_gate, grad_active)
    up_term = run(dot_w, normed_two_all, grad_upper)
    up_mine = scatter_tile(up_term)

    def activate(v, w, value, back):
        upper = dot(v, w)
        sigma = jax.nn.sigmoid(value)
        return (
            (value * sigma * upper).astype(low),
            (back * upper * sigma * (1.0 + value * (1.0 - sigma))).astype(low),
        )

    active, grad_gate = run(activate, normed_two_all, w_up, gate, grad_active)
    two_back = Scatter(
        run(
            lambda a, b, wa, wb: split_sum((dot_t(a, wa) + dot_t(b, wb)).astype(low)),
            grad_gate,
            grad_upper,
            w_gate,
            w_up,
        )
    )
    gate_mine = scatter_tile(run(dot_w, normed_two_all, grad_gate))
    two_back.turn(line)

    def feed_slots(a, w):
        value = dot(a, w, low).reshape(2, ycount, spread, -1, width)
        return [[value[:, k, i] for i in range(spread)] for k in range(ycount)]

    feed_parts = run(feed_slots, active, w_down)

    def middle_back(rest, values, scale, gain, back, weights):
        grad_normed = Scatter.sum(*rest).reshape(batch, local, width)
        result, grad_gain = norm_back(values, scale, gain, grad_normed)
        result = result + back.astype(wide) * mask
        parts = core_halves(result.astype(low).reshape(-1, width))
        own = sum(dot_t(m, w) for m, w in zip(parts, weights)).astype(low)
        ranks = ycount * spread

        def slot(at):
            pieces = [
                own[:, (h * ranks + at) * half : (h * ranks + at + 1) * half] for h in range(2)
            ]
            return jnp.concatenate(pieces, axis=1)

        slots = [[slot(k * spread + i) for i in range(spread)] for k in range(ycount)]
        rounded = result.astype(low)
        return result, grad_gain, rounded[: batch // 2], rounded[batch // 2 :], slots

    grad_middle, grad_feed_gain, first, second, grad_slots = run(
        middle_back, two_back.rest(), middle, scale_two, feed_gain, cotangent, w_out
    )
    grad_got = swap_slots(grad_slots)
    down_mine = scatter_tile(run(dot_w, active, grad_feed_all))
    mix_move = Gather(first, second)

    def conv_grads(got, result, value, weights, rates):
        grad = jnp.stack([jnp.stack(row) for row in got])
        grad = grad.reshape(ycount, spread, 2, batch // 2, local, channels)
        grad = jnp.moveaxis(grad, 2, 0).reshape(grid + (channels,)).astype(wide)
        grad_query = grad * result.astype(wide)
        grad_conv = (grad * short_of(value, weights, 0)).astype(low)
        return grad_query, grad_conv, later_of(spot, grad_conv, rates)

    grad_query, grad_conv, later_end = run(conv_grads, grad_got, convolved, mixed, taps, decay)
    laters = [passed(later_end, "z", -k) for k in range(1, depth)]
    mix_move.turn(line)

    def short_back(grad, weights):
        head = jnp.roll(grad[:, :, :, :2], -1, axis=1)
        whole = jnp.concatenate([grad, jnp.where(closing, 0.0, head)], axis=3)
        result = (
            weights[0] * whole[:, :, :, :-2]
            + weights[1] * whole[:, :, :, 1:-1]
            + weights[2] * whole[:, :, :, 2:]
        )
        one, two = grad[:, :, :, :1], grad[:, :, :, 1:2]
        earlier = jnp.concatenate([weights[2] * one, weights[1] * one + weights[2] * two], axis=3)
        rest = jnp.zeros(grad.shape[:3] + (extra - 2, grad.shape[-1]), wide)
        result = jnp.concatenate([result, jnp.where(opening, earlier, 0.0), rest], axis=3)
        return result.astype(low).reshape(-1, grad.shape[-1])

    feed_got = swap_slots(feed_parts)
    up_parts_got = owner_moves(run(owner_parts, up_mine))
    gate_got = owner_moves(run(owner_parts, gate_mine))

    def conv_back(signal, grad, rates, amounts, begin, ends_later, value, weights):
        later = combine(ends_later, rates)
        grad_product, grad_residue, grad_decay = backward_of(
            spot, signal, grad, rates, amounts, begin, later
        )
        grad_product = grad_product.astype(wide)
        keys, values = (short_of(value, weights, g) for g in (1, 2))
        pair = jnp.concatenate([grad_product * values, grad_product * keys], axis=-1)
        return pair, grad_residue, grad_decay

    grad_pair, grad_residue, grad_decay = run(
        conv_back, product, grad_conv, decay, residue, start, laters, mixed, taps
    )

    mix_move.got = run(lambda got: got, mix_move.got)
    up_held = run(owner_held, up_parts_got)
    up_got = moved(up_held, "y", -1)

    def in_back(query, pair, weights, v):
        result = jnp.concatenate(
            [
                short_back(query, weights[:, :channels]),
                short_back(pair, weights[:, channels:]),
            ],
            axis=1,
        )
        return result, dot_w(v, result)

    grad_mixed, in_term = run(in_back, grad_query, grad_pair, taps, normed_all)
    in_mine = scatter_tile(in_term)
    gate_held = run(owner_held, gate_got)
    gate_got = moved(gate_held, "y", -1)
    one_back = Scatter(run(lambda a, w: split_sum(dot_t(a, w, low)), grad_mixed, w_in))
    grad_mix_all = mix_move.end(line)
    out_mine = scatter_tile(run(dot_w, gated_all, grad_mix_all))
    up_held = run(stacked, up_held, up_got)
    up_got = moved(up_held, "c", -1)
    gate_held = run(stacked, gate_held, gate_got)
    gate_got = moved(gate_held, "c", -1)

    def tap_sums(query, pair, value):
        sums = []
        for g, part in enumerate((query, pair[..., :channels], pair[..., channels:])):
            own = extend(value, g)
            sums += [
                jnp.sum(part * own[:, :, :, 2 - j : local + 2 - j], axis=(0, 1, 2, 3))
                for j in range(3)
            ]
        return jnp.stack(sums)

    grad_taps = run(tap_sums, grad_query, grad_pair, mixed)

    def column_whole(own, got):
        return owner_whole(lax.axis_index("c"), [own] + got, depth)

    grad_up_weight = run(column_whole, up_held, up_got)
    one_back.turn(line)
    down_held = run(lambda v: v[None], down_mine)
    down_got = moved(down_held, "y", -1)
    grad_gate_weight = run(column_whole, gate_held, gate_got)
    def normed_sum(rest):
        value = Scatter.sum(*rest).reshape(batch, local + extra, width)
        return value[:, :local], value[:, local : local + 2].astype(low)

    grad_normed, grad_before = run(normed_sum, one_back.rest())
    grad_after = lax.ppermute(grad_before, ("z", "x"), [(j, i) for i, j in last])
    in_got = owner_moves(run(owner_parts, in_mine))

    def tokens_back(grad, extension, values, scale, gain, back, small):
        values = values.astype(wide)
        grad = jnp.concatenate(
            [grad[:, : local - 2], grad[:, local - 2 :] + extension.astype(wide)], axis=1
        )
        result, grad_gain = norm_back(values, scale, gain, grad)
        gains = jnp.stack([grad_gain, small[0]]).reshape(-1, channels)
        return (result + back).astype(low), jnp.concatenate(list(small[1:]) + [gains], axis=0)

    grad_tokens, small = run(
        tokens_back,
        grad_normed,
        grad_after,
        tokens,
        scale_one,
        norm_gain,
        grad_middle,
        (grad_feed_gain, grad_residue, grad_decay, grad_taps),
    )
    small_got = moved(small, "c", 1)
    down_held = run(lambda own, got: jnp.concatenate([own] + got), down_held, down_got)
    down_got = moved(down_held, "c", -1)
    in_held = run(owner_held, in_got)
    in_got = moved(in_held, "y", -1)
    output = run(
        lambda got, values: (
            mask
            * (values + add_up(got[0][:1], got[0][1:] + sum(got[1:], [])).reshape(batch, local, width))
        ).astype(low),
        feed_got,
        middle,
    )
    small = run(lambda v, got: v + sum(got), small, small_got)
    small_got = moved(small, "z", 1)

    def rows_whole(own, got):
        whole = in_order(jnp.swapaxes(in_order(jnp.stack([own] + got), "c"), 0, 1), "y")
        return whole.reshape(-1, width).astype(wide)

    grad_down = run(rows_whole, down_held, down_got)
    small = run(lambda v, got: v + sum(got), small, small_got)
    small_got = moved(small, "x", -1)
    in_held = run(stacked, in_held, in_got)
    in_got = moved(in_held, "c", -1)
    out_held = run(lambda v: v[None], out_mine)
    out_got = moved(out_held, "y", -1)
    small = run(stacked, small, small_got)
    small_got = moved(small, "y", -1)
    grad_in_weight = run(
        lambda own, got: owner_whole(lax.axis_index("c"), [own] + got, count), in_held, in_got
    )
    out_held = run(lambda own, got: jnp.concatenate([own] + got), out_held, out_got)
    out_got = moved(out_held, "c", -1)
    poles = decay.shape[0]

    def small_whole(own, got):
        slots = jnp.stack([own] + got)
        rows = 2 * poles + 9
        gains = jnp.sum(slots[:, :, rows:], axis=(0, 1)).reshape(2, width)
        whole = all_channels(slots[:, :, :rows])
        grad_conv_taps = jnp.concatenate(
            [whole[2 * poles + 3 * g : 2 * poles + 3 * g + 3] for g in range(3)], axis=1
        )
        return gains[0], gains[1], grad_conv_taps, whole[:poles].T, whole[poles : 2 * poles].T

    grad_norm_gain, feed_gain_sum, grad_conv_taps, residue_sum, decay_sum = run(
        small_whole, small, small_got
    )

    def out_whole(core, own, got):
        ccount = lax.axis_size("c")
        slots = jnp.stack([own] + got)
        slots = jnp.stack(
            [lax.dynamic_index_in_dim(slots, (j - core) % ccount, 0, False) for j in range(ccount)]
        )
        whole = in_order(jnp.swapaxes(slots, 0, 1), "y")
        return whole.reshape(-1, width).astype(wide)

    grad_out_weight = line.finish(out_whole, out_held, out_got)
    return (
        output,
        grad_tokens,
        grad_norm_gain,
        grad_in_weight,
        grad_conv_taps,
        residue_sum,
        decay_sum,
        grad_out_weight,
        feed_gain_sum,
        grad_gate_weight,
        grad_up_weight,
        grad_down,
    )


def solution(mesh):
    pairs, blocks = mesh.shape["dp"], mesh.shape["seq"]
    devices = mesh.devices.reshape(pairs // cores, cores, depth, blocks // depth)
    inner = Mesh(devices, ("y", "c", "z", "x"))
    dp, seq = ("y", "c"), ("z", "x")
    tokens, rows = P(dp, seq, None), P(seq, None)
    return jax.shard_map(
        body,
        mesh=inner,
        in_specs=(
            tokens,
            P(dp),
            P(),
            rows,
            P(),
            P(),
            P(),
            rows,
            P(),
            rows,
            rows,
            rows,
            tokens,
        ),
        out_specs=(tokens, tokens, P(), rows, P(), P(), P(), rows, P(), rows, rows, rows),
        check_vma=False,
    )
```

```python
import functools

import jax
import jax.numpy as jnp
from jax import lax
from jax.experimental import pallas as pl
from jax.experimental.pallas import tpu as pltpu
from jax.sharding import Mesh, PartitionSpec as P

epsilon = 1e-06
low = jnp.bfloat16
wide = jnp.float32
tile = 8
depth = 4
cores = 2


def turned(value, axis, by):
    length = lax.axis_size(axis)
    return lax.ppermute(value, axis, [(i, (i + by) % length) for i in range(length)])


def passed(value, axis, by):
    length = lax.axis_size(axis)
    pairs = [(i, i + by) for i in range(length) if 0 <= i + by < length]
    return lax.ppermute(value, axis, pairs)


def swap_slots(slots):
    ycount, spread = lax.axis_size("y"), lax.axis_size("x")
    result = []
    for dy in range(ycount):
        line = []
        for dx in range(spread):
            sy, sx = (ycount - dy) % ycount, (spread - dx) % spread
            if sy == 0 and sx == 0:
                line.append(slots[0][0])
                continue
            pairs = [
                (i * spread + j, (i + sy) % ycount * spread + (j + sx) % spread)
                for i in range(ycount)
                for j in range(spread)
            ]
            line.append(lax.ppermute(slots[sy][sx], ("y", "x"), pairs))
        result.append(line)
    return result


class Line:
    def __init__(self, token):
        self.token = token

    def run(self, work, *values):
        values, token = lax.optimization_barrier((values, self.token))
        result, self.token = lax.optimization_barrier((work(*values), token))
        return result

    def finish(self, work, *values):
        values, token = lax.optimization_barrier((values, self.token))
        return work(token, *values)


def moved(value, axis, sign):
    return [turned(value, axis, sign * d) for d in range(1, lax.axis_size(axis))]


class Gather:
    def __init__(self, first, second):
        self.held = (first, second)
        self.got = (moved(first, "x", -1), moved(second, "y", -1))

    def turn(self, line):
        self.held = line.run(
            lambda held, got: tuple(jnp.stack([h] + g) for h, g in zip(held, got)), self.held, self.got
        )
        self.got = (moved(self.held[0], "y", -1), moved(self.held[1], "x", -1))

    def end(self, line):
        def work(held, got):
            first = jnp.stack([held[0]] + got[0])
            second = jnp.swapaxes(jnp.stack([held[1]] + got[1]), 0, 1)
            return jnp.stack([first, second]).reshape(-1, first.shape[-1])

        return line.run(work, self.held, self.got)


def split_sum(partial):
    grid = partial.reshape(2, lax.axis_size("y"), lax.axis_size("x"), -1, partial.shape[-1])
    first = [grid[0][:, d].astype(low) for d in range(grid.shape[2])]
    second = [grid[1][d].astype(low) for d in range(grid.shape[1])]
    return first, second


def add_up(parts, got):
    total = parts[0].astype(wide)
    for g in got:
        total = total + g.astype(wide)
    return total


class Scatter:
    def __init__(self, parts):
        self.parts = parts
        self.send("x", "y")

    def send(self, *axes):
        self.got = [
            [turned(p, axis, d + 1) for d, p in enumerate(part[1:])]
            for part, axis in zip(self.parts, axes)
        ]

    def turn(self, line):
        def work(parts, got):
            result = []
            for part, g in zip(parts, got):
                total = add_up(part, g).astype(low)
                result.append([total[d] for d in range(total.shape[0])])
            return result

        self.parts = line.run(work, self.parts, self.got)
        self.send("y", "x")

    def rest(self):
        return self.parts, self.got

    @staticmethod
    def sum(parts, got):
        return jnp.stack([add_up(part, g) for part, g in zip(parts, got)])


def pick_kernel(count, part, stride, start_ref, source, *refs):
    targets, sems = refs[:-1], refs[-1]
    copies = []
    for d, target in enumerate(targets):
        for k in range(count):
            at = pl.multiple_of((k * stride + start_ref[d]) * part, part)
            copies.append(
                pltpu.make_async_copy(
                    source.at[:, pl.ds(at, part)],
                    target.at[:, k * part : (k + 1) * part],
                    sems.at[d * count + k],
                )
            )
    for copy in copies:
        copy.start()
    for copy in copies:
        copy.wait()


def column_pieces(weight, groups):
    spread, ycount = lax.axis_size("x"), lax.axis_size("y")
    rows = weight.shape[0]
    count = groups * depth
    part = weight.shape[1] // (count * spread * ycount)
    starts = [
        (lax.axis_index("x") + d) % spread * ycount + lax.axis_index("y") for d in range(spread)
    ]
    if part % 128 == 0:
        return pl.pallas_call(
            functools.partial(pick_kernel, count, part, spread * ycount),
            out_shape=[jax.ShapeDtypeStruct((rows, count * part), weight.dtype)] * spread,
            grid_spec=pltpu.PrefetchScalarGridSpec(
                num_scalar_prefetch=1,
                in_specs=[pl.BlockSpec(memory_space=pl.ANY)],
                out_specs=[pl.BlockSpec(memory_space=pltpu.VMEM)] * spread,
                scratch_shapes=[pltpu.SemaphoreType.DMA((count * spread,))],
            ),
            cost_estimate=pl.CostEstimate(
                flops=0, transcendentals=0, bytes_accessed=4 * rows * count * part * spread
            ),
        )(jnp.stack(starts).astype(jnp.int32), weight)
    return [
        jnp.concatenate(
            [
                lax.dynamic_slice_in_dim(weight, (k * spread * ycount + start) * part, part, 1)
                for k in range(count)
            ],
            axis=1,
        )
        for start in starts
    ]


def column_moves(pieces):
    spread, ccount = lax.axis_size("x"), lax.axis_size("c")
    share = spread // ccount
    got = [pieces[0]]
    for d in range(1, spread):
        pairs = [
            (i // share * spread + i, i // share * spread + (i + d) % spread) for i in range(spread)
        ]
        got.append(lax.ppermute(pieces[d], ("c", "x"), pairs))
    return got


def column_block(got):
    spread, ccount = lax.axis_size("x"), lax.axis_size("c")
    share = spread // ccount
    place, core = lax.axis_index("x"), lax.axis_index("c")
    got = jnp.stack(got)
    return jnp.concatenate(
        [
            lax.dynamic_index_in_dim(got, (place - core * share - j) % spread, 0, False)
            for j in range(share)
        ]
    )


def row_block(weight):
    ycount, ccount = lax.axis_size("y"), lax.axis_size("c")
    part = weight.shape[0] // (ycount * ccount)
    pair = lax.axis_index("y") * ccount + lax.axis_index("c")
    return lax.dynamic_slice_in_dim(weight, pair * part, part, 0)


def core_halves(value):
    ccount = lax.axis_size("c")
    width = value.shape[1] // ccount
    core = lax.axis_index("c")
    return [
        lax.dynamic_slice_in_dim(value, (core + d) % ccount * width, width, 1)
        for d in range(ccount)
    ]


def out_block(weight):
    part = weight.shape[0] // lax.axis_size("y")
    rows = lax.dynamic_slice_in_dim(weight, lax.axis_index("y") * part, part, 0)
    return core_halves(rows)[0]


def gather_tile(block):
    return lax.all_gather(block, ("z", "c"), axis=0, tiled=True)


def scatter_tile(term):
    return lax.psum_scatter(term, ("z", "c"), scatter_dimension=0, tiled=True)


def owner_parts(mine):
    spread, ccount = lax.axis_size("x"), lax.axis_size("c")
    share = spread // ccount
    place, core = lax.axis_index("x"), lax.axis_index("c")
    parts = mine.reshape(share, -1, mine.shape[-1])
    return [
        lax.dynamic_index_in_dim(
            parts, jnp.clip((place + d) % spread - core * share, 0, share - 1), 0, False
        )
        for d in range(spread)
    ]


def owner_moves(parts):
    spread, ccount = lax.axis_size("x"), lax.axis_size("c")
    share = spread // ccount
    got = [parts[0]]
    for d in range(1, spread):
        pairs = [
            ((i + d) % spread // share * spread + i, i // share * spread + (i + d) % spread)
            for i in range(spread)
        ]
        got.append(lax.ppermute(parts[d], ("c", "x"), pairs))
    return got


def owner_held(got):
    spread, ccount = lax.axis_size("x"), lax.axis_size("c")
    share = spread // ccount
    place, core = lax.axis_index("x"), lax.axis_index("c")
    got = jnp.stack(got)
    return jnp.stack(
        [
            lax.dynamic_index_in_dim(got, (place - core * share - j) % spread, 0, False)
            for j in range(share)
        ]
    )


def assemble_kernel(count, width, order_ref, *refs):
    sources, target = refs[:-1], refs[-1]
    part = width // count
    ranks = order_ref.shape[0] // 2
    for r in range(ranks):
        core, slot = order_ref[2 * r], order_ref[2 * r + 1]
        value = sources[0][slot]
        for c in range(1, len(sources)):
            value = jnp.where(core == c, sources[c][slot], value)
        value = value.astype(wide)
        for at in range(count):
            start = (at * ranks + r) * part
            target[:, start : start + part] = value[:, at * part : (at + 1) * part]


def owner_whole(core, sources, count):
    spread, ccount, ycount = lax.axis_size("x"), lax.axis_size("c"), lax.axis_size("y")
    share = spread // ccount
    yplace = lax.axis_index("y")
    order = []
    for i in range(spread):
        for k in range(ycount):
            order += [(i // share - core) % ccount, (k - yplace) % ycount * share + i % share]
    sources = [v.reshape((-1,) + v.shape[2:]) for v in sources]
    held, rows, width = sources[0].shape
    block = min(rows, 64)
    return pl.pallas_call(
        functools.partial(assemble_kernel, count, width),
        out_shape=jax.ShapeDtypeStruct((rows, width * spread * ycount), wide),
        grid_spec=pltpu.PrefetchScalarGridSpec(
            num_scalar_prefetch=1,
            grid=(rows // block,),
            in_specs=[pl.BlockSpec((held, block, width), lambda i, order: (0, i, 0))]
            * len(sources),
            out_specs=pl.BlockSpec((block, width * spread * ycount), lambda i, order: (i, 0)),
        ),
        compiler_params=pltpu.CompilerParams(vmem_limit_bytes=56 << 20),
        cost_estimate=pl.CostEstimate(
            flops=0, transcendentals=0, bytes_accessed=6 * rows * width * spread * ycount
        ),
    )(jnp.stack(order).astype(jnp.int32), *sources)


def in_order(slots, axis):
    length = lax.axis_size(axis)
    place = lax.axis_index(axis)
    return jnp.stack(
        [lax.dynamic_index_in_dim(slots, (j - place) % length, 0, False) for j in range(length)]
    )


def rank_rows(values, axis):
    spread, ycount = lax.axis_size("x"), lax.axis_size("y")
    part = values.shape[axis] // (depth * spread * ycount)
    place = lax.axis_index("x") * ycount + lax.axis_index("y")
    return jnp.concatenate(
        [
            lax.dynamic_slice_in_dim(values, (k * spread * ycount + place) * part, part, axis)
            for k in range(depth)
        ],
        axis=axis,
    )


def all_channels(slots):
    whole = in_order(slots, "y")
    whole = in_order(jnp.swapaxes(whole, 0, 1), "x")
    spread, ycount, rows = whole.shape[:3]
    whole = whole.reshape(spread, ycount, rows, depth, -1)
    return jnp.transpose(whole, (2, 3, 0, 1, 4)).reshape(rows, -1)


def fill(source, target, place):
    groups, parts, inner, length = source.shape[:4]
    for j in range(parts):
        slot = lax.rem(j + parts - place, parts)
        for g in range(groups):
            for b in range(inner):
                target[g * inner + b, j * length : (j + 1) * length, :] = source[g, slot, b].astype(
                    wide
                )


def empty(source, target, place):
    groups, parts, inner, length = target.shape[:4]
    for j in range(parts):
        slot = lax.rem(j + parts - place, parts)
        for g in range(groups):
            for b in range(inner):
                target[g, slot, b] = source[g * inner + b, j * length : (j + 1) * length, :].astype(
                    low
                )


def halves(ref):
    return [ref[k * tile : (k + 1) * tile, :] for k in range(ref.shape[0] // tile)]


def row_of(ref, seq, at):
    return ref[seq, pl.ds(at, tile, stride=0), :]


def states_kernel(place_ref, signal_ref, decay_ref, state_ref, held):
    fill(signal_ref, held, place_ref[0])
    seqs, length, lanes = held.shape
    keep = [jnp.exp(-d) for d in halves(decay_ref)]
    count = len(keep)

    def step(i, carry):
        state = list(carry)
        for k in range(tile):
            for n in range(seqs):
                new = row_of(held, n, i * tile + k)
                for h in range(count):
                    at = n * count + h
                    state[at] = keep[h] * state[at] + new
        return tuple(state)

    zero = jnp.zeros((tile, lanes), wide)
    state = lax.fori_loop(0, length // tile, step, tuple(zero for _ in range(seqs * count)))
    for n in range(seqs):
        for h in range(count):
            state_ref[n, h * tile : (h + 1) * tile, :] = state[n * count + h]


def forward_kernel(place_ref, signal_ref, decay_ref, residue_ref, start_ref, out_ref, held, terms, made):
    fill(signal_ref, held, place_ref[0])
    seqs, length, lanes = held.shape
    keep = [jnp.exp(-d) for d in halves(decay_ref)]
    weigh = halves(residue_ref)
    count = len(keep)

    def step(i, carry):
        state = list(carry)
        for k in range(tile):
            for n in range(seqs):
                new = row_of(held, n, i * tile + k)
                total = None
                for h in range(count):
                    at = n * count + h
                    state[at] = keep[h] * state[at] + new
                    term = weigh[h] * state[at]
                    total = term if total is None else total + term
                terms[n, k * tile : (k + 1) * tile, :] = total
        for n in range(seqs):
            result = terms[n, pl.ds(0, tile, stride=tile), :]
            for p in range(1, tile):
                result = result + terms[n, pl.ds(p, tile, stride=tile), :]
            made[n, pl.ds(i * tile, tile), :] = result
        return tuple(state)

    start = tuple(
        start_ref[n, h * tile : (h + 1) * tile, :] for n in range(seqs) for h in range(count)
    )
    lax.fori_loop(0, length // tile, step, start)
    empty(made, out_ref, place_ref[0])


def later_kernel(place_ref, signal_ref, decay_ref, state_ref, held):
    fill(signal_ref, held, place_ref[0])
    seqs, length, lanes = held.shape
    keep = [jnp.exp(-d) for d in halves(decay_ref)]
    count = len(keep)

    def step(i, carry):
        state = list(carry)
        base = length - tile - i * tile
        for k in range(tile - 1, -1, -1):
            for n in range(seqs):
                new = row_of(held, n, base + k)
                for h in range(count):
                    at = n * count + h
                    state[at] = keep[h] * state[at] + new
        return tuple(state)

    zero = jnp.zeros((tile, lanes), wide)
    state = lax.fori_loop(0, length // tile, step, tuple(zero for _ in range(seqs * count)))
    for n in range(seqs):
        for h in range(count):
            state_ref[n, h * tile : (h + 1) * tile, :] = state[n * count + h]


def backward_kernel(
    place_ref,
    signal_ref,
    grad_ref,
    decay_ref,
    residue_ref,
    start_ref,
    end_ref,
    out_ref,
    residue_grad_ref,
    decay_grad_ref,
    held,
    grads,
    terms,
    made,
    later,
):
    fill(signal_ref, held, place_ref[0])
    fill(grad_ref, grads, place_ref[0])
    seqs, length, lanes = held.shape
    keep = [jnp.exp(-d) for d in halves(decay_ref)]
    weigh = halves(residue_ref)
    count = len(keep)
    group = later.shape[0]
    zero = jnp.zeros((tile, lanes), wide)
    none = tuple(zero for _ in range(group * count))
    sum_first = [zero] * count
    sum_second = [zero] * count
    for base_seq in range(0, seqs, group):

        def load(ref):
            return tuple(
                ref[base_seq + n, h * tile : (h + 1) * tile, :]
                for n in range(group)
                for h in range(count)
            )

        def back_step(i, carry):
            state, first = [list(v) for v in carry]
            base = length - tile - i * tile
            for k in range(tile - 1, -1, -1):
                for n in range(group):
                    back = row_of(grads, base_seq + n, base + k)
                    new = row_of(held, base_seq + n, base + k)
                    total = None
                    for h in range(count):
                        at = n * count + h
                        state[at] = keep[h] * state[at] + back
                        first[at] = first[at] + new * state[at]
                        later[n, pl.ds(((base + k) * count + h) * tile, tile), :] = state[at]
                        term = weigh[h] * state[at]
                        total = term if total is None else total + term
                    terms[n, k * tile : (k + 1) * tile, :] = total
            for n in range(group):
                result = terms[n, pl.ds(0, tile, stride=tile), :]
                for p in range(1, tile):
                    result = result + terms[n, pl.ds(p, tile, stride=tile), :]
                made[base_seq + n, pl.ds(base, tile), :] = result
            return tuple(state), tuple(first)

        _, first = lax.fori_loop(0, length // tile, back_step, (load(end_ref), none))

        def ahead(i, carry):
            state, second = [list(v) for v in carry]
            for k in range(tile):
                for n in range(group):
                    new = row_of(held, base_seq + n, i * tile + k)
                    for h in range(count):
                        at = n * count + h
                        state[at] = keep[h] * state[at] + new
                        other = later[n, pl.ds(((i * tile + k) * count + h) * tile, tile), :]
                        second[at] = second[at] + state[at] * other
            return tuple(state), tuple(second)

        _, second = lax.fori_loop(0, length // tile, ahead, (load(start_ref), none))
        for n in range(group):
            for h in range(count):
                at = n * count + h
                sum_first[h] = sum_first[h] + first[at]
                sum_second[h] = sum_second[h] + (second[at] - first[at])
    for h in range(count):
        residue_grad_ref[h * tile : (h + 1) * tile, :] = sum_first[h]
        decay_grad_ref[h * tile : (h + 1) * tile, :] = -weigh[h] * sum_second[h]
    empty(made, out_ref, place_ref[0])


def conv_call(kernel, place, arrays, results, scratch, flops):
    channels = arrays[0].shape[-1]
    lanes = min(channels, 128)

    def spec(shape):
        lead = len(shape) - 1
        return pl.BlockSpec(shape[:-1] + (lanes,), lambda i, *_: (0,) * lead + (i,))

    return pl.pallas_call(
        kernel,
        out_shape=results,
        grid_spec=pltpu.PrefetchScalarGridSpec(
            num_scalar_prefetch=1,
            grid=(channels // lanes,),
            in_specs=[spec(a.shape) for a in arrays],
            out_specs=[spec(r.shape) for r in results],
            scratch_shapes=[pltpu.VMEM(s + (lanes,), wide) for s in scratch],
        ),
        compiler_params=pltpu.CompilerParams(
            dimension_semantics=("arbitrary",), vmem_limit_bytes=56 << 20
        ),
        cost_estimate=pl.CostEstimate(
            flops=flops, transcendentals=0, bytes_accessed=sum(a.size * 4 for a in arrays)
        ),
    )(place, *arrays)


def sizes(signal, poles):
    groups, parts, inner, length, channels = signal.shape
    return groups * inner, parts * length, channels, signal.size * poles


def states_of(place, signal, decay):
    seqs, length, channels, work = sizes(signal, decay.shape[0])
    shape = jax.ShapeDtypeStruct((seqs, decay.shape[0], channels), wide)
    return conv_call(states_kernel, place, [signal, decay], [shape], [(seqs, length)], 2 * work)[0]


def forward_of(place, signal, decay, residue, start):
    seqs, length, channels, work = sizes(signal, decay.shape[0])
    return conv_call(
        forward_kernel,
        place,
        [signal, decay, residue, start],
        [jax.ShapeDtypeStruct(signal.shape, low)],
        [(seqs, length), (seqs, tile * tile), (seqs, length)],
        4 * work,
    )[0]


def later_of(place, signal, decay):
    seqs, length, channels, work = sizes(signal, decay.shape[0])
    shape = jax.ShapeDtypeStruct((seqs, decay.shape[0], channels), wide)
    return conv_call(later_kernel, place, [signal, decay], [shape], [(seqs, length)], 2 * work)[0]


def backward_of(place, signal, grad, decay, residue, start, end):
    poles = decay.shape[0]
    seqs, length, channels, work = sizes(signal, poles)
    shape = jax.ShapeDtypeStruct(decay.shape, wide)
    group = min(seqs, 4)
    return conv_call(
        backward_kernel,
        place,
        [signal, grad, decay, residue, start, end],
        [jax.ShapeDtypeStruct(signal.shape, low), shape, shape],
        [
            (seqs, length),
            (seqs, length),
            (group, tile * tile),
            (seqs, length),
            (group, length * poles),
        ],
        12 * work,
    )


def rms_scale(values):
    return lax.rsqrt(jnp.mean(values * values, axis=-1, keepdims=True) + epsilon)


def norm_back(values, scale, gain, grad_normed):
    grad_gain = jnp.sum(grad_normed * values * scale, axis=(0, 1))
    scaled = grad_normed * gain
    grad_values = scale * scaled - values * scale * scale * scale * jnp.mean(
        scaled * values, axis=-1, keepdims=True
    )
    return (grad_values, grad_gain)


def dot(a, b, kind=wide):
    return jnp.dot(a, b, preferred_element_type=wide).astype(kind)


def dot_t(a, b, kind=wide):
    return lax.dot_general(a, b, (((1,), (1,)), ((), ())), preferred_element_type=wide).astype(kind)


def dot_w(a, b):
    return lax.dot_general(a, b, (((0,), (0,)), ((), ())), preferred_element_type=wide).astype(low)


def body(
    tokens,
    lengths,
    norm_gain,
    in_weight,
    conv_taps,
    filter_residue,
    filter_decay,
    out_weight,
    feed_gain,
    gate_weight,
    up_weight,
    down_weight,
    cotangent,
):
    spread, ycount = lax.axis_size("x"), lax.axis_size("y")
    batch, local, width = tokens.shape
    place = lax.axis_index("z") * spread + lax.axis_index("x")
    position = place * local + jnp.arange(local)
    mask = (position[None, :] < lengths[:, None]).astype(wide)[..., None]
    block = spread * local

    count = 3 * depth
    extra = 8
    line = Line(lax.axis_index("c"))
    run = line.run

    def stacked(value, got):
        return jnp.stack([value] + got)

    w_out = lax.all_gather(run(out_block, out_weight), "z", axis=0, tiled=True)
    in_got = column_moves(run(lambda w: column_pieces(w, 3), in_weight))
    last = [(i * spread + spread - 1, (i + 1) * spread) for i in range(depth - 1)]

    def norm_one(values, gain):
        values = values.astype(wide)
        scale = rms_scale(values)
        normed = (values * scale * gain).astype(low)
        return normed, normed[:, local - 2 :], scale

    normed, ending, scale_one = run(norm_one, tokens, norm_gain)
    before = lax.ppermute(ending, ("z", "x"), last)

    def lengthen(values, rows):
        rest = jnp.zeros((batch, extra - 2, width), values.dtype)
        values = jnp.concatenate([values, rows, rest], axis=1)
        return values[: batch // 2], values[batch // 2 :]

    normed_move = Gather(*run(lengthen, normed, before))
    gate_got = column_moves(run(lambda w: column_pieces(w, 1), gate_weight))
    in_block, w_out = run(lambda got, w: (column_block(got), w), in_got, w_out)
    w_in = gather_tile(in_block)
    normed_move.turn(line)
    w_down = gather_tile(run(row_block, down_weight))
    out_move = Gather(*run(lambda w: (w[None, : w.shape[0] // 2], w[None, w.shape[0] // 2 :]), w_out))
    up_got = column_moves(run(lambda w: column_pieces(w, 1), up_weight))
    normed_all = normed_move.end(line)
    out_move.turn(line)

    channels = w_in.shape[1] // 3
    half = channels // 2
    grid = (2 * ycount, spread, batch // 2, local)

    def rank_values(all_taps, all_decay, all_residue):
        return (
            jnp.concatenate(
                [rank_rows(all_taps[:, g * width : (g + 1) * width], 1) for g in range(3)], axis=1
            ),
            rank_rows(all_decay, 0).T,
            rank_rows(all_residue, 0).T,
        )

    taps, decay, residue = run(rank_values, conv_taps, filter_decay, filter_residue)
    opening = (lax.axis_index("x") + jnp.arange(spread)) % spread == 0
    opening = opening[None, :, None, None, None]
    closing = (lax.axis_index("x") + jnp.arange(spread)) % spread == spread - 1
    closing = closing[None, :, None, None, None]

    def project(v, w):
        return dot(v, w, low).reshape(grid[:3] + (local + extra, 3 * channels))

    mixed = run(project, normed_all, w_in)

    def extend(value, g):
        own = value[..., g * channels : (g + 1) * channels]
        earlier = jnp.roll(own[:, :, :, local - 2 : local], 1, axis=1)
        earlier = jnp.where(opening, own[:, :, :, local : local + 2], earlier)
        return jnp.concatenate([earlier, own[:, :, :, :local]], axis=3).astype(wide)

    def short_of(value, weights, g):
        longer = extend(value, g)
        own = weights[:, g * channels : (g + 1) * channels]
        return own[0] * longer[:, :, :, 2:] + own[1] * longer[:, :, :, 1:-1] + own[2] * longer[:, :, :, :-2]

    spot = lax.axis_index("x").astype(jnp.int32).reshape(1)

    def multiply(value, weights, rates):
        keys, values = (short_of(value, weights, g) for g in (1, 2))
        product = (keys * values).astype(low)
        return product, states_of(spot, product, rates)

    product, state_end = run(multiply, mixed, taps, decay)
    states = [passed(state_end, "z", k) for k in range(1, depth)]
    w_gate = gather_tile(run(column_block, gate_got))
    out_own = out_move.end(line)
    w_out = [out_own] + moved(out_own, "c", -1)

    def feed_grad(values):
        values = (values.astype(wide) * mask).astype(low)
        return values[: batch // 2], values[batch // 2 :]

    feed_move = Gather(*run(feed_grad, cotangent))

    def combine(parts, rates):
        total = parts[0]
        for k in range(1, depth - 1):
            total = total + jnp.exp(-rates * (k * block)) * parts[k]
        return total

    def convolve(parts, value, weights, signal, rates, amounts):
        start = combine(parts, rates)
        result = forward_of(spot, signal, rates, amounts, start)
        query = short_of(value, weights, 0)
        gated = (query * result.astype(wide)).astype(low)
        slots = gated.reshape(2, ycount, spread, -1, channels)
        return (
            start,
            result,
            gated.reshape(-1, channels),
            [[slots[:, k, i].reshape(-1, channels) for i in range(spread)] for k in range(ycount)],
        )

    start, convolved, gated_all, gated = run(
        convolve, states, mixed, taps, product, decay, residue
    )
    gated_got = swap_slots(gated)
    w_up = gather_tile(run(column_block, up_got))
    feed_move.turn(line)

    def mix(got, weights, values, gain):
        own = jnp.concatenate(
            [g[:, h * half : (h + 1) * half] for h in range(2) for row in got for g in row], axis=1
        )
        mixer = in_order(jnp.stack([dot(own, w) for w in weights]), "c")
        mixer = jnp.concatenate([m for m in mixer], axis=1).reshape(batch, local, width)
        middle = values.astype(wide) + mixer
        scale = rms_scale(middle)
        normed = (middle * scale * gain).astype(low)
        return middle, scale, normed[: batch // 2], normed[batch // 2 :]

    middle, scale_two, first, second = run(mix, gated_got, w_out, tokens, feed_gain)

    two_move = Gather(first, second)
    two_move.turn(line)
    grad_feed_all = feed_move.end(line)
    grad_active = run(dot_t, grad_feed_all, w_down)
    normed_two_all = two_move.end(line)

    def open_gate(v, w, back):
        value = dot(v, w)
        return value, (back * value * jax.nn.sigmoid(value)).astype(low)

    gate, grad_upper = run(open_gate, normed_two_all, w_gate, grad_active)
    up_term = run(dot_w, normed_two_all, grad_upper)
    up_mine = scatter_tile(up_term)

    def activate(v, w, value, back):
        upper = dot(v, w)
        sigma = jax.nn.sigmoid(value)
        return (
            (value * sigma * upper).astype(low),
            (back * upper * sigma * (1.0 + value * (1.0 - sigma))).astype(low),
        )

    active, grad_gate = run(activate, normed_two_all, w_up, gate, grad_active)
    two_back = Scatter(
        run(
            lambda a, b, wa, wb: split_sum((dot_t(a, wa) + dot_t(b, wb)).astype(low)),
            grad_gate,
            grad_upper,
            w_gate,
            w_up,
        )
    )
    gate_mine = scatter_tile(run(dot_w, normed_two_all, grad_gate))
    two_back.turn(line)
    feed_parts = run(lambda a, w: split_sum(dot(a, w, low)), active, w_down)

    def middle_back(rest, values, scale, gain, back, weights):
        grad_normed = Scatter.sum(*rest).reshape(batch, local, width)
        result, grad_gain = norm_back(values, scale, gain, grad_normed)
        result = result + back.astype(wide) * mask
        parts = core_halves(result.astype(low).reshape(-1, width))
        own = sum(dot_t(m, w) for m, w in zip(parts, weights)).astype(low)
        ranks = ycount * spread

        def slot(at):
            pieces = [
                own[:, (h * ranks + at) * half : (h * ranks + at + 1) * half] for h in range(2)
            ]
            return jnp.concatenate(pieces, axis=1)

        slots = [[slot(k * spread + i) for i in range(spread)] for k in range(ycount)]
        rounded = result.astype(low)
        return result, grad_gain, rounded[: batch // 2], rounded[batch // 2 :], slots

    grad_middle, grad_feed_gain, first, second, grad_slots = run(
        middle_back, two_back.rest(), middle, scale_two, feed_gain, cotangent, w_out
    )
    grad_got = swap_slots(grad_slots)
    down_mine = scatter_tile(run(dot_w, active, grad_feed_all))
    mix_move = Gather(first, second)

    def conv_grads(got, result, value, weights, rates):
        grad = jnp.stack([jnp.stack(row) for row in got])
        grad = grad.reshape(ycount, spread, 2, batch // 2, local, channels)
        grad = jnp.moveaxis(grad, 2, 0).reshape(grid + (channels,)).astype(wide)
        grad_query = grad * result.astype(wide)
        grad_conv = (grad * short_of(value, weights, 0)).astype(low)
        return grad_query, grad_conv, later_of(spot, grad_conv, rates)

    grad_query, grad_conv, later_end = run(conv_grads, grad_got, convolved, mixed, taps, decay)
    laters = [passed(later_end, "z", -k) for k in range(1, depth)]
    mix_move.turn(line)

    def short_back(grad, weights):
        head = jnp.roll(grad[:, :, :, :2], -1, axis=1)
        whole = jnp.concatenate([grad, jnp.where(closing, 0.0, head)], axis=3)
        result = (
            weights[0] * whole[:, :, :, :-2]
            + weights[1] * whole[:, :, :, 1:-1]
            + weights[2] * whole[:, :, :, 2:]
        )
        one, two = grad[:, :, :, :1], grad[:, :, :, 1:2]
        earlier = jnp.concatenate([weights[2] * one, weights[1] * one + weights[2] * two], axis=3)
        rest = jnp.zeros(grad.shape[:3] + (extra - 2, grad.shape[-1]), wide)
        result = jnp.concatenate([result, jnp.where(opening, earlier, 0.0), rest], axis=3)
        return result.astype(low).reshape(-1, grad.shape[-1])

    feed_back = Scatter(feed_parts)
    up_parts_got = owner_moves(run(owner_parts, up_mine))
    gate_got = owner_moves(run(owner_parts, gate_mine))

    def conv_back(signal, grad, rates, amounts, begin, ends_later, value, weights):
        later = combine(ends_later, rates)
        grad_product, grad_residue, grad_decay = backward_of(
            spot, signal, grad, rates, amounts, begin, later
        )
        grad_product = grad_product.astype(wide)
        keys, values = (short_of(value, weights, g) for g in (1, 2))
        pair = jnp.concatenate([grad_product * values, grad_product * keys], axis=-1)
        return pair, grad_residue, grad_decay

    grad_pair, grad_residue, grad_decay = run(
        conv_back, product, grad_conv, decay, residue, start, laters, mixed, taps
    )

    mix_move.got = run(lambda got: got, mix_move.got)
    up_held = run(owner_held, up_parts_got)
    up_got = moved(up_held, "y", -1)

    def in_back(query, pair, weights, v):
        result = jnp.concatenate(
            [
                short_back(query, weights[:, :channels]),
                short_back(pair, weights[:, channels:]),
            ],
            axis=1,
        )
        return result, dot_w(v, result)

    grad_mixed, in_term = run(in_back, grad_query, grad_pair, taps, normed_all)
    in_mine = scatter_tile(in_term)
    feed_back.turn(line)
    gate_held = run(owner_held, gate_got)
    gate_got = moved(gate_held, "y", -1)
    one_back = Scatter(run(lambda a, w: split_sum(dot_t(a, w, low)), grad_mixed, w_in))
    feed_back.got = run(lambda got: got, feed_back.got)
    grad_mix_all = mix_move.end(line)
    out_mine = scatter_tile(run(dot_w, gated_all, grad_mix_all))
    up_held = run(stacked, up_held, up_got)
    up_got = moved(up_held, "c", -1)
    gate_held = run(stacked, gate_held, gate_got)
    gate_got = moved(gate_held, "c", -1)

    def tap_sums(query, pair, value):
        sums = []
        for g, part in enumerate((query, pair[..., :channels], pair[..., channels:])):
            own = extend(value, g)
            sums += [
                jnp.sum(part * own[:, :, :, 2 - j : local + 2 - j], axis=(0, 1, 2, 3))
                for j in range(3)
            ]
        return jnp.stack(sums)

    grad_taps = run(tap_sums, grad_query, grad_pair, mixed)

    def column_whole(own, got):
        return owner_whole(lax.axis_index("c"), [own] + got, depth)

    grad_up_weight = run(column_whole, up_held, up_got)
    one_back.turn(line)
    down_held = run(lambda v: v[None], down_mine)
    down_got = moved(down_held, "y", -1)
    grad_gate_weight = run(column_whole, gate_held, gate_got)
    def normed_sum(rest):
        value = Scatter.sum(*rest).reshape(batch, local + extra, width)
        return value[:, :local], value[:, local : local + 2].astype(low)

    grad_normed, grad_before = run(normed_sum, one_back.rest())
    grad_after = lax.ppermute(grad_before, ("z", "x"), [(j, i) for i, j in last])
    in_got = owner_moves(run(owner_parts, in_mine))

    def tokens_back(grad, extension, values, scale, gain, back, small):
        values = values.astype(wide)
        grad = jnp.concatenate(
            [grad[:, : local - 2], grad[:, local - 2 :] + extension.astype(wide)], axis=1
        )
        result, grad_gain = norm_back(values, scale, gain, grad)
        gains = jnp.stack([grad_gain, small[0]]).reshape(-1, channels)
        return (result + back).astype(low), jnp.concatenate(list(small[1:]) + [gains], axis=0)

    grad_tokens, small = run(
        tokens_back,
        grad_normed,
        grad_after,
        tokens,
        scale_one,
        norm_gain,
        grad_middle,
        (grad_feed_gain, grad_residue, grad_decay, grad_taps),
    )
    small_got = moved(small, "c", 1)
    down_held = run(lambda own, got: jnp.concatenate([own] + got), down_held, down_got)
    down_got = moved(down_held, "c", -1)
    in_held = run(owner_held, in_got)
    in_got = moved(in_held, "y", -1)
    output = run(
        lambda rest, values: (
            mask * (values + Scatter.sum(*rest).reshape(batch, local, width))
        ).astype(low),
        feed_back.rest(),
        middle,
    )
    small = run(lambda v, got: v + sum(got), small, small_got)
    small_got = moved(small, "z", 1)

    def rows_whole(own, got):
        whole = in_order(jnp.swapaxes(in_order(jnp.stack([own] + got), "c"), 0, 1), "y")
        return whole.reshape(-1, width).astype(wide)

    grad_down = run(rows_whole, down_held, down_got)
    small = run(lambda v, got: v + sum(got), small, small_got)
    small_got = moved(small, "x", -1)
    in_held = run(stacked, in_held, in_got)
    in_got = moved(in_held, "c", -1)
    out_held = run(lambda v: v[None], out_mine)
    out_got = moved(out_held, "y", -1)
    small = run(stacked, small, small_got)
    small_got = moved(small, "y", -1)
    grad_in_weight = run(
        lambda own, got: owner_whole(lax.axis_index("c"), [own] + got, count), in_held, in_got
    )
    out_held = run(lambda own, got: jnp.concatenate([own] + got), out_held, out_got)
    out_got = moved(out_held, "c", -1)
    poles = decay.shape[0]

    def small_whole(own, got):
        slots = jnp.stack([own] + got)
        rows = 2 * poles + 9
        gains = jnp.sum(slots[:, :, rows:], axis=(0, 1)).reshape(2, width)
        whole = all_channels(slots[:, :, :rows])
        grad_conv_taps = jnp.concatenate(
            [whole[2 * poles + 3 * g : 2 * poles + 3 * g + 3] for g in range(3)], axis=1
        )
        return gains[0], gains[1], grad_conv_taps, whole[:poles].T, whole[poles : 2 * poles].T

    grad_norm_gain, feed_gain_sum, grad_conv_taps, residue_sum, decay_sum = run(
        small_whole, small, small_got
    )

    def out_whole(core, own, got):
        ccount = lax.axis_size("c")
        slots = jnp.stack([own] + got)
        slots = jnp.stack(
            [lax.dynamic_index_in_dim(slots, (j - core) % ccount, 0, False) for j in range(ccount)]
        )
        whole = in_order(jnp.swapaxes(slots, 0, 1), "y")
        return whole.reshape(-1, width).astype(wide)

    grad_out_weight = line.finish(out_whole, out_held, out_got)
    return (
        output,
        grad_tokens,
        grad_norm_gain,
        grad_in_weight,
        grad_conv_taps,
        residue_sum,
        decay_sum,
        grad_out_weight,
        feed_gain_sum,
        grad_gate_weight,
        grad_up_weight,
        grad_down,
    )


def solution(mesh):
    pairs, blocks = mesh.shape["dp"], mesh.shape["seq"]
    devices = mesh.devices.reshape(pairs // cores, cores, depth, blocks // depth)
    inner = Mesh(devices, ("y", "c", "z", "x"))
    dp, seq = ("y", "c"), ("z", "x")
    tokens, rows = P(dp, seq, None), P(seq, None)
    return jax.shard_map(
        body,
        mesh=inner,
        in_specs=(
            tokens,
            P(dp),
            P(),
            rows,
            P(),
            P(),
            P(),
            rows,
            P(),
            rows,
            rows,
            rows,
            tokens,
        ),
        out_specs=(tokens, tokens, P(), rows, P(), P(), P(), rows, P(), rows, rows, rows),
        check_vma=False,
    )
```

```python
import functools

import jax
import jax.numpy as jnp
from jax import lax
from jax.experimental import pallas as pl
from jax.experimental.pallas import tpu as pltpu
from jax.sharding import Mesh, PartitionSpec as P

epsilon = 1e-06
low = jnp.bfloat16
wide = jnp.float32
tile = 8
depth = 4
cores = 2


def turned(value, axis, by):
    length = lax.axis_size(axis)
    return lax.ppermute(value, axis, [(i, (i + by) % length) for i in range(length)])


def passed(value, axis, by):
    length = lax.axis_size(axis)
    pairs = [(i, i + by) for i in range(length) if 0 <= i + by < length]
    return lax.ppermute(value, axis, pairs)


def swap_slots(slots):
    ycount, spread = lax.axis_size("y"), lax.axis_size("x")
    result = []
    for dy in range(ycount):
        line = []
        for dx in range(spread):
            sy, sx = (ycount - dy) % ycount, (spread - dx) % spread
            if sy == 0 and sx == 0:
                line.append(slots[0][0])
                continue
            pairs = [
                (i * spread + j, (i + sy) % ycount * spread + (j + sx) % spread)
                for i in range(ycount)
                for j in range(spread)
            ]
            line.append(lax.ppermute(slots[sy][sx], ("y", "x"), pairs))
        result.append(line)
    return result


class Line:
    def __init__(self, token):
        self.token = token

    def run(self, work, *values):
        values, token = lax.optimization_barrier((values, self.token))
        result, self.token = lax.optimization_barrier((work(*values), token))
        return result

    def finish(self, work, *values):
        values, token = lax.optimization_barrier((values, self.token))
        return work(token, *values)


def moved(value, axis, sign):
    return [turned(value, axis, sign * d) for d in range(1, lax.axis_size(axis))]


class Gather:
    def __init__(self, first, second):
        self.held = (first, second)
        self.got = (moved(first, "x", -1), moved(second, "y", -1))

    def turn(self, line):
        self.held = line.run(
            lambda held, got: tuple(jnp.stack([h] + g) for h, g in zip(held, got)), self.held, self.got
        )
        self.got = (moved(self.held[0], "y", -1), moved(self.held[1], "x", -1))

    def end(self, line):
        def work(held, got):
            first = jnp.stack([held[0]] + got[0])
            second = jnp.swapaxes(jnp.stack([held[1]] + got[1]), 0, 1)
            return jnp.stack([first, second]).reshape(-1, first.shape[-1])

        return line.run(work, self.held, self.got)


def split_sum(partial):
    grid = partial.reshape(2, lax.axis_size("y"), lax.axis_size("x"), -1, partial.shape[-1])
    first = [grid[0][:, d].astype(low) for d in range(grid.shape[2])]
    second = [grid[1][d].astype(low) for d in range(grid.shape[1])]
    return first, second


def add_up(parts, got):
    total = parts[0].astype(wide)
    for g in got:
        total = total + g.astype(wide)
    return total


class Scatter:
    def __init__(self, parts):
        self.parts = parts
        self.send("x", "y")

    def send(self, *axes):
        self.got = [
            [turned(p, axis, d + 1) for d, p in enumerate(part[1:])]
            for part, axis in zip(self.parts, axes)
        ]

    def turn(self, line):
        def work(parts, got):
            result = []
            for part, g in zip(parts, got):
                total = add_up(part, g).astype(low)
                result.append([total[d] for d in range(total.shape[0])])
            return result

        self.parts = line.run(work, self.parts, self.got)
        self.send("y", "x")

    def rest(self):
        return self.parts, self.got

    @staticmethod
    def sum(parts, got):
        return jnp.stack([add_up(part, g) for part, g in zip(parts, got)])


def pick_kernel(count, part, stride, start_ref, source, *refs):
    targets, sems = refs[:-1], refs[-1]
    copies = []
    for d, target in enumerate(targets):
        for k in range(count):
            at = pl.multiple_of((k * stride + start_ref[d]) * part, part)
            copies.append(
                pltpu.make_async_copy(
                    source.at[:, pl.ds(at, part)],
                    target.at[:, k * part : (k + 1) * part],
                    sems.at[d * count + k],
                )
            )
    for copy in copies:
        copy.start()
    for copy in copies:
        copy.wait()


def column_pieces(weight, groups):
    spread, ycount = lax.axis_size("x"), lax.axis_size("y")
    rows = weight.shape[0]
    count = groups * depth
    part = weight.shape[1] // (count * spread * ycount)
    starts = [
        (lax.axis_index("x") + d) % spread * ycount + lax.axis_index("y") for d in range(spread)
    ]
    if part % 128 == 0:
        return pl.pallas_call(
            functools.partial(pick_kernel, count, part, spread * ycount),
            out_shape=[jax.ShapeDtypeStruct((rows, count * part), weight.dtype)] * spread,
            grid_spec=pltpu.PrefetchScalarGridSpec(
                num_scalar_prefetch=1,
                in_specs=[pl.BlockSpec(memory_space=pl.ANY)],
                out_specs=[pl.BlockSpec(memory_space=pltpu.VMEM)] * spread,
                scratch_shapes=[pltpu.SemaphoreType.DMA((count * spread,))],
            ),
            cost_estimate=pl.CostEstimate(
                flops=0, transcendentals=0, bytes_accessed=4 * rows * count * part * spread
            ),
        )(jnp.stack(starts).astype(jnp.int32), weight)
    return [
        jnp.concatenate(
            [
                lax.dynamic_slice_in_dim(weight, (k * spread * ycount + start) * part, part, 1)
                for k in range(count)
            ],
            axis=1,
        )
        for start in starts
    ]


def column_moves(pieces):
    spread, ccount = lax.axis_size("x"), lax.axis_size("c")
    share = spread // ccount
    got = [pieces[0]]
    for d in range(1, spread):
        pairs = [
            (i // share * spread + i, i // share * spread + (i + d) % spread) for i in range(spread)
        ]
        got.append(lax.ppermute(pieces[d], ("c", "x"), pairs))
    return got


def column_block(got):
    spread, ccount = lax.axis_size("x"), lax.axis_size("c")
    share = spread // ccount
    place, core = lax.axis_index("x"), lax.axis_index("c")
    got = jnp.stack(got)
    return jnp.concatenate(
        [
            lax.dynamic_index_in_dim(got, (place - core * share - j) % spread, 0, False)
            for j in range(share)
        ]
    )


def row_block(weight):
    ycount, ccount = lax.axis_size("y"), lax.axis_size("c")
    part = weight.shape[0] // (ycount * ccount)
    pair = lax.axis_index("y") * ccount + lax.axis_index("c")
    return lax.dynamic_slice_in_dim(weight, pair * part, part, 0)


def core_halves(value):
    ccount = lax.axis_size("c")
    width = value.shape[1] // ccount
    core = lax.axis_index("c")
    return [
        lax.dynamic_slice_in_dim(value, (core + d) % ccount * width, width, 1)
        for d in range(ccount)
    ]


def out_block(weight):
    part = weight.shape[0] // lax.axis_size("y")
    rows = lax.dynamic_slice_in_dim(weight, lax.axis_index("y") * part, part, 0)
    return core_halves(rows)[0]


def gather_tile(block):
    return lax.all_gather(block, ("z", "c"), axis=0, tiled=True)


def scatter_tile(term):
    return lax.psum_scatter(term, ("z", "c"), scatter_dimension=0, tiled=True)


def owner_parts(mine):
    spread, ccount = lax.axis_size("x"), lax.axis_size("c")
    share = spread // ccount
    place, core = lax.axis_index("x"), lax.axis_index("c")
    parts = mine.reshape(share, -1, mine.shape[-1])
    return [
        lax.dynamic_index_in_dim(
            parts, jnp.clip((place + d) % spread - core * share, 0, share - 1), 0, False
        )
        for d in range(spread)
    ]


def owner_moves(parts):
    spread, ccount = lax.axis_size("x"), lax.axis_size("c")
    share = spread // ccount
    got = [parts[0]]
    for d in range(1, spread):
        pairs = [
            ((i + d) % spread // share * spread + i, i // share * spread + (i + d) % spread)
            for i in range(spread)
        ]
        got.append(lax.ppermute(parts[d], ("c", "x"), pairs))
    return got


def owner_held(got):
    spread, ccount = lax.axis_size("x"), lax.axis_size("c")
    share = spread // ccount
    place, core = lax.axis_index("x"), lax.axis_index("c")
    got = jnp.stack(got)
    return jnp.stack(
        [
            lax.dynamic_index_in_dim(got, (place - core * share - j) % spread, 0, False)
            for j in range(share)
        ]
    )


def assemble_kernel(count, width, order_ref, *refs):
    sources, target = refs[:-1], refs[-1]
    part = width // count
    ranks = order_ref.shape[0] // 2
    for r in range(ranks):
        core, slot = order_ref[2 * r], order_ref[2 * r + 1]
        value = sources[0][slot]
        for c in range(1, len(sources)):
            value = jnp.where(core == c, sources[c][slot], value)
        value = value.astype(wide)
        for at in range(count):
            start = (at * ranks + r) * part
            target[:, start : start + part] = value[:, at * part : (at + 1) * part]


def owner_whole(core, sources, count):
    spread, ccount, ycount = lax.axis_size("x"), lax.axis_size("c"), lax.axis_size("y")
    share = spread // ccount
    yplace = lax.axis_index("y")
    order = []
    for i in range(spread):
        for k in range(ycount):
            order += [(i // share - core) % ccount, (k - yplace) % ycount * share + i % share]
    sources = [v.reshape((-1,) + v.shape[2:]) for v in sources]
    held, rows, width = sources[0].shape
    block = min(rows, 64)
    return pl.pallas_call(
        functools.partial(assemble_kernel, count, width),
        out_shape=jax.ShapeDtypeStruct((rows, width * spread * ycount), wide),
        grid_spec=pltpu.PrefetchScalarGridSpec(
            num_scalar_prefetch=1,
            grid=(rows // block,),
            in_specs=[pl.BlockSpec((held, block, width), lambda i, order: (0, i, 0))]
            * len(sources),
            out_specs=pl.BlockSpec((block, width * spread * ycount), lambda i, order: (i, 0)),
        ),
        compiler_params=pltpu.CompilerParams(vmem_limit_bytes=56 << 20),
        cost_estimate=pl.CostEstimate(
            flops=0, transcendentals=0, bytes_accessed=6 * rows * width * spread * ycount
        ),
    )(jnp.stack(order).astype(jnp.int32), *sources)


def in_order(slots, axis):
    length = lax.axis_size(axis)
    place = lax.axis_index(axis)
    return jnp.stack(
        [lax.dynamic_index_in_dim(slots, (j - place) % length, 0, False) for j in range(length)]
    )


def rank_rows(values, axis):
    spread, ycount = lax.axis_size("x"), lax.axis_size("y")
    part = values.shape[axis] // (depth * spread * ycount)
    place = lax.axis_index("x") * ycount + lax.axis_index("y")
    return jnp.concatenate(
        [
            lax.dynamic_slice_in_dim(values, (k * spread * ycount + place) * part, part, axis)
            for k in range(depth)
        ],
        axis=axis,
    )


def all_channels(slots):
    whole = in_order(slots, "y")
    whole = in_order(jnp.swapaxes(whole, 0, 1), "x")
    spread, ycount, rows = whole.shape[:3]
    whole = whole.reshape(spread, ycount, rows, depth, -1)
    return jnp.transpose(whole, (2, 3, 0, 1, 4)).reshape(rows, -1)


def fill(source, target, place):
    groups, parts, inner, length = source.shape[:4]
    for j in range(parts):
        slot = lax.rem(j + parts - place, parts)
        for g in range(groups):
            for b in range(inner):
                target[g * inner + b, j * length : (j + 1) * length, :] = source[g, slot, b].astype(
                    wide
                )


def empty(source, target, place):
    groups, parts, inner, length = target.shape[:4]
    for j in range(parts):
        slot = lax.rem(j + parts - place, parts)
        for g in range(groups):
            for b in range(inner):
                target[g, slot, b] = source[g * inner + b, j * length : (j + 1) * length, :].astype(
                    low
                )


def halves(ref):
    return [ref[k * tile : (k + 1) * tile, :] for k in range(ref.shape[0] // tile)]


def row_of(ref, seq, at):
    return ref[seq, pl.ds(at, tile, stride=0), :]


def states_kernel(place_ref, signal_ref, decay_ref, state_ref, held):
    fill(signal_ref, held, place_ref[0])
    seqs, length, lanes = held.shape
    keep = [jnp.exp(-d) for d in halves(decay_ref)]
    count = len(keep)

    def step(i, carry):
        state = list(carry)
        for k in range(tile):
            for n in range(seqs):
                new = row_of(held, n, i * tile + k)
                for h in range(count):
                    at = n * count + h
                    state[at] = keep[h] * state[at] + new
        return tuple(state)

    zero = jnp.zeros((tile, lanes), wide)
    state = lax.fori_loop(0, length // tile, step, tuple(zero for _ in range(seqs * count)))
    for n in range(seqs):
        for h in range(count):
            state_ref[n, h * tile : (h + 1) * tile, :] = state[n * count + h]


def forward_kernel(place_ref, signal_ref, decay_ref, residue_ref, start_ref, out_ref, held, terms, made):
    fill(signal_ref, held, place_ref[0])
    seqs, length, lanes = held.shape
    keep = [jnp.exp(-d) for d in halves(decay_ref)]
    weigh = halves(residue_ref)
    count = len(keep)

    def step(i, carry):
        state = list(carry)
        for k in range(tile):
            for n in range(seqs):
                new = row_of(held, n, i * tile + k)
                total = None
                for h in range(count):
                    at = n * count + h
                    state[at] = keep[h] * state[at] + new
                    term = weigh[h] * state[at]
                    total = term if total is None else total + term
                terms[n, k * tile : (k + 1) * tile, :] = total
        for n in range(seqs):
            result = terms[n, pl.ds(0, tile, stride=tile), :]
            for p in range(1, tile):
                result = result + terms[n, pl.ds(p, tile, stride=tile), :]
            made[n, pl.ds(i * tile, tile), :] = result
        return tuple(state)

    start = tuple(
        start_ref[n, h * tile : (h + 1) * tile, :] for n in range(seqs) for h in range(count)
    )
    lax.fori_loop(0, length // tile, step, start)
    empty(made, out_ref, place_ref[0])


def later_kernel(place_ref, signal_ref, decay_ref, state_ref, held):
    fill(signal_ref, held, place_ref[0])
    seqs, length, lanes = held.shape
    keep = [jnp.exp(-d) for d in halves(decay_ref)]
    count = len(keep)

    def step(i, carry):
        state = list(carry)
        base = length - tile - i * tile
        for k in range(tile - 1, -1, -1):
            for n in range(seqs):
                new = row_of(held, n, base + k)
                for h in range(count):
                    at = n * count + h
                    state[at] = keep[h] * state[at] + new
        return tuple(state)

    zero = jnp.zeros((tile, lanes), wide)
    state = lax.fori_loop(0, length // tile, step, tuple(zero for _ in range(seqs * count)))
    for n in range(seqs):
        for h in range(count):
            state_ref[n, h * tile : (h + 1) * tile, :] = state[n * count + h]


def backward_kernel(
    place_ref,
    signal_ref,
    grad_ref,
    decay_ref,
    residue_ref,
    start_ref,
    end_ref,
    out_ref,
    residue_grad_ref,
    decay_grad_ref,
    held,
    grads,
    terms,
    made,
    later,
):
    fill(signal_ref, held, place_ref[0])
    fill(grad_ref, grads, place_ref[0])
    seqs, length, lanes = held.shape
    keep = [jnp.exp(-d) for d in halves(decay_ref)]
    weigh = halves(residue_ref)
    count = len(keep)
    group = later.shape[0]
    zero = jnp.zeros((tile, lanes), wide)
    none = tuple(zero for _ in range(group * count))
    sum_first = [zero] * count
    sum_second = [zero] * count
    for base_seq in range(0, seqs, group):

        def load(ref):
            return tuple(
                ref[base_seq + n, h * tile : (h + 1) * tile, :]
                for n in range(group)
                for h in range(count)
            )

        def back_step(i, carry):
            state, first = [list(v) for v in carry]
            base = length - tile - i * tile
            for k in range(tile - 1, -1, -1):
                for n in range(group):
                    back = row_of(grads, base_seq + n, base + k)
                    new = row_of(held, base_seq + n, base + k)
                    total = None
                    for h in range(count):
                        at = n * count + h
                        state[at] = keep[h] * state[at] + back
                        first[at] = first[at] + new * state[at]
                        later[n, pl.ds(((base + k) * count + h) * tile, tile), :] = state[at]
                        term = weigh[h] * state[at]
                        total = term if total is None else total + term
                    terms[n, k * tile : (k + 1) * tile, :] = total
            for n in range(group):
                result = terms[n, pl.ds(0, tile, stride=tile), :]
                for p in range(1, tile):
                    result = result + terms[n, pl.ds(p, tile, stride=tile), :]
                made[base_seq + n, pl.ds(base, tile), :] = result
            return tuple(state), tuple(first)

        _, first = lax.fori_loop(0, length // tile, back_step, (load(end_ref), none))

        def ahead(i, carry):
            state, second = [list(v) for v in carry]
            for k in range(tile):
                for n in range(group):
                    new = row_of(held, base_seq + n, i * tile + k)
                    for h in range(count):
                        at = n * count + h
                        state[at] = keep[h] * state[at] + new
                        other = later[n, pl.ds(((i * tile + k) * count + h) * tile, tile), :]
                        second[at] = second[at] + state[at] * other
            return tuple(state), tuple(second)

        _, second = lax.fori_loop(0, length // tile, ahead, (load(start_ref), none))
        for n in range(group):
            for h in range(count):
                at = n * count + h
                sum_first[h] = sum_first[h] + first[at]
                sum_second[h] = sum_second[h] + (second[at] - first[at])
    for h in range(count):
        residue_grad_ref[h * tile : (h + 1) * tile, :] = sum_first[h]
        decay_grad_ref[h * tile : (h + 1) * tile, :] = -weigh[h] * sum_second[h]
    empty(made, out_ref, place_ref[0])


def conv_call(kernel, place, arrays, results, scratch, flops):
    channels = arrays[0].shape[-1]
    lanes = min(channels, 128)

    def spec(shape):
        lead = len(shape) - 1
        return pl.BlockSpec(shape[:-1] + (lanes,), lambda i, *_: (0,) * lead + (i,))

    return pl.pallas_call(
        kernel,
        out_shape=results,
        grid_spec=pltpu.PrefetchScalarGridSpec(
            num_scalar_prefetch=1,
            grid=(channels // lanes,),
            in_specs=[spec(a.shape) for a in arrays],
            out_specs=[spec(r.shape) for r in results],
            scratch_shapes=[pltpu.VMEM(s + (lanes,), wide) for s in scratch],
        ),
        compiler_params=pltpu.CompilerParams(
            dimension_semantics=("arbitrary",), vmem_limit_bytes=56 << 20
        ),
        cost_estimate=pl.CostEstimate(
            flops=flops, transcendentals=0, bytes_accessed=sum(a.size * 4 for a in arrays)
        ),
    )(place, *arrays)


def sizes(signal, poles):
    groups, parts, inner, length, channels = signal.shape
    return groups * inner, parts * length, channels, signal.size * poles


def states_of(place, signal, decay):
    seqs, length, channels, work = sizes(signal, decay.shape[0])
    shape = jax.ShapeDtypeStruct((seqs, decay.shape[0], channels), wide)
    return conv_call(states_kernel, place, [signal, decay], [shape], [(seqs, length)], 2 * work)[0]


def forward_of(place, signal, decay, residue, start):
    seqs, length, channels, work = sizes(signal, decay.shape[0])
    return conv_call(
        forward_kernel,
        place,
        [signal, decay, residue, start],
        [jax.ShapeDtypeStruct(signal.shape, low)],
        [(seqs, length), (seqs, tile * tile), (seqs, length)],
        4 * work,
    )[0]


def later_of(place, signal, decay):
    seqs, length, channels, work = sizes(signal, decay.shape[0])
    shape = jax.ShapeDtypeStruct((seqs, decay.shape[0], channels), wide)
    return conv_call(later_kernel, place, [signal, decay], [shape], [(seqs, length)], 2 * work)[0]


def backward_of(place, signal, grad, decay, residue, start, end):
    poles = decay.shape[0]
    seqs, length, channels, work = sizes(signal, poles)
    shape = jax.ShapeDtypeStruct(decay.shape, wide)
    group = min(seqs, 4)
    return conv_call(
        backward_kernel,
        place,
        [signal, grad, decay, residue, start, end],
        [jax.ShapeDtypeStruct(signal.shape, low), shape, shape],
        [
            (seqs, length),
            (seqs, length),
            (group, tile * tile),
            (seqs, length),
            (group, length * poles),
        ],
        12 * work,
    )


def rms_scale(values):
    return lax.rsqrt(jnp.mean(values * values, axis=-1, keepdims=True) + epsilon)


def norm_back(values, scale, gain, grad_normed):
    grad_gain = jnp.sum(grad_normed * values * scale, axis=(0, 1))
    scaled = grad_normed * gain
    grad_values = scale * scaled - values * scale * scale * scale * jnp.mean(
        scaled * values, axis=-1, keepdims=True
    )
    return (grad_values, grad_gain)


def dot(a, b, kind=wide):
    return jnp.dot(a, b, preferred_element_type=wide).astype(kind)


def dot_t(a, b, kind=wide):
    return lax.dot_general(a, b, (((1,), (1,)), ((), ())), preferred_element_type=wide).astype(kind)


def dot_w(a, b):
    return lax.dot_general(a, b, (((0,), (0,)), ((), ())), preferred_element_type=wide).astype(low)


def body(
    tokens,
    lengths,
    norm_gain,
    in_weight,
    conv_taps,
    filter_residue,
    filter_decay,
    out_weight,
    feed_gain,
    gate_weight,
    up_weight,
    down_weight,
    cotangent,
):
    spread, ycount = lax.axis_size("x"), lax.axis_size("y")
    batch, local, width = tokens.shape
    place = lax.axis_index("z") * spread + lax.axis_index("x")
    position = place * local + jnp.arange(local)
    mask = (position[None, :] < lengths[:, None]).astype(wide)[..., None]
    block = spread * local

    count = 3 * depth
    extra = 8
    line = Line(lax.axis_index("c"))
    run = line.run

    def stacked(value, got):
        return jnp.stack([value] + got)

    w_out = lax.all_gather(run(out_block, out_weight), "z", axis=0, tiled=True)
    in_got = column_moves(run(lambda w: column_pieces(w, 3), in_weight))
    last = [(i * spread + spread - 1, (i + 1) * spread) for i in range(depth - 1)]

    def norm_one(values, gain):
        values = values.astype(wide)
        scale = rms_scale(values)
        normed = (values * scale * gain).astype(low)
        return normed, normed[:, local - 2 :], scale

    normed, ending, scale_one = run(norm_one, tokens, norm_gain)
    before = lax.ppermute(ending, ("z", "x"), last)

    def lengthen(values, rows):
        rest = jnp.zeros((batch, extra - 2, width), values.dtype)
        values = jnp.concatenate([values, rows, rest], axis=1)
        return values[: batch // 2], values[batch // 2 :]

    normed_move = Gather(*run(lengthen, normed, before))
    gate_got = column_moves(run(lambda w: column_pieces(w, 1), gate_weight))
    in_block, w_out = run(lambda got, w: (column_block(got), w), in_got, w_out)
    w_in = gather_tile(in_block)
    normed_move.turn(line)
    w_down = gather_tile(run(row_block, down_weight))
    out_move = Gather(*run(lambda w: (w[None, : w.shape[0] // 2], w[None, w.shape[0] // 2 :]), w_out))
    up_got = column_moves(run(lambda w: column_pieces(w, 1), up_weight))
    normed_all = normed_move.end(line)
    out_move.turn(line)

    channels = w_in.shape[1] // 3
    half = channels // 2
    grid = (2 * ycount, spread, batch // 2, local)

    def rank_values(all_taps, all_decay, all_residue):
        return (
            jnp.concatenate(
                [rank_rows(all_taps[:, g * width : (g + 1) * width], 1) for g in range(3)], axis=1
            ),
            rank_rows(all_decay, 0).T,
            rank_rows(all_residue, 0).T,
        )

    taps, decay, residue = run(rank_values, conv_taps, filter_decay, filter_residue)
    opening = (lax.axis_index("x") + jnp.arange(spread)) % spread == 0
    opening = opening[None, :, None, None, None]
    closing = (lax.axis_index("x") + jnp.arange(spread)) % spread == spread - 1
    closing = closing[None, :, None, None, None]

    def project(v, w):
        return dot(v, w, low).reshape(grid[:3] + (local + extra, 3 * channels))

    mixed = run(project, normed_all, w_in)
    out_move.got = run(lambda got: got, out_move.got)

    def extend(value, g):
        own = value[..., g * channels : (g + 1) * channels]
        earlier = jnp.roll(own[:, :, :, local - 2 : local], 1, axis=1)
        earlier = jnp.where(opening, own[:, :, :, local : local + 2], earlier)
        return jnp.concatenate([earlier, own[:, :, :, :local]], axis=3).astype(wide)

    def short_of(value, weights, g):
        longer = extend(value, g)
        own = weights[:, g * channels : (g + 1) * channels]
        return own[0] * longer[:, :, :, 2:] + own[1] * longer[:, :, :, 1:-1] + own[2] * longer[:, :, :, :-2]

    spot = lax.axis_index("x").astype(jnp.int32).reshape(1)

    def multiply(value, weights, rates):
        keys, values = (short_of(value, weights, g) for g in (1, 2))
        product = (keys * values).astype(low)
        return product, states_of(spot, product, rates)

    product, state_end = run(multiply, mixed, taps, decay)
    states = [passed(state_end, "z", k) for k in range(1, depth)]
    w_gate = gather_tile(run(column_block, gate_got))
    out_own = out_move.end(line)
    w_out = [out_own] + moved(out_own, "c", -1)

    def feed_grad(values):
        values = (values.astype(wide) * mask).astype(low)
        return values[: batch // 2], values[batch // 2 :]

    feed_move = Gather(*run(feed_grad, cotangent))

    def combine(parts, rates):
        total = parts[0]
        for k in range(1, depth - 1):
            total = total + jnp.exp(-rates * (k * block)) * parts[k]
        return total

    def convolve(parts, value, weights, signal, rates, amounts):
        start = combine(parts, rates)
        result = forward_of(spot, signal, rates, amounts, start)
        query = short_of(value, weights, 0)
        gated = (query * result.astype(wide)).astype(low)
        slots = gated.reshape(2, ycount, spread, -1, channels)
        return (
            start,
            result,
            gated.reshape(-1, channels),
            [[slots[:, k, i].reshape(-1, channels) for i in range(spread)] for k in range(ycount)],
        )

    start, convolved, gated_all, gated = run(
        convolve, states, mixed, taps, product, decay, residue
    )
    gated_got = swap_slots(gated)
    w_up = gather_tile(run(column_block, up_got))
    feed_move.turn(line)

    def mix(got, weights, values, gain):
        own = jnp.concatenate(
            [g[:, h * half : (h + 1) * half] for h in range(2) for row in got for g in row], axis=1
        )
        mixer = in_order(jnp.stack([dot(own, w) for w in weights]), "c")
        mixer = jnp.concatenate([m for m in mixer], axis=1).reshape(batch, local, width)
        middle = values.astype(wide) + mixer
        scale = rms_scale(middle)
        normed = (middle * scale * gain).astype(low)
        return middle, scale, normed[: batch // 2], normed[batch // 2 :]

    middle, scale_two, first, second = run(mix, gated_got, w_out, tokens, feed_gain)

    two_move = Gather(first, second)
    two_move.turn(line)
    grad_feed_all = feed_move.end(line)
    grad_active = run(dot_t, grad_feed_all, w_down)
    normed_two_all = two_move.end(line)

    def open_gate(v, w, back):
        value = dot(v, w)
        return value, (back * value * jax.nn.sigmoid(value)).astype(low)

    gate, grad_upper = run(open_gate, normed_two_all, w_gate, grad_active)
    up_term = run(dot_w, normed_two_all, grad_upper)
    up_mine = scatter_tile(up_term)

    def activate(v, w, value, back):
        upper = dot(v, w)
        sigma = jax.nn.sigmoid(value)
        return (
            (value * sigma * upper).astype(low),
            (back * upper * sigma * (1.0 + value * (1.0 - sigma))).astype(low),
        )

    active, grad_gate = run(activate, normed_two_all, w_up, gate, grad_active)
    two_back = Scatter(
        run(
            lambda a, b, wa, wb: split_sum((dot_t(a, wa) + dot_t(b, wb)).astype(low)),
            grad_gate,
            grad_upper,
            w_gate,
            w_up,
        )
    )
    gate_mine = scatter_tile(run(dot_w, normed_two_all, grad_gate))
    two_back.turn(line)
    feed_parts = run(lambda a, w: split_sum(dot(a, w, low)), active, w_down)

    def middle_back(rest, values, scale, gain, back, weights):
        grad_normed = Scatter.sum(*rest).reshape(batch, local, width)
        result, grad_gain = norm_back(values, scale, gain, grad_normed)
        result = result + back.astype(wide) * mask
        parts = core_halves(result.astype(low).reshape(-1, width))
        own = sum(dot_t(m, w) for m, w in zip(parts, weights)).astype(low)
        ranks = ycount * spread

        def slot(at):
            pieces = [
                own[:, (h * ranks + at) * half : (h * ranks + at + 1) * half] for h in range(2)
            ]
            return jnp.concatenate(pieces, axis=1)

        slots = [[slot(k * spread + i) for i in range(spread)] for k in range(ycount)]
        rounded = result.astype(low)
        return result, grad_gain, rounded[: batch // 2], rounded[batch // 2 :], slots

    grad_middle, grad_feed_gain, first, second, grad_slots = run(
        middle_back, two_back.rest(), middle, scale_two, feed_gain, cotangent, w_out
    )
    grad_got = swap_slots(grad_slots)
    down_mine = scatter_tile(run(dot_w, active, grad_feed_all))
    mix_move = Gather(first, second)

    def conv_grads(got, result, value, weights, rates):
        grad = jnp.stack([jnp.stack(row) for row in got])
        grad = grad.reshape(ycount, spread, 2, batch // 2, local, channels)
        grad = jnp.moveaxis(grad, 2, 0).reshape(grid + (channels,)).astype(wide)
        grad_query = grad * result.astype(wide)
        grad_conv = (grad * short_of(value, weights, 0)).astype(low)
        return grad_query, grad_conv, later_of(spot, grad_conv, rates)

    grad_query, grad_conv, later_end = run(conv_grads, grad_got, convolved, mixed, taps, decay)
    laters = [passed(later_end, "z", -k) for k in range(1, depth)]
    mix_move.turn(line)

    def short_back(grad, weights):
        head = jnp.roll(grad[:, :, :, :2], -1, axis=1)
        whole = jnp.concatenate([grad, jnp.where(closing, 0.0, head)], axis=3)
        result = (
            weights[0] * whole[:, :, :, :-2]
            + weights[1] * whole[:, :, :, 1:-1]
            + weights[2] * whole[:, :, :, 2:]
        )
        one, two = grad[:, :, :, :1], grad[:, :, :, 1:2]
        earlier = jnp.concatenate([weights[2] * one, weights[1] * one + weights[2] * two], axis=3)
        rest = jnp.zeros(grad.shape[:3] + (extra - 2, grad.shape[-1]), wide)
        result = jnp.concatenate([result, jnp.where(opening, earlier, 0.0), rest], axis=3)
        return result.astype(low).reshape(-1, grad.shape[-1])

    feed_back = Scatter(feed_parts)
    up_parts_got = owner_moves(run(owner_parts, up_mine))
    gate_got = owner_moves(run(owner_parts, gate_mine))

    def conv_back(signal, grad, rates, amounts, begin, ends_later, value, weights):
        later = combine(ends_later, rates)
        grad_product, grad_residue, grad_decay = backward_of(
            spot, signal, grad, rates, amounts, begin, later
        )
        grad_product = grad_product.astype(wide)
        keys, values = (short_of(value, weights, g) for g in (1, 2))
        pair = jnp.concatenate([grad_product * values, grad_product * keys], axis=-1)
        return pair, grad_residue, grad_decay

    grad_pair, grad_residue, grad_decay = run(
        conv_back, product, grad_conv, decay, residue, start, laters, mixed, taps
    )

    mix_move.got = run(lambda got: got, mix_move.got)
    up_held = run(owner_held, up_parts_got)
    up_got = moved(up_held, "y", -1)

    def in_back(query, pair, weights, v):
        result = jnp.concatenate(
            [
                short_back(query, weights[:, :channels]),
                short_back(pair, weights[:, channels:]),
            ],
            axis=1,
        )
        return result, dot_w(v, result)

    grad_mixed, in_term = run(in_back, grad_query, grad_pair, taps, normed_all)
    in_mine = scatter_tile(in_term)
    feed_back.turn(line)
    gate_held = run(owner_held, gate_got)
    gate_got = moved(gate_held, "y", -1)
    one_back = Scatter(run(lambda a, w: split_sum(dot_t(a, w, low)), grad_mixed, w_in))
    feed_back.got = run(lambda got: got, feed_back.got)
    grad_mix_all = mix_move.end(line)
    out_mine = scatter_tile(run(dot_w, gated_all, grad_mix_all))
    up_held = run(stacked, up_held, up_got)
    up_got = moved(up_held, "c", -1)

    def tap_sums(query, pair, value):
        sums = []
        for g, part in enumerate((query, pair[..., :channels], pair[..., channels:])):
            own = extend(value, g)
            sums += [
                jnp.sum(part * own[:, :, :, 2 - j : local + 2 - j], axis=(0, 1, 2, 3))
                for j in range(3)
            ]
        return jnp.stack(sums)

    grad_taps = run(tap_sums, grad_query, grad_pair, mixed)

    def column_whole(own, got):
        return owner_whole(lax.axis_index("c"), [own] + got, depth)

    grad_up_weight = run(column_whole, up_held, up_got)
    gate_held = run(stacked, gate_held, gate_got)
    gate_got = moved(gate_held, "c", -1)
    one_back.turn(line)
    grad_gate_weight = run(column_whole, gate_held, gate_got)
    in_got = owner_moves(run(owner_parts, in_mine))

    def normed_sum(rest):
        value = Scatter.sum(*rest).reshape(batch, local + extra, width)
        return value[:, :local], value[:, local : local + 2].astype(low)

    grad_normed, grad_before = run(normed_sum, one_back.rest())
    grad_after = lax.ppermute(grad_before, ("z", "x"), [(j, i) for i, j in last])
    output = run(
        lambda rest, values: (
            mask * (values + Scatter.sum(*rest).reshape(batch, local, width))
        ).astype(low),
        feed_back.rest(),
        middle,
    )
    in_held = run(owner_held, in_got)
    in_got = moved(in_held, "y", -1)
    down_held = run(lambda v: v[None], down_mine)
    down_got = moved(down_held, "y", -1)

    def tokens_back(grad, extension, values, scale, gain, back, small):
        values = values.astype(wide)
        grad = jnp.concatenate(
            [grad[:, : local - 2], grad[:, local - 2 :] + extension.astype(wide)], axis=1
        )
        result, grad_gain = norm_back(values, scale, gain, grad)
        gains = jnp.stack([grad_gain, small[0]]).reshape(-1, channels)
        return (result + back).astype(low), jnp.concatenate(list(small[1:]) + [gains], axis=0)

    grad_tokens, small = run(
        tokens_back,
        grad_normed,
        grad_after,
        tokens,
        scale_one,
        norm_gain,
        grad_middle,
        (grad_feed_gain, grad_residue, grad_decay, grad_taps),
    )
    small_got = moved(small, "c", 1)
    small = run(lambda v, got: v + sum(got), small, small_got)
    small_got = moved(small, "z", 1)
    in_held = run(stacked, in_held, in_got)
    in_got = moved(in_held, "c", -1)
    small = run(lambda v, got: v + sum(got), small, small_got)
    small_got = moved(small, "x", -1)
    grad_in_weight = run(
        lambda own, got: owner_whole(lax.axis_index("c"), [own] + got, count), in_held, in_got
    )
    down_held = run(lambda own, got: jnp.concatenate([own] + got), down_held, down_got)
    down_got = moved(down_held, "c", -1)
    out_held = run(lambda v: v[None], out_mine)
    out_got = moved(out_held, "y", -1)
    small = run(stacked, small, small_got)
    small_got = moved(small, "y", -1)

    def rows_whole(own, got):
        whole = in_order(jnp.swapaxes(in_order(jnp.stack([own] + got), "c"), 0, 1), "y")
        return whole.reshape(-1, width).astype(wide)

    grad_down = run(rows_whole, down_held, down_got)
    out_held = run(lambda own, got: jnp.concatenate([own] + got), out_held, out_got)
    out_got = moved(out_held, "c", -1)
    poles = decay.shape[0]

    def small_whole(own, got):
        slots = jnp.stack([own] + got)
        rows = 2 * poles + 9
        gains = jnp.sum(slots[:, :, rows:], axis=(0, 1)).reshape(2, width)
        whole = all_channels(slots[:, :, :rows])
        grad_conv_taps = jnp.concatenate(
            [whole[2 * poles + 3 * g : 2 * poles + 3 * g + 3] for g in range(3)], axis=1
        )
        return gains[0], gains[1], grad_conv_taps, whole[:poles].T, whole[poles : 2 * poles].T

    grad_norm_gain, feed_gain_sum, grad_conv_taps, residue_sum, decay_sum = run(
        small_whole, small, small_got
    )

    def out_whole(core, own, got):
        ccount = lax.axis_size("c")
        slots = jnp.stack([own] + got)
        slots = jnp.stack(
            [lax.dynamic_index_in_dim(slots, (j - core) % ccount, 0, False) for j in range(ccount)]
        )
        whole = in_order(jnp.swapaxes(slots, 0, 1), "y")
        return whole.reshape(-1, width).astype(wide)

    grad_out_weight = line.finish(out_whole, out_held, out_got)
    return (
        output,
        grad_tokens,
        grad_norm_gain,
        grad_in_weight,
        grad_conv_taps,
        residue_sum,
        decay_sum,
        grad_out_weight,
        feed_gain_sum,
        grad_gate_weight,
        grad_up_weight,
        grad_down,
    )


def solution(mesh):
    pairs, blocks = mesh.shape["dp"], mesh.shape["seq"]
    devices = mesh.devices.reshape(pairs // cores, cores, depth, blocks // depth)
    inner = Mesh(devices, ("y", "c", "z", "x"))
    dp, seq = ("y", "c"), ("z", "x")
    tokens, rows = P(dp, seq, None), P(seq, None)
    return jax.shard_map(
        body,
        mesh=inner,
        in_specs=(
            tokens,
            P(dp),
            P(),
            rows,
            P(),
            P(),
            P(),
            rows,
            P(),
            rows,
            rows,
            rows,
            tokens,
        ),
        out_specs=(tokens, tokens, P(), rows, P(), P(), P(), rows, P(), rows, rows, rows),
        check_vma=False,
    )
```

```python
import functools

import jax
import jax.numpy as jnp
from jax import lax
from jax.experimental import pallas as pl
from jax.experimental.pallas import tpu as pltpu
from jax.sharding import Mesh, PartitionSpec as P

epsilon = 1e-06
low = jnp.bfloat16
wide = jnp.float32
tile = 8
depth = 4
cores = 2


def turned(value, axis, by):
    length = lax.axis_size(axis)
    return lax.ppermute(value, axis, [(i, (i + by) % length) for i in range(length)])


def passed(value, axis, by):
    length = lax.axis_size(axis)
    pairs = [(i, i + by) for i in range(length) if 0 <= i + by < length]
    return lax.ppermute(value, axis, pairs)


def swap_slots(slots):
    ycount, spread = lax.axis_size("y"), lax.axis_size("x")
    result = []
    for dy in range(ycount):
        line = []
        for dx in range(spread):
            sy, sx = (ycount - dy) % ycount, (spread - dx) % spread
            if sy == 0 and sx == 0:
                line.append(slots[0][0])
                continue
            pairs = [
                (i * spread + j, (i + sy) % ycount * spread + (j + sx) % spread)
                for i in range(ycount)
                for j in range(spread)
            ]
            line.append(lax.ppermute(slots[sy][sx], ("y", "x"), pairs))
        result.append(line)
    return result


class Line:
    def __init__(self, token):
        self.token = token

    def run(self, work, *values):
        values, token = lax.optimization_barrier((values, self.token))
        result, self.token = lax.optimization_barrier((work(*values), token))
        return result

    def finish(self, work, *values):
        values, token = lax.optimization_barrier((values, self.token))
        return work(token, *values)


def moved(value, axis, sign):
    return [turned(value, axis, sign * d) for d in range(1, lax.axis_size(axis))]


class Gather:
    def __init__(self, first, second):
        self.held = (first, second)
        self.got = (moved(first, "x", -1), moved(second, "y", -1))

    def turn(self, line):
        self.held = line.run(
            lambda held, got: tuple(jnp.stack([h] + g) for h, g in zip(held, got)), self.held, self.got
        )
        self.got = (moved(self.held[0], "y", -1), moved(self.held[1], "x", -1))

    def end(self, line):
        def work(held, got):
            first = jnp.stack([held[0]] + got[0])
            second = jnp.swapaxes(jnp.stack([held[1]] + got[1]), 0, 1)
            return jnp.stack([first, second]).reshape(-1, first.shape[-1])

        return line.run(work, self.held, self.got)


def split_sum(partial):
    grid = partial.reshape(2, lax.axis_size("y"), lax.axis_size("x"), -1, partial.shape[-1])
    first = [grid[0][:, d].astype(low) for d in range(grid.shape[2])]
    second = [grid[1][d].astype(low) for d in range(grid.shape[1])]
    return first, second


def add_up(parts, got):
    total = parts[0].astype(wide)
    for g in got:
        total = total + g.astype(wide)
    return total


class Scatter:
    def __init__(self, parts):
        self.parts = parts
        self.send("x", "y")

    def send(self, *axes):
        self.got = [
            [turned(p, axis, d + 1) for d, p in enumerate(part[1:])]
            for part, axis in zip(self.parts, axes)
        ]

    def turn(self, line):
        def work(parts, got):
            result = []
            for part, g in zip(parts, got):
                total = add_up(part, g).astype(low)
                result.append([total[d] for d in range(total.shape[0])])
            return result

        self.parts = line.run(work, self.parts, self.got)
        self.send("y", "x")

    def rest(self):
        return self.parts, self.got

    @staticmethod
    def sum(parts, got):
        return jnp.stack([add_up(part, g) for part, g in zip(parts, got)])


def pick_kernel(count, part, stride, start_ref, source, *refs):
    targets, sems = refs[:-1], refs[-1]
    copies = []
    for d, target in enumerate(targets):
        for k in range(count):
            at = pl.multiple_of((k * stride + start_ref[d]) * part, part)
            copies.append(
                pltpu.make_async_copy(
                    source.at[:, pl.ds(at, part)],
                    target.at[:, k * part : (k + 1) * part],
                    sems.at[d * count + k],
                )
            )
    for copy in copies:
        copy.start()
    for copy in copies:
        copy.wait()


def column_pieces(weight, groups):
    spread, ycount = lax.axis_size("x"), lax.axis_size("y")
    rows = weight.shape[0]
    count = groups * depth
    part = weight.shape[1] // (count * spread * ycount)
    starts = [
        (lax.axis_index("x") + d) % spread * ycount + lax.axis_index("y") for d in range(spread)
    ]
    if part % 128 == 0:
        return pl.pallas_call(
            functools.partial(pick_kernel, count, part, spread * ycount),
            out_shape=[jax.ShapeDtypeStruct((rows, count * part), weight.dtype)] * spread,
            grid_spec=pltpu.PrefetchScalarGridSpec(
                num_scalar_prefetch=1,
                in_specs=[pl.BlockSpec(memory_space=pl.ANY)],
                out_specs=[pl.BlockSpec(memory_space=pltpu.VMEM)] * spread,
                scratch_shapes=[pltpu.SemaphoreType.DMA((count * spread,))],
            ),
            cost_estimate=pl.CostEstimate(
                flops=0, transcendentals=0, bytes_accessed=4 * rows * count * part * spread
            ),
        )(jnp.stack(starts).astype(jnp.int32), weight)
    return [
        jnp.concatenate(
            [
                lax.dynamic_slice_in_dim(weight, (k * spread * ycount + start) * part, part, 1)
                for k in range(count)
            ],
            axis=1,
        )
        for start in starts
    ]


def column_moves(pieces):
    spread, ccount = lax.axis_size("x"), lax.axis_size("c")
    share = spread // ccount
    got = [pieces[0]]
    for d in range(1, spread):
        pairs = [
            (i // share * spread + i, i // share * spread + (i + d) % spread) for i in range(spread)
        ]
        got.append(lax.ppermute(pieces[d], ("c", "x"), pairs))
    return got


def column_block(got):
    spread, ccount = lax.axis_size("x"), lax.axis_size("c")
    share = spread // ccount
    place, core = lax.axis_index("x"), lax.axis_index("c")
    got = jnp.stack(got)
    return jnp.concatenate(
        [
            lax.dynamic_index_in_dim(got, (place - core * share - j) % spread, 0, False)
            for j in range(share)
        ]
    )


def row_block(weight):
    ycount, ccount = lax.axis_size("y"), lax.axis_size("c")
    part = weight.shape[0] // (ycount * ccount)
    pair = lax.axis_index("y") * ccount + lax.axis_index("c")
    return lax.dynamic_slice_in_dim(weight, pair * part, part, 0)


def core_halves(value):
    ccount = lax.axis_size("c")
    width = value.shape[1] // ccount
    core = lax.axis_index("c")
    return [
        lax.dynamic_slice_in_dim(value, (core + d) % ccount * width, width, 1)
        for d in range(ccount)
    ]


def out_block(weight):
    part = weight.shape[0] // lax.axis_size("y")
    rows = lax.dynamic_slice_in_dim(weight, lax.axis_index("y") * part, part, 0)
    return core_halves(rows)[0]


def gather_tile(block):
    return lax.all_gather(block, ("z", "c"), axis=0, tiled=True)


def scatter_tile(term):
    return lax.psum_scatter(term, ("z", "c"), scatter_dimension=0, tiled=True)


def owner_parts(mine):
    spread, ccount = lax.axis_size("x"), lax.axis_size("c")
    share = spread // ccount
    place, core = lax.axis_index("x"), lax.axis_index("c")
    parts = mine.reshape(share, -1, mine.shape[-1])
    return [
        lax.dynamic_index_in_dim(
            parts, jnp.clip((place + d) % spread - core * share, 0, share - 1), 0, False
        )
        for d in range(spread)
    ]


def owner_moves(parts):
    spread, ccount = lax.axis_size("x"), lax.axis_size("c")
    share = spread // ccount
    got = [parts[0]]
    for d in range(1, spread):
        pairs = [
            ((i + d) % spread // share * spread + i, i // share * spread + (i + d) % spread)
            for i in range(spread)
        ]
        got.append(lax.ppermute(parts[d], ("c", "x"), pairs))
    return got


def owner_held(got):
    spread, ccount = lax.axis_size("x"), lax.axis_size("c")
    share = spread // ccount
    place, core = lax.axis_index("x"), lax.axis_index("c")
    got = jnp.stack(got)
    return jnp.stack(
        [
            lax.dynamic_index_in_dim(got, (place - core * share - j) % spread, 0, False)
            for j in range(share)
        ]
    )


def assemble_kernel(count, width, order_ref, *refs):
    sources, target = refs[:-1], refs[-1]
    part = width // count
    ranks = order_ref.shape[0] // 2
    for r in range(ranks):
        core, slot = order_ref[2 * r], order_ref[2 * r + 1]
        value = sources[0][slot]
        for c in range(1, len(sources)):
            value = jnp.where(core == c, sources[c][slot], value)
        value = value.astype(wide)
        for at in range(count):
            start = (at * ranks + r) * part
            target[:, start : start + part] = value[:, at * part : (at + 1) * part]


def owner_whole(core, sources, count):
    spread, ccount, ycount = lax.axis_size("x"), lax.axis_size("c"), lax.axis_size("y")
    share = spread // ccount
    yplace = lax.axis_index("y")
    order = []
    for i in range(spread):
        for k in range(ycount):
            order += [(i // share - core) % ccount, (k - yplace) % ycount * share + i % share]
    sources = [v.reshape((-1,) + v.shape[2:]) for v in sources]
    held, rows, width = sources[0].shape
    block = min(rows, 64)
    return pl.pallas_call(
        functools.partial(assemble_kernel, count, width),
        out_shape=jax.ShapeDtypeStruct((rows, width * spread * ycount), wide),
        grid_spec=pltpu.PrefetchScalarGridSpec(
            num_scalar_prefetch=1,
            grid=(rows // block,),
            in_specs=[pl.BlockSpec((held, block, width), lambda i, order: (0, i, 0))]
            * len(sources),
            out_specs=pl.BlockSpec((block, width * spread * ycount), lambda i, order: (i, 0)),
        ),
        compiler_params=pltpu.CompilerParams(vmem_limit_bytes=56 << 20),
        cost_estimate=pl.CostEstimate(
            flops=0, transcendentals=0, bytes_accessed=6 * rows * width * spread * ycount
        ),
    )(jnp.stack(order).astype(jnp.int32), *sources)


def in_order(slots, axis):
    length = lax.axis_size(axis)
    place = lax.axis_index(axis)
    return jnp.stack(
        [lax.dynamic_index_in_dim(slots, (j - place) % length, 0, False) for j in range(length)]
    )


def rank_rows(values, axis):
    spread, ycount = lax.axis_size("x"), lax.axis_size("y")
    part = values.shape[axis] // (depth * spread * ycount)
    place = lax.axis_index("x") * ycount + lax.axis_index("y")
    return jnp.concatenate(
        [
            lax.dynamic_slice_in_dim(values, (k * spread * ycount + place) * part, part, axis)
            for k in range(depth)
        ],
        axis=axis,
    )


def all_channels(slots):
    whole = in_order(slots, "y")
    whole = in_order(jnp.swapaxes(whole, 0, 1), "x")
    spread, ycount, rows = whole.shape[:3]
    whole = whole.reshape(spread, ycount, rows, depth, -1)
    return jnp.transpose(whole, (2, 3, 0, 1, 4)).reshape(rows, -1)


def fill(source, target, place):
    groups, parts, inner, length = source.shape[:4]
    for j in range(parts):
        slot = lax.rem(j + parts - place, parts)
        for g in range(groups):
            for b in range(inner):
                target[g * inner + b, j * length : (j + 1) * length, :] = source[g, slot, b].astype(
                    wide
                )


def empty(source, target, place):
    groups, parts, inner, length = target.shape[:4]
    for j in range(parts):
        slot = lax.rem(j + parts - place, parts)
        for g in range(groups):
            for b in range(inner):
                target[g, slot, b] = source[g * inner + b, j * length : (j + 1) * length, :].astype(
                    low
                )


def halves(ref):
    return [ref[k * tile : (k + 1) * tile, :] for k in range(ref.shape[0] // tile)]


def row_of(ref, seq, at):
    return ref[seq, pl.ds(at, tile, stride=0), :]


def states_kernel(place_ref, signal_ref, decay_ref, state_ref, held):
    fill(signal_ref, held, place_ref[0])
    seqs, length, lanes = held.shape
    keep = [jnp.exp(-d) for d in halves(decay_ref)]
    count = len(keep)

    def step(i, carry):
        state = list(carry)
        for k in range(tile):
            for n in range(seqs):
                new = row_of(held, n, i * tile + k)
                for h in range(count):
                    at = n * count + h
                    state[at] = keep[h] * state[at] + new
        return tuple(state)

    zero = jnp.zeros((tile, lanes), wide)
    state = lax.fori_loop(0, length // tile, step, tuple(zero for _ in range(seqs * count)))
    for n in range(seqs):
        for h in range(count):
            state_ref[n, h * tile : (h + 1) * tile, :] = state[n * count + h]


def forward_kernel(place_ref, signal_ref, decay_ref, residue_ref, start_ref, out_ref, held, terms, made):
    fill(signal_ref, held, place_ref[0])
    seqs, length, lanes = held.shape
    keep = [jnp.exp(-d) for d in halves(decay_ref)]
    weigh = halves(residue_ref)
    count = len(keep)

    def step(i, carry):
        state = list(carry)
        for k in range(tile):
            for n in range(seqs):
                new = row_of(held, n, i * tile + k)
                total = None
                for h in range(count):
                    at = n * count + h
                    state[at] = keep[h] * state[at] + new
                    term = weigh[h] * state[at]
                    total = term if total is None else total + term
                terms[n, k * tile : (k + 1) * tile, :] = total
        for n in range(seqs):
            result = terms[n, pl.ds(0, tile, stride=tile), :]
            for p in range(1, tile):
                result = result + terms[n, pl.ds(p, tile, stride=tile), :]
            made[n, pl.ds(i * tile, tile), :] = result
        return tuple(state)

    start = tuple(
        start_ref[n, h * tile : (h + 1) * tile, :] for n in range(seqs) for h in range(count)
    )
    lax.fori_loop(0, length // tile, step, start)
    empty(made, out_ref, place_ref[0])


def later_kernel(place_ref, signal_ref, decay_ref, state_ref, held):
    fill(signal_ref, held, place_ref[0])
    seqs, length, lanes = held.shape
    keep = [jnp.exp(-d) for d in halves(decay_ref)]
    count = len(keep)

    def step(i, carry):
        state = list(carry)
        base = length - tile - i * tile
        for k in range(tile - 1, -1, -1):
            for n in range(seqs):
                new = row_of(held, n, base + k)
                for h in range(count):
                    at = n * count + h
                    state[at] = keep[h] * state[at] + new
        return tuple(state)

    zero = jnp.zeros((tile, lanes), wide)
    state = lax.fori_loop(0, length // tile, step, tuple(zero for _ in range(seqs * count)))
    for n in range(seqs):
        for h in range(count):
            state_ref[n, h * tile : (h + 1) * tile, :] = state[n * count + h]


def backward_kernel(
    place_ref,
    signal_ref,
    grad_ref,
    decay_ref,
    residue_ref,
    start_ref,
    end_ref,
    out_ref,
    residue_grad_ref,
    decay_grad_ref,
    held,
    grads,
    terms,
    made,
    later,
):
    fill(signal_ref, held, place_ref[0])
    fill(grad_ref, grads, place_ref[0])
    seqs, length, lanes = held.shape
    keep = [jnp.exp(-d) for d in halves(decay_ref)]
    weigh = halves(residue_ref)
    count = len(keep)
    group = later.shape[0]
    zero = jnp.zeros((tile, lanes), wide)
    none = tuple(zero for _ in range(group * count))
    sum_first = [zero] * count
    sum_second = [zero] * count
    for base_seq in range(0, seqs, group):

        def load(ref):
            return tuple(
                ref[base_seq + n, h * tile : (h + 1) * tile, :]
                for n in range(group)
                for h in range(count)
            )

        def back_step(i, carry):
            state, first = [list(v) for v in carry]
            base = length - tile - i * tile
            for k in range(tile - 1, -1, -1):
                for n in range(group):
                    back = row_of(grads, base_seq + n, base + k)
                    new = row_of(held, base_seq + n, base + k)
                    total = None
                    for h in range(count):
                        at = n * count + h
                        state[at] = keep[h] * state[at] + back
                        first[at] = first[at] + new * state[at]
                        later[n, pl.ds(((base + k) * count + h) * tile, tile), :] = state[at]
                        term = weigh[h] * state[at]
                        total = term if total is None else total + term
                    terms[n, k * tile : (k + 1) * tile, :] = total
            for n in range(group):
                result = terms[n, pl.ds(0, tile, stride=tile), :]
                for p in range(1, tile):
                    result = result + terms[n, pl.ds(p, tile, stride=tile), :]
                made[base_seq + n, pl.ds(base, tile), :] = result
            return tuple(state), tuple(first)

        _, first = lax.fori_loop(0, length // tile, back_step, (load(end_ref), none))

        def ahead(i, carry):
            state, second = [list(v) for v in carry]
            for k in range(tile):
                for n in range(group):
                    new = row_of(held, base_seq + n, i * tile + k)
                    for h in range(count):
                        at = n * count + h
                        state[at] = keep[h] * state[at] + new
                        other = later[n, pl.ds(((i * tile + k) * count + h) * tile, tile), :]
                        second[at] = second[at] + state[at] * other
            return tuple(state), tuple(second)

        _, second = lax.fori_loop(0, length // tile, ahead, (load(start_ref), none))
        for n in range(group):
            for h in range(count):
                at = n * count + h
                sum_first[h] = sum_first[h] + first[at]
                sum_second[h] = sum_second[h] + (second[at] - first[at])
    for h in range(count):
        residue_grad_ref[h * tile : (h + 1) * tile, :] = sum_first[h]
        decay_grad_ref[h * tile : (h + 1) * tile, :] = -weigh[h] * sum_second[h]
    empty(made, out_ref, place_ref[0])


def conv_call(kernel, place, arrays, results, scratch, flops):
    channels = arrays[0].shape[-1]
    lanes = min(channels, 128)

    def spec(shape):
        lead = len(shape) - 1
        return pl.BlockSpec(shape[:-1] + (lanes,), lambda i, *_: (0,) * lead + (i,))

    return pl.pallas_call(
        kernel,
        out_shape=results,
        grid_spec=pltpu.PrefetchScalarGridSpec(
            num_scalar_prefetch=1,
            grid=(channels // lanes,),
            in_specs=[spec(a.shape) for a in arrays],
            out_specs=[spec(r.shape) for r in results],
            scratch_shapes=[pltpu.VMEM(s + (lanes,), wide) for s in scratch],
        ),
        compiler_params=pltpu.CompilerParams(
            dimension_semantics=("arbitrary",), vmem_limit_bytes=56 << 20
        ),
        cost_estimate=pl.CostEstimate(
            flops=flops, transcendentals=0, bytes_accessed=sum(a.size * 4 for a in arrays)
        ),
    )(place, *arrays)


def sizes(signal, poles):
    groups, parts, inner, length, channels = signal.shape
    return groups * inner, parts * length, channels, signal.size * poles


def states_of(place, signal, decay):
    seqs, length, channels, work = sizes(signal, decay.shape[0])
    shape = jax.ShapeDtypeStruct((seqs, decay.shape[0], channels), wide)
    return conv_call(states_kernel, place, [signal, decay], [shape], [(seqs, length)], 2 * work)[0]


def forward_of(place, signal, decay, residue, start):
    seqs, length, channels, work = sizes(signal, decay.shape[0])
    return conv_call(
        forward_kernel,
        place,
        [signal, decay, residue, start],
        [jax.ShapeDtypeStruct(signal.shape, low)],
        [(seqs, length), (seqs, tile * tile), (seqs, length)],
        4 * work,
    )[0]


def later_of(place, signal, decay):
    seqs, length, channels, work = sizes(signal, decay.shape[0])
    shape = jax.ShapeDtypeStruct((seqs, decay.shape[0], channels), wide)
    return conv_call(later_kernel, place, [signal, decay], [shape], [(seqs, length)], 2 * work)[0]


def backward_of(place, signal, grad, decay, residue, start, end):
    poles = decay.shape[0]
    seqs, length, channels, work = sizes(signal, poles)
    shape = jax.ShapeDtypeStruct(decay.shape, wide)
    group = min(seqs, 4)
    return conv_call(
        backward_kernel,
        place,
        [signal, grad, decay, residue, start, end],
        [jax.ShapeDtypeStruct(signal.shape, low), shape, shape],
        [
            (seqs, length),
            (seqs, length),
            (group, tile * tile),
            (seqs, length),
            (group, length * poles),
        ],
        12 * work,
    )


def rms_scale(values):
    return lax.rsqrt(jnp.mean(values * values, axis=-1, keepdims=True) + epsilon)


def norm_back(values, scale, gain, grad_normed):
    grad_gain = jnp.sum(grad_normed * values * scale, axis=(0, 1))
    scaled = grad_normed * gain
    grad_values = scale * scaled - values * scale * scale * scale * jnp.mean(
        scaled * values, axis=-1, keepdims=True
    )
    return (grad_values, grad_gain)


def dot(a, b, kind=wide):
    return jnp.dot(a, b, preferred_element_type=wide).astype(kind)


def dot_t(a, b, kind=wide):
    return lax.dot_general(a, b, (((1,), (1,)), ((), ())), preferred_element_type=wide).astype(kind)


def dot_w(a, b):
    return lax.dot_general(a, b, (((0,), (0,)), ((), ())), preferred_element_type=wide).astype(low)


def body(
    tokens,
    lengths,
    norm_gain,
    in_weight,
    conv_taps,
    filter_residue,
    filter_decay,
    out_weight,
    feed_gain,
    gate_weight,
    up_weight,
    down_weight,
    cotangent,
):
    spread, ycount = lax.axis_size("x"), lax.axis_size("y")
    batch, local, width = tokens.shape
    place = lax.axis_index("z") * spread + lax.axis_index("x")
    position = place * local + jnp.arange(local)
    mask = (position[None, :] < lengths[:, None]).astype(wide)[..., None]
    block = spread * local

    count = 3 * depth
    extra = 8
    line = Line(lax.axis_index("c"))
    run = line.run

    def stacked(value, got):
        return jnp.stack([value] + got)

    w_out = lax.all_gather(run(out_block, out_weight), "z", axis=0, tiled=True)
    in_got = column_moves(run(lambda w: column_pieces(w, 3), in_weight))
    last = [(i * spread + spread - 1, (i + 1) * spread) for i in range(depth - 1)]

    def norm_one(values, gain):
        values = values.astype(wide)
        scale = rms_scale(values)
        normed = (values * scale * gain).astype(low)
        return normed, normed[:, local - 2 :], scale

    normed, ending, scale_one = run(norm_one, tokens, norm_gain)
    before = lax.ppermute(ending, ("z", "x"), last)

    def lengthen(values, rows):
        rest = jnp.zeros((batch, extra - 2, width), values.dtype)
        values = jnp.concatenate([values, rows, rest], axis=1)
        return values[: batch // 2], values[batch // 2 :]

    normed_move = Gather(*run(lengthen, normed, before))
    gate_got = column_moves(run(lambda w: column_pieces(w, 1), gate_weight))
    in_block, w_out = run(lambda got, w: (column_block(got), w), in_got, w_out)
    w_in = gather_tile(in_block)
    normed_move.turn(line)
    w_down = gather_tile(run(row_block, down_weight))
    out_move = Gather(*run(lambda w: (w[None, : w.shape[0] // 2], w[None, w.shape[0] // 2 :]), w_out))
    up_got = column_moves(run(lambda w: column_pieces(w, 1), up_weight))
    normed_all = normed_move.end(line)
    out_move.turn(line)

    channels = w_in.shape[1] // 3
    half = channels // 2
    grid = (2 * ycount, spread, batch // 2, local)

    def rank_values(all_taps, all_decay, all_residue):
        return (
            jnp.concatenate(
                [rank_rows(all_taps[:, g * width : (g + 1) * width], 1) for g in range(3)], axis=1
            ),
            rank_rows(all_decay, 0).T,
            rank_rows(all_residue, 0).T,
        )

    taps, decay, residue = run(rank_values, conv_taps, filter_decay, filter_residue)
    opening = (lax.axis_index("x") + jnp.arange(spread)) % spread == 0
    opening = opening[None, :, None, None, None]
    closing = (lax.axis_index("x") + jnp.arange(spread)) % spread == spread - 1
    closing = closing[None, :, None, None, None]

    def project(v, w):
        return dot(v, w, low).reshape(grid[:3] + (local + extra, 3 * channels))

    mixed = run(project, normed_all, w_in)
    out_move.got = run(lambda got: got, out_move.got)

    def extend(value, g):
        own = value[..., g * channels : (g + 1) * channels]
        earlier = jnp.roll(own[:, :, :, local - 2 : local], 1, axis=1)
        earlier = jnp.where(opening, own[:, :, :, local : local + 2], earlier)
        return jnp.concatenate([earlier, own[:, :, :, :local]], axis=3).astype(wide)

    def short_of(value, weights, g):
        longer = extend(value, g)
        own = weights[:, g * channels : (g + 1) * channels]
        return own[0] * longer[:, :, :, 2:] + own[1] * longer[:, :, :, 1:-1] + own[2] * longer[:, :, :, :-2]

    spot = lax.axis_index("x").astype(jnp.int32).reshape(1)

    def multiply(value, weights, rates):
        keys, values = (short_of(value, weights, g) for g in (1, 2))
        product = (keys * values).astype(low)
        return product, states_of(spot, product, rates)

    product, state_end = run(multiply, mixed, taps, decay)
    states = [passed(state_end, "z", k) for k in range(1, depth)]
    w_gate = gather_tile(run(column_block, gate_got))
    out_own = out_move.end(line)
    w_out = [out_own] + moved(out_own, "c", -1)

    def feed_grad(values):
        values = (values.astype(wide) * mask).astype(low)
        return values[: batch // 2], values[batch // 2 :]

    feed_move = Gather(*run(feed_grad, cotangent))

    def combine(parts, rates):
        total = parts[0]
        for k in range(1, depth - 1):
            total = total + jnp.exp(-rates * (k * block)) * parts[k]
        return total

    def convolve(parts, value, weights, signal, rates, amounts):
        start = combine(parts, rates)
        result = forward_of(spot, signal, rates, amounts, start)
        query = short_of(value, weights, 0)
        gated = (query * result.astype(wide)).astype(low)
        slots = gated.reshape(2, ycount, spread, -1, channels)
        return (
            start,
            result,
            gated.reshape(-1, channels),
            [[slots[:, k, i].reshape(-1, channels) for i in range(spread)] for k in range(ycount)],
        )

    start, convolved, gated_all, gated = run(
        convolve, states, mixed, taps, product, decay, residue
    )
    gated_got = swap_slots(gated)
    w_up = gather_tile(run(column_block, up_got))
    feed_move.turn(line)

    def mix(got, weights, values, gain):
        own = jnp.concatenate(
            [g[:, h * half : (h + 1) * half] for h in range(2) for row in got for g in row], axis=1
        )
        mixer = in_order(jnp.stack([dot(own, w) for w in weights]), "c")
        mixer = jnp.concatenate([m for m in mixer], axis=1).reshape(batch, local, width)
        middle = values.astype(wide) + mixer
        scale = rms_scale(middle)
        normed = (middle * scale * gain).astype(low)
        return middle, scale, normed[: batch // 2], normed[batch // 2 :]

    middle, scale_two, first, second = run(mix, gated_got, w_out, tokens, feed_gain)

    two_move = Gather(first, second)
    two_move.turn(line)
    grad_feed_all = feed_move.end(line)
    grad_active = run(dot_t, grad_feed_all, w_down)
    normed_two_all = two_move.end(line)

    def open_gate(v, w, back):
        value = dot(v, w)
        return value, (back * value * jax.nn.sigmoid(value)).astype(low)

    gate, grad_upper = run(open_gate, normed_two_all, w_gate, grad_active)
    up_term = run(dot_w, normed_two_all, grad_upper)
    up_mine = scatter_tile(up_term)

    def activate(v, w, value, back):
        upper = dot(v, w)
        sigma = jax.nn.sigmoid(value)
        return (
            (value * sigma * upper).astype(low),
            (back * upper * sigma * (1.0 + value * (1.0 - sigma))).astype(low),
        )

    active, grad_gate = run(activate, normed_two_all, w_up, gate, grad_active)
    two_back = Scatter(
        run(
            lambda a, b, wa, wb: split_sum((dot_t(a, wa) + dot_t(b, wb)).astype(low)),
            grad_gate,
            grad_upper,
            w_gate,
            w_up,
        )
    )
    gate_mine = scatter_tile(run(dot_w, normed_two_all, grad_gate))
    two_back.turn(line)
    feed_parts = run(lambda a, w: split_sum(dot(a, w, low)), active, w_down)

    def middle_back(rest, values, scale, gain, back, weights):
        grad_normed = Scatter.sum(*rest).reshape(batch, local, width)
        result, grad_gain = norm_back(values, scale, gain, grad_normed)
        result = result + back.astype(wide) * mask
        parts = core_halves(result.astype(low).reshape(-1, width))
        own = sum(dot_t(m, w) for m, w in zip(parts, weights)).astype(low)
        ranks = ycount * spread

        def slot(at):
            pieces = [
                own[:, (h * ranks + at) * half : (h * ranks + at + 1) * half] for h in range(2)
            ]
            return jnp.concatenate(pieces, axis=1)

        slots = [[slot(k * spread + i) for i in range(spread)] for k in range(ycount)]
        rounded = result.astype(low)
        return result, grad_gain, rounded[: batch // 2], rounded[batch // 2 :], slots

    grad_middle, grad_feed_gain, first, second, grad_slots = run(
        middle_back, two_back.rest(), middle, scale_two, feed_gain, cotangent, w_out
    )
    grad_got = swap_slots(grad_slots)
    down_mine = scatter_tile(run(dot_w, active, grad_feed_all))
    mix_move = Gather(first, second)

    def conv_grads(got, result, value, weights, rates):
        grad = jnp.stack([jnp.stack(row) for row in got])
        grad = grad.reshape(ycount, spread, 2, batch // 2, local, channels)
        grad = jnp.moveaxis(grad, 2, 0).reshape(grid + (channels,)).astype(wide)
        grad_query = grad * result.astype(wide)
        grad_conv = (grad * short_of(value, weights, 0)).astype(low)
        return grad_query, grad_conv, later_of(spot, grad_conv, rates)

    grad_query, grad_conv, later_end = run(conv_grads, grad_got, convolved, mixed, taps, decay)
    laters = [passed(later_end, "z", -k) for k in range(1, depth)]
    mix_move.turn(line)

    def short_back(grad, weights):
        head = jnp.roll(grad[:, :, :, :2], -1, axis=1)
        whole = jnp.concatenate([grad, jnp.where(closing, 0.0, head)], axis=3)
        result = (
            weights[0] * whole[:, :, :, :-2]
            + weights[1] * whole[:, :, :, 1:-1]
            + weights[2] * whole[:, :, :, 2:]
        )
        one, two = grad[:, :, :, :1], grad[:, :, :, 1:2]
        earlier = jnp.concatenate([weights[2] * one, weights[1] * one + weights[2] * two], axis=3)
        rest = jnp.zeros(grad.shape[:3] + (extra - 2, grad.shape[-1]), wide)
        result = jnp.concatenate([result, jnp.where(opening, earlier, 0.0), rest], axis=3)
        return result.astype(low).reshape(-1, grad.shape[-1])

    feed_back = Scatter(feed_parts)
    up_parts_got = owner_moves(run(owner_parts, up_mine))
    gate_got = owner_moves(run(owner_parts, gate_mine))

    def conv_back(signal, grad, rates, amounts, begin, ends_later, value, weights):
        later = combine(ends_later, rates)
        grad_product, grad_residue, grad_decay = backward_of(
            spot, signal, grad, rates, amounts, begin, later
        )
        grad_product = grad_product.astype(wide)
        keys, values = (short_of(value, weights, g) for g in (1, 2))
        pair = jnp.concatenate([grad_product * values, grad_product * keys], axis=-1)
        return pair, grad_residue, grad_decay

    grad_pair, grad_residue, grad_decay = run(
        conv_back, product, grad_conv, decay, residue, start, laters, mixed, taps
    )

    mix_move.got = run(lambda got: got, mix_move.got)
    up_held = run(owner_held, up_parts_got)
    up_got = moved(up_held, "y", -1)
    grad_mix_all = mix_move.end(line)
    feed_back.got = run(lambda got: got, feed_back.got)

    def in_back(query, pair, weights, v):
        result = jnp.concatenate(
            [
                short_back(query, weights[:, :channels]),
                short_back(pair, weights[:, channels:]),
            ],
            axis=1,
        )
        return result, dot_w(v, result)

    grad_mixed, in_term = run(in_back, grad_query, grad_pair, taps, normed_all)
    in_mine = scatter_tile(in_term)
    feed_back.turn(line)
    gate_held = run(owner_held, gate_got)
    gate_got = moved(gate_held, "y", -1)
    one_back = Scatter(run(lambda a, w: split_sum(dot_t(a, w, low)), grad_mixed, w_in))
    feed_back.got = run(lambda got: got, feed_back.got)
    out_mine = scatter_tile(run(dot_w, gated_all, grad_mix_all))
    up_held = run(stacked, up_held, up_got)
    up_got = moved(up_held, "c", -1)

    def tap_sums(query, pair, value):
        sums = []
        for g, part in enumerate((query, pair[..., :channels], pair[..., channels:])):
            own = extend(value, g)
            sums += [
                jnp.sum(part * own[:, :, :, 2 - j : local + 2 - j], axis=(0, 1, 2, 3))
                for j in range(3)
            ]
        return jnp.stack(sums)

    grad_taps = run(tap_sums, grad_query, grad_pair, mixed)

    def column_whole(own, got):
        return owner_whole(lax.axis_index("c"), [own] + got, depth)

    grad_up_weight = run(column_whole, up_held, up_got)
    gate_held = run(stacked, gate_held, gate_got)
    gate_got = moved(gate_held, "c", -1)
    one_back.turn(line)
    down_held = run(lambda v: v[None], down_mine)
    down_got = moved(down_held, "y", -1)
    grad_gate_weight = run(column_whole, gate_held, gate_got)
    in_got = owner_moves(run(owner_parts, in_mine))

    def normed_sum(rest):
        value = Scatter.sum(*rest).reshape(batch, local + extra, width)
        return value[:, :local], value[:, local : local + 2].astype(low)

    grad_normed, grad_before = run(normed_sum, one_back.rest())
    grad_after = lax.ppermute(grad_before, ("z", "x"), [(j, i) for i, j in last])
    output = run(
        lambda rest, values: (
            mask * (values + Scatter.sum(*rest).reshape(batch, local, width))
        ).astype(low),
        feed_back.rest(),
        middle,
    )
    in_held = run(owner_held, in_got)
    in_got = moved(in_held, "y", -1)

    def tokens_back(grad, extension, values, scale, gain, back, small):
        values = values.astype(wide)
        grad = jnp.concatenate(
            [grad[:, : local - 2], grad[:, local - 2 :] + extension.astype(wide)], axis=1
        )
        result, grad_gain = norm_back(values, scale, gain, grad)
        gains = jnp.stack([grad_gain, small[0]]).reshape(-1, channels)
        return (result + back).astype(low), jnp.concatenate(list(small[1:]) + [gains], axis=0)

    grad_tokens, small = run(
        tokens_back,
        grad_normed,
        grad_after,
        tokens,
        scale_one,
        norm_gain,
        grad_middle,
        (grad_feed_gain, grad_residue, grad_decay, grad_taps),
    )
    small_got = moved(small, "c", 1)
    small = run(lambda v, got: v + sum(got), small, small_got)
    small_got = moved(small, "z", 1)
    in_held = run(stacked, in_held, in_got)
    in_got = moved(in_held, "c", -1)
    small = run(lambda v, got: v + sum(got), small, small_got)
    small_got = moved(small, "x", -1)
    grad_in_weight = run(
        lambda own, got: owner_whole(lax.axis_index("c"), [own] + got, count), in_held, in_got
    )
    down_held = run(lambda own, got: jnp.concatenate([own] + got), down_held, down_got)
    down_got = moved(down_held, "c", -1)
    out_held = run(lambda v: v[None], out_mine)
    out_got = moved(out_held, "y", -1)
    small = run(stacked, small, small_got)
    small_got = moved(small, "y", -1)

    def rows_whole(own, got):
        whole = in_order(jnp.swapaxes(in_order(jnp.stack([own] + got), "c"), 0, 1), "y")
        return whole.reshape(-1, width).astype(wide)

    grad_down = run(rows_whole, down_held, down_got)
    out_held = run(lambda own, got: jnp.concatenate([own] + got), out_held, out_got)
    out_got = moved(out_held, "c", -1)
    poles = decay.shape[0]

    def small_whole(own, got):
        slots = jnp.stack([own] + got)
        rows = 2 * poles + 9
        gains = jnp.sum(slots[:, :, rows:], axis=(0, 1)).reshape(2, width)
        whole = all_channels(slots[:, :, :rows])
        grad_conv_taps = jnp.concatenate(
            [whole[2 * poles + 3 * g : 2 * poles + 3 * g + 3] for g in range(3)], axis=1
        )
        return gains[0], gains[1], grad_conv_taps, whole[:poles].T, whole[poles : 2 * poles].T

    grad_norm_gain, feed_gain_sum, grad_conv_taps, residue_sum, decay_sum = run(
        small_whole, small, small_got
    )

    def out_whole(core, own, got):
        ccount = lax.axis_size("c")
        slots = jnp.stack([own] + got)
        slots = jnp.stack(
            [lax.dynamic_index_in_dim(slots, (j - core) % ccount, 0, False) for j in range(ccount)]
        )
        whole = in_order(jnp.swapaxes(slots, 0, 1), "y")
        return whole.reshape(-1, width).astype(wide)

    grad_out_weight = line.finish(out_whole, out_held, out_got)
    return (
        output,
        grad_tokens,
        grad_norm_gain,
        grad_in_weight,
        grad_conv_taps,
        residue_sum,
        decay_sum,
        grad_out_weight,
        feed_gain_sum,
        grad_gate_weight,
        grad_up_weight,
        grad_down,
    )


def solution(mesh):
    pairs, blocks = mesh.shape["dp"], mesh.shape["seq"]
    devices = mesh.devices.reshape(pairs // cores, cores, depth, blocks // depth)
    inner = Mesh(devices, ("y", "c", "z", "x"))
    dp, seq = ("y", "c"), ("z", "x")
    tokens, rows = P(dp, seq, None), P(seq, None)
    return jax.shard_map(
        body,
        mesh=inner,
        in_specs=(
            tokens,
            P(dp),
            P(),
            rows,
            P(),
            P(),
            P(),
            rows,
            P(),
            rows,
            rows,
            rows,
            tokens,
        ),
        out_specs=(tokens, tokens, P(), rows, P(), P(), P(), rows, P(), rows, rows, rows),
        check_vma=False,
    )
```

```python
import functools

import jax
import jax.numpy as jnp
from jax import lax
from jax.experimental import pallas as pl
from jax.experimental.pallas import tpu as pltpu
from jax.sharding import Mesh, PartitionSpec as P

epsilon = 1e-06
low = jnp.bfloat16
wide = jnp.float32
tile = 8
depth = 4
cores = 2


def turned(value, axis, by):
    length = lax.axis_size(axis)
    return lax.ppermute(value, axis, [(i, (i + by) % length) for i in range(length)])


def passed(value, axis, by):
    length = lax.axis_size(axis)
    pairs = [(i, i + by) for i in range(length) if 0 <= i + by < length]
    return lax.ppermute(value, axis, pairs)


def swap_slots(slots):
    ycount, spread = lax.axis_size("y"), lax.axis_size("x")
    result = []
    for dy in range(ycount):
        line = []
        for dx in range(spread):
            sy, sx = (ycount - dy) % ycount, (spread - dx) % spread
            if sy == 0 and sx == 0:
                line.append(slots[0][0])
                continue
            pairs = [
                (i * spread + j, (i + sy) % ycount * spread + (j + sx) % spread)
                for i in range(ycount)
                for j in range(spread)
            ]
            line.append(lax.ppermute(slots[sy][sx], ("y", "x"), pairs))
        result.append(line)
    return result


class Line:
    def __init__(self, token):
        self.token = token

    def run(self, work, *values):
        values, token = lax.optimization_barrier((values, self.token))
        result, self.token = lax.optimization_barrier((work(*values), token))
        return result

    def finish(self, work, *values):
        values, token = lax.optimization_barrier((values, self.token))
        return work(token, *values)


def moved(value, axis, sign):
    return [turned(value, axis, sign * d) for d in range(1, lax.axis_size(axis))]


class Gather:
    def __init__(self, first, second):
        self.held = (first, second)
        self.got = (moved(first, "x", -1), moved(second, "y", -1))

    def turn(self, line):
        self.held = line.run(
            lambda held, got: tuple(jnp.stack([h] + g) for h, g in zip(held, got)), self.held, self.got
        )
        self.got = (moved(self.held[0], "y", -1), moved(self.held[1], "x", -1))

    def end(self, line):
        def work(held, got):
            first = jnp.stack([held[0]] + got[0])
            second = jnp.swapaxes(jnp.stack([held[1]] + got[1]), 0, 1)
            return jnp.stack([first, second]).reshape(-1, first.shape[-1])

        return line.run(work, self.held, self.got)


def split_sum(partial):
    grid = partial.reshape(2, lax.axis_size("y"), lax.axis_size("x"), -1, partial.shape[-1])
    first = [grid[0][:, d].astype(low) for d in range(grid.shape[2])]
    second = [grid[1][d].astype(low) for d in range(grid.shape[1])]
    return first, second


def add_up(parts, got):
    total = parts[0].astype(wide)
    for g in got:
        total = total + g.astype(wide)
    return total


class Scatter:
    def __init__(self, parts):
        self.parts = parts
        self.send("x", "y")

    def send(self, *axes):
        self.got = [
            [turned(p, axis, d + 1) for d, p in enumerate(part[1:])]
            for part, axis in zip(self.parts, axes)
        ]

    def turn(self, line):
        def work(parts, got):
            result = []
            for part, g in zip(parts, got):
                total = add_up(part, g).astype(low)
                result.append([total[d] for d in range(total.shape[0])])
            return result

        self.parts = line.run(work, self.parts, self.got)
        self.send("y", "x")

    def rest(self):
        return self.parts, self.got

    @staticmethod
    def sum(parts, got):
        return jnp.stack([add_up(part, g) for part, g in zip(parts, got)])


def pick_kernel(count, part, stride, start_ref, source, *refs):
    targets, sems = refs[:-1], refs[-1]
    copies = []
    for d, target in enumerate(targets):
        for k in range(count):
            at = pl.multiple_of((k * stride + start_ref[d]) * part, part)
            copies.append(
                pltpu.make_async_copy(
                    source.at[:, pl.ds(at, part)],
                    target.at[:, k * part : (k + 1) * part],
                    sems.at[d * count + k],
                )
            )
    for copy in copies:
        copy.start()
    for copy in copies:
        copy.wait()


def column_pieces(weight, groups):
    spread, ycount = lax.axis_size("x"), lax.axis_size("y")
    rows = weight.shape[0]
    count = groups * depth
    part = weight.shape[1] // (count * spread * ycount)
    starts = [
        (lax.axis_index("x") + d) % spread * ycount + lax.axis_index("y") for d in range(spread)
    ]
    if part % 128 == 0:
        return pl.pallas_call(
            functools.partial(pick_kernel, count, part, spread * ycount),
            out_shape=[jax.ShapeDtypeStruct((rows, count * part), weight.dtype)] * spread,
            grid_spec=pltpu.PrefetchScalarGridSpec(
                num_scalar_prefetch=1,
                in_specs=[pl.BlockSpec(memory_space=pl.ANY)],
                out_specs=[pl.BlockSpec(memory_space=pltpu.VMEM)] * spread,
                scratch_shapes=[pltpu.SemaphoreType.DMA((count * spread,))],
            ),
            cost_estimate=pl.CostEstimate(
                flops=0, transcendentals=0, bytes_accessed=4 * rows * count * part * spread
            ),
        )(jnp.stack(starts).astype(jnp.int32), weight)
    return [
        jnp.concatenate(
            [
                lax.dynamic_slice_in_dim(weight, (k * spread * ycount + start) * part, part, 1)
                for k in range(count)
            ],
            axis=1,
        )
        for start in starts
    ]


def column_moves(pieces):
    spread, ccount = lax.axis_size("x"), lax.axis_size("c")
    share = spread // ccount
    got = [pieces[0]]
    for d in range(1, spread):
        pairs = [
            (i // share * spread + i, i // share * spread + (i + d) % spread) for i in range(spread)
        ]
        got.append(lax.ppermute(pieces[d], ("c", "x"), pairs))
    return got


def column_block(got):
    spread, ccount = lax.axis_size("x"), lax.axis_size("c")
    share = spread // ccount
    place, core = lax.axis_index("x"), lax.axis_index("c")
    got = jnp.stack(got)
    return jnp.concatenate(
        [
            lax.dynamic_index_in_dim(got, (place - core * share - j) % spread, 0, False)
            for j in range(share)
        ]
    )


def row_block(weight):
    ycount, ccount = lax.axis_size("y"), lax.axis_size("c")
    part = weight.shape[0] // (ycount * ccount)
    pair = lax.axis_index("y") * ccount + lax.axis_index("c")
    return lax.dynamic_slice_in_dim(weight, pair * part, part, 0)


def core_halves(value):
    ccount = lax.axis_size("c")
    width = value.shape[1] // ccount
    core = lax.axis_index("c")
    return [
        lax.dynamic_slice_in_dim(value, (core + d) % ccount * width, width, 1)
        for d in range(ccount)
    ]


def out_block(weight):
    part = weight.shape[0] // lax.axis_size("y")
    rows = lax.dynamic_slice_in_dim(weight, lax.axis_index("y") * part, part, 0)
    return core_halves(rows)[0]


def gather_tile(block):
    return lax.all_gather(block, ("z", "c"), axis=0, tiled=True)


def scatter_tile(term):
    return lax.psum_scatter(term, ("z", "c"), scatter_dimension=0, tiled=True)


def owner_parts(mine):
    spread, ccount = lax.axis_size("x"), lax.axis_size("c")
    share = spread // ccount
    place, core = lax.axis_index("x"), lax.axis_index("c")
    parts = mine.reshape(share, -1, mine.shape[-1])
    return [
        lax.dynamic_index_in_dim(
            parts, jnp.clip((place + d) % spread - core * share, 0, share - 1), 0, False
        )
        for d in range(spread)
    ]


def owner_moves(parts):
    spread, ccount = lax.axis_size("x"), lax.axis_size("c")
    share = spread // ccount
    got = [parts[0]]
    for d in range(1, spread):
        pairs = [
            ((i + d) % spread // share * spread + i, i // share * spread + (i + d) % spread)
            for i in range(spread)
        ]
        got.append(lax.ppermute(parts[d], ("c", "x"), pairs))
    return got


def owner_held(got):
    spread, ccount = lax.axis_size("x"), lax.axis_size("c")
    share = spread // ccount
    place, core = lax.axis_index("x"), lax.axis_index("c")
    got = jnp.stack(got)
    return jnp.stack(
        [
            lax.dynamic_index_in_dim(got, (place - core * share - j) % spread, 0, False)
            for j in range(share)
        ]
    )


def assemble_kernel(count, width, order_ref, *refs):
    sources, target = refs[:-1], refs[-1]
    part = width // count
    ranks = order_ref.shape[0] // 2
    for r in range(ranks):
        core, slot = order_ref[2 * r], order_ref[2 * r + 1]
        value = sources[0][slot]
        for c in range(1, len(sources)):
            value = jnp.where(core == c, sources[c][slot], value)
        value = value.astype(wide)
        for at in range(count):
            start = (at * ranks + r) * part
            target[:, start : start + part] = value[:, at * part : (at + 1) * part]


def owner_whole(core, sources, count):
    spread, ccount, ycount = lax.axis_size("x"), lax.axis_size("c"), lax.axis_size("y")
    share = spread // ccount
    yplace = lax.axis_index("y")
    order = []
    for i in range(spread):
        for k in range(ycount):
            order += [(i // share - core) % ccount, (k - yplace) % ycount * share + i % share]
    sources = [v.reshape((-1,) + v.shape[2:]) for v in sources]
    held, rows, width = sources[0].shape
    block = min(rows, 64)
    return pl.pallas_call(
        functools.partial(assemble_kernel, count, width),
        out_shape=jax.ShapeDtypeStruct((rows, width * spread * ycount), wide),
        grid_spec=pltpu.PrefetchScalarGridSpec(
            num_scalar_prefetch=1,
            grid=(rows // block,),
            in_specs=[pl.BlockSpec((held, block, width), lambda i, order: (0, i, 0))]
            * len(sources),
            out_specs=pl.BlockSpec((block, width * spread * ycount), lambda i, order: (i, 0)),
        ),
        compiler_params=pltpu.CompilerParams(vmem_limit_bytes=56 << 20),
        cost_estimate=pl.CostEstimate(
            flops=0, transcendentals=0, bytes_accessed=6 * rows * width * spread * ycount
        ),
    )(jnp.stack(order).astype(jnp.int32), *sources)


def in_order(slots, axis):
    length = lax.axis_size(axis)
    place = lax.axis_index(axis)
    return jnp.stack(
        [lax.dynamic_index_in_dim(slots, (j - place) % length, 0, False) for j in range(length)]
    )


def rank_rows(values, axis):
    spread, ycount = lax.axis_size("x"), lax.axis_size("y")
    part = values.shape[axis] // (depth * spread * ycount)
    place = lax.axis_index("x") * ycount + lax.axis_index("y")
    return jnp.concatenate(
        [
            lax.dynamic_slice_in_dim(values, (k * spread * ycount + place) * part, part, axis)
            for k in range(depth)
        ],
        axis=axis,
    )


def all_channels(slots):
    whole = in_order(slots, "y")
    whole = in_order(jnp.swapaxes(whole, 0, 1), "x")
    spread, ycount, rows = whole.shape[:3]
    whole = whole.reshape(spread, ycount, rows, depth, -1)
    return jnp.transpose(whole, (2, 3, 0, 1, 4)).reshape(rows, -1)


def fill(source, target, place):
    groups, parts, inner, length = source.shape[:4]
    for j in range(parts):
        slot = lax.rem(j + parts - place, parts)
        for g in range(groups):
            for b in range(inner):
                target[g * inner + b, j * length : (j + 1) * length, :] = source[g, slot, b].astype(
                    wide
                )


def empty(source, target, place):
    groups, parts, inner, length = target.shape[:4]
    for j in range(parts):
        slot = lax.rem(j + parts - place, parts)
        for g in range(groups):
            for b in range(inner):
                target[g, slot, b] = source[g * inner + b, j * length : (j + 1) * length, :].astype(
                    low
                )


def halves(ref):
    return [ref[k * tile : (k + 1) * tile, :] for k in range(ref.shape[0] // tile)]


def row_of(ref, seq, at):
    return ref[seq, pl.ds(at, tile, stride=0), :]


def states_kernel(place_ref, signal_ref, decay_ref, state_ref, held):
    fill(signal_ref, held, place_ref[0])
    seqs, length, lanes = held.shape
    keep = [jnp.exp(-d) for d in halves(decay_ref)]
    count = len(keep)

    def step(i, carry):
        state = list(carry)
        for k in range(tile):
            for n in range(seqs):
                new = row_of(held, n, i * tile + k)
                for h in range(count):
                    at = n * count + h
                    state[at] = keep[h] * state[at] + new
        return tuple(state)

    zero = jnp.zeros((tile, lanes), wide)
    state = lax.fori_loop(0, length // tile, step, tuple(zero for _ in range(seqs * count)))
    for n in range(seqs):
        for h in range(count):
            state_ref[n, h * tile : (h + 1) * tile, :] = state[n * count + h]


def forward_kernel(place_ref, signal_ref, decay_ref, residue_ref, start_ref, out_ref, held, terms, made):
    fill(signal_ref, held, place_ref[0])
    seqs, length, lanes = held.shape
    keep = [jnp.exp(-d) for d in halves(decay_ref)]
    weigh = halves(residue_ref)
    count = len(keep)

    def step(i, carry):
        state = list(carry)
        for k in range(tile):
            for n in range(seqs):
                new = row_of(held, n, i * tile + k)
                total = None
                for h in range(count):
                    at = n * count + h
                    state[at] = keep[h] * state[at] + new
                    term = weigh[h] * state[at]
                    total = term if total is None else total + term
                terms[n, k * tile : (k + 1) * tile, :] = total
        for n in range(seqs):
            result = terms[n, pl.ds(0, tile, stride=tile), :]
            for p in range(1, tile):
                result = result + terms[n, pl.ds(p, tile, stride=tile), :]
            made[n, pl.ds(i * tile, tile), :] = result
        return tuple(state)

    start = tuple(
        start_ref[n, h * tile : (h + 1) * tile, :] for n in range(seqs) for h in range(count)
    )
    lax.fori_loop(0, length // tile, step, start)
    empty(made, out_ref, place_ref[0])


def later_kernel(place_ref, signal_ref, decay_ref, state_ref, held):
    fill(signal_ref, held, place_ref[0])
    seqs, length, lanes = held.shape
    keep = [jnp.exp(-d) for d in halves(decay_ref)]
    count = len(keep)

    def step(i, carry):
        state = list(carry)
        base = length - tile - i * tile
        for k in range(tile - 1, -1, -1):
            for n in range(seqs):
                new = row_of(held, n, base + k)
                for h in range(count):
                    at = n * count + h
                    state[at] = keep[h] * state[at] + new
        return tuple(state)

    zero = jnp.zeros((tile, lanes), wide)
    state = lax.fori_loop(0, length // tile, step, tuple(zero for _ in range(seqs * count)))
    for n in range(seqs):
        for h in range(count):
            state_ref[n, h * tile : (h + 1) * tile, :] = state[n * count + h]


def backward_kernel(
    place_ref,
    signal_ref,
    grad_ref,
    decay_ref,
    residue_ref,
    start_ref,
    end_ref,
    out_ref,
    residue_grad_ref,
    decay_grad_ref,
    held,
    grads,
    terms,
    made,
    later,
):
    fill(signal_ref, held, place_ref[0])
    fill(grad_ref, grads, place_ref[0])
    seqs, length, lanes = held.shape
    keep = [jnp.exp(-d) for d in halves(decay_ref)]
    weigh = halves(residue_ref)
    count = len(keep)
    group = later.shape[0]
    zero = jnp.zeros((tile, lanes), wide)
    none = tuple(zero for _ in range(group * count))
    sum_first = [zero] * count
    sum_second = [zero] * count
    for base_seq in range(0, seqs, group):

        def load(ref):
            return tuple(
                ref[base_seq + n, h * tile : (h + 1) * tile, :]
                for n in range(group)
                for h in range(count)
            )

        def back_step(i, carry):
            state, first = [list(v) for v in carry]
            base = length - tile - i * tile
            for k in range(tile - 1, -1, -1):
                for n in range(group):
                    back = row_of(grads, base_seq + n, base + k)
                    new = row_of(held, base_seq + n, base + k)
                    total = None
                    for h in range(count):
                        at = n * count + h
                        state[at] = keep[h] * state[at] + back
                        first[at] = first[at] + new * state[at]
                        later[n, pl.ds(((base + k) * count + h) * tile, tile), :] = state[at]
                        term = weigh[h] * state[at]
                        total = term if total is None else total + term
                    terms[n, k * tile : (k + 1) * tile, :] = total
            for n in range(group):
                result = terms[n, pl.ds(0, tile, stride=tile), :]
                for p in range(1, tile):
                    result = result + terms[n, pl.ds(p, tile, stride=tile), :]
                made[base_seq + n, pl.ds(base, tile), :] = result
            return tuple(state), tuple(first)

        _, first = lax.fori_loop(0, length // tile, back_step, (load(end_ref), none))

        def ahead(i, carry):
            state, second = [list(v) for v in carry]
            for k in range(tile):
                for n in range(group):
                    new = row_of(held, base_seq + n, i * tile + k)
                    for h in range(count):
                        at = n * count + h
                        state[at] = keep[h] * state[at] + new
                        other = later[n, pl.ds(((i * tile + k) * count + h) * tile, tile), :]
                        second[at] = second[at] + state[at] * other
            return tuple(state), tuple(second)

        _, second = lax.fori_loop(0, length // tile, ahead, (load(start_ref), none))
        for n in range(group):
            for h in range(count):
                at = n * count + h
                sum_first[h] = sum_first[h] + first[at]
                sum_second[h] = sum_second[h] + (second[at] - first[at])
    for h in range(count):
        residue_grad_ref[h * tile : (h + 1) * tile, :] = sum_first[h]
        decay_grad_ref[h * tile : (h + 1) * tile, :] = -weigh[h] * sum_second[h]
    empty(made, out_ref, place_ref[0])


def conv_call(kernel, place, arrays, results, scratch, flops):
    channels = arrays[0].shape[-1]
    lanes = min(channels, 128)

    def spec(shape):
        lead = len(shape) - 1
        return pl.BlockSpec(shape[:-1] + (lanes,), lambda i, *_: (0,) * lead + (i,))

    return pl.pallas_call(
        kernel,
        out_shape=results,
        grid_spec=pltpu.PrefetchScalarGridSpec(
            num_scalar_prefetch=1,
            grid=(channels // lanes,),
            in_specs=[spec(a.shape) for a in arrays],
            out_specs=[spec(r.shape) for r in results],
            scratch_shapes=[pltpu.VMEM(s + (lanes,), wide) for s in scratch],
        ),
        compiler_params=pltpu.CompilerParams(
            dimension_semantics=("arbitrary",), vmem_limit_bytes=56 << 20
        ),
        cost_estimate=pl.CostEstimate(
            flops=flops, transcendentals=0, bytes_accessed=sum(a.size * 4 for a in arrays)
        ),
    )(place, *arrays)


def sizes(signal, poles):
    groups, parts, inner, length, channels = signal.shape
    return groups * inner, parts * length, channels, signal.size * poles


def states_of(place, signal, decay):
    seqs, length, channels, work = sizes(signal, decay.shape[0])
    shape = jax.ShapeDtypeStruct((seqs, decay.shape[0], channels), wide)
    return conv_call(states_kernel, place, [signal, decay], [shape], [(seqs, length)], 2 * work)[0]


def forward_of(place, signal, decay, residue, start):
    seqs, length, channels, work = sizes(signal, decay.shape[0])
    return conv_call(
        forward_kernel,
        place,
        [signal, decay, residue, start],
        [jax.ShapeDtypeStruct(signal.shape, low)],
        [(seqs, length), (seqs, tile * tile), (seqs, length)],
        4 * work,
    )[0]


def later_of(place, signal, decay):
    seqs, length, channels, work = sizes(signal, decay.shape[0])
    shape = jax.ShapeDtypeStruct((seqs, decay.shape[0], channels), wide)
    return conv_call(later_kernel, place, [signal, decay], [shape], [(seqs, length)], 2 * work)[0]


def backward_of(place, signal, grad, decay, residue, start, end):
    poles = decay.shape[0]
    seqs, length, channels, work = sizes(signal, poles)
    shape = jax.ShapeDtypeStruct(decay.shape, wide)
    group = min(seqs, 4)
    return conv_call(
        backward_kernel,
        place,
        [signal, grad, decay, residue, start, end],
        [jax.ShapeDtypeStruct(signal.shape, low), shape, shape],
        [
            (seqs, length),
            (seqs, length),
            (group, tile * tile),
            (seqs, length),
            (group, length * poles),
        ],
        12 * work,
    )


def rms_scale(values):
    return lax.rsqrt(jnp.mean(values * values, axis=-1, keepdims=True) + epsilon)


def norm_back(values, scale, gain, grad_normed):
    grad_gain = jnp.sum(grad_normed * values * scale, axis=(0, 1))
    scaled = grad_normed * gain
    grad_values = scale * scaled - values * scale * scale * scale * jnp.mean(
        scaled * values, axis=-1, keepdims=True
    )
    return (grad_values, grad_gain)


def dot(a, b, kind=wide):
    return jnp.dot(a, b, preferred_element_type=wide).astype(kind)


def dot_t(a, b, kind=wide):
    return lax.dot_general(a, b, (((1,), (1,)), ((), ())), preferred_element_type=wide).astype(kind)


def dot_w(a, b):
    return lax.dot_general(a, b, (((0,), (0,)), ((), ())), preferred_element_type=wide).astype(low)


def body(
    tokens,
    lengths,
    norm_gain,
    in_weight,
    conv_taps,
    filter_residue,
    filter_decay,
    out_weight,
    feed_gain,
    gate_weight,
    up_weight,
    down_weight,
    cotangent,
):
    spread, ycount = lax.axis_size("x"), lax.axis_size("y")
    batch, local, width = tokens.shape
    place = lax.axis_index("z") * spread + lax.axis_index("x")
    position = place * local + jnp.arange(local)
    mask = (position[None, :] < lengths[:, None]).astype(wide)[..., None]
    block = spread * local

    count = 3 * depth
    extra = 8
    line = Line(lax.axis_index("c"))
    run = line.run

    def stacked(value, got):
        return jnp.stack([value] + got)

    w_out = lax.all_gather(run(out_block, out_weight), "z", axis=0, tiled=True)
    in_got = column_moves(run(lambda w: column_pieces(w, 3), in_weight))
    last = [(i * spread + spread - 1, (i + 1) * spread) for i in range(depth - 1)]

    def norm_one(values, gain):
        values = values.astype(wide)
        scale = rms_scale(values)
        normed = (values * scale * gain).astype(low)
        return normed, normed[:, local - 2 :], scale

    normed, ending, scale_one = run(norm_one, tokens, norm_gain)
    before = lax.ppermute(ending, ("z", "x"), last)

    def lengthen(values, rows):
        rest = jnp.zeros((batch, extra - 2, width), values.dtype)
        values = jnp.concatenate([values, rows, rest], axis=1)
        return values[: batch // 2], values[batch // 2 :]

    normed_move = Gather(*run(lengthen, normed, before))
    gate_got = column_moves(run(lambda w: column_pieces(w, 1), gate_weight))
    in_block, w_out = run(lambda got, w: (column_block(got), w), in_got, w_out)
    w_in = gather_tile(in_block)
    normed_move.turn(line)
    w_down = gather_tile(run(row_block, down_weight))
    out_move = Gather(*run(lambda w: (w[None, : w.shape[0] // 2], w[None, w.shape[0] // 2 :]), w_out))
    up_got = column_moves(run(lambda w: column_pieces(w, 1), up_weight))
    normed_all = normed_move.end(line)
    out_move.turn(line)

    channels = w_in.shape[1] // 3
    half = channels // 2
    grid = (2 * ycount, spread, batch // 2, local)

    def rank_values(all_taps, all_decay, all_residue):
        return (
            jnp.concatenate(
                [rank_rows(all_taps[:, g * width : (g + 1) * width], 1) for g in range(3)], axis=1
            ),
            rank_rows(all_decay, 0).T,
            rank_rows(all_residue, 0).T,
        )

    taps, decay, residue = run(rank_values, conv_taps, filter_decay, filter_residue)
    opening = (lax.axis_index("x") + jnp.arange(spread)) % spread == 0
    opening = opening[None, :, None, None, None]
    closing = (lax.axis_index("x") + jnp.arange(spread)) % spread == spread - 1
    closing = closing[None, :, None, None, None]

    def project(v, w):
        return dot(v, w, low).reshape(grid[:3] + (local + extra, 3 * channels))

    mixed = run(project, normed_all, w_in)
    out_move.got = run(lambda got: got, out_move.got)

    def extend(value, g):
        own = value[..., g * channels : (g + 1) * channels]
        earlier = jnp.roll(own[:, :, :, local - 2 : local], 1, axis=1)
        earlier = jnp.where(opening, own[:, :, :, local : local + 2], earlier)
        return jnp.concatenate([earlier, own[:, :, :, :local]], axis=3).astype(wide)

    def short_of(value, weights, g):
        longer = extend(value, g)
        own = weights[:, g * channels : (g + 1) * channels]
        return own[0] * longer[:, :, :, 2:] + own[1] * longer[:, :, :, 1:-1] + own[2] * longer[:, :, :, :-2]

    spot = lax.axis_index("x").astype(jnp.int32).reshape(1)

    def multiply(value, weights, rates):
        keys, values = (short_of(value, weights, g) for g in (1, 2))
        product = (keys * values).astype(low)
        return product, states_of(spot, product, rates)

    product, state_end = run(multiply, mixed, taps, decay)
    states = [passed(state_end, "z", k) for k in range(1, depth)]
    w_gate = gather_tile(run(column_block, gate_got))
    out_own = out_move.end(line)
    w_out = [out_own] + moved(out_own, "c", -1)

    def feed_grad(values):
        values = (values.astype(wide) * mask).astype(low)
        return values[: batch // 2], values[batch // 2 :]

    feed_move = Gather(*run(feed_grad, cotangent))

    def combine(parts, rates):
        total = parts[0]
        for k in range(1, depth - 1):
            total = total + jnp.exp(-rates * (k * block)) * parts[k]
        return total

    def convolve(parts, value, weights, signal, rates, amounts):
        start = combine(parts, rates)
        result = forward_of(spot, signal, rates, amounts, start)
        query = short_of(value, weights, 0)
        gated = (query * result.astype(wide)).astype(low)
        slots = gated.reshape(2, ycount, spread, -1, channels)
        return (
            start,
            result,
            gated.reshape(-1, channels),
            [[slots[:, k, i].reshape(-1, channels) for i in range(spread)] for k in range(ycount)],
        )

    start, convolved, gated_all, gated = run(
        convolve, states, mixed, taps, product, decay, residue
    )
    gated_got = swap_slots(gated)
    w_up = gather_tile(run(column_block, up_got))
    feed_move.turn(line)

    def mix(got, weights, values, gain):
        own = jnp.concatenate(
            [g[:, h * half : (h + 1) * half] for h in range(2) for row in got for g in row], axis=1
        )
        mixer = in_order(jnp.stack([dot(own, w) for w in weights]), "c")
        mixer = jnp.concatenate([m for m in mixer], axis=1).reshape(batch, local, width)
        middle = values.astype(wide) + mixer
        scale = rms_scale(middle)
        normed = (middle * scale * gain).astype(low)
        return middle, scale, normed[: batch // 2], normed[batch // 2 :]

    middle, scale_two, first, second = run(mix, gated_got, w_out, tokens, feed_gain)

    two_move = Gather(first, second)
    two_move.turn(line)
    grad_feed_all = feed_move.end(line)
    grad_active = run(dot_t, grad_feed_all, w_down)
    normed_two_all = two_move.end(line)

    def open_gate(v, w, back):
        value = dot(v, w)
        return value, (back * value * jax.nn.sigmoid(value)).astype(low)

    gate, grad_upper = run(open_gate, normed_two_all, w_gate, grad_active)
    up_term = run(dot_w, normed_two_all, grad_upper)
    up_mine = scatter_tile(up_term)

    def activate(v, w, value, back):
        upper = dot(v, w)
        sigma = jax.nn.sigmoid(value)
        return (
            (value * sigma * upper).astype(low),
            (back * upper * sigma * (1.0 + value * (1.0 - sigma))).astype(low),
        )

    active, grad_gate = run(activate, normed_two_all, w_up, gate, grad_active)
    two_back = Scatter(
        run(
            lambda a, b, wa, wb: split_sum((dot_t(a, wa) + dot_t(b, wb)).astype(low)),
            grad_gate,
            grad_upper,
            w_gate,
            w_up,
        )
    )
    gate_mine = scatter_tile(run(dot_w, normed_two_all, grad_gate))
    two_back.turn(line)
    feed_parts = run(lambda a, w: split_sum(dot(a, w, low)), active, w_down)

    def middle_back(rest, values, scale, gain, back, weights):
        grad_normed = Scatter.sum(*rest).reshape(batch, local, width)
        result, grad_gain = norm_back(values, scale, gain, grad_normed)
        result = result + back.astype(wide) * mask
        parts = core_halves(result.astype(low).reshape(-1, width))
        own = sum(dot_t(m, w) for m, w in zip(parts, weights)).astype(low)
        ranks = ycount * spread

        def slot(at):
            pieces = [
                own[:, (h * ranks + at) * half : (h * ranks + at + 1) * half] for h in range(2)
            ]
            return jnp.concatenate(pieces, axis=1)

        slots = [[slot(k * spread + i) for i in range(spread)] for k in range(ycount)]
        rounded = result.astype(low)
        return result, grad_gain, rounded[: batch // 2], rounded[batch // 2 :], slots

    grad_middle, grad_feed_gain, first, second, grad_slots = run(
        middle_back, two_back.rest(), middle, scale_two, feed_gain, cotangent, w_out
    )
    grad_got = swap_slots(grad_slots)
    down_mine = scatter_tile(run(dot_w, active, grad_feed_all))
    mix_move = Gather(first, second)

    def conv_grads(got, result, value, weights, rates):
        grad = jnp.stack([jnp.stack(row) for row in got])
        grad = grad.reshape(ycount, spread, 2, batch // 2, local, channels)
        grad = jnp.moveaxis(grad, 2, 0).reshape(grid + (channels,)).astype(wide)
        grad_query = grad * result.astype(wide)
        grad_conv = (grad * short_of(value, weights, 0)).astype(low)
        return grad_query, grad_conv, later_of(spot, grad_conv, rates)

    grad_query, grad_conv, later_end = run(conv_grads, grad_got, convolved, mixed, taps, decay)
    laters = [passed(later_end, "z", -k) for k in range(1, depth)]
    mix_move.turn(line)

    def short_back(grad, weights):
        head = jnp.roll(grad[:, :, :, :2], -1, axis=1)
        whole = jnp.concatenate([grad, jnp.where(closing, 0.0, head)], axis=3)
        result = (
            weights[0] * whole[:, :, :, :-2]
            + weights[1] * whole[:, :, :, 1:-1]
            + weights[2] * whole[:, :, :, 2:]
        )
        one, two = grad[:, :, :, :1], grad[:, :, :, 1:2]
        earlier = jnp.concatenate([weights[2] * one, weights[1] * one + weights[2] * two], axis=3)
        rest = jnp.zeros(grad.shape[:3] + (extra - 2, grad.shape[-1]), wide)
        result = jnp.concatenate([result, jnp.where(opening, earlier, 0.0), rest], axis=3)
        return result.astype(low).reshape(-1, grad.shape[-1])

    feed_back = Scatter(feed_parts)
    up_parts_got = owner_moves(run(owner_parts, up_mine))
    gate_got = owner_moves(run(owner_parts, gate_mine))

    def conv_back(signal, grad, rates, amounts, begin, ends_later, value, weights):
        later = combine(ends_later, rates)
        grad_product, grad_residue, grad_decay = backward_of(
            spot, signal, grad, rates, amounts, begin, later
        )
        grad_product = grad_product.astype(wide)
        keys, values = (short_of(value, weights, g) for g in (1, 2))
        pair = jnp.concatenate([grad_product * values, grad_product * keys], axis=-1)
        return pair, grad_residue, grad_decay

    grad_pair, grad_residue, grad_decay = run(
        conv_back, product, grad_conv, decay, residue, start, laters, mixed, taps
    )

    mix_move.got = run(lambda got: got, mix_move.got)
    up_held = run(owner_held, up_parts_got)
    up_got = moved(up_held, "y", -1)
    grad_mix_all = mix_move.end(line)
    feed_back.got = run(lambda got: got, feed_back.got)

    def in_back(query, pair, weights, v):
        result = jnp.concatenate(
            [
                short_back(query, weights[:, :channels]),
                short_back(pair, weights[:, channels:]),
            ],
            axis=1,
        )
        return result, dot_w(v, result)

    grad_mixed, in_term = run(in_back, grad_query, grad_pair, taps, normed_all)
    in_mine = scatter_tile(in_term)
    feed_back.turn(line)
    gate_held = run(owner_held, gate_got)
    gate_got = moved(gate_held, "y", -1)
    one_back = Scatter(run(lambda a, w: split_sum(dot_t(a, w, low)), grad_mixed, w_in))
    feed_back.got = run(lambda got: got, feed_back.got)
    out_mine = scatter_tile(run(dot_w, gated_all, grad_mix_all))
    up_held = run(stacked, up_held, up_got)
    up_got = moved(up_held, "c", -1)

    def tap_sums(query, pair, value):
        sums = []
        for g, part in enumerate((query, pair[..., :channels], pair[..., channels:])):
            own = extend(value, g)
            sums += [
                jnp.sum(part * own[:, :, :, 2 - j : local + 2 - j], axis=(0, 1, 2, 3))
                for j in range(3)
            ]
        return jnp.stack(sums)

    grad_taps = run(tap_sums, grad_query, grad_pair, mixed)

    def column_whole(own, got):
        return owner_whole(lax.axis_index("c"), [own] + got, depth)

    small = run(
        lambda a, b, c, gain: jnp.concatenate([a, b, c, gain.reshape(-1, channels)], axis=0),
        grad_residue,
        grad_decay,
        grad_taps,
        grad_feed_gain,
    )
    small_got = moved(small, "c", 1)
    grad_up_weight = run(column_whole, up_held, up_got)
    small = run(lambda v, got: v + sum(got), small, small_got)
    small_got = moved(small, "z", 1)
    gate_held = run(stacked, gate_held, gate_got)
    gate_got = moved(gate_held, "c", -1)
    one_back.turn(line)
    down_held = run(lambda v: v[None], down_mine)
    down_got = moved(down_held, "y", -1)
    grad_gate_weight = run(column_whole, gate_held, gate_got)
    in_got = owner_moves(run(owner_parts, in_mine))

    def normed_sum(rest):
        value = Scatter.sum(*rest).reshape(batch, local + extra, width)
        return value[:, :local], value[:, local : local + 2].astype(low)

    grad_normed, grad_before = run(normed_sum, one_back.rest())
    grad_after = lax.ppermute(grad_before, ("z", "x"), [(j, i) for i, j in last])
    output = run(
        lambda rest, values: (
            mask * (values + Scatter.sum(*rest).reshape(batch, local, width))
        ).astype(low),
        feed_back.rest(),
        middle,
    )
    small = run(lambda v, got: v + sum(got), small, small_got)
    small_got = moved(small, "x", -1)
    in_held = run(owner_held, in_got)
    in_got = moved(in_held, "y", -1)
    small = run(stacked, small, small_got)
    small_got = moved(small, "y", -1)

    def tokens_back(grad, extension, values, scale, gain, back):
        values = values.astype(wide)
        grad = jnp.concatenate(
            [grad[:, : local - 2], grad[:, local - 2 :] + extension.astype(wide)], axis=1
        )
        result, grad_gain = norm_back(values, scale, gain, grad)
        return (result + back).astype(low), grad_gain.reshape(-1, channels)

    grad_tokens, gain_sum = run(
        tokens_back, grad_normed, grad_after, tokens, scale_one, norm_gain, grad_middle
    )
    gain_got = moved(gain_sum, "c", 1)
    poles = decay.shape[0]

    def small_whole(own, got):
        slots = jnp.stack([own] + got)
        rows = 2 * poles + 9
        gain = jnp.sum(slots[:, :, rows:], axis=(0, 1)).reshape(width)
        whole = all_channels(slots[:, :, :rows])
        grad_conv_taps = jnp.concatenate(
            [whole[2 * poles + 3 * g : 2 * poles + 3 * g + 3] for g in range(3)], axis=1
        )
        return gain, grad_conv_taps, whole[:poles].T, whole[poles : 2 * poles].T

    feed_gain_sum, grad_conv_taps, residue_sum, decay_sum = run(small_whole, small, small_got)
    gain_sum = run(lambda v, got: v + sum(got), gain_sum, gain_got)
    gain_got = moved(gain_sum, "z", 1)
    in_held = run(stacked, in_held, in_got)
    in_got = moved(in_held, "c", -1)
    down_held = run(lambda own, got: jnp.concatenate([own] + got), down_held, down_got)
    down_got = moved(down_held, "c", -1)
    out_held = run(lambda v: v[None], out_mine)
    out_got = moved(out_held, "y", -1)
    grad_in_weight = run(
        lambda own, got: owner_whole(lax.axis_index("c"), [own] + got, count), in_held, in_got
    )
    gain_sum = run(lambda v, got: v + sum(got), gain_sum, gain_got)
    gain_got = swap_slots([[gain_sum] * spread] * ycount)

    def rows_whole(own, got):
        whole = in_order(jnp.swapaxes(in_order(jnp.stack([own] + got), "c"), 0, 1), "y")
        return whole.reshape(-1, width).astype(wide)

    grad_down = run(rows_whole, down_held, down_got)
    out_held = run(lambda own, got: jnp.concatenate([own] + got), out_held, out_got)
    out_got = moved(out_held, "c", -1)
    grad_norm_gain = run(lambda got: sum(sum(got, [])).reshape(width), gain_got)

    def out_whole(core, own, got):
        ccount = lax.axis_size("c")
        slots = jnp.stack([own] + got)
        slots = jnp.stack(
            [lax.dynamic_index_in_dim(slots, (j - core) % ccount, 0, False) for j in range(ccount)]
        )
        whole = in_order(jnp.swapaxes(slots, 0, 1), "y")
        return whole.reshape(-1, width).astype(wide)

    grad_out_weight = line.finish(out_whole, out_held, out_got)
    return (
        output,
        grad_tokens,
        grad_norm_gain,
        grad_in_weight,
        grad_conv_taps,
        residue_sum,
        decay_sum,
        grad_out_weight,
        feed_gain_sum,
        grad_gate_weight,
        grad_up_weight,
        grad_down,
    )


def solution(mesh):
    pairs, blocks = mesh.shape["dp"], mesh.shape["seq"]
    devices = mesh.devices.reshape(pairs // cores, cores, depth, blocks // depth)
    inner = Mesh(devices, ("y", "c", "z", "x"))
    dp, seq = ("y", "c"), ("z", "x")
    tokens, rows = P(dp, seq, None), P(seq, None)
    return jax.shard_map(
        body,
        mesh=inner,
        in_specs=(
            tokens,
            P(dp),
            P(),
            rows,
            P(),
            P(),
            P(),
            rows,
            P(),
            rows,
            rows,
            rows,
            tokens,
        ),
        out_specs=(tokens, tokens, P(), rows, P(), P(), P(), rows, P(), rows, rows, rows),
        check_vma=False,
    )
```

```python
import functools

import jax
import jax.numpy as jnp
from jax import lax
from jax.experimental import pallas as pl
from jax.experimental.pallas import tpu as pltpu
from jax.sharding import Mesh, PartitionSpec as P

epsilon = 1e-06
low = jnp.bfloat16
wide = jnp.float32
tile = 8
depth = 4
cores = 2


def turned(value, axis, by):
    length = lax.axis_size(axis)
    return lax.ppermute(value, axis, [(i, (i + by) % length) for i in range(length)])


def passed(value, axis, by):
    length = lax.axis_size(axis)
    pairs = [(i, i + by) for i in range(length) if 0 <= i + by < length]
    return lax.ppermute(value, axis, pairs)


def swap_slots(slots):
    ycount, spread = lax.axis_size("y"), lax.axis_size("x")
    result = []
    for dy in range(ycount):
        line = []
        for dx in range(spread):
            sy, sx = (ycount - dy) % ycount, (spread - dx) % spread
            if sy == 0 and sx == 0:
                line.append(slots[0][0])
                continue
            pairs = [
                (i * spread + j, (i + sy) % ycount * spread + (j + sx) % spread)
                for i in range(ycount)
                for j in range(spread)
            ]
            line.append(lax.ppermute(slots[sy][sx], ("y", "x"), pairs))
        result.append(line)
    return result


class Line:
    def __init__(self, token):
        self.token = token

    def run(self, work, *values):
        values, token = lax.optimization_barrier((values, self.token))
        result, self.token = lax.optimization_barrier((work(*values), token))
        return result

    def finish(self, work, *values):
        values, token = lax.optimization_barrier((values, self.token))
        return work(token, *values)


def moved(value, axis, sign):
    return [turned(value, axis, sign * d) for d in range(1, lax.axis_size(axis))]


class Gather:
    def __init__(self, first, second):
        self.held = (first, second)
        self.got = (moved(first, "x", -1), moved(second, "y", -1))

    def turn(self, line):
        self.held = line.run(
            lambda held, got: tuple(jnp.stack([h] + g) for h, g in zip(held, got)), self.held, self.got
        )
        self.got = (moved(self.held[0], "y", -1), moved(self.held[1], "x", -1))

    def end(self, line):
        def work(held, got):
            first = jnp.stack([held[0]] + got[0])
            second = jnp.swapaxes(jnp.stack([held[1]] + got[1]), 0, 1)
            return jnp.stack([first, second]).reshape(-1, first.shape[-1])

        return line.run(work, self.held, self.got)


def split_sum(partial):
    grid = partial.reshape(2, lax.axis_size("y"), lax.axis_size("x"), -1, partial.shape[-1])
    first = [grid[0][:, d].astype(low) for d in range(grid.shape[2])]
    second = [grid[1][d].astype(low) for d in range(grid.shape[1])]
    return first, second


def add_up(parts, got):
    total = parts[0].astype(wide)
    for g in got:
        total = total + g.astype(wide)
    return total


class Scatter:
    def __init__(self, parts):
        self.parts = parts
        self.send("x", "y")

    def send(self, *axes):
        self.got = [
            [turned(p, axis, d + 1) for d, p in enumerate(part[1:])]
            for part, axis in zip(self.parts, axes)
        ]

    def turn(self, line):
        def work(parts, got):
            result = []
            for part, g in zip(parts, got):
                total = add_up(part, g).astype(low)
                result.append([total[d] for d in range(total.shape[0])])
            return result

        self.parts = line.run(work, self.parts, self.got)
        self.send("y", "x")

    def rest(self):
        return self.parts, self.got

    @staticmethod
    def sum(parts, got):
        return jnp.stack([add_up(part, g) for part, g in zip(parts, got)])


def pick_kernel(count, part, stride, start_ref, source, *refs):
    targets, sems = refs[:-1], refs[-1]
    copies = []
    for d, target in enumerate(targets):
        for k in range(count):
            at = pl.multiple_of((k * stride + start_ref[d]) * part, part)
            copies.append(
                pltpu.make_async_copy(
                    source.at[:, pl.ds(at, part)],
                    target.at[:, k * part : (k + 1) * part],
                    sems.at[d * count + k],
                )
            )
    for copy in copies:
        copy.start()
    for copy in copies:
        copy.wait()


def column_pieces(weight, groups):
    spread, ycount = lax.axis_size("x"), lax.axis_size("y")
    rows = weight.shape[0]
    count = groups * depth
    part = weight.shape[1] // (count * spread * ycount)
    starts = [
        (lax.axis_index("x") + d) % spread * ycount + lax.axis_index("y") for d in range(spread)
    ]
    if part % 128 == 0:
        return pl.pallas_call(
            functools.partial(pick_kernel, count, part, spread * ycount),
            out_shape=[jax.ShapeDtypeStruct((rows, count * part), weight.dtype)] * spread,
            grid_spec=pltpu.PrefetchScalarGridSpec(
                num_scalar_prefetch=1,
                in_specs=[pl.BlockSpec(memory_space=pl.ANY)],
                out_specs=[pl.BlockSpec(memory_space=pltpu.VMEM)] * spread,
                scratch_shapes=[pltpu.SemaphoreType.DMA((count * spread,))],
            ),
            cost_estimate=pl.CostEstimate(
                flops=0, transcendentals=0, bytes_accessed=4 * rows * count * part * spread
            ),
        )(jnp.stack(starts).astype(jnp.int32), weight)
    return [
        jnp.concatenate(
            [
                lax.dynamic_slice_in_dim(weight, (k * spread * ycount + start) * part, part, 1)
                for k in range(count)
            ],
            axis=1,
        )
        for start in starts
    ]


def column_moves(pieces):
    spread, ccount = lax.axis_size("x"), lax.axis_size("c")
    share = spread // ccount
    got = [pieces[0]]
    for d in range(1, spread):
        pairs = [
            (i // share * spread + i, i // share * spread + (i + d) % spread) for i in range(spread)
        ]
        got.append(lax.ppermute(pieces[d], ("c", "x"), pairs))
    return got


def column_block(got):
    spread, ccount = lax.axis_size("x"), lax.axis_size("c")
    share = spread // ccount
    place, core = lax.axis_index("x"), lax.axis_index("c")
    got = jnp.stack(got)
    return jnp.concatenate(
        [
            lax.dynamic_index_in_dim(got, (place - core * share - j) % spread, 0, False)
            for j in range(share)
        ]
    )


def row_block(weight):
    ycount, ccount = lax.axis_size("y"), lax.axis_size("c")
    part = weight.shape[0] // (ycount * ccount)
    pair = lax.axis_index("y") * ccount + lax.axis_index("c")
    return lax.dynamic_slice_in_dim(weight, pair * part, part, 0)


def core_halves(value):
    ccount = lax.axis_size("c")
    width = value.shape[1] // ccount
    core = lax.axis_index("c")
    return [
        lax.dynamic_slice_in_dim(value, (core + d) % ccount * width, width, 1)
        for d in range(ccount)
    ]


def out_block(weight):
    part = weight.shape[0] // lax.axis_size("y")
    rows = lax.dynamic_slice_in_dim(weight, lax.axis_index("y") * part, part, 0)
    return core_halves(rows)[0]


def gather_tile(block):
    return lax.all_gather(block, ("z", "c"), axis=0, tiled=True)


def scatter_tile(term):
    return lax.psum_scatter(term, ("z", "c"), scatter_dimension=0, tiled=True)


def owner_parts(mine):
    spread, ccount = lax.axis_size("x"), lax.axis_size("c")
    share = spread // ccount
    place, core = lax.axis_index("x"), lax.axis_index("c")
    parts = mine.reshape(share, -1, mine.shape[-1])
    return [
        lax.dynamic_index_in_dim(
            parts, jnp.clip((place + d) % spread - core * share, 0, share - 1), 0, False
        )
        for d in range(spread)
    ]


def owner_moves(parts):
    spread, ccount = lax.axis_size("x"), lax.axis_size("c")
    share = spread // ccount
    got = [parts[0]]
    for d in range(1, spread):
        pairs = [
            ((i + d) % spread // share * spread + i, i // share * spread + (i + d) % spread)
            for i in range(spread)
        ]
        got.append(lax.ppermute(parts[d], ("c", "x"), pairs))
    return got


def owner_held(got):
    spread, ccount = lax.axis_size("x"), lax.axis_size("c")
    share = spread // ccount
    place, core = lax.axis_index("x"), lax.axis_index("c")
    got = jnp.stack(got)
    return jnp.stack(
        [
            lax.dynamic_index_in_dim(got, (place - core * share - j) % spread, 0, False)
            for j in range(share)
        ]
    )


def assemble_kernel(count, width, order_ref, *refs):
    sources, target = refs[:-1], refs[-1]
    part = width // count
    ranks = order_ref.shape[0] // 2
    for r in range(ranks):
        core, slot = order_ref[2 * r], order_ref[2 * r + 1]
        value = sources[0][slot]
        for c in range(1, len(sources)):
            value = jnp.where(core == c, sources[c][slot], value)
        value = value.astype(wide)
        for at in range(count):
            start = (at * ranks + r) * part
            target[:, start : start + part] = value[:, at * part : (at + 1) * part]


def owner_whole(core, sources, count):
    spread, ccount, ycount = lax.axis_size("x"), lax.axis_size("c"), lax.axis_size("y")
    share = spread // ccount
    yplace = lax.axis_index("y")
    order = []
    for i in range(spread):
        for k in range(ycount):
            order += [(i // share - core) % ccount, (k - yplace) % ycount * share + i % share]
    sources = [v.reshape((-1,) + v.shape[2:]) for v in sources]
    held, rows, width = sources[0].shape
    block = min(rows, 64)
    return pl.pallas_call(
        functools.partial(assemble_kernel, count, width),
        out_shape=jax.ShapeDtypeStruct((rows, width * spread * ycount), wide),
        grid_spec=pltpu.PrefetchScalarGridSpec(
            num_scalar_prefetch=1,
            grid=(rows // block,),
            in_specs=[pl.BlockSpec((held, block, width), lambda i, order: (0, i, 0))]
            * len(sources),
            out_specs=pl.BlockSpec((block, width * spread * ycount), lambda i, order: (i, 0)),
        ),
        compiler_params=pltpu.CompilerParams(vmem_limit_bytes=56 << 20),
        cost_estimate=pl.CostEstimate(
            flops=0, transcendentals=0, bytes_accessed=6 * rows * width * spread * ycount
        ),
    )(jnp.stack(order).astype(jnp.int32), *sources)


def in_order(slots, axis):
    length = lax.axis_size(axis)
    place = lax.axis_index(axis)
    return jnp.stack(
        [lax.dynamic_index_in_dim(slots, (j - place) % length, 0, False) for j in range(length)]
    )


def rank_rows(values, axis):
    spread, ycount = lax.axis_size("x"), lax.axis_size("y")
    part = values.shape[axis] // (depth * spread * ycount)
    place = lax.axis_index("x") * ycount + lax.axis_index("y")
    return jnp.concatenate(
        [
            lax.dynamic_slice_in_dim(values, (k * spread * ycount + place) * part, part, axis)
            for k in range(depth)
        ],
        axis=axis,
    )


def all_channels(slots):
    whole = in_order(slots, "y")
    whole = in_order(jnp.swapaxes(whole, 0, 1), "x")
    spread, ycount, rows = whole.shape[:3]
    whole = whole.reshape(spread, ycount, rows, depth, -1)
    return jnp.transpose(whole, (2, 3, 0, 1, 4)).reshape(rows, -1)


def fill(source, target, place):
    groups, parts, inner, length = source.shape[:4]
    for j in range(parts):
        slot = lax.rem(j + parts - place, parts)
        for g in range(groups):
            for b in range(inner):
                target[g * inner + b, j * length : (j + 1) * length, :] = source[g, slot, b].astype(
                    wide
                )


def empty(source, target, place):
    groups, parts, inner, length = target.shape[:4]
    for j in range(parts):
        slot = lax.rem(j + parts - place, parts)
        for g in range(groups):
            for b in range(inner):
                target[g, slot, b] = source[g * inner + b, j * length : (j + 1) * length, :].astype(
                    low
                )


def halves(ref):
    return [ref[k * tile : (k + 1) * tile, :] for k in range(ref.shape[0] // tile)]


def row_of(ref, seq, at):
    return ref[seq, pl.ds(at, tile, stride=0), :]


def states_kernel(place_ref, signal_ref, decay_ref, state_ref, held):
    fill(signal_ref, held, place_ref[0])
    seqs, length, lanes = held.shape
    keep = [jnp.exp(-d) for d in halves(decay_ref)]
    count = len(keep)

    def step(i, carry):
        state = list(carry)
        for k in range(tile):
            for n in range(seqs):
                new = row_of(held, n, i * tile + k)
                for h in range(count):
                    at = n * count + h
                    state[at] = keep[h] * state[at] + new
        return tuple(state)

    zero = jnp.zeros((tile, lanes), wide)
    state = lax.fori_loop(0, length // tile, step, tuple(zero for _ in range(seqs * count)))
    for n in range(seqs):
        for h in range(count):
            state_ref[n, h * tile : (h + 1) * tile, :] = state[n * count + h]


def forward_kernel(place_ref, signal_ref, decay_ref, residue_ref, start_ref, out_ref, held, terms, made):
    fill(signal_ref, held, place_ref[0])
    seqs, length, lanes = held.shape
    keep = [jnp.exp(-d) for d in halves(decay_ref)]
    weigh = halves(residue_ref)
    count = len(keep)

    def step(i, carry):
        state = list(carry)
        for k in range(tile):
            for n in range(seqs):
                new = row_of(held, n, i * tile + k)
                total = None
                for h in range(count):
                    at = n * count + h
                    state[at] = keep[h] * state[at] + new
                    term = weigh[h] * state[at]
                    total = term if total is None else total + term
                terms[n, k * tile : (k + 1) * tile, :] = total
        for n in range(seqs):
            result = terms[n, pl.ds(0, tile, stride=tile), :]
            for p in range(1, tile):
                result = result + terms[n, pl.ds(p, tile, stride=tile), :]
            made[n, pl.ds(i * tile, tile), :] = result
        return tuple(state)

    start = tuple(
        start_ref[n, h * tile : (h + 1) * tile, :] for n in range(seqs) for h in range(count)
    )
    lax.fori_loop(0, length // tile, step, start)
    empty(made, out_ref, place_ref[0])


def later_kernel(place_ref, signal_ref, decay_ref, state_ref, held):
    fill(signal_ref, held, place_ref[0])
    seqs, length, lanes = held.shape
    keep = [jnp.exp(-d) for d in halves(decay_ref)]
    count = len(keep)

    def step(i, carry):
        state = list(carry)
        base = length - tile - i * tile
        for k in range(tile - 1, -1, -1):
            for n in range(seqs):
                new = row_of(held, n, base + k)
                for h in range(count):
                    at = n * count + h
                    state[at] = keep[h] * state[at] + new
        return tuple(state)

    zero = jnp.zeros((tile, lanes), wide)
    state = lax.fori_loop(0, length // tile, step, tuple(zero for _ in range(seqs * count)))
    for n in range(seqs):
        for h in range(count):
            state_ref[n, h * tile : (h + 1) * tile, :] = state[n * count + h]


def backward_kernel(
    place_ref,
    signal_ref,
    grad_ref,
    decay_ref,
    residue_ref,
    start_ref,
    end_ref,
    out_ref,
    residue_grad_ref,
    decay_grad_ref,
    held,
    grads,
    terms,
    made,
    later,
):
    fill(signal_ref, held, place_ref[0])
    fill(grad_ref, grads, place_ref[0])
    seqs, length, lanes = held.shape
    keep = [jnp.exp(-d) for d in halves(decay_ref)]
    weigh = halves(residue_ref)
    count = len(keep)
    group = later.shape[0]
    zero = jnp.zeros((tile, lanes), wide)
    none = tuple(zero for _ in range(group * count))
    sum_first = [zero] * count
    sum_second = [zero] * count
    for base_seq in range(0, seqs, group):

        def load(ref):
            return tuple(
                ref[base_seq + n, h * tile : (h + 1) * tile, :]
                for n in range(group)
                for h in range(count)
            )

        def back_step(i, carry):
            state, first = [list(v) for v in carry]
            base = length - tile - i * tile
            for k in range(tile - 1, -1, -1):
                for n in range(group):
                    back = row_of(grads, base_seq + n, base + k)
                    new = row_of(held, base_seq + n, base + k)
                    total = None
                    for h in range(count):
                        at = n * count + h
                        state[at] = keep[h] * state[at] + back
                        first[at] = first[at] + new * state[at]
                        later[n, pl.ds(((base + k) * count + h) * tile, tile), :] = state[at]
                        term = weigh[h] * state[at]
                        total = term if total is None else total + term
                    terms[n, k * tile : (k + 1) * tile, :] = total
            for n in range(group):
                result = terms[n, pl.ds(0, tile, stride=tile), :]
                for p in range(1, tile):
                    result = result + terms[n, pl.ds(p, tile, stride=tile), :]
                made[base_seq + n, pl.ds(base, tile), :] = result
            return tuple(state), tuple(first)

        _, first = lax.fori_loop(0, length // tile, back_step, (load(end_ref), none))

        def ahead(i, carry):
            state, second = [list(v) for v in carry]
            for k in range(tile):
                for n in range(group):
                    new = row_of(held, base_seq + n, i * tile + k)
                    for h in range(count):
                        at = n * count + h
                        state[at] = keep[h] * state[at] + new
                        other = later[n, pl.ds(((i * tile + k) * count + h) * tile, tile), :]
                        second[at] = second[at] + state[at] * other
            return tuple(state), tuple(second)

        _, second = lax.fori_loop(0, length // tile, ahead, (load(start_ref), none))
        for n in range(group):
            for h in range(count):
                at = n * count + h
                sum_first[h] = sum_first[h] + first[at]
                sum_second[h] = sum_second[h] + (second[at] - first[at])
    for h in range(count):
        residue_grad_ref[h * tile : (h + 1) * tile, :] = sum_first[h]
        decay_grad_ref[h * tile : (h + 1) * tile, :] = -weigh[h] * sum_second[h]
    empty(made, out_ref, place_ref[0])


def conv_call(kernel, place, arrays, results, scratch, flops):
    channels = arrays[0].shape[-1]
    lanes = min(channels, 128)

    def spec(shape):
        lead = len(shape) - 1
        return pl.BlockSpec(shape[:-1] + (lanes,), lambda i, *_: (0,) * lead + (i,))

    return pl.pallas_call(
        kernel,
        out_shape=results,
        grid_spec=pltpu.PrefetchScalarGridSpec(
            num_scalar_prefetch=1,
            grid=(channels // lanes,),
            in_specs=[spec(a.shape) for a in arrays],
            out_specs=[spec(r.shape) for r in results],
            scratch_shapes=[pltpu.VMEM(s + (lanes,), wide) for s in scratch],
        ),
        compiler_params=pltpu.CompilerParams(
            dimension_semantics=("arbitrary",), vmem_limit_bytes=56 << 20
        ),
        cost_estimate=pl.CostEstimate(
            flops=flops, transcendentals=0, bytes_accessed=sum(a.size * 4 for a in arrays)
        ),
    )(place, *arrays)


def sizes(signal, poles):
    groups, parts, inner, length, channels = signal.shape
    return groups * inner, parts * length, channels, signal.size * poles


def states_of(place, signal, decay):
    seqs, length, channels, work = sizes(signal, decay.shape[0])
    shape = jax.ShapeDtypeStruct((seqs, decay.shape[0], channels), wide)
    return conv_call(states_kernel, place, [signal, decay], [shape], [(seqs, length)], 2 * work)[0]


def forward_of(place, signal, decay, residue, start):
    seqs, length, channels, work = sizes(signal, decay.shape[0])
    return conv_call(
        forward_kernel,
        place,
        [signal, decay, residue, start],
        [jax.ShapeDtypeStruct(signal.shape, low)],
        [(seqs, length), (seqs, tile * tile), (seqs, length)],
        4 * work,
    )[0]


def later_of(place, signal, decay):
    seqs, length, channels, work = sizes(signal, decay.shape[0])
    shape = jax.ShapeDtypeStruct((seqs, decay.shape[0], channels), wide)
    return conv_call(later_kernel, place, [signal, decay], [shape], [(seqs, length)], 2 * work)[0]


def backward_of(place, signal, grad, decay, residue, start, end):
    poles = decay.shape[0]
    seqs, length, channels, work = sizes(signal, poles)
    shape = jax.ShapeDtypeStruct(decay.shape, wide)
    group = min(seqs, 4)
    return conv_call(
        backward_kernel,
        place,
        [signal, grad, decay, residue, start, end],
        [jax.ShapeDtypeStruct(signal.shape, low), shape, shape],
        [
            (seqs, length),
            (seqs, length),
            (group, tile * tile),
            (seqs, length),
            (group, length * poles),
        ],
        12 * work,
    )


def rms_scale(values):
    return lax.rsqrt(jnp.mean(values * values, axis=-1, keepdims=True) + epsilon)


def norm_back(values, scale, gain, grad_normed):
    grad_gain = jnp.sum(grad_normed * values * scale, axis=(0, 1))
    scaled = grad_normed * gain
    grad_values = scale * scaled - values * scale * scale * scale * jnp.mean(
        scaled * values, axis=-1, keepdims=True
    )
    return (grad_values, grad_gain)


def dot(a, b, kind=wide):
    return jnp.dot(a, b, preferred_element_type=wide).astype(kind)


def dot_t(a, b, kind=wide):
    return lax.dot_general(a, b, (((1,), (1,)), ((), ())), preferred_element_type=wide).astype(kind)


def dot_w(a, b):
    return lax.dot_general(a, b, (((0,), (0,)), ((), ())), preferred_element_type=wide).astype(low)


def body(
    tokens,
    lengths,
    norm_gain,
    in_weight,
    conv_taps,
    filter_residue,
    filter_decay,
    out_weight,
    feed_gain,
    gate_weight,
    up_weight,
    down_weight,
    cotangent,
):
    spread, ycount = lax.axis_size("x"), lax.axis_size("y")
    batch, local, width = tokens.shape
    place = lax.axis_index("z") * spread + lax.axis_index("x")
    position = place * local + jnp.arange(local)
    mask = (position[None, :] < lengths[:, None]).astype(wide)[..., None]
    block = spread * local

    count = 3 * depth
    extra = 8
    line = Line(lax.axis_index("c"))
    run = line.run

    def stacked(value, got):
        return jnp.stack([value] + got)

    w_out = lax.all_gather(run(out_block, out_weight), "z", axis=0, tiled=True)
    in_got = column_moves(run(lambda w: column_pieces(w, 3), in_weight))
    last = [(i * spread + spread - 1, (i + 1) * spread) for i in range(depth - 1)]

    def norm_one(values, gain):
        values = values.astype(wide)
        scale = rms_scale(values)
        normed = (values * scale * gain).astype(low)
        return normed, normed[:, local - 2 :], scale

    normed, ending, scale_one = run(norm_one, tokens, norm_gain)
    before = lax.ppermute(ending, ("z", "x"), last)

    def lengthen(values, rows):
        rest = jnp.zeros((batch, extra - 2, width), values.dtype)
        values = jnp.concatenate([values, rows, rest], axis=1)
        return values[: batch // 2], values[batch // 2 :]

    normed_move = Gather(*run(lengthen, normed, before))
    gate_got = column_moves(run(lambda w: column_pieces(w, 1), gate_weight))
    in_block, w_out = run(lambda got, w: (column_block(got), w), in_got, w_out)
    w_in = gather_tile(in_block)
    normed_move.turn(line)
    w_down = gather_tile(run(row_block, down_weight))
    out_move = Gather(*run(lambda w: (w[None, : w.shape[0] // 2], w[None, w.shape[0] // 2 :]), w_out))
    up_got = column_moves(run(lambda w: column_pieces(w, 1), up_weight))
    normed_all = normed_move.end(line)
    out_move.turn(line)

    channels = w_in.shape[1] // 3
    half = channels // 2
    grid = (2 * ycount, spread, batch // 2, local)

    def rank_values(all_taps, all_decay, all_residue):
        return (
            jnp.concatenate(
                [rank_rows(all_taps[:, g * width : (g + 1) * width], 1) for g in range(3)], axis=1
            ),
            rank_rows(all_decay, 0).T,
            rank_rows(all_residue, 0).T,
        )

    taps, decay, residue = run(rank_values, conv_taps, filter_decay, filter_residue)
    opening = (lax.axis_index("x") + jnp.arange(spread)) % spread == 0
    opening = opening[None, :, None, None, None]
    closing = (lax.axis_index("x") + jnp.arange(spread)) % spread == spread - 1
    closing = closing[None, :, None, None, None]

    def project(v, w):
        return dot(v, w, low).reshape(grid[:3] + (local + extra, 3 * channels))

    mixed = run(project, normed_all, w_in)
    out_move.got = run(lambda got: got, out_move.got)

    def extend(value, g):
        own = value[..., g * channels : (g + 1) * channels]
        earlier = jnp.roll(own[:, :, :, local - 2 : local], 1, axis=1)
        earlier = jnp.where(opening, own[:, :, :, local : local + 2], earlier)
        return jnp.concatenate([earlier, own[:, :, :, :local]], axis=3).astype(wide)

    def short_of(value, weights, g):
        longer = extend(value, g)
        own = weights[:, g * channels : (g + 1) * channels]
        return own[0] * longer[:, :, :, 2:] + own[1] * longer[:, :, :, 1:-1] + own[2] * longer[:, :, :, :-2]

    spot = lax.axis_index("x").astype(jnp.int32).reshape(1)

    def multiply(value, weights, rates):
        keys, values = (short_of(value, weights, g) for g in (1, 2))
        product = (keys * values).astype(low)
        return product, states_of(spot, product, rates)

    product, state_end = run(multiply, mixed, taps, decay)
    states = [passed(state_end, "z", k) for k in range(1, depth)]
    w_gate = gather_tile(run(column_block, gate_got))
    out_own = out_move.end(line)
    w_out = [out_own] + moved(out_own, "c", -1)

    def feed_grad(values):
        values = (values.astype(wide) * mask).astype(low)
        return values[: batch // 2], values[batch // 2 :]

    feed_move = Gather(*run(feed_grad, cotangent))

    def combine(parts, rates):
        total = parts[0]
        for k in range(1, depth - 1):
            total = total + jnp.exp(-rates * (k * block)) * parts[k]
        return total

    def convolve(parts, value, weights, signal, rates, amounts):
        start = combine(parts, rates)
        result = forward_of(spot, signal, rates, amounts, start)
        query = short_of(value, weights, 0)
        gated = (query * result.astype(wide)).astype(low)
        slots = gated.reshape(2, ycount, spread, -1, channels)
        return (
            start,
            result,
            gated.reshape(-1, channels),
            [[slots[:, k, i].reshape(-1, channels) for i in range(spread)] for k in range(ycount)],
        )

    start, convolved, gated_all, gated = run(
        convolve, states, mixed, taps, product, decay, residue
    )
    gated_got = swap_slots(gated)
    w_up = gather_tile(run(column_block, up_got))
    feed_move.turn(line)

    def mix(got, weights, values, gain):
        own = jnp.concatenate(
            [g[:, h * half : (h + 1) * half] for h in range(2) for row in got for g in row], axis=1
        )
        mixer = in_order(jnp.stack([dot(own, w) for w in weights]), "c")
        mixer = jnp.concatenate([m for m in mixer], axis=1).reshape(batch, local, width)
        middle = values.astype(wide) + mixer
        scale = rms_scale(middle)
        normed = (middle * scale * gain).astype(low)
        return middle, scale, normed[: batch // 2], normed[batch // 2 :]

    middle, scale_two, first, second = run(mix, gated_got, w_out, tokens, feed_gain)

    two_move = Gather(first, second)
    two_move.turn(line)
    grad_feed_all = feed_move.end(line)
    grad_active = run(dot_t, grad_feed_all, w_down)
    normed_two_all = two_move.end(line)

    def open_gate(v, w, back):
        value = dot(v, w)
        return value, (back * value * jax.nn.sigmoid(value)).astype(low)

    gate, grad_upper = run(open_gate, normed_two_all, w_gate, grad_active)
    up_term = run(dot_w, normed_two_all, grad_upper)
    up_mine = scatter_tile(up_term)

    def activate(v, w, value, back):
        upper = dot(v, w)
        sigma = jax.nn.sigmoid(value)
        return (
            (value * sigma * upper).astype(low),
            (back * upper * sigma * (1.0 + value * (1.0 - sigma))).astype(low),
        )

    active, grad_gate = run(activate, normed_two_all, w_up, gate, grad_active)
    two_back = Scatter(
        run(
            lambda a, b, wa, wb: split_sum((dot_t(a, wa) + dot_t(b, wb)).astype(low)),
            grad_gate,
            grad_upper,
            w_gate,
            w_up,
        )
    )
    gate_mine = scatter_tile(run(dot_w, normed_two_all, grad_gate))
    two_back.turn(line)
    feed_parts = run(lambda a, w: split_sum(dot(a, w, low)), active, w_down)

    def middle_back(rest, values, scale, gain, back, weights):
        grad_normed = Scatter.sum(*rest).reshape(batch, local, width)
        result, grad_gain = norm_back(values, scale, gain, grad_normed)
        result = result + back.astype(wide) * mask
        parts = core_halves(result.astype(low).reshape(-1, width))
        own = sum(dot_t(m, w) for m, w in zip(parts, weights)).astype(low)
        ranks = ycount * spread

        def slot(at):
            pieces = [
                own[:, (h * ranks + at) * half : (h * ranks + at + 1) * half] for h in range(2)
            ]
            return jnp.concatenate(pieces, axis=1)

        slots = [[slot(k * spread + i) for i in range(spread)] for k in range(ycount)]
        rounded = result.astype(low)
        return result, grad_gain, rounded[: batch // 2], rounded[batch // 2 :], slots

    grad_middle, grad_feed_gain, first, second, grad_slots = run(
        middle_back, two_back.rest(), middle, scale_two, feed_gain, cotangent, w_out
    )
    grad_got = swap_slots(grad_slots)
    down_mine = scatter_tile(run(dot_w, active, grad_feed_all))
    mix_move = Gather(first, second)

    def conv_grads(got, result, value, weights, rates):
        grad = jnp.stack([jnp.stack(row) for row in got])
        grad = grad.reshape(ycount, spread, 2, batch // 2, local, channels)
        grad = jnp.moveaxis(grad, 2, 0).reshape(grid + (channels,)).astype(wide)
        grad_query = grad * result.astype(wide)
        grad_conv = (grad * short_of(value, weights, 0)).astype(low)
        return grad_query, grad_conv, later_of(spot, grad_conv, rates)

    grad_query, grad_conv, later_end = run(conv_grads, grad_got, convolved, mixed, taps, decay)
    laters = [passed(later_end, "z", -k) for k in range(1, depth)]
    mix_move.turn(line)

    def short_back(grad, weights):
        head = jnp.roll(grad[:, :, :, :2], -1, axis=1)
        whole = jnp.concatenate([grad, jnp.where(closing, 0.0, head)], axis=3)
        result = (
            weights[0] * whole[:, :, :, :-2]
            + weights[1] * whole[:, :, :, 1:-1]
            + weights[2] * whole[:, :, :, 2:]
        )
        one, two = grad[:, :, :, :1], grad[:, :, :, 1:2]
        earlier = jnp.concatenate([weights[2] * one, weights[1] * one + weights[2] * two], axis=3)
        rest = jnp.zeros(grad.shape[:3] + (extra - 2, grad.shape[-1]), wide)
        result = jnp.concatenate([result, jnp.where(opening, earlier, 0.0), rest], axis=3)
        return result.astype(low).reshape(-1, grad.shape[-1])

    feed_back = Scatter(feed_parts)
    up_parts_got = owner_moves(run(owner_parts, up_mine))
    gate_got = owner_moves(run(owner_parts, gate_mine))

    def conv_back(signal, grad, rates, amounts, begin, ends_later, value, weights):
        later = combine(ends_later, rates)
        grad_product, grad_residue, grad_decay = backward_of(
            spot, signal, grad, rates, amounts, begin, later
        )
        grad_product = grad_product.astype(wide)
        keys, values = (short_of(value, weights, g) for g in (1, 2))
        pair = jnp.concatenate([grad_product * values, grad_product * keys], axis=-1)
        return pair, grad_residue, grad_decay

    grad_pair, grad_residue, grad_decay = run(
        conv_back, product, grad_conv, decay, residue, start, laters, mixed, taps
    )

    mix_move.got = run(lambda got: got, mix_move.got)
    up_held = run(owner_held, up_parts_got)
    up_got = moved(up_held, "y", -1)
    grad_mix_all = mix_move.end(line)
    feed_back.got = run(lambda got: got, feed_back.got)

    def in_back(query, pair, weights, v):
        result = jnp.concatenate(
            [
                short_back(query, weights[:, :channels]),
                short_back(pair, weights[:, channels:]),
            ],
            axis=1,
        )
        return result, dot_w(v, result)

    grad_mixed, in_term = run(in_back, grad_query, grad_pair, taps, normed_all)
    in_mine = scatter_tile(in_term)
    feed_back.turn(line)
    gate_held = run(owner_held, gate_got)
    gate_got = moved(gate_held, "y", -1)
    one_back = Scatter(run(lambda a, w: split_sum(dot_t(a, w, low)), grad_mixed, w_in))
    feed_back.got = run(lambda got: got, feed_back.got)
    out_mine = scatter_tile(run(dot_w, gated_all, grad_mix_all))
    up_held = run(stacked, up_held, up_got)
    up_got = moved(up_held, "c", -1)

    def tap_sums(query, pair, value):
        sums = []
        for g, part in enumerate((query, pair[..., :channels], pair[..., channels:])):
            own = extend(value, g)
            sums += [
                jnp.sum(part * own[:, :, :, 2 - j : local + 2 - j], axis=(0, 1, 2, 3))
                for j in range(3)
            ]
        return jnp.stack(sums)

    grad_taps = run(tap_sums, grad_query, grad_pair, mixed)

    def column_whole(own, got):
        return owner_whole(lax.axis_index("c"), [own] + got, depth)

    small = run(
        lambda a, b, c, gain: jnp.concatenate([a, b, c, gain.reshape(-1, channels)], axis=0),
        grad_residue,
        grad_decay,
        grad_taps,
        grad_feed_gain,
    )
    small_got = moved(small, "c", 1)
    grad_up_weight = run(column_whole, up_held, up_got)
    small = run(lambda v, got: v + sum(got), small, small_got)
    small_got = moved(small, "z", 1)
    gate_held = run(stacked, gate_held, gate_got)
    gate_got = moved(gate_held, "c", -1)
    one_back.turn(line)
    in_got = owner_moves(run(owner_parts, in_mine))
    down_held = run(lambda v: v[None], down_mine)
    down_got = moved(down_held, "y", -1)
    grad_gate_weight = run(column_whole, gate_held, gate_got)
    in_held = run(owner_held, in_got)
    in_got = moved(in_held, "y", -1)

    def normed_sum(rest):
        value = Scatter.sum(*rest).reshape(batch, local + extra, width)
        return value[:, :local], value[:, local : local + 2].astype(low)

    grad_normed, grad_before = run(normed_sum, one_back.rest())
    grad_after = lax.ppermute(grad_before, ("z", "x"), [(j, i) for i, j in last])
    output = run(
        lambda rest, values: (
            mask * (values + Scatter.sum(*rest).reshape(batch, local, width))
        ).astype(low),
        feed_back.rest(),
        middle,
    )
    small = run(lambda v, got: v + sum(got), small, small_got)
    small_got = moved(small, "x", -1)
    small = run(stacked, small, small_got)
    small_got = moved(small, "y", -1)

    def tokens_back(grad, extension, values, scale, gain, back):
        values = values.astype(wide)
        grad = jnp.concatenate(
            [grad[:, : local - 2], grad[:, local - 2 :] + extension.astype(wide)], axis=1
        )
        result, grad_gain = norm_back(values, scale, gain, grad)
        return (result + back).astype(low), grad_gain.reshape(-1, channels)

    grad_tokens, gain_sum = run(
        tokens_back, grad_normed, grad_after, tokens, scale_one, norm_gain, grad_middle
    )
    gain_got = moved(gain_sum, "c", 1)
    in_held = run(stacked, in_held, in_got)
    in_got = moved(in_held, "c", -1)
    poles = decay.shape[0]

    def small_whole(own, got):
        slots = jnp.stack([own] + got)
        rows = 2 * poles + 9
        gain = jnp.sum(slots[:, :, rows:], axis=(0, 1)).reshape(width)
        whole = all_channels(slots[:, :, :rows])
        grad_conv_taps = jnp.concatenate(
            [whole[2 * poles + 3 * g : 2 * poles + 3 * g + 3] for g in range(3)], axis=1
        )
        return gain, grad_conv_taps, whole[:poles].T, whole[poles : 2 * poles].T

    feed_gain_sum, grad_conv_taps, residue_sum, decay_sum = run(small_whole, small, small_got)
    gain_sum = run(lambda v, got: v + sum(got), gain_sum, gain_got)
    gain_got = moved(gain_sum, "z", 1)
    down_held = run(lambda own, got: jnp.concatenate([own] + got), down_held, down_got)
    down_got = moved(down_held, "c", -1)
    out_held = run(lambda v: v[None], out_mine)
    out_got = moved(out_held, "y", -1)
    grad_in_weight = run(
        lambda own, got: owner_whole(lax.axis_index("c"), [own] + got, count), in_held, in_got
    )
    gain_sum = run(lambda v, got: v + sum(got), gain_sum, gain_got)
    gain_got = swap_slots([[gain_sum] * spread] * ycount)

    def rows_whole(own, got):
        whole = in_order(jnp.swapaxes(in_order(jnp.stack([own] + got), "c"), 0, 1), "y")
        return whole.reshape(-1, width).astype(wide)

    grad_down = run(rows_whole, down_held, down_got)
    out_held = run(lambda own, got: jnp.concatenate([own] + got), out_held, out_got)
    out_got = moved(out_held, "c", -1)
    grad_norm_gain = run(lambda got: sum(sum(got, [])).reshape(width), gain_got)

    def out_whole(core, own, got):
        ccount = lax.axis_size("c")
        slots = jnp.stack([own] + got)
        slots = jnp.stack(
            [lax.dynamic_index_in_dim(slots, (j - core) % ccount, 0, False) for j in range(ccount)]
        )
        whole = in_order(jnp.swapaxes(slots, 0, 1), "y")
        return whole.reshape(-1, width).astype(wide)

    grad_out_weight = line.finish(out_whole, out_held, out_got)
    return (
        output,
        grad_tokens,
        grad_norm_gain,
        grad_in_weight,
        grad_conv_taps,
        residue_sum,
        decay_sum,
        grad_out_weight,
        feed_gain_sum,
        grad_gate_weight,
        grad_up_weight,
        grad_down,
    )


def solution(mesh):
    pairs, blocks = mesh.shape["dp"], mesh.shape["seq"]
    devices = mesh.devices.reshape(pairs // cores, cores, depth, blocks // depth)
    inner = Mesh(devices, ("y", "c", "z", "x"))
    dp, seq = ("y", "c"), ("z", "x")
    tokens, rows = P(dp, seq, None), P(seq, None)
    return jax.shard_map(
        body,
        mesh=inner,
        in_specs=(
            tokens,
            P(dp),
            P(),
            rows,
            P(),
            P(),
            P(),
            rows,
            P(),
            rows,
            rows,
            rows,
            tokens,
        ),
        out_specs=(tokens, tokens, P(), rows, P(), P(), P(), rows, P(), rows, rows, rows),
        check_vma=False,
    )
```

```python
import functools

import jax
import jax.numpy as jnp
from jax import lax
from jax.experimental import pallas as pl
from jax.experimental.pallas import tpu as pltpu
from jax.sharding import Mesh, PartitionSpec as P

epsilon = 1e-06
low = jnp.bfloat16
wide = jnp.float32
tile = 8
depth = 4
cores = 2


def turned(value, axis, by):
    length = lax.axis_size(axis)
    return lax.ppermute(value, axis, [(i, (i + by) % length) for i in range(length)])


def passed(value, axis, by):
    length = lax.axis_size(axis)
    pairs = [(i, i + by) for i in range(length) if 0 <= i + by < length]
    return lax.ppermute(value, axis, pairs)


def swap_slots(slots):
    ycount, spread = lax.axis_size("y"), lax.axis_size("x")
    result = []
    for dy in range(ycount):
        line = []
        for dx in range(spread):
            sy, sx = (ycount - dy) % ycount, (spread - dx) % spread
            if sy == 0 and sx == 0:
                line.append(slots[0][0])
                continue
            pairs = [
                (i * spread + j, (i + sy) % ycount * spread + (j + sx) % spread)
                for i in range(ycount)
                for j in range(spread)
            ]
            line.append(lax.ppermute(slots[sy][sx], ("y", "x"), pairs))
        result.append(line)
    return result


class Line:
    def __init__(self, token):
        self.token = token

    def run(self, work, *values):
        values, token = lax.optimization_barrier((values, self.token))
        result, self.token = lax.optimization_barrier((work(*values), token))
        return result

    def finish(self, work, *values):
        values, token = lax.optimization_barrier((values, self.token))
        return work(token, *values)


def moved(value, axis, sign):
    return [turned(value, axis, sign * d) for d in range(1, lax.axis_size(axis))]


class Gather:
    def __init__(self, first, second):
        self.held = (first, second)
        self.got = (moved(first, "x", -1), moved(second, "y", -1))

    def turn(self, line):
        self.held = line.run(
            lambda held, got: tuple(jnp.stack([h] + g) for h, g in zip(held, got)), self.held, self.got
        )
        self.got = (moved(self.held[0], "y", -1), moved(self.held[1], "x", -1))

    def end(self, line):
        def work(held, got):
            first = jnp.stack([held[0]] + got[0])
            second = jnp.swapaxes(jnp.stack([held[1]] + got[1]), 0, 1)
            return jnp.stack([first, second]).reshape(-1, first.shape[-1])

        return line.run(work, self.held, self.got)


def split_sum(partial):
    grid = partial.reshape(2, lax.axis_size("y"), lax.axis_size("x"), -1, partial.shape[-1])
    first = [grid[0][:, d].astype(low) for d in range(grid.shape[2])]
    second = [grid[1][d].astype(low) for d in range(grid.shape[1])]
    return first, second


def add_up(parts, got):
    total = parts[0].astype(wide)
    for g in got:
        total = total + g.astype(wide)
    return total


class Scatter:
    def __init__(self, parts):
        self.parts = parts
        self.send("x", "y")

    def send(self, *axes):
        self.got = [
            [turned(p, axis, d + 1) for d, p in enumerate(part[1:])]
            for part, axis in zip(self.parts, axes)
        ]

    def turn(self, line):
        def work(parts, got):
            result = []
            for part, g in zip(parts, got):
                total = add_up(part, g).astype(low)
                result.append([total[d] for d in range(total.shape[0])])
            return result

        self.parts = line.run(work, self.parts, self.got)
        self.send("y", "x")

    def rest(self):
        return self.parts, self.got

    @staticmethod
    def sum(parts, got):
        return jnp.stack([add_up(part, g) for part, g in zip(parts, got)])


def pick_kernel(count, part, stride, start_ref, source, *refs):
    targets, sems = refs[:-1], refs[-1]
    copies = []
    for d, target in enumerate(targets):
        for k in range(count):
            at = pl.multiple_of((k * stride + start_ref[d]) * part, part)
            copies.append(
                pltpu.make_async_copy(
                    source.at[:, pl.ds(at, part)],
                    target.at[:, k * part : (k + 1) * part],
                    sems.at[d * count + k],
                )
            )
    for copy in copies:
        copy.start()
    for copy in copies:
        copy.wait()


def column_pieces(weight, groups):
    spread, ycount = lax.axis_size("x"), lax.axis_size("y")
    rows = weight.shape[0]
    count = groups * depth
    part = weight.shape[1] // (count * spread * ycount)
    starts = [
        (lax.axis_index("x") + d) % spread * ycount + lax.axis_index("y") for d in range(spread)
    ]
    if part % 128 == 0:
        return pl.pallas_call(
            functools.partial(pick_kernel, count, part, spread * ycount),
            out_shape=[jax.ShapeDtypeStruct((rows, count * part), weight.dtype)] * spread,
            grid_spec=pltpu.PrefetchScalarGridSpec(
                num_scalar_prefetch=1,
                in_specs=[pl.BlockSpec(memory_space=pl.ANY)],
                out_specs=[pl.BlockSpec(memory_space=pltpu.VMEM)] * spread,
                scratch_shapes=[pltpu.SemaphoreType.DMA((count * spread,))],
            ),
            cost_estimate=pl.CostEstimate(
                flops=0, transcendentals=0, bytes_accessed=4 * rows * count * part * spread
            ),
        )(jnp.stack(starts).astype(jnp.int32), weight)
    return [
        jnp.concatenate(
            [
                lax.dynamic_slice_in_dim(weight, (k * spread * ycount + start) * part, part, 1)
                for k in range(count)
            ],
            axis=1,
        )
        for start in starts
    ]


def column_moves(pieces):
    spread, ccount = lax.axis_size("x"), lax.axis_size("c")
    share = spread // ccount
    got = [pieces[0]]
    for d in range(1, spread):
        pairs = [
            (i // share * spread + i, i // share * spread + (i + d) % spread) for i in range(spread)
        ]
        got.append(lax.ppermute(pieces[d], ("c", "x"), pairs))
    return got


def column_block(got):
    spread, ccount = lax.axis_size("x"), lax.axis_size("c")
    share = spread // ccount
    place, core = lax.axis_index("x"), lax.axis_index("c")
    got = jnp.stack(got)
    return jnp.concatenate(
        [
            lax.dynamic_index_in_dim(got, (place - core * share - j) % spread, 0, False)
            for j in range(share)
        ]
    )


def row_block(weight):
    ycount, ccount = lax.axis_size("y"), lax.axis_size("c")
    part = weight.shape[0] // (ycount * ccount)
    pair = lax.axis_index("y") * ccount + lax.axis_index("c")
    return lax.dynamic_slice_in_dim(weight, pair * part, part, 0)


def core_halves(value):
    ccount = lax.axis_size("c")
    width = value.shape[1] // ccount
    core = lax.axis_index("c")
    return [
        lax.dynamic_slice_in_dim(value, (core + d) % ccount * width, width, 1)
        for d in range(ccount)
    ]


def out_block(weight):
    part = weight.shape[0] // lax.axis_size("y")
    rows = lax.dynamic_slice_in_dim(weight, lax.axis_index("y") * part, part, 0)
    return core_halves(rows)[0]


def gather_tile(block):
    return lax.all_gather(block, ("z", "c"), axis=0, tiled=True)


def scatter_tile(term):
    return lax.psum_scatter(term, ("z", "c"), scatter_dimension=0, tiled=True)


def owner_parts(mine):
    spread, ccount = lax.axis_size("x"), lax.axis_size("c")
    share = spread // ccount
    place, core = lax.axis_index("x"), lax.axis_index("c")
    parts = mine.reshape(share, -1, mine.shape[-1])
    return [
        lax.dynamic_index_in_dim(
            parts, jnp.clip((place + d) % spread - core * share, 0, share - 1), 0, False
        )
        for d in range(spread)
    ]


def owner_moves(parts):
    spread, ccount = lax.axis_size("x"), lax.axis_size("c")
    share = spread // ccount
    got = [parts[0]]
    for d in range(1, spread):
        pairs = [
            ((i + d) % spread // share * spread + i, i // share * spread + (i + d) % spread)
            for i in range(spread)
        ]
        got.append(lax.ppermute(parts[d], ("c", "x"), pairs))
    return got


def owner_held(got):
    spread, ccount = lax.axis_size("x"), lax.axis_size("c")
    share = spread // ccount
    place, core = lax.axis_index("x"), lax.axis_index("c")
    got = jnp.stack(got)
    return jnp.stack(
        [
            lax.dynamic_index_in_dim(got, (place - core * share - j) % spread, 0, False)
            for j in range(share)
        ]
    )


def assemble_kernel(count, width, order_ref, *refs):
    sources, target = refs[:-1], refs[-1]
    part = width // count
    ranks = order_ref.shape[0] // 2
    for r in range(ranks):
        core, slot = order_ref[2 * r], order_ref[2 * r + 1]
        value = sources[0][slot]
        for c in range(1, len(sources)):
            value = jnp.where(core == c, sources[c][slot], value)
        value = value.astype(wide)
        for at in range(count):
            start = (at * ranks + r) * part
            target[:, start : start + part] = value[:, at * part : (at + 1) * part]


def owner_whole(core, sources, count):
    spread, ccount, ycount = lax.axis_size("x"), lax.axis_size("c"), lax.axis_size("y")
    share = spread // ccount
    yplace = lax.axis_index("y")
    order = []
    for i in range(spread):
        for k in range(ycount):
            order += [(i // share - core) % ccount, (k - yplace) % ycount * share + i % share]
    sources = [v.reshape((-1,) + v.shape[2:]) for v in sources]
    held, rows, width = sources[0].shape
    block = min(rows, 64)
    return pl.pallas_call(
        functools.partial(assemble_kernel, count, width),
        out_shape=jax.ShapeDtypeStruct((rows, width * spread * ycount), wide),
        grid_spec=pltpu.PrefetchScalarGridSpec(
            num_scalar_prefetch=1,
            grid=(rows // block,),
            in_specs=[pl.BlockSpec((held, block, width), lambda i, order: (0, i, 0))]
            * len(sources),
            out_specs=pl.BlockSpec((block, width * spread * ycount), lambda i, order: (i, 0)),
        ),
        compiler_params=pltpu.CompilerParams(vmem_limit_bytes=56 << 20),
        cost_estimate=pl.CostEstimate(
            flops=0, transcendentals=0, bytes_accessed=6 * rows * width * spread * ycount
        ),
    )(jnp.stack(order).astype(jnp.int32), *sources)


def in_order(slots, axis):
    length = lax.axis_size(axis)
    place = lax.axis_index(axis)
    return jnp.stack(
        [lax.dynamic_index_in_dim(slots, (j - place) % length, 0, False) for j in range(length)]
    )


def rank_rows(values, axis):
    spread, ycount = lax.axis_size("x"), lax.axis_size("y")
    part = values.shape[axis] // (depth * spread * ycount)
    place = lax.axis_index("x") * ycount + lax.axis_index("y")
    return jnp.concatenate(
        [
            lax.dynamic_slice_in_dim(values, (k * spread * ycount + place) * part, part, axis)
            for k in range(depth)
        ],
        axis=axis,
    )


def all_channels(slots):
    whole = in_order(slots, "y")
    whole = in_order(jnp.swapaxes(whole, 0, 1), "x")
    spread, ycount, rows = whole.shape[:3]
    whole = whole.reshape(spread, ycount, rows, depth, -1)
    return jnp.transpose(whole, (2, 3, 0, 1, 4)).reshape(rows, -1)


def fill(source, target, place):
    groups, parts, inner, length = source.shape[:4]
    for j in range(parts):
        slot = lax.rem(j + parts - place, parts)
        for g in range(groups):
            for b in range(inner):
                target[g * inner + b, j * length : (j + 1) * length, :] = source[g, slot, b].astype(
                    wide
                )


def empty(source, target, place):
    groups, parts, inner, length = target.shape[:4]
    for j in range(parts):
        slot = lax.rem(j + parts - place, parts)
        for g in range(groups):
            for b in range(inner):
                target[g, slot, b] = source[g * inner + b, j * length : (j + 1) * length, :].astype(
                    low
                )


def halves(ref):
    return [ref[k * tile : (k + 1) * tile, :] for k in range(ref.shape[0] // tile)]


def row_of(ref, seq, at):
    return ref[seq, pl.ds(at, tile, stride=0), :]


def states_kernel(place_ref, signal_ref, decay_ref, state_ref, held):
    fill(signal_ref, held, place_ref[0])
    seqs, length, lanes = held.shape
    keep = [jnp.exp(-d) for d in halves(decay_ref)]
    count = len(keep)

    def step(i, carry):
        state = list(carry)
        for k in range(tile):
            for n in range(seqs):
                new = row_of(held, n, i * tile + k)
                for h in range(count):
                    at = n * count + h
                    state[at] = keep[h] * state[at] + new
        return tuple(state)

    zero = jnp.zeros((tile, lanes), wide)
    state = lax.fori_loop(0, length // tile, step, tuple(zero for _ in range(seqs * count)))
    for n in range(seqs):
        for h in range(count):
            state_ref[n, h * tile : (h + 1) * tile, :] = state[n * count + h]


def forward_kernel(place_ref, signal_ref, decay_ref, residue_ref, start_ref, out_ref, held, terms, made):
    fill(signal_ref, held, place_ref[0])
    seqs, length, lanes = held.shape
    keep = [jnp.exp(-d) for d in halves(decay_ref)]
    weigh = halves(residue_ref)
    count = len(keep)

    def step(i, carry):
        state = list(carry)
        for k in range(tile):
            for n in range(seqs):
                new = row_of(held, n, i * tile + k)
                total = None
                for h in range(count):
                    at = n * count + h
                    state[at] = keep[h] * state[at] + new
                    term = weigh[h] * state[at]
                    total = term if total is None else total + term
                terms[n, k * tile : (k + 1) * tile, :] = total
        for n in range(seqs):
            result = terms[n, pl.ds(0, tile, stride=tile), :]
            for p in range(1, tile):
                result = result + terms[n, pl.ds(p, tile, stride=tile), :]
            made[n, pl.ds(i * tile, tile), :] = result
        return tuple(state)

    start = tuple(
        start_ref[n, h * tile : (h + 1) * tile, :] for n in range(seqs) for h in range(count)
    )
    lax.fori_loop(0, length // tile, step, start)
    empty(made, out_ref, place_ref[0])


def later_kernel(place_ref, signal_ref, decay_ref, state_ref, held):
    fill(signal_ref, held, place_ref[0])
    seqs, length, lanes = held.shape
    keep = [jnp.exp(-d) for d in halves(decay_ref)]
    count = len(keep)

    def step(i, carry):
        state = list(carry)
        base = length - tile - i * tile
        for k in range(tile - 1, -1, -1):
            for n in range(seqs):
                new = row_of(held, n, base + k)
                for h in range(count):
                    at = n * count + h
                    state[at] = keep[h] * state[at] + new
        return tuple(state)

    zero = jnp.zeros((tile, lanes), wide)
    state = lax.fori_loop(0, length // tile, step, tuple(zero for _ in range(seqs * count)))
    for n in range(seqs):
        for h in range(count):
            state_ref[n, h * tile : (h + 1) * tile, :] = state[n * count + h]


def backward_kernel(
    place_ref,
    signal_ref,
    grad_ref,
    decay_ref,
    residue_ref,
    start_ref,
    end_ref,
    out_ref,
    residue_grad_ref,
    decay_grad_ref,
    held,
    grads,
    terms,
    made,
    later,
):
    fill(signal_ref, held, place_ref[0])
    fill(grad_ref, grads, place_ref[0])
    seqs, length, lanes = held.shape
    keep = [jnp.exp(-d) for d in halves(decay_ref)]
    weigh = halves(residue_ref)
    count = len(keep)
    group = later.shape[0]
    zero = jnp.zeros((tile, lanes), wide)
    none = tuple(zero for _ in range(group * count))
    sum_first = [zero] * count
    sum_second = [zero] * count
    for base_seq in range(0, seqs, group):

        def load(ref):
            return tuple(
                ref[base_seq + n, h * tile : (h + 1) * tile, :]
                for n in range(group)
                for h in range(count)
            )

        def back_step(i, carry):
            state, first = [list(v) for v in carry]
            base = length - tile - i * tile
            for k in range(tile - 1, -1, -1):
                for n in range(group):
                    back = row_of(grads, base_seq + n, base + k)
                    new = row_of(held, base_seq + n, base + k)
                    total = None
                    for h in range(count):
                        at = n * count + h
                        state[at] = keep[h] * state[at] + back
                        first[at] = first[at] + new * state[at]
                        later[n, pl.ds(((base + k) * count + h) * tile, tile), :] = state[at]
                        term = weigh[h] * state[at]
                        total = term if total is None else total + term
                    terms[n, k * tile : (k + 1) * tile, :] = total
            for n in range(group):
                result = terms[n, pl.ds(0, tile, stride=tile), :]
                for p in range(1, tile):
                    result = result + terms[n, pl.ds(p, tile, stride=tile), :]
                made[base_seq + n, pl.ds(base, tile), :] = result
            return tuple(state), tuple(first)

        _, first = lax.fori_loop(0, length // tile, back_step, (load(end_ref), none))

        def ahead(i, carry):
            state, second = [list(v) for v in carry]
            for k in range(tile):
                for n in range(group):
                    new = row_of(held, base_seq + n, i * tile + k)
                    for h in range(count):
                        at = n * count + h
                        state[at] = keep[h] * state[at] + new
                        other = later[n, pl.ds(((i * tile + k) * count + h) * tile, tile), :]
                        second[at] = second[at] + state[at] * other
            return tuple(state), tuple(second)

        _, second = lax.fori_loop(0, length // tile, ahead, (load(start_ref), none))
        for n in range(group):
            for h in range(count):
                at = n * count + h
                sum_first[h] = sum_first[h] + first[at]
                sum_second[h] = sum_second[h] + (second[at] - first[at])
    for h in range(count):
        residue_grad_ref[h * tile : (h + 1) * tile, :] = sum_first[h]
        decay_grad_ref[h * tile : (h + 1) * tile, :] = -weigh[h] * sum_second[h]
    empty(made, out_ref, place_ref[0])


def conv_call(kernel, place, arrays, results, scratch, flops):
    channels = arrays[0].shape[-1]
    lanes = min(channels, 128)

    def spec(shape):
        lead = len(shape) - 1
        return pl.BlockSpec(shape[:-1] + (lanes,), lambda i, *_: (0,) * lead + (i,))

    return pl.pallas_call(
        kernel,
        out_shape=results,
        grid_spec=pltpu.PrefetchScalarGridSpec(
            num_scalar_prefetch=1,
            grid=(channels // lanes,),
            in_specs=[spec(a.shape) for a in arrays],
            out_specs=[spec(r.shape) for r in results],
            scratch_shapes=[pltpu.VMEM(s + (lanes,), wide) for s in scratch],
        ),
        compiler_params=pltpu.CompilerParams(
            dimension_semantics=("arbitrary",), vmem_limit_bytes=56 << 20
        ),
        cost_estimate=pl.CostEstimate(
            flops=flops, transcendentals=0, bytes_accessed=sum(a.size * 4 for a in arrays)
        ),
    )(place, *arrays)


def sizes(signal, poles):
    groups, parts, inner, length, channels = signal.shape
    return groups * inner, parts * length, channels, signal.size * poles


def states_of(place, signal, decay):
    seqs, length, channels, work = sizes(signal, decay.shape[0])
    shape = jax.ShapeDtypeStruct((seqs, decay.shape[0], channels), wide)
    return conv_call(states_kernel, place, [signal, decay], [shape], [(seqs, length)], 2 * work)[0]


def forward_of(place, signal, decay, residue, start):
    seqs, length, channels, work = sizes(signal, decay.shape[0])
    return conv_call(
        forward_kernel,
        place,
        [signal, decay, residue, start],
        [jax.ShapeDtypeStruct(signal.shape, low)],
        [(seqs, length), (seqs, tile * tile), (seqs, length)],
        4 * work,
    )[0]


def later_of(place, signal, decay):
    seqs, length, channels, work = sizes(signal, decay.shape[0])
    shape = jax.ShapeDtypeStruct((seqs, decay.shape[0], channels), wide)
    return conv_call(later_kernel, place, [signal, decay], [shape], [(seqs, length)], 2 * work)[0]


def backward_of(place, signal, grad, decay, residue, start, end):
    poles = decay.shape[0]
    seqs, length, channels, work = sizes(signal, poles)
    shape = jax.ShapeDtypeStruct(decay.shape, wide)
    group = min(seqs, 4)
    return conv_call(
        backward_kernel,
        place,
        [signal, grad, decay, residue, start, end],
        [jax.ShapeDtypeStruct(signal.shape, low), shape, shape],
        [
            (seqs, length),
            (seqs, length),
            (group, tile * tile),
            (seqs, length),
            (group, length * poles),
        ],
        12 * work,
    )


def rms_scale(values):
    return lax.rsqrt(jnp.mean(values * values, axis=-1, keepdims=True) + epsilon)


def norm_back(values, scale, gain, grad_normed):
    grad_gain = jnp.sum(grad_normed * values * scale, axis=(0, 1))
    scaled = grad_normed * gain
    grad_values = scale * scaled - values * scale * scale * scale * jnp.mean(
        scaled * values, axis=-1, keepdims=True
    )
    return (grad_values, grad_gain)


def dot(a, b, kind=wide):
    return jnp.dot(a, b, preferred_element_type=wide).astype(kind)


def dot_t(a, b, kind=wide):
    return lax.dot_general(a, b, (((1,), (1,)), ((), ())), preferred_element_type=wide).astype(kind)


def dot_w(a, b):
    return lax.dot_general(a, b, (((0,), (0,)), ((), ())), preferred_element_type=wide).astype(low)


def body(
    tokens,
    lengths,
    norm_gain,
    in_weight,
    conv_taps,
    filter_residue,
    filter_decay,
    out_weight,
    feed_gain,
    gate_weight,
    up_weight,
    down_weight,
    cotangent,
):
    spread, ycount = lax.axis_size("x"), lax.axis_size("y")
    batch, local, width = tokens.shape
    place = lax.axis_index("z") * spread + lax.axis_index("x")
    position = place * local + jnp.arange(local)
    mask = (position[None, :] < lengths[:, None]).astype(wide)[..., None]
    block = spread * local

    count = 3 * depth
    extra = 8
    line = Line(lax.axis_index("c"))
    run = line.run

    def stacked(value, got):
        return jnp.stack([value] + got)

    w_out = lax.all_gather(run(out_block, out_weight), "z", axis=0, tiled=True)
    in_got = column_moves(run(lambda w: column_pieces(w, 3), in_weight))
    last = [(i * spread + spread - 1, (i + 1) * spread) for i in range(depth - 1)]

    def norm_one(values, gain):
        values = values.astype(wide)
        scale = rms_scale(values)
        normed = (values * scale * gain).astype(low)
        return normed, normed[:, local - 2 :], scale

    normed, ending, scale_one = run(norm_one, tokens, norm_gain)
    before = lax.ppermute(ending, ("z", "x"), last)

    def lengthen(values, rows):
        rest = jnp.zeros((batch, extra - 2, width), values.dtype)
        values = jnp.concatenate([values, rows, rest], axis=1)
        return values[: batch // 2], values[batch // 2 :]

    normed_move = Gather(*run(lengthen, normed, before))
    gate_got = column_moves(run(lambda w: column_pieces(w, 1), gate_weight))
    in_block, w_out = run(lambda got, w: (column_block(got), w), in_got, w_out)
    w_in = gather_tile(in_block)
    normed_move.turn(line)
    w_down = gather_tile(run(row_block, down_weight))
    out_move = Gather(*run(lambda w: (w[None, : w.shape[0] // 2], w[None, w.shape[0] // 2 :]), w_out))
    up_got = column_moves(run(lambda w: column_pieces(w, 1), up_weight))
    normed_all = normed_move.end(line)
    out_move.turn(line)

    channels = w_in.shape[1] // 3
    half = channels // 2
    grid = (2 * ycount, spread, batch // 2, local)

    def rank_values(all_taps, all_decay, all_residue):
        return (
            jnp.concatenate(
                [rank_rows(all_taps[:, g * width : (g + 1) * width], 1) for g in range(3)], axis=1
            ),
            rank_rows(all_decay, 0).T,
            rank_rows(all_residue, 0).T,
        )

    taps, decay, residue = run(rank_values, conv_taps, filter_decay, filter_residue)
    opening = (lax.axis_index("x") + jnp.arange(spread)) % spread == 0
    opening = opening[None, :, None, None, None]
    closing = (lax.axis_index("x") + jnp.arange(spread)) % spread == spread - 1
    closing = closing[None, :, None, None, None]

    def project(v, w):
        return dot(v, w, low).reshape(grid[:3] + (local + extra, 3 * channels))

    mixed = run(project, normed_all, w_in)
    out_move.got = run(lambda got: got, out_move.got)

    def extend(value, g):
        own = value[..., g * channels : (g + 1) * channels]
        earlier = jnp.roll(own[:, :, :, local - 2 : local], 1, axis=1)
        earlier = jnp.where(opening, own[:, :, :, local : local + 2], earlier)
        return jnp.concatenate([earlier, own[:, :, :, :local]], axis=3).astype(wide)

    def short_of(value, weights, g):
        longer = extend(value, g)
        own = weights[:, g * channels : (g + 1) * channels]
        return own[0] * longer[:, :, :, 2:] + own[1] * longer[:, :, :, 1:-1] + own[2] * longer[:, :, :, :-2]

    spot = lax.axis_index("x").astype(jnp.int32).reshape(1)

    def multiply(value, weights, rates):
        keys, values = (short_of(value, weights, g) for g in (1, 2))
        product = (keys * values).astype(low)
        return product, states_of(spot, product, rates)

    product, state_end = run(multiply, mixed, taps, decay)
    states = [passed(state_end, "z", k) for k in range(1, depth)]
    w_gate = gather_tile(run(column_block, gate_got))
    out_own = out_move.end(line)
    w_out = [out_own] + moved(out_own, "c", -1)

    def feed_grad(values):
        values = (values.astype(wide) * mask).astype(low)
        return values[: batch // 2], values[batch // 2 :]

    feed_move = Gather(*run(feed_grad, cotangent))

    def combine(parts, rates):
        total = parts[0]
        for k in range(1, depth - 1):
            total = total + jnp.exp(-rates * (k * block)) * parts[k]
        return total

    def convolve(parts, value, weights, signal, rates, amounts):
        start = combine(parts, rates)
        result = forward_of(spot, signal, rates, amounts, start)
        query = short_of(value, weights, 0)
        gated = (query * result.astype(wide)).astype(low)
        slots = gated.reshape(2, ycount, spread, -1, channels)
        return (
            start,
            result,
            gated.reshape(-1, channels),
            [[slots[:, k, i].reshape(-1, channels) for i in range(spread)] for k in range(ycount)],
        )

    start, convolved, gated_all, gated = run(
        convolve, states, mixed, taps, product, decay, residue
    )
    gated_got = swap_slots(gated)
    w_up = gather_tile(run(column_block, up_got))
    feed_move.turn(line)

    def mix(got, weights, values, gain):
        own = jnp.concatenate(
            [g[:, h * half : (h + 1) * half] for h in range(2) for row in got for g in row], axis=1
        )
        mixer = in_order(jnp.stack([dot(own, w) for w in weights]), "c")
        mixer = jnp.concatenate([m for m in mixer], axis=1).reshape(batch, local, width)
        middle = values.astype(wide) + mixer
        scale = rms_scale(middle)
        normed = (middle * scale * gain).astype(low)
        return middle, scale, normed[: batch // 2], normed[batch // 2 :]

    middle, scale_two, first, second = run(mix, gated_got, w_out, tokens, feed_gain)

    two_move = Gather(first, second)
    two_move.turn(line)
    grad_feed_all = feed_move.end(line)
    grad_active = run(dot_t, grad_feed_all, w_down)
    normed_two_all = two_move.end(line)

    def open_gate(v, w, back):
        value = dot(v, w)
        return value, (back * value * jax.nn.sigmoid(value)).astype(low)

    gate, grad_upper = run(open_gate, normed_two_all, w_gate, grad_active)
    up_term = run(dot_w, normed_two_all, grad_upper)
    up_mine = scatter_tile(up_term)

    def activate(v, w, value, back):
        upper = dot(v, w)
        sigma = jax.nn.sigmoid(value)
        return (
            (value * sigma * upper).astype(low),
            (back * upper * sigma * (1.0 + value * (1.0 - sigma))).astype(low),
        )

    active, grad_gate = run(activate, normed_two_all, w_up, gate, grad_active)
    two_back = Scatter(
        run(
            lambda a, b, wa, wb: split_sum((dot_t(a, wa) + dot_t(b, wb)).astype(low)),
            grad_gate,
            grad_upper,
            w_gate,
            w_up,
        )
    )
    gate_mine = scatter_tile(run(dot_w, normed_two_all, grad_gate))
    two_back.turn(line)
    feed_parts = run(lambda a, w: split_sum(dot(a, w, low)), active, w_down)

    def middle_back(rest, values, scale, gain, back, weights):
        grad_normed = Scatter.sum(*rest).reshape(batch, local, width)
        result, grad_gain = norm_back(values, scale, gain, grad_normed)
        result = result + back.astype(wide) * mask
        parts = core_halves(result.astype(low).reshape(-1, width))
        own = sum(dot_t(m, w) for m, w in zip(parts, weights)).astype(low)
        ranks = ycount * spread

        def slot(at):
            pieces = [
                own[:, (h * ranks + at) * half : (h * ranks + at + 1) * half] for h in range(2)
            ]
            return jnp.concatenate(pieces, axis=1)

        slots = [[slot(k * spread + i) for i in range(spread)] for k in range(ycount)]
        rounded = result.astype(low)
        return result, grad_gain, rounded[: batch // 2], rounded[batch // 2 :], slots

    grad_middle, grad_feed_gain, first, second, grad_slots = run(
        middle_back, two_back.rest(), middle, scale_two, feed_gain, cotangent, w_out
    )
    grad_got = swap_slots(grad_slots)
    down_mine = scatter_tile(run(dot_w, active, grad_feed_all))
    mix_move = Gather(first, second)

    def conv_grads(got, result, value, weights, rates):
        grad = jnp.stack([jnp.stack(row) for row in got])
        grad = grad.reshape(ycount, spread, 2, batch // 2, local, channels)
        grad = jnp.moveaxis(grad, 2, 0).reshape(grid + (channels,)).astype(wide)
        grad_query = grad * result.astype(wide)
        grad_conv = (grad * short_of(value, weights, 0)).astype(low)
        return grad_query, grad_conv, later_of(spot, grad_conv, rates)

    grad_query, grad_conv, later_end = run(conv_grads, grad_got, convolved, mixed, taps, decay)
    laters = [passed(later_end, "z", -k) for k in range(1, depth)]
    mix_move.turn(line)

    def short_back(grad, weights):
        head = jnp.roll(grad[:, :, :, :2], -1, axis=1)
        whole = jnp.concatenate([grad, jnp.where(closing, 0.0, head)], axis=3)
        result = (
            weights[0] * whole[:, :, :, :-2]
            + weights[1] * whole[:, :, :, 1:-1]
            + weights[2] * whole[:, :, :, 2:]
        )
        one, two = grad[:, :, :, :1], grad[:, :, :, 1:2]
        earlier = jnp.concatenate([weights[2] * one, weights[1] * one + weights[2] * two], axis=3)
        rest = jnp.zeros(grad.shape[:3] + (extra - 2, grad.shape[-1]), wide)
        result = jnp.concatenate([result, jnp.where(opening, earlier, 0.0), rest], axis=3)
        return result.astype(low).reshape(-1, grad.shape[-1])

    feed_back = Scatter(feed_parts)
    up_parts_got = owner_moves(run(owner_parts, up_mine))
    gate_got = owner_moves(run(owner_parts, gate_mine))

    def conv_back(signal, grad, rates, amounts, begin, ends_later, value, weights):
        later = combine(ends_later, rates)
        grad_product, grad_residue, grad_decay = backward_of(
            spot, signal, grad, rates, amounts, begin, later
        )
        grad_product = grad_product.astype(wide)
        keys, values = (short_of(value, weights, g) for g in (1, 2))
        pair = jnp.concatenate([grad_product * values, grad_product * keys], axis=-1)
        return pair, grad_residue, grad_decay

    grad_pair, grad_residue, grad_decay = run(
        conv_back, product, grad_conv, decay, residue, start, laters, mixed, taps
    )

    mix_move.got = run(lambda got: got, mix_move.got)
    up_held = run(owner_held, up_parts_got)
    up_got = moved(up_held, "y", -1)
    grad_mix_all = mix_move.end(line)
    feed_back.got = run(lambda got: got, feed_back.got)

    def in_back(query, pair, weights, v):
        result = jnp.concatenate(
            [
                short_back(query, weights[:, :channels]),
                short_back(pair, weights[:, channels:]),
            ],
            axis=1,
        )
        return result, dot_w(v, result)

    grad_mixed, in_term = run(in_back, grad_query, grad_pair, taps, normed_all)
    in_mine = scatter_tile(in_term)
    feed_back.turn(line)
    gate_held = run(owner_held, gate_got)
    gate_got = moved(gate_held, "y", -1)
    one_back = Scatter(run(lambda a, w: split_sum(dot_t(a, w, low)), grad_mixed, w_in))
    feed_back.got = run(lambda got: got, feed_back.got)
    out_mine = scatter_tile(run(dot_w, gated_all, grad_mix_all))
    up_held = run(stacked, up_held, up_got)
    up_got = moved(up_held, "c", -1)

    def tap_sums(query, pair, value):
        sums = []
        for g, part in enumerate((query, pair[..., :channels], pair[..., channels:])):
            own = extend(value, g)
            sums += [
                jnp.sum(part * own[:, :, :, 2 - j : local + 2 - j], axis=(0, 1, 2, 3))
                for j in range(3)
            ]
        return jnp.stack(sums)

    grad_taps = run(tap_sums, grad_query, grad_pair, mixed)

    def column_whole(own, got):
        return owner_whole(lax.axis_index("c"), [own] + got, depth)

    small = run(
        lambda a, b, c, gain: jnp.concatenate([a, b, c, gain.reshape(-1, channels)], axis=0),
        grad_residue,
        grad_decay,
        grad_taps,
        grad_feed_gain,
    )
    small_got = moved(small, "c", 1)
    grad_up_weight = run(column_whole, up_held, up_got)
    small = run(lambda v, got: v + sum(got), small, small_got)
    small_got = moved(small, "z", 1)
    gate_held = run(stacked, gate_held, gate_got)
    gate_got = moved(gate_held, "c", -1)
    one_back.turn(line)
    down_held = run(lambda v: v[None], down_mine)
    down_got = moved(down_held, "y", -1)
    in_got = owner_moves(run(owner_parts, in_mine))
    grad_gate_weight = run(column_whole, gate_held, gate_got)
    in_held = run(owner_held, in_got)
    in_got = moved(in_held, "y", -1)

    def normed_sum(rest):
        value = Scatter.sum(*rest).reshape(batch, local + extra, width)
        return value[:, :local], value[:, local : local + 2].astype(low)

    grad_normed, grad_before = run(normed_sum, one_back.rest())
    grad_after = lax.ppermute(grad_before, ("z", "x"), [(j, i) for i, j in last])
    output = run(
        lambda rest, values: (
            mask * (values + Scatter.sum(*rest).reshape(batch, local, width))
        ).astype(low),
        feed_back.rest(),
        middle,
    )
    small = run(lambda v, got: v + sum(got), small, small_got)
    small_got = moved(small, "x", -1)
    small = run(stacked, small, small_got)
    small_got = moved(small, "y", -1)

    def tokens_back(grad, extension, values, scale, gain, back):
        values = values.astype(wide)
        grad = jnp.concatenate(
            [grad[:, : local - 2], grad[:, local - 2 :] + extension.astype(wide)], axis=1
        )
        result, grad_gain = norm_back(values, scale, gain, grad)
        return (result + back).astype(low), grad_gain.reshape(-1, channels)

    grad_tokens, gain_sum = run(
        tokens_back, grad_normed, grad_after, tokens, scale_one, norm_gain, grad_middle
    )
    gain_got = moved(gain_sum, "c", 1)
    in_held = run(stacked, in_held, in_got)
    in_got = moved(in_held, "c", -1)
    poles = decay.shape[0]

    def small_whole(own, got):
        slots = jnp.stack([own] + got)
        rows = 2 * poles + 9
        gain = jnp.sum(slots[:, :, rows:], axis=(0, 1)).reshape(width)
        whole = all_channels(slots[:, :, :rows])
        grad_conv_taps = jnp.concatenate(
            [whole[2 * poles + 3 * g : 2 * poles + 3 * g + 3] for g in range(3)], axis=1
        )
        return gain, grad_conv_taps, whole[:poles].T, whole[poles : 2 * poles].T

    feed_gain_sum, grad_conv_taps, residue_sum, decay_sum = run(small_whole, small, small_got)
    gain_sum = run(lambda v, got: v + sum(got), gain_sum, gain_got)
    gain_got = moved(gain_sum, "z", 1)
    down_held = run(lambda own, got: jnp.concatenate([own] + got), down_held, down_got)
    down_got = moved(down_held, "c", -1)
    out_held = run(lambda v: v[None], out_mine)
    out_got = moved(out_held, "y", -1)
    grad_in_weight = run(
        lambda own, got: owner_whole(lax.axis_index("c"), [own] + got, count), in_held, in_got
    )
    gain_sum = run(lambda v, got: v + sum(got), gain_sum, gain_got)
    gain_got = swap_slots([[gain_sum] * spread] * ycount)

    def rows_whole(own, got):
        whole = in_order(jnp.swapaxes(in_order(jnp.stack([own] + got), "c"), 0, 1), "y")
        return whole.reshape(-1, width).astype(wide)

    grad_down = run(rows_whole, down_held, down_got)
    out_held = run(lambda own, got: jnp.concatenate([own] + got), out_held, out_got)
    out_got = moved(out_held, "c", -1)
    grad_norm_gain = run(lambda got: sum(sum(got, [])).reshape(width), gain_got)

    def out_whole(core, own, got):
        ccount = lax.axis_size("c")
        slots = jnp.stack([own] + got)
        slots = jnp.stack(
            [lax.dynamic_index_in_dim(slots, (j - core) % ccount, 0, False) for j in range(ccount)]
        )
        whole = in_order(jnp.swapaxes(slots, 0, 1), "y")
        return whole.reshape(-1, width).astype(wide)

    grad_out_weight = line.finish(out_whole, out_held, out_got)
    return (
        output,
        grad_tokens,
        grad_norm_gain,
        grad_in_weight,
        grad_conv_taps,
        residue_sum,
        decay_sum,
        grad_out_weight,
        feed_gain_sum,
        grad_gate_weight,
        grad_up_weight,
        grad_down,
    )


def solution(mesh):
    pairs, blocks = mesh.shape["dp"], mesh.shape["seq"]
    devices = mesh.devices.reshape(pairs // cores, cores, depth, blocks // depth)
    inner = Mesh(devices, ("y", "c", "z", "x"))
    dp, seq = ("y", "c"), ("z", "x")
    tokens, rows = P(dp, seq, None), P(seq, None)
    return jax.shard_map(
        body,
        mesh=inner,
        in_specs=(
            tokens,
            P(dp),
            P(),
            rows,
            P(),
            P(),
            P(),
            rows,
            P(),
            rows,
            rows,
            rows,
            tokens,
        ),
        out_specs=(tokens, tokens, P(), rows, P(), P(), P(), rows, P(), rows, rows, rows),
        check_vma=False,
    )
```
